32 devices in a mesh: dp: 8 (over y, x, core), head: 4 (over z).
Axes of the slice: x: 2, y: 2, z: 4, core: 2. Of those that a mesh axis runs over, the one named last changes fastest.
Arguments:
- block_input: bfloat16 [16384, 1024], P('dp'), may hold values from -6 to 6
- cotangent: bfloat16 [16384, 1024], P(('dp', 'head')), may hold values from -6 to 6
- expert_ids: int32 [16384, 2], P(('dp', 'head')), may hold values from 0 to 7, all different within a row
- priority: int32 [32, 512], P(('dp', 'head')), may hold values from 0 to 511, each once within a row
- rel_bucket: int32 [1023], replicated, may hold values from 0 to 31, as said below
- norm1_gain: float32 [1024], replicated, may hold values from 0.5 to 1.5
- w_query: bfloat16 [1024, 1024], P(None, 'head'), may hold values from -0.1875 to 0.1875
- w_key: bfloat16 [1024, 1024], P(None, 'head'), may hold values from -0.1875 to 0.1875
- w_value: bfloat16 [1024, 1024], P(None, 'head'), may hold values from -0.1875 to 0.1875
- w_out: bfloat16 [1024, 1024], P('head'), may hold values from -1.5 to 1.5
- pos_bias: float32 [32, 16], P(None, 'head'), may hold values from -4 to 4
- norm2_gain: float32 [1024], replicated, may hold values from 0.5 to 1.5
- w_router: bfloat16 [1024, 8], replicated, may hold values from -0.125 to 0.125
- w_gate: bfloat16 [8, 1024, 2816], P('dp'), may hold values from -0.1875 to 0.1875
- w_up: bfloat16 [8, 1024, 2816], P('dp'), may hold values from -0.1875 to 0.1875
- w_down: bfloat16 [8, 2816, 1024], P('dp'), may hold values from -0.109375 to 0.109375
Outputs:
- output: float32 [16384, 1024], P(('dp', 'head'))
- grad_input: float32 [16384, 1024], P(('dp', 'head'))
- grad_norm1: float32 [1024], replicated
- grad_query_w: float32 [1024, 1024], P(None, 'head')
- grad_key_w: float32 [1024, 1024], P(None, 'head')
- grad_value_w: float32 [1024, 1024], P(None, 'head')
- grad_out_proj: float32 [1024, 1024], P('head')
- grad_pos_bias: float32 [32, 16], P(None, 'head')
- grad_norm2: float32 [1024], replicated
- grad_router: float32 [1024, 8], replicated
- grad_gate_w: float32 [8, 1024, 2816], P('dp', 'head')
- grad_up_w: float32 [8, 1024, 2816], P('dp', 'head')
- grad_down_w: float32 [8, 2816, 1024], P('dp', 'head')
The draws below stay inside these ranges and needn't reach their ends.
Inputs may be any that keep to these rules, and one draw needn't show every extreme that they name: `expert_ids`: the two ids of a row differ. `priority`: each row is a permutation of 0 to 511. `rel_bucket`: entry 511 + d is the bucket of a key d positions after its query; distances under 8 have buckets of their own, buckets never fall as the distance grows on either side, and keys after the query use buckets 16 and above.
All inputs are finite; a program needn't handle non-finite values.
Results may differ from the reference program's by a relative error of at most 0.024.
Values may be sent and summed in bfloat16 or wider, within the bound.
A program may use at most 256 MiB of HBM per device.

```python
import jax
import jax.numpy as jnp
from jax import lax

D = 1024
FF = 2816
HEADS = 16
DH = 64
BUCKETS = 32
LEN = 512
SEQ_DEV = 4
HD = 1024
EXPERTS = 8
TOKENS = 16384
TOK_DEV = 512
CAP = 160
DEVICES = 32


def draw_rel_bucket(key, part):
    steps = jax.random.randint(key, (LEN,), 0, 32)
    rises = (steps == 0).astype(jnp.int32)
    climbed = jnp.cumsum(rises).astype(jnp.int32)
    offsets = jnp.arange(2 * LEN - 1, dtype=jnp.int32) - (LEN - 1)
    reach = jnp.abs(offsets).astype(jnp.int32)
    far = 8 + jnp.minimum(7, climbed[reach] + jnp.where(reach == LEN - 1, 7, 0))
    near = jnp.where(reach < 8, reach, far)
    return (near + jnp.where(offsets > 0, 16, 0)).astype(jnp.int32)


def block_scale(own_key, extent, pieces, least, top_value):
    loudness, own = 1.0, jax.random.fold_in(own_key, 6)
    for axis_at, blocks in pieces:
        steps = jnp.exp(jax.random.uniform(jax.random.fold_in(own, axis_at), (blocks,), jnp.float32, least / len(pieces), top_value / len(pieces)))
        loudness = loudness * jnp.repeat(steps, extent[axis_at] // blocks).reshape([-1 if axis == axis_at else 1 for axis in range(len(extent))])
    return loudness


def picks_of(key, rows, number_of, top, lift):
    order = jax.random.permutation(jax.random.fold_in(key, 1), number_of)
    favour = order
    for power in range(3):
        favour = favour * favour // number_of
    favour = favour * lift // number_of
    chance = jax.random.randint(jax.random.fold_in(key, 2), (rows, number_of), 0, 4096) + favour
    holders = jax.random.permutation(jax.random.fold_in(key, 3), rows)[jnp.arange(number_of) % rows]
    chance = jnp.where(jnp.arange(rows)[:, None] == holders[None, :], 1 << 14, chance)
    score = chance * number_of + jnp.arange(number_of)
    return lax.top_k(score.astype(jnp.int32), top)[1].astype(jnp.int32)


def centred(key, dims, spread, limit, cuts=(), held_as=jnp.bfloat16):
    factor_of = block_scale(key, dims, cuts, -0.22, 0.18) if cuts else 1.0
    values = jax.random.normal(key, dims, jnp.float32) * spread * factor_of
    return jnp.minimum(jnp.maximum(values, -limit), limit).astype(held_as)


def setup_inputs(seed: int = 0) -> dict:
    splits = jax.random.split(jax.random.key(seed), 17)
    return {
        "block_input": centred(splits[0], (TOKENS, D), 1.0, 6.0, ((0, 8),)),
        "cotangent": centred(splits[1], (TOKENS, D), 1.0, 6.0, ((0, 32),)),
        "expert_ids": picks_of(splits[2], TOKENS, EXPERTS, 2, 4096),
        "priority": jax.vmap(lambda own: jax.random.permutation(own, TOK_DEV))(jax.random.split(splits[3], DEVICES)).reshape((DEVICES, TOK_DEV)).astype(jnp.int32),
        "rel_bucket": draw_rel_bucket(jax.random.fold_in(splits[16], 71), 0),
        "norm1_gain": jnp.clip(1.0 + 0.1 * jax.random.normal(splits[5], (D,), jnp.float32), 0.5, 1.5),
        "w_query": centred(splits[6], (D, HD), D ** -0.5, 0.1875, ((1, 4),)),
        "w_key": centred(splits[7], (D, HD), D ** -0.5, 0.1875, ((1, 4),)),
        "w_value": centred(splits[8], (D, HD), D ** -0.5, 0.1875, ((1, 4),)),
        "w_out": centred(splits[9], (HD, D), (D // 64) ** -0.5, 1.5, ((0, 4),)),
        "pos_bias": centred(splits[10], (BUCKETS, HEADS), 1.0, 4.0, ((1, 4),), jnp.float32),
        "norm2_gain": jnp.clip(1.0 + 0.1 * jax.random.normal(splits[11], (D,), jnp.float32), 0.5, 1.5),
        "w_router": centred(splits[12], (D, EXPERTS), 0.022, 0.125),
        "w_gate": centred(splits[13], (EXPERTS, D, FF), D ** -0.5, 0.1875, ((0, 8),)),
        "w_up": centred(splits[14], (EXPERTS, D, FF), D ** -0.5, 0.1875, ((0, 8),)),
        "w_down": centred(splits[15], (EXPERTS, FF, D), FF ** -0.5, 0.109375, ((0, 8),)),
    }


EPS = 1e-06
HIGH = lax.Precision.HIGHEST

@jax.custom_vjp
def low(v):
    return lax.optimization_barrier(v.astype(jnp.bfloat16)).astype(jnp.float32)

@jax.custom_vjp
def low_back(v):
    return v

def low_keep(v):
    return (low(v), None)

def low_pass(kept, grad):
    return (grad,)

def back_keep(v):
    return (v, None)

def back_low(kept, grad):
    return (low(grad),)
low.defvjp(low_keep, low_pass)
low_back.defvjp(back_keep, back_low)

def low_both(value):
    return low(low_back(value))

def rms_norm(value, gain):
    return value * lax.rsqrt(lax.optimization_barrier(jnp.mean(value * value, axis=-1, keepdims=True)) + EPS) * gain

def matmul(left, right):
    return jnp.dot(left, right, precision=HIGH, preferred_element_type=jnp.float32)

def route_slots(chosen, ranks, experts, capacity):
    count = chosen.shape[0]
    keys = jnp.concatenate([ranks, ranks + count]).astype(jnp.int32)
    wanted = jnp.concatenate([chosen[:, 0], chosen[:, 1]]).astype(jnp.int32)
    by_key = jnp.zeros((2 * count,), jnp.int32).at[keys].set(wanted)
    member = (by_key[:, None] == jnp.arange(experts, dtype=jnp.int32)[None, :]).astype(jnp.int32)
    before = jnp.cumsum(member, axis=0).astype(jnp.int32) - member
    rank_key = lax.optimization_barrier(jnp.sum(before * member, axis=1)).astype(jnp.int32)
    place = rank_key[keys]
    dest = jnp.where(place < capacity, wanted * capacity + place, experts * capacity).astype(jnp.int32)
    return jnp.stack([dest[:count], dest[count:]], axis=1)

def attend(query, key, value, bias_full):
    scores = jnp.einsum('sqhd,skhd->shqk', query, key, precision=HIGH) * 0.125 + bias_full[None]
    probs = jax.nn.softmax(low_back(scores), axis=-1)
    return low_both(jnp.einsum('shqk,skhd->sqhd', low(probs), value, precision=HIGH))

def expert(parts):
    routed, gate_w, up_w, down_w = parts
    gate = low_back(matmul(routed, gate_w))
    up_part = low_back(matmul(routed, up_w))
    hidden = low(jax.nn.gelu(gate) * up_part)
    return low_both(matmul(hidden, down_w))

def reference(block_input, cotangent, expert_ids, priority, rel_bucket, norm1_gain, w_query, w_key, w_value, w_out, pos_bias, norm2_gain, w_router, w_gate, w_up, w_down):
    tokens = block_input.shape[0]
    devices = tokens // TOK_DEV
    slots = EXPERTS * CAP
    local_dest = jax.vmap(lambda chosen, ranks: route_slots(chosen, ranks, EXPERTS, CAP))(expert_ids.reshape(devices, TOK_DEV, 2), priority)
    offset = (jnp.arange(devices, dtype=jnp.int32) * slots)[:, None, None]
    dummy = devices * slots
    dest = jnp.where(local_dest < slots, local_dest + offset, dummy).reshape(tokens * 2).astype(jnp.int32)
    positions = jnp.arange(LEN, dtype=jnp.int32)
    table = rel_bucket[(positions[None, :] - positions[:, None] + LEN - 1).astype(jnp.int32)]
    shape = (tokens // (SEQ_DEV * LEN), SEQ_DEV, LEN, HEADS, DH)

    def forward(inputs, gain1, query_w, key_w, value_w, out_w, bias, gain2, router_w, gate_w, up_w, down_w):
        normed = low(rms_norm(inputs, gain1))
        query = low_both(matmul(normed, query_w)).reshape(shape)
        key = low_both(matmul(normed, key_w)).reshape(shape)
        value = low_both(matmul(normed, value_w)).reshape(shape)
        bias_full = jnp.transpose(jnp.take(bias, table, axis=0), (2, 0, 1))

        def block(parts):
            return attend(parts[0], parts[1], parts[2], bias_full)
        attended = lax.map(jax.checkpoint(block), (query, key, value)).reshape(tokens, HEADS * DH)
        mixed = inputs + low_back(matmul(attended, out_w))
        normed2 = low(rms_norm(mixed, gain2))
        logits = matmul(normed2, router_w)
        gates = jax.nn.softmax(jnp.take_along_axis(logits, expert_ids, axis=1), axis=-1)
        rows = jnp.broadcast_to(normed2[:, None, :], (tokens, 2, D)).reshape(tokens * 2, D)
        buffer = jnp.zeros((dummy + 1, D), jnp.float32).at[dest].add(rows)
        routed = low_back(buffer[:dummy]).reshape(devices, EXPERTS, CAP, D)
        routed = jnp.transpose(routed, (1, 0, 2, 3)).reshape(EXPERTS, devices * CAP, D)
        returned = lax.map(jax.checkpoint(expert), (routed, gate_w, up_w, down_w))
        returned = jnp.transpose(returned.reshape(EXPERTS, devices, CAP, D), (1, 0, 2, 3)).reshape(dummy, D)
        returned = jnp.concatenate([returned, jnp.zeros((1, D), jnp.float32)], axis=0)
        picked = returned[dest].reshape(tokens, 2, D)
        return mixed + lax.optimization_barrier(jnp.sum(gates[:, :, None] * picked, axis=1))
    output, pull = jax.vjp(forward, block_input.astype(jnp.float32), norm1_gain.astype(jnp.float32), w_query.astype(jnp.float32), w_key.astype(jnp.float32), w_value.astype(jnp.float32), w_out.astype(jnp.float32), pos_bias.astype(jnp.float32), norm2_gain.astype(jnp.float32), w_router.astype(jnp.float32), w_gate.astype(jnp.float32), w_up.astype(jnp.float32), w_down.astype(jnp.float32))
    grads = pull(cotangent.astype(jnp.float32))
    return (output, grads[0], grads[1], grads[2], grads[3], grads[4], grads[5], grads[6], grads[7], grads[8], grads[9], grads[10], grads[11])
```

```python
import functools

import jax
import jax.numpy as jnp
from jax import lax
from jax.experimental import pallas as pl
from jax.experimental.pallas import tpu as pltpu
from jax.sharding import PartitionSpec as P

EPS = 1e-06
SCALE = 0.125
HIGH = lax.Precision.HIGHEST
TILE = 128
BF = jnp.bfloat16
F32 = jnp.float32
VMEM_LIMIT = 48 << 20


def rms_norm(value, gain):
    return value * lax.rsqrt(jnp.mean(value * value, axis=-1, keepdims=True) + EPS) * gain


def geglu(gate, up_part):
    return jax.nn.gelu(gate) * up_part


def contract(left, right, left_dim, right_dim, precision=None):
    return lax.dot_general(
        left,
        right,
        (((left_dim,), (right_dim,)), ((), ())),
        precision=precision,
        preferred_element_type=jnp.float32,
    )


def route_slots(chosen, ranks, experts, capacity):
    count = chosen.shape[0]
    keys = jnp.concatenate([ranks, ranks + count])
    wanted = jnp.concatenate([chosen[:, 0], chosen[:, 1]])
    smaller = (wanted[:, None] == wanted[None, :]) & (keys[None, :] < keys[:, None])
    place = jnp.sum(smaller.astype(jnp.int32), axis=1)
    dest = jnp.where(place < capacity, wanted * capacity + place, experts * capacity)
    return jnp.stack([dest[:count], dest[count:]], axis=1)


def skew_kernel(line_ref, table_ref):
    heads, rows, cols = table_ref.shape
    row = lax.broadcasted_iota(jnp.int32, (rows, cols), 0)
    for h in range(heads):
        value = jnp.broadcast_to(line_ref[h], (rows, cols))
        shift = 1
        while shift < rows:
            value = jnp.where((row & shift) != 0, pltpu.roll(value, shift, 1), value)
            shift *= 2
        table_ref[h] = value


def unskew_kernel(table_ref, line_ref):
    heads, rows, cols = table_ref.shape
    row = lax.broadcasted_iota(jnp.int32, (rows, cols), 0)
    for h in range(heads):
        value = table_ref[h]
        shift = 1
        while shift < rows:
            value = jnp.where((row & shift) != 0, pltpu.roll(value, cols - shift, 1), value)
            shift *= 2
        line_ref[h] = jnp.sum(value, axis=0, keepdims=True)


def skew(line):
    heads, cols = line.shape
    return pl.pallas_call(
        skew_kernel,
        out_shape=jax.ShapeDtypeStruct((heads, TILE, cols), F32),
        compiler_params=pltpu.CompilerParams(vmem_limit_bytes=VMEM_LIMIT),
        name="skew",
    )(line[:, None, :])


def unskew(table):
    heads, _, cols = table.shape
    return pl.pallas_call(
        unskew_kernel,
        out_shape=jax.ShapeDtypeStruct((heads, 1, cols), F32),
        compiler_params=pltpu.CompilerParams(vmem_limit_bytes=VMEM_LIMIT),
        name="unskew",
    )(table)[:, 0]


def lanes_of(shape, half, part):
    lane = lax.broadcasted_iota(jnp.int32, shape, 1)
    return (lane >= half) if part else (lane < half)


def attend_fwd_kernel(seq_ref, q_ref, k_ref, v_ref, table_ref, out_ref, probs_ref, acc_ref):
    del seq_ref
    length, lanes = q_ref.shape
    half = lanes // 2
    chunk = 2 * TILE
    key = k_ref[...]
    value_t = v_ref[...].T
    for part in range(2):
        query = jnp.where(lanes_of((length, lanes), half, part), q_ref[...] * SCALE, 0).astype(BF)
        for c in range(length // chunk):
            cols = slice(c * chunk, (c + 1) * chunk)
            scores = contract(key, query[cols], 1, 1)
            pieces = []
            for kb in range(length // TILE):
                at = length - TILE * kb + chunk * c
                pieces.append(
                    scores[kb * TILE : (kb + 1) * TILE] + table_ref[part, :, at : at + chunk]
                )
            scores = jnp.concatenate(pieces, axis=0)
            top = jnp.max(scores, axis=0, keepdims=True)
            shifted = jnp.exp(scores - top)
            total = jnp.sum(shifted, axis=0, keepdims=True)
            probs = (shifted * (1.0 / total)).astype(BF)
            probs_ref[part, :, cols] = probs
            acc_ref[part * half : (part + 1) * half, cols] = jnp.dot(
                value_t[part * half : (part + 1) * half], probs, preferred_element_type=F32
            )
    out_ref[...] = acc_ref[...].T.astype(BF)


def attend_fwd(seq, qkv, table, length):
    heads, _, width = table.shape
    columns = qkv.shape[1] // 3
    pairs = heads // 2
    lanes = columns // pairs
    spec = [
        pl.BlockSpec((length, lanes), lambda p, s, j=j: (s[0], j * pairs + p)) for j in range(3)
    ]
    return pl.pallas_call(
        attend_fwd_kernel,
        out_shape=(
            jax.ShapeDtypeStruct((length, columns), BF),
            jax.ShapeDtypeStruct((heads, length, length), BF),
        ),
        grid_spec=pltpu.PrefetchScalarGridSpec(
            num_scalar_prefetch=1,
            grid=(pairs,),
            in_specs=spec + [pl.BlockSpec((2, TILE, width), lambda p, s: (p, 0, 0))],
            out_specs=[
                pl.BlockSpec((length, lanes), lambda p, s: (0, p)),
                pl.BlockSpec((2, length, length), lambda p, s: (p, 0, 0)),
            ],
            scratch_shapes=[pltpu.VMEM((lanes, length), F32)],
        ),
        compiler_params=pltpu.CompilerParams(vmem_limit_bytes=VMEM_LIMIT),
        cost_estimate=pl.CostEstimate(
            flops=heads * 8 * length * length * lanes,
            bytes_accessed=heads * length * length * 2 + 8 * length * columns,
            transcendentals=heads * length * length,
        ),
        name="attend_fwd",
    )(seq, qkv, qkv, qkv, table)


def attend_bwd_kernel(
    seq_ref, q_ref, k_ref, v_ref, grad_ref, probs_ref, sums_in_ref, out_ref, sums_ref, acc_ref
):
    del seq_ref
    length, lanes = q_ref.shape
    half = lanes // 2
    chunk = 2 * TILE
    pair = pl.program_id(0)
    columns = out_ref.shape[1] // 3
    key_t = k_ref[...].T
    value = v_ref[...]
    sums_ref[...] = sums_in_ref[...]
    grad_keys, grad_values = [], []
    for part in range(2):
        mask = lanes_of((length, lanes), half, part)
        grad = jnp.where(mask, grad_ref[...], 0).astype(BF)
        grad_key = jnp.zeros((length, lanes), F32)
        grad_value = jnp.zeros((length, lanes), F32)
        for c in range(length // chunk):
            cols = slice(c * chunk, (c + 1) * chunk)
            grad_probs = contract(value, grad[cols], 1, 1)
            probs_low = probs_ref[part, :, cols]
            probs = probs_low.astype(F32)
            delta = jnp.sum(probs * grad_probs, axis=0, keepdims=True)
            grad_scores = (probs * (grad_probs - delta)).astype(BF)
            grad_value += jnp.dot(probs_low, grad_ref[cols, :], preferred_element_type=F32)
            grad_key += jnp.dot(grad_scores, q_ref[cols, :], preferred_element_type=F32)
            acc_ref[part * half : (part + 1) * half, cols] = jnp.dot(
                key_t[part * half : (part + 1) * half], grad_scores, preferred_element_type=F32
            )
            for kb in range(length // TILE):
                at = length - TILE * kb + chunk * c
                sums_ref[part, :, at : at + chunk] += grad_scores[
                    kb * TILE : (kb + 1) * TILE
                ].astype(F32)
        grad_keys.append(grad_key)
        grad_values.append(grad_value)
    first = lanes_of((length, lanes), half, 0)
    at = pl.multiple_of(pair * lanes, lanes)
    out_ref[:, pl.ds(at, lanes)] = (acc_ref[...].T * SCALE).astype(BF)
    at = pl.multiple_of(columns + pair * lanes, lanes)
    out_ref[:, pl.ds(at, lanes)] = (jnp.where(first, *grad_keys) * SCALE).astype(BF)
    at = pl.multiple_of(2 * columns + pair * lanes, lanes)
    out_ref[:, pl.ds(at, lanes)] = jnp.where(first, *grad_values).astype(BF)


def attend_bwd(seq, qkv, grad, probs, sums, length):
    heads, _, width = sums.shape
    columns = qkv.shape[1] // 3
    pairs = heads // 2
    lanes = columns // pairs
    spec = [
        pl.BlockSpec((length, lanes), lambda p, s, j=j: (s[0], j * pairs + p)) for j in range(3)
    ]
    sums_spec = pl.BlockSpec((2, TILE, width), lambda p, s: (p, 0, 0))
    return pl.pallas_call(
        attend_bwd_kernel,
        out_shape=(
            jax.ShapeDtypeStruct((length, 3 * columns), BF),
            jax.ShapeDtypeStruct(sums.shape, F32),
        ),
        grid_spec=pltpu.PrefetchScalarGridSpec(
            num_scalar_prefetch=1,
            grid=(pairs,),
            in_specs=spec
            + [
                pl.BlockSpec((length, lanes), lambda p, s: (0, p)),
                pl.BlockSpec((2, length, length), lambda p, s: (p, 0, 0)),
                sums_spec,
            ],
            out_specs=[pl.BlockSpec((length, 3 * columns), lambda p, s: (0, 0)), sums_spec],
            scratch_shapes=[pltpu.VMEM((lanes, length), F32)],
        ),
        compiler_params=pltpu.CompilerParams(vmem_limit_bytes=VMEM_LIMIT),
        cost_estimate=pl.CostEstimate(
            flops=heads * 16 * length * length * lanes,
            bytes_accessed=heads * length * length * 2 + 16 * length * columns,
            transcendentals=0,
        ),
        name="attend_bwd",
    )(seq, qkv, qkv, qkv, grad, probs, sums)


def expert_forward(rows, gate_w, up_w, grad_unscaled, slot_gates):
    gate_pre = jnp.dot(rows, gate_w, preferred_element_type=F32)
    up_pre = jnp.dot(rows, up_w, preferred_element_type=F32)
    hidden, pull = jax.vjp(geglu, gate_pre, up_pre)
    grad_gate_pre, grad_up_pre = pull(grad_unscaled * slot_gates)
    return hidden.astype(BF), grad_gate_pre.astype(BF), grad_up_pre.astype(BF)


def body(
    block_input,
    cotangent,
    expert_ids,
    priority,
    rel_bucket,
    norm1_gain,
    w_query,
    w_key,
    w_value,
    w_out,
    pos_bias,
    norm2_gain,
    w_router,
    w_gate,
    w_up,
    w_down,
):
    group_rows, width = block_input.shape
    own_rows = cotangent.shape[0]
    buckets, heads_here = pos_bias.shape
    head_cols = w_query.shape[1]
    length = (rel_bucket.shape[0] + 1) // 2
    sequences = group_rows // length
    experts = w_router.shape[1]
    capacity = 5 * 2 * own_rows // (4 * experts)
    slot_count = experts * capacity
    replicas = lax.axis_size("head")
    groups = lax.axis_size("dp")
    me = lax.axis_index("head")
    far = replicas // 2
    far_perm = [(i, i ^ far) for i in range(replicas)]
    stepwise = own_rows == length and sequences == replicas

    def hop(value, r):
        return lax.ppermute(value, "head", [(i, i ^ r) for i in range(replicas)])

    def exchange(value):
        parts = value.reshape(experts, capacity, -1)
        return lax.all_to_all(parts, "dp", split_axis=0, concat_axis=0, tiled=True).reshape(
            slot_count, -1
        )

    dest = route_slots(expert_ids, priority[0], experts, capacity)
    dest_far = lax.ppermute(dest, "head", far_perm)
    slot_range = jnp.arange(slot_count, dtype=jnp.int32)[None, :]
    picks = [(dest[:, k : k + 1] == slot_range).astype(BF) for k in range(2)]
    both = picks[0] + picks[1]
    both_far = sum((dest_far[:, k : k + 1] == slot_range).astype(BF) for k in range(2))

    down_w, gate_w, up_w = w_down[0], w_gate[0], w_up[0]
    cot_here = exchange(contract(both, cotangent, 0, 0).astype(BF))
    cot_far_own = lax.ppermute(cotangent, "head", far_perm)
    cot_far = exchange(contract(both_far, cot_far_own, 0, 0).astype(BF))
    unscaled_here = contract(cot_here, down_w, 1, 1)
    unscaled_far = contract(cot_far, down_w, 1, 1)

    dp_at = lax.axis_index("dp")
    out_rows = head_cols // groups
    piece = lax.dynamic_slice_in_dim(w_out, dp_at * out_rows, out_rows, 0)
    w_out_all = lax.all_gather(piece, ("head", "dp"), axis=0, tiled=True)
    w_qkv = jnp.concatenate([w_query, w_key, w_value], axis=1)
    qkv_rows = width // groups
    piece = lax.dynamic_slice_in_dim(w_qkv, dp_at * qkv_rows, qkv_rows, 0)
    w_qkv_all = lax.all_gather(piece, ("head", "dp"), axis=0, tiled=True)
    if stepwise:
        order = [me ^ r for r in range(replicas)]
    else:
        order = list(range(replicas))
    w_out_all = w_out_all.reshape(replicas, head_cols, width)
    w_qkv_all = w_qkv_all.reshape(replicas, width, 3 * head_cols)
    w_out_cat = jnp.concatenate(
        [lax.dynamic_index_in_dim(w_out_all, o, 0, keepdims=False) for o in order], axis=0
    )

    inputs_all = block_input.astype(F32)
    normed = rms_norm(inputs_all, norm1_gain).astype(BF)
    qkv = jnp.dot(normed, w_qkv, preferred_element_type=F32).astype(BF)
    line = (rel_bucket[::-1][None, :] == jnp.arange(buckets, dtype=jnp.int32)[:, None]).astype(F32)
    line = jnp.pad(line, ((0, 0), (1, 0)))
    table = skew(contract(pos_bias, line, 0, 0, HIGH))
    kept = {}
    if stepwise:
        blocks = [None] * replicas
        for r in reversed(range(replicas)):
            attended_seq, probs = attend_fwd(order[r].reshape(1), qkv, table, length)
            kept[r] = probs
            blocks[r] = hop(attended_seq, r) if r else attended_seq
    else:
        seqs = []
        for s in range(sequences):
            attended_seq, kept[s] = attend_fwd(jnp.full((1,), s, jnp.int32), qkv, table, length)
            seqs.append(attended_seq)
        attended_all = jnp.concatenate(seqs, axis=0).reshape(replicas, own_rows, head_cols)
        attended_all = lax.all_to_all(attended_all, "head", split_axis=0, concat_axis=0, tiled=True)
        blocks = [attended_all[i] for i in range(replicas)]
    attended = jnp.concatenate(blocks, axis=1)

    branch = jnp.dot(attended, w_out_cat, preferred_element_type=F32)
    start_own = me * own_rows
    inputs_own = lax.dynamic_slice_in_dim(block_input, start_own, own_rows, 0).astype(F32)
    mixed = inputs_own + branch
    normed2_full, norm2_pull = jax.vjp(rms_norm, mixed, norm2_gain)
    normed2 = normed2_full.astype(BF)
    logits = jnp.dot(normed2, w_router, preferred_element_type=F32)
    expert_range = jnp.arange(experts, dtype=jnp.int32)
    chosen = (expert_ids[:, :, None] == expert_range[None, None, :]).astype(F32)
    gates = jax.nn.softmax(jnp.sum(chosen * logits[:, None, :], axis=2), axis=-1)

    def slot_gates_of(places, values):
        terms = sum(
            jnp.where(places[:, k : k + 1] == slot_range, values[:, k : k + 1], 0.0)
            for k in range(2)
        )
        return jnp.sum(terms, axis=0)

    rows_here = exchange(contract(both, normed2, 0, 0).astype(BF))
    gates_here = exchange(slot_gates_of(dest, gates))
    normed2_far = lax.ppermute(normed2, "head", far_perm)
    gates_far_own = lax.ppermute(gates, "head", far_perm)
    rows_far = exchange(contract(both_far, normed2_far, 0, 0).astype(BF))
    gates_far = exchange(slot_gates_of(dest_far, gates_far_own))

    hidden_here, ggp_here, gup_here = expert_forward(
        rows_here, gate_w, up_w, unscaled_here, gates_here
    )
    returned = jnp.dot(hidden_here, down_w, preferred_element_type=F32).astype(BF)
    came_back = exchange(returned)
    grad_routed = (contract(ggp_here, gate_w, 1, 1) + contract(gup_here, up_w, 1, 1)).astype(BF)
    grad_back = exchange(grad_routed)
    hidden_far, ggp_far, gup_far = expert_forward(rows_far, gate_w, up_w, unscaled_far, gates_far)
    scaled_here = (cot_here.astype(F32) * gates_here).astype(BF)
    scaled_far = (cot_far.astype(F32) * gates_far).astype(BF)

    low = me % far
    high = me // far

    def reduced(lefts, rights):
        rows = lefts[0].shape[1] // replicas

        def part(at):
            return sum(
                contract(lax.dynamic_slice_in_dim(left, at * rows, rows, 1), right, 0, 0)
                for left, right in zip(lefts, rights)
            )

        if far == 2:
            sent = hop(part(high * far + (1 - low)).astype(BF), 1)
            return (part(me) + sent.astype(F32))[None]
        whole = jnp.concatenate([part(high * far + i) for i in range(far)], axis=0).astype(BF)
        member = [[h * far + i for i in range(far)] for h in range(2)]
        return lax.psum_scatter(
            whole, "head", scatter_dimension=0, axis_index_groups=member, tiled=True
        ).astype(F32)[None]

    grad_down_w = reduced((hidden_here, hidden_far), (scaled_here, scaled_far))
    grad_gate_w = reduced((rows_here, rows_far), (ggp_here, ggp_far))
    grad_up_w = reduced((rows_here, rows_far), (gup_here, gup_far))

    chosen_rows = [jnp.dot(pick, came_back, preferred_element_type=F32) for pick in picks]
    output = mixed + sum(gates[:, k : k + 1] * chosen_rows[k] for k in range(2))
    grad_output = cotangent.astype(F32)
    grad_gates = jnp.stack([jnp.sum(grad_output * rows, axis=1) for rows in chosen_rows], axis=1)
    grad_normed2 = jnp.dot(both, grad_back, preferred_element_type=F32)
    grad_picked = gates * (grad_gates - jnp.sum(gates * grad_gates, axis=1, keepdims=True))
    grad_logits = jnp.sum(chosen * grad_picked[:, :, None], axis=1)
    grad_normed2 = grad_normed2 + contract(grad_logits, w_router.astype(F32), 1, 1, HIGH)
    grad_router = contract(normed2.astype(F32), grad_logits, 0, 0, HIGH)
    grad_mixed, grad_norm2 = norm2_pull(grad_normed2)
    grad_mixed = grad_mixed + grad_output
    grad_branch = grad_mixed.astype(BF)

    grad_wout = contract(attended, grad_branch, 0, 0).astype(BF)
    grad_wout = grad_wout.reshape(replicas, groups, out_rows, width)
    grad_wout = lax.psum_scatter(grad_wout, "dp", scatter_dimension=1, tiled=True)[:, 0]
    if stepwise:
        grad_wout = sum(
            (hop(grad_wout[r], r) if r else grad_wout[r]).astype(F32) for r in range(replicas)
        ).astype(BF)
    else:
        grad_wout = lax.psum_scatter(
            grad_wout.reshape(replicas * out_rows, width), "head", scatter_dimension=0, tiled=True
        )
    grad_out_proj = lax.all_gather(grad_wout, "dp", axis=0, tiled=True).astype(F32)

    grad_heads = contract(grad_branch, w_out_cat, 1, 1).astype(BF)
    sums = jnp.zeros((heads_here, TILE, 2 * length), F32)
    grad_blocks = [grad_heads[:, i * head_cols : (i + 1) * head_cols] for i in range(replicas)]
    grad_total = None
    weight_terms = []
    if stepwise:
        arrived = [hop(grad_blocks[r], r) if r else grad_blocks[0] for r in range(replicas)]
        for r in (0, 2, 3, 1):
            grad_qkv, sums = attend_bwd(order[r].reshape(1), qkv, arrived[r], kept[r], sums, length)
            normed_seq = lax.dynamic_slice_in_dim(normed, order[r] * length, length, 0)
            weight_terms.append(contract(normed_seq, grad_qkv, 0, 0))
            mine = hop(grad_qkv, r) if r else grad_qkv
            weight = lax.dynamic_index_in_dim(w_qkv_all, order[r], 0, keepdims=False)
            term = contract(mine, weight, 1, 1)
            grad_total = term if grad_total is None else grad_total + term
        grad_normed = grad_total
        grad_qkv_w = sum(weight_terms)
    else:
        stacked = jnp.stack(grad_blocks, axis=0)
        stacked = lax.all_to_all(stacked, "head", split_axis=0, concat_axis=0, tiled=True)
        stacked = stacked.reshape(group_rows, head_cols)
        seqs = []
        for s in range(sequences):
            grad_seq = stacked[s * length : (s + 1) * length]
            grad_qkv, sums = attend_bwd(
                jnp.full((1,), s, jnp.int32), qkv, grad_seq, kept[s], sums, length
            )
            seqs.append(grad_qkv)
        grad_qkv = jnp.concatenate(seqs, axis=0)
        grad_qkv_w = contract(normed, grad_qkv, 0, 0)
        grad_qkv = lax.all_to_all(
            grad_qkv.reshape(replicas, own_rows, 3 * head_cols),
            "head",
            split_axis=0,
            concat_axis=0,
            tiled=True,
        )
        grad_normed = sum(contract(grad_qkv[i], w_qkv_all[i], 1, 1) for i in range(replicas))

    _, norm1_pull = jax.vjp(rms_norm, inputs_own, norm1_gain)
    grad_first, grad_norm1 = norm1_pull(grad_normed)
    grad_input = grad_mixed + grad_first
    grad_bias = contract(unskew(sums), line, 1, 1, HIGH)
    grad_qkv_w, grad_bias = lax.psum((grad_qkv_w.astype(BF), grad_bias), "dp")
    grad_qkv_w = grad_qkv_w.astype(F32)
    grad_norm1, grad_norm2, grad_router = lax.psum(
        (grad_norm1, grad_norm2, grad_router), ("dp", "head")
    )
    return (
        output,
        grad_input,
        grad_norm1,
        grad_qkv_w[:, :head_cols],
        grad_qkv_w[:, head_cols : 2 * head_cols],
        grad_qkv_w[:, 2 * head_cols :],
        grad_out_proj,
        jnp.transpose(grad_bias),
        grad_norm2,
        grad_router,
        grad_gate_w,
        grad_up_w,
        grad_down_w,
    )


def solution(mesh):
    placed = (
        P("dp", None),
        P(("dp", "head"), None),
        P(("dp", "head"), None),
        P(("dp", "head"), None),
        P(),
        P(),
        P(None, "head"),
        P(None, "head"),
        P(None, "head"),
        P("head", None),
        P(None, "head"),
        P(),
        P(),
        P("dp", None, None),
        P("dp", None, None),
        P("dp", None, None),
    )
    return jax.shard_map(
        body,
        mesh=mesh,
        in_specs=placed,
        out_specs=(
            P(("dp", "head"), None),
            P(("dp", "head"), None),
            P(),
            P(None, "head"),
            P(None, "head"),
            P(None, "head"),
            P("head", None),
            P(None, "head"),
            P(),
            P(),
            P("dp", "head", None),
            P("dp", "head", None),
            P("dp", "head", None),
        ),
        check_vma=False,
    )
```

```python
import functools

import jax
import jax.numpy as jnp
from jax import lax
from jax.experimental import pallas as pl
from jax.experimental.pallas import tpu as pltpu
from jax.sharding import PartitionSpec as P

EPS = 1e-06
SCALE = 0.125
HIGH = lax.Precision.HIGHEST
TILE = 128
BF = jnp.bfloat16
F32 = jnp.float32
VMEM_LIMIT = 48 << 20
VMEM_MOST = 60 << 20
GELU_A = 0.7978845608028654
GELU_B = 0.044715


def rms_norm(value, gain):
    return value * lax.rsqrt(jnp.mean(value * value, axis=-1, keepdims=True) + EPS) * gain


def geglu(gate, up_part):
    return jax.nn.gelu(gate) * up_part


def contract(left, right, left_dim, right_dim, precision=None):
    return lax.dot_general(
        left,
        right,
        (((left_dim,), (right_dim,)), ((), ())),
        precision=precision,
        preferred_element_type=jnp.float32,
    )


def route_slots(chosen, ranks, experts, capacity):
    count = chosen.shape[0]
    keys = jnp.concatenate([ranks, ranks + count])
    wanted = jnp.concatenate([chosen[:, 0], chosen[:, 1]])
    smaller = (wanted[:, None] == wanted[None, :]) & (keys[None, :] < keys[:, None])
    place = jnp.sum(smaller.astype(jnp.int32), axis=1)
    dest = jnp.where(place < capacity, wanted * capacity + place, experts * capacity)
    return jnp.stack([dest[:count], dest[count:]], axis=1)


def skew_kernel(line_ref, table_ref):
    heads, rows, cols = table_ref.shape
    row = lax.broadcasted_iota(jnp.int32, (rows, cols), 0)
    for h in range(heads):
        value = jnp.broadcast_to(line_ref[h], (rows, cols))
        shift = 1
        while shift < rows:
            value = jnp.where((row & shift) != 0, pltpu.roll(value, shift, 1), value)
            shift *= 2
        table_ref[h] = value


def unskew_kernel(table_ref, line_ref):
    heads, rows, cols = table_ref.shape
    row = lax.broadcasted_iota(jnp.int32, (rows, cols), 0)
    for h in range(heads):
        value = table_ref[h]
        shift = 1
        while shift < rows:
            value = jnp.where((row & shift) != 0, pltpu.roll(value, cols - shift, 1), value)
            shift *= 2
        line_ref[h] = jnp.sum(value, axis=0, keepdims=True)


def skew(line):
    heads, cols = line.shape
    return pl.pallas_call(
        skew_kernel,
        out_shape=jax.ShapeDtypeStruct((heads, TILE, cols), F32),
        compiler_params=pltpu.CompilerParams(vmem_limit_bytes=VMEM_LIMIT),
        name="skew",
    )(line[:, None, :])


def unskew(table):
    heads, _, cols = table.shape
    return pl.pallas_call(
        unskew_kernel,
        out_shape=jax.ShapeDtypeStruct((heads, 1, cols), F32),
        compiler_params=pltpu.CompilerParams(vmem_limit_bytes=VMEM_LIMIT),
        name="unskew",
    )(table)[:, 0]


def lanes_of(shape, half, part):
    lane = lax.broadcasted_iota(jnp.int32, shape, 1)
    return (lane >= half) if part else (lane < half)


def attend_fwd_kernel(seq_ref, q_ref, k_ref, v_ref, table_ref, out_ref, probs_ref, acc_ref):
    del seq_ref
    length, lanes = q_ref.shape
    half = lanes // 2
    chunk = 2 * TILE
    key = k_ref[...]
    value_t = v_ref[...].T
    for part in range(2):
        query = jnp.where(lanes_of((length, lanes), half, part), q_ref[...] * SCALE, 0).astype(BF)
        for c in range(length // chunk):
            cols = slice(c * chunk, (c + 1) * chunk)
            scores = contract(key, query[cols], 1, 1)
            pieces = []
            for kb in range(length // TILE):
                at = length - TILE * kb + chunk * c
                pieces.append(
                    scores[kb * TILE : (kb + 1) * TILE] + table_ref[part, :, at : at + chunk]
                )
            scores = jnp.concatenate(pieces, axis=0)
            top = jnp.max(scores, axis=0, keepdims=True)
            shifted = jnp.exp(scores - top)
            total = jnp.sum(shifted, axis=0, keepdims=True)
            probs = (shifted * (1.0 / total)).astype(BF)
            probs_ref[part, :, cols] = probs
            acc_ref[part * half : (part + 1) * half, cols] = jnp.dot(
                value_t[part * half : (part + 1) * half], probs, preferred_element_type=F32
            )
    out_ref[...] = acc_ref[...].T.astype(BF)


def attend_fwd(seq, qkv, table, length):
    heads, _, width = table.shape
    columns = qkv.shape[1] // 3
    pairs = heads // 2
    lanes = columns // pairs
    spec = [
        pl.BlockSpec((length, lanes), lambda p, s, j=j: (s[0], j * pairs + p)) for j in range(3)
    ]
    return pl.pallas_call(
        attend_fwd_kernel,
        out_shape=(
            jax.ShapeDtypeStruct((length, columns), BF),
            jax.ShapeDtypeStruct((heads, length, length), BF),
        ),
        grid_spec=pltpu.PrefetchScalarGridSpec(
            num_scalar_prefetch=1,
            grid=(pairs,),
            in_specs=spec + [pl.BlockSpec((2, TILE, width), lambda p, s: (p, 0, 0))],
            out_specs=[
                pl.BlockSpec((length, lanes), lambda p, s: (0, p)),
                pl.BlockSpec((2, length, length), lambda p, s: (p, 0, 0)),
            ],
            scratch_shapes=[pltpu.VMEM((lanes, length), F32)],
        ),
        compiler_params=pltpu.CompilerParams(vmem_limit_bytes=VMEM_LIMIT),
        cost_estimate=pl.CostEstimate(
            flops=heads * 8 * length * length * lanes,
            bytes_accessed=heads * length * length * 2 + 8 * length * columns,
            transcendentals=heads * length * length,
        ),
        name="attend_fwd",
    )(seq, qkv, qkv, qkv, table)


def attend_bwd_kernel(
    seq_ref, q_ref, k_ref, v_ref, grad_ref, probs_ref, sums_in_ref, out_ref, sums_ref, acc_ref
):
    del seq_ref
    length, lanes = q_ref.shape
    half = lanes // 2
    chunk = 2 * TILE
    pair = pl.program_id(0)
    columns = out_ref.shape[1] // 3
    key_t = k_ref[...].T
    value = v_ref[...]
    sums_ref[...] = sums_in_ref[...]
    grad_keys, grad_values = [], []
    for part in range(2):
        mask = lanes_of((length, lanes), half, part)
        grad = jnp.where(mask, grad_ref[...], 0).astype(BF)
        grad_key = jnp.zeros((length, lanes), F32)
        grad_value = jnp.zeros((length, lanes), F32)
        for c in range(length // chunk):
            cols = slice(c * chunk, (c + 1) * chunk)
            grad_probs = contract(value, grad[cols], 1, 1)
            probs_low = probs_ref[part, :, cols]
            probs = probs_low.astype(F32)
            delta = jnp.sum(probs * grad_probs, axis=0, keepdims=True)
            grad_scores = (probs * (grad_probs - delta)).astype(BF)
            grad_value += jnp.dot(probs_low, grad_ref[cols, :], preferred_element_type=F32)
            grad_key += jnp.dot(grad_scores, q_ref[cols, :], preferred_element_type=F32)
            acc_ref[part * half : (part + 1) * half, cols] = jnp.dot(
                key_t[part * half : (part + 1) * half], grad_scores, preferred_element_type=F32
            )
            for kb in range(length // TILE):
                at = length - TILE * kb + chunk * c
                sums_ref[part, :, at : at + chunk] += grad_scores[
                    kb * TILE : (kb + 1) * TILE
                ].astype(F32)
        grad_keys.append(grad_key)
        grad_values.append(grad_value)
    first = lanes_of((length, lanes), half, 0)
    at = pl.multiple_of(pair * lanes, lanes)
    out_ref[:, pl.ds(at, lanes)] = (acc_ref[...].T * SCALE).astype(BF)
    at = pl.multiple_of(columns + pair * lanes, lanes)
    out_ref[:, pl.ds(at, lanes)] = (jnp.where(first, *grad_keys) * SCALE).astype(BF)
    at = pl.multiple_of(2 * columns + pair * lanes, lanes)
    out_ref[:, pl.ds(at, lanes)] = jnp.where(first, *grad_values).astype(BF)


def attend_bwd(seq, qkv, grad, probs, sums, length):
    heads, _, width = sums.shape
    columns = qkv.shape[1] // 3
    pairs = heads // 2
    lanes = columns // pairs
    spec = [
        pl.BlockSpec((length, lanes), lambda p, s, j=j: (s[0], j * pairs + p)) for j in range(3)
    ]
    sums_spec = pl.BlockSpec((2, TILE, width), lambda p, s: (p, 0, 0))
    return pl.pallas_call(
        attend_bwd_kernel,
        out_shape=(
            jax.ShapeDtypeStruct((length, 3 * columns), BF),
            jax.ShapeDtypeStruct(sums.shape, F32),
        ),
        grid_spec=pltpu.PrefetchScalarGridSpec(
            num_scalar_prefetch=1,
            grid=(pairs,),
            in_specs=spec
            + [
                pl.BlockSpec((length, lanes), lambda p, s: (0, p)),
                pl.BlockSpec((2, length, length), lambda p, s: (p, 0, 0)),
                sums_spec,
            ],
            out_specs=[pl.BlockSpec((length, 3 * columns), lambda p, s: (0, 0)), sums_spec],
            scratch_shapes=[pltpu.VMEM((lanes, length), F32)],
        ),
        compiler_params=pltpu.CompilerParams(vmem_limit_bytes=VMEM_LIMIT),
        cost_estimate=pl.CostEstimate(
            flops=heads * 16 * length * length * lanes,
            bytes_accessed=heads * length * length * 2 + 16 * length * columns,
            transcendentals=0,
        ),
        name="attend_bwd",
    )(seq, qkv, qkv, qkv, grad, probs, sums)


def flipped(index, bits):
    out, step = index, 1
    while step <= bits:
        if bits & step:
            out = out + step * (1 - 2 * lax.rem(index // step, 2))
        step *= 2
    return out


def greet(peers):
    barrier = pltpu.get_barrier_semaphore()
    for peer in peers:
        pl.semaphore_signal(barrier, inc=1, device_id=peer, device_id_type=pl.DeviceIdType.MESH)
    pl.semaphore_wait(barrier, len(peers))


def remote(source, target, send_sem, recv_sem, peer):
    return pltpu.make_async_remote_copy(
        src_ref=source,
        dst_ref=target,
        send_sem=send_sem,
        recv_sem=recv_sem,
        device_id=peer,
        device_id_type=pl.DeviceIdType.MESH,
    )


def attend_all_kernel(
    groups,
    replicas,
    qkv_ref,
    table_ref,
    sent_ref,
    out_ref,
    probs_ref,
    came_ref,
    acc_ref,
    block_ref,
    hold_ref,
    row_send,
    row_recv,
    hop_send,
    hop_recv,
    hold_sem,
    own_sem,
):
    z, d = lax.axis_index("head"), lax.axis_index("dp")
    heads, _, _ = table_ref.shape
    length = block_ref.shape[1]
    columns = block_ref.shape[2]
    pairs = heads // 2
    lanes = columns // pairs
    half = lanes // 2
    chunk = 2 * TILE
    hops = range(1, replicas)
    offs = [2, 4, 3, 5, 6, 7, 1]
    greet([{"dp": flipped(d, o)} for o in offs] + [{"head": flipped(z, r)} for r in hops])
    copies = []
    for o in offs:
        copies.append(
            remote(
                sent_ref.at[o],
                came_ref.at[o],
                row_send.at[o],
                row_recv.at[o],
                {"dp": flipped(d, o)},
            )
        )
        copies[-1].start()
    own = pltpu.make_async_copy(sent_ref.at[0], came_ref.at[0], own_sem.at[0])
    own.start()

    moves = []
    for turn, r in enumerate(reversed(range(replicas))):
        start = pl.multiple_of(flipped(z, r) * length, length)
        slot = turn % 2
        if turn >= 2:
            moves[turn - 2].wait()

        def pair_step(pair, carry, start=start, slot=slot, r=r):
            def part_of(j):
                at = pl.multiple_of(j * columns + pair * lanes, lanes)
                return qkv_ref[pl.ds(start, length), pl.ds(at, lanes)]

            key = part_of(1)
            value_t = part_of(2).T
            scaled = part_of(0) * SCALE
            for part in range(2):
                query = jnp.where(lanes_of((length, lanes), half, part), scaled, 0).astype(BF)
                for c in range(length // chunk):
                    cols = slice(c * chunk, (c + 1) * chunk)
                    scores = contract(key, query[cols], 1, 1)
                    pieces = []
                    for kb in range(length // TILE):
                        at = length - TILE * kb + chunk * c
                        pieces.append(
                            scores[kb * TILE : (kb + 1) * TILE]
                            + table_ref[pair * 2 + part, :, at : at + chunk]
                        )
                    scores = jnp.concatenate(pieces, axis=0)
                    top = jnp.max(scores, axis=0, keepdims=True)
                    shifted = jnp.exp(scores - top)
                    total = jnp.sum(shifted, axis=0, keepdims=True)
                    probs = (shifted * (1.0 / total)).astype(BF)
                    hold_ref[slot, pair * 2 + part, :, cols] = probs
                    acc_ref[part * half : (part + 1) * half, cols] = jnp.dot(
                        value_t[part * half : (part + 1) * half],
                        probs,
                        preferred_element_type=F32,
                    )
            at = pl.multiple_of(pair * lanes, lanes)
            block_ref[r, :, pl.ds(at, lanes)] = acc_ref[...].T.astype(BF)
            return carry

        lax.fori_loop(0, pairs, pair_step, 0)
        move = pltpu.make_async_copy(hold_ref.at[slot], probs_ref.at[r], hold_sem.at[slot])
        move.start()
        moves.append(move)
        target = out_ref.at[:, pl.ds(r * columns, columns)]
        if r:
            hop = remote(
                block_ref.at[r], target, hop_send.at[r], hop_recv.at[r], {"head": flipped(z, r)}
            )
            hop.start()
            copies.append(hop)
        else:
            last = pltpu.make_async_copy(block_ref.at[0], target, own_sem.at[1])
            last.start()
    moves[-2].wait()
    moves[-1].wait()
    own.wait()
    last.wait()
    for copy in copies:
        copy.wait()


def attend_all(qkv, table, sent, length, replicas):
    heads, _, width = table.shape
    columns = qkv.shape[1] // 3
    lanes = 2 * columns // heads
    groups = sent.shape[0]
    vmem = pl.BlockSpec(memory_space=pltpu.VMEM)
    hbm = pl.BlockSpec(memory_space=pl.ANY)
    return pl.pallas_call(
        functools.partial(attend_all_kernel, groups, replicas),
        out_shape=(
            jax.ShapeDtypeStruct((length, replicas * columns), BF),
            jax.ShapeDtypeStruct((replicas, heads, length, length), BF),
            jax.ShapeDtypeStruct(sent.shape, BF),
        ),
        in_specs=[vmem, vmem, hbm],
        out_specs=[hbm, hbm, hbm],
        scratch_shapes=[
            pltpu.VMEM((lanes, length), F32),
            pltpu.VMEM((replicas, length, columns), BF),
            pltpu.VMEM((2, heads, length, length), BF),
            pltpu.SemaphoreType.DMA((groups,)),
            pltpu.SemaphoreType.DMA((groups,)),
            pltpu.SemaphoreType.DMA((replicas,)),
            pltpu.SemaphoreType.DMA((replicas,)),
            pltpu.SemaphoreType.DMA((2,)),
            pltpu.SemaphoreType.DMA((2,)),
        ],
        compiler_params=pltpu.CompilerParams(
            vmem_limit_bytes=VMEM_LIMIT, collective_id=1, has_side_effects=True
        ),
        cost_estimate=pl.CostEstimate(
            flops=replicas * heads * 8 * length * length * lanes,
            bytes_accessed=replicas * heads * length * length * 4,
            transcendentals=replicas * heads * length * length,
        ),
        name="attend_all",
    )(qkv, table, sent)


def expert_tile(rows, scaled, gate_w, up_w, down_w):
    gate = jnp.dot(rows, gate_w, preferred_element_type=F32)
    up_part = jnp.dot(rows, up_w, preferred_element_type=F32)
    grad_hidden = contract(scaled, down_w, 1, 1)
    square = gate * gate
    bend = jnp.tanh(gate * (GELU_A + GELU_A * GELU_B * square))
    half = 0.5 + 0.5 * bend
    active = gate * half
    slope = half + 0.5 * gate * (1.0 - bend * bend) * (GELU_A + 3.0 * GELU_A * GELU_B * square)
    hidden = (active * up_part).astype(BF)
    grad_gate = (grad_hidden * up_part * slope).astype(BF)
    grad_up = (grad_hidden * active).astype(BF)
    return hidden, grad_gate, grad_up


def scaled_rows(rows, extended, router, width):
    logits = jnp.dot(rows, router, preferred_element_type=F32)
    sign = extended[:, width:].astype(F32)
    gap = jnp.sum(logits * sign, axis=1, keepdims=True)
    return (extended[:, :width].astype(F32) * (1.0 / (1.0 + jnp.exp(gap)))).astype(BF)


def expert_kernel(
    width,
    tile,
    normed_ref,
    both_ref,
    cot_ref,
    router_ref,
    gate_hbm,
    up_hbm,
    down_hbm,
    rows_out,
    hidden_out,
    grad_gate_out,
    grad_up_out,
    scaled_out,
    back_out,
    grad_back_out,
    gate_w,
    up_w,
    down_w,
    rows,
    sends,
    back,
    grad_back,
    hidden,
    grad_gate,
    grad_up,
    scaled,
    weight_sem,
    row_send,
    row_recv,
    back_send,
    back_recv,
    grad_send,
    grad_recv,
    unit_sem,
    keep_sem,
):
    d = lax.axis_index("dp")
    groups, capacity, _ = rows.shape
    units = gate_w.shape[1]
    tiles = units // tile
    count = 2 * capacity
    offs = [2, 4, 3, 5, 6, 7, 1]

    def weights_of(t):
        at = pl.multiple_of(t * tile, tile)
        return [
            pltpu.make_async_copy(
                gate_hbm.at[:, pl.ds(at, tile)], gate_w.at[:, pl.ds(at, tile)], weight_sem.at[0, t]
            ),
            pltpu.make_async_copy(
                up_hbm.at[:, pl.ds(at, tile)], up_w.at[:, pl.ds(at, tile)], weight_sem.at[1, t]
            ),
            pltpu.make_async_copy(
                down_hbm.at[pl.ds(at, tile), :], down_w.at[pl.ds(at, tile), :], weight_sem.at[2, t]
            ),
        ]

    def start_weights(t, carry):
        for copy in weights_of(t):
            copy.start()
        return carry

    lax.fori_loop(0, tiles, start_weights, 0)
    greet([{"dp": flipped(d, o)} for o in offs])
    pending = []
    arrivals = {}
    for o in offs:
        sends[o] = jnp.dot(
            both_ref[o * capacity : (o + 1) * capacity],
            normed_ref[...],
            preferred_element_type=F32,
        ).astype(BF)
        arrivals[o] = remote(
            sends.at[o], rows.at[o], row_send.at[o], row_recv.at[o], {"dp": flipped(d, o)}
        )
        arrivals[o].start()
    rows[0] = jnp.dot(
        both_ref[:capacity], normed_ref[...], preferred_element_type=F32
    ).astype(BF)

    unit_copies = {}
    for j in range(groups // 2):
        pair = (2 * j, 2 * j + 1)
        slot = j % 2
        for o in pair:
            if o:
                arrivals[o].wait_recv()
        if j >= 2:
            for copy in unit_copies[j - 2]:
                copy.wait()
        here = rows[2 * j : 2 * j + 2].reshape(count, width)
        extended = cot_ref[2 * j : 2 * j + 2].reshape(count, cot_ref.shape[2])
        scaled[2 * j : 2 * j + 2] = scaled_rows(here, extended, router_ref[...], width).reshape(
            2, capacity, width
        )

        def tile_step(t, carry, j=j, slot=slot):
            at = pl.multiple_of(t * tile, tile)
            if j == 0:
                for copy in weights_of(t):
                    copy.wait()
            values = expert_tile(
                rows[2 * j : 2 * j + 2].reshape(count, width),
                scaled[2 * j : 2 * j + 2].reshape(count, width),
                gate_w[:, pl.ds(at, tile)],
                up_w[:, pl.ds(at, tile)],
                down_w[pl.ds(at, tile), :],
            )
            for ref, value in zip((hidden, grad_gate, grad_up), values):
                ref[slot, :, pl.ds(at, tile)] = value
            return carry

        lax.fori_loop(0, tiles, tile_step, 0)
        span = pl.ds(j * count, count)
        unit_copies[j] = [
            pltpu.make_async_copy(ref.at[slot], out.at[span], unit_sem.at[slot, i])
            for i, (ref, out) in enumerate(
                ((hidden, hidden_out), (grad_gate, grad_gate_out), (grad_up, grad_up_out))
            )
        ]
        for copy in unit_copies[j]:
            copy.start()

        def back_step(t, carry, j=j, slot=slot):
            at = pl.multiple_of(t * tile, tile)
            value = jnp.dot(hidden[slot], down_w[:, pl.ds(at, tile)], preferred_element_type=F32)
            back[2 * j : 2 * j + 2, :, pl.ds(at, tile)] = value.astype(BF).reshape(
                2, capacity, tile
            )
            return carry

        def grad_step(t, carry, j=j, slot=slot):
            at = pl.multiple_of(t * tile, tile)
            value = contract(grad_gate[slot], gate_w[pl.ds(at, tile), :], 1, 1) + contract(
                grad_up[slot], up_w[pl.ds(at, tile), :], 1, 1
            )
            grad_back[2 * j : 2 * j + 2, :, pl.ds(at, tile)] = value.astype(BF).reshape(
                2, capacity, tile
            )
            return carry

        for step, buffer, out, send_sem, recv_sem in (
            (back_step, back, back_out, back_send, back_recv),
            (grad_step, grad_back, grad_back_out, grad_send, grad_recv),
        ):
            lax.fori_loop(0, width // tile, step, 0)
            for o in pair:
                if o:
                    copy = remote(
                        buffer.at[o],
                        out.at[o],
                        send_sem.at[o],
                        recv_sem.at[o],
                        {"dp": flipped(d, o)},
                    )
                else:
                    copy = pltpu.make_async_copy(buffer.at[0], out.at[0], send_sem.at[0])
                copy.start()
                pending.append(copy)

    keeps = [
        pltpu.make_async_copy(rows, rows_out, keep_sem.at[0]),
        pltpu.make_async_copy(scaled, scaled_out, keep_sem.at[1]),
    ]
    for copy in keeps:
        copy.start()
    for j in range(groups // 2 - 2, groups // 2):
        for copy in unit_copies[j]:
            copy.wait()
    for o in offs:
        arrivals[o].wait_send()
    for copy in pending + keeps:
        copy.wait()


def expert_stage(normed2, both, cot, router, gate_w, up_w, down_w, groups, capacity, tile):
    width, units = gate_w.shape
    slots = groups * capacity
    vmem = pl.BlockSpec(memory_space=pltpu.VMEM)
    hbm = pl.BlockSpec(memory_space=pl.ANY)
    row_shape = jax.ShapeDtypeStruct((groups, capacity, width), BF)
    unit_shape = jax.ShapeDtypeStruct((slots, units), BF)
    row_buffer = pltpu.VMEM((groups, capacity, width), BF)
    unit_buffer = pltpu.VMEM((2, 2 * capacity, units), BF)
    row_sem = pltpu.SemaphoreType.DMA((groups,))
    return pl.pallas_call(
        functools.partial(expert_kernel, width, tile),
        out_shape=(row_shape,) + (unit_shape,) * 3 + (row_shape,) * 3,
        in_specs=[vmem] * 4 + [hbm] * 3,
        out_specs=[hbm] * 7,
        scratch_shapes=[
            pltpu.VMEM((width, units), BF),
            pltpu.VMEM((width, units), BF),
            pltpu.VMEM((units, width), BF),
            row_buffer,
            row_buffer,
            row_buffer,
            row_buffer,
            unit_buffer,
            unit_buffer,
            unit_buffer,
            row_buffer,
            pltpu.SemaphoreType.DMA((3, units // tile)),
            row_sem,
            row_sem,
            row_sem,
            row_sem,
            row_sem,
            row_sem,
            pltpu.SemaphoreType.DMA((2, 3)),
            pltpu.SemaphoreType.DMA((2,)),
        ],
        compiler_params=pltpu.CompilerParams(
            vmem_limit_bytes=VMEM_MOST, collective_id=2, has_side_effects=True
        ),
        cost_estimate=pl.CostEstimate(
            flops=12 * slots * width * units,
            bytes_accessed=6 * width * units + 6 * slots * units,
            transcendentals=slots * units,
        ),
        name="expert_stage",
    )(normed2, both, cot, router, gate_w, up_w, down_w)


def far_kernel(
    width,
    rows_ref,
    cot_ref,
    router_ref,
    gate_w,
    up_w,
    down_w,
    hidden_out,
    grad_gate_out,
    grad_up_out,
    scaled_out,
):
    slots = rows_ref.shape[0]
    count = slots // 4

    @pl.when(pl.program_id(0) == 0)
    def _():
        for i in range(4):
            span = slice(i * count, (i + 1) * count)
            scaled_out[span] = scaled_rows(
                rows_ref[span], cot_ref[span], router_ref[...], width
            )

    def step(i, carry):
        span = pl.ds(pl.multiple_of(i * count, count), count)
        values = expert_tile(
            rows_ref[span], scaled_out[span], gate_w[...], up_w[...], down_w[...]
        )
        for ref, value in zip((hidden_out, grad_gate_out, grad_up_out), values):
            ref[span] = value
        return carry

    lax.fori_loop(0, 4, step, 0)


def far_stage(rows, cot, router, gate_w, up_w, down_w, tile):
    width, units = gate_w.shape
    slots = rows.shape[0]

    def whole(shape):
        return pl.BlockSpec(shape, lambda t: (0, 0))

    unit_shape = jax.ShapeDtypeStruct((slots, units), BF)
    unit_spec = pl.BlockSpec((slots, tile), lambda t: (0, t))
    return pl.pallas_call(
        functools.partial(far_kernel, width),
        out_shape=(unit_shape,) * 3 + (jax.ShapeDtypeStruct((slots, width), BF),),
        grid=(units // tile,),
        in_specs=[
            whole(rows.shape),
            whole(cot.shape),
            whole(router.shape),
            pl.BlockSpec((width, tile), lambda t: (0, t)),
            pl.BlockSpec((width, tile), lambda t: (0, t)),
            pl.BlockSpec((tile, width), lambda t: (t, 0)),
        ],
        out_specs=[unit_spec] * 3 + [whole((slots, width))],
        compiler_params=pltpu.CompilerParams(vmem_limit_bytes=VMEM_LIMIT),
        cost_estimate=pl.CostEstimate(
            flops=6 * slots * width * units,
            bytes_accessed=6 * width * units + 6 * slots * units,
            transcendentals=slots * units,
        ),
        name="far_stage",
    )(rows, cot, router, gate_w, up_w, down_w)


def expert_forward(rows, gate_w, up_w, grad_unscaled, slot_gates):
    gate_pre = jnp.dot(rows, gate_w, preferred_element_type=F32)
    up_pre = jnp.dot(rows, up_w, preferred_element_type=F32)
    hidden, pull = jax.vjp(geglu, gate_pre, up_pre)
    grad_gate_pre, grad_up_pre = pull(grad_unscaled * slot_gates)
    return hidden.astype(BF), grad_gate_pre.astype(BF), grad_up_pre.astype(BF)


def body_plain(
    block_input,
    cotangent,
    expert_ids,
    priority,
    rel_bucket,
    norm1_gain,
    w_query,
    w_key,
    w_value,
    w_out,
    pos_bias,
    norm2_gain,
    w_router,
    w_gate,
    w_up,
    w_down,
):
    group_rows, width = block_input.shape
    own_rows = cotangent.shape[0]
    buckets, heads_here = pos_bias.shape
    head_cols = w_query.shape[1]
    length = (rel_bucket.shape[0] + 1) // 2
    sequences = group_rows // length
    experts = w_router.shape[1]
    capacity = 5 * 2 * own_rows // (4 * experts)
    slot_count = experts * capacity
    replicas = lax.axis_size("head")
    groups = lax.axis_size("dp")
    me = lax.axis_index("head")
    far = replicas // 2
    far_perm = [(i, i ^ far) for i in range(replicas)]
    stepwise = own_rows == length and sequences == replicas

    def hop(value, r):
        return lax.ppermute(value, "head", [(i, i ^ r) for i in range(replicas)])

    def exchange(value):
        parts = value.reshape(experts, capacity, -1)
        return lax.all_to_all(parts, "dp", split_axis=0, concat_axis=0, tiled=True).reshape(
            slot_count, -1
        )

    dest = route_slots(expert_ids, priority[0], experts, capacity)
    dest_far = lax.ppermute(dest, "head", far_perm)
    slot_range = jnp.arange(slot_count, dtype=jnp.int32)[None, :]
    picks = [(dest[:, k : k + 1] == slot_range).astype(BF) for k in range(2)]
    both = picks[0] + picks[1]
    both_far = sum((dest_far[:, k : k + 1] == slot_range).astype(BF) for k in range(2))

    down_w, gate_w, up_w = w_down[0], w_gate[0], w_up[0]
    cot_here = exchange(contract(both, cotangent, 0, 0).astype(BF))
    cot_far_own = lax.ppermute(cotangent, "head", far_perm)
    cot_far = exchange(contract(both_far, cot_far_own, 0, 0).astype(BF))
    unscaled_here = contract(cot_here, down_w, 1, 1)
    unscaled_far = contract(cot_far, down_w, 1, 1)

    dp_at = lax.axis_index("dp")
    out_rows = head_cols // groups
    piece = lax.dynamic_slice_in_dim(w_out, dp_at * out_rows, out_rows, 0)
    w_out_all = lax.all_gather(piece, ("head", "dp"), axis=0, tiled=True)
    w_qkv = jnp.concatenate([w_query, w_key, w_value], axis=1)
    qkv_rows = width // groups
    piece = lax.dynamic_slice_in_dim(w_qkv, dp_at * qkv_rows, qkv_rows, 0)
    w_qkv_all = lax.all_gather(piece, ("head", "dp"), axis=0, tiled=True)
    if stepwise:
        order = [me ^ r for r in range(replicas)]
    else:
        order = list(range(replicas))
    w_out_all = w_out_all.reshape(replicas, head_cols, width)
    w_qkv_all = w_qkv_all.reshape(replicas, width, 3 * head_cols)
    w_out_cat = jnp.concatenate(
        [lax.dynamic_index_in_dim(w_out_all, o, 0, keepdims=False) for o in order], axis=0
    )

    inputs_all = block_input.astype(F32)
    normed = rms_norm(inputs_all, norm1_gain).astype(BF)
    qkv = jnp.dot(normed, w_qkv, preferred_element_type=F32).astype(BF)
    line = (rel_bucket[::-1][None, :] == jnp.arange(buckets, dtype=jnp.int32)[:, None]).astype(F32)
    line = jnp.pad(line, ((0, 0), (1, 0)))
    table = skew(contract(pos_bias, line, 0, 0, HIGH))
    kept = {}
    if stepwise:
        blocks = [None] * replicas
        for r in reversed(range(replicas)):
            attended_seq, probs = attend_fwd(order[r].reshape(1), qkv, table, length)
            kept[r] = probs
            blocks[r] = hop(attended_seq, r) if r else attended_seq
    else:
        seqs = []
        for s in range(sequences):
            attended_seq, kept[s] = attend_fwd(jnp.full((1,), s, jnp.int32), qkv, table, length)
            seqs.append(attended_seq)
        attended_all = jnp.concatenate(seqs, axis=0).reshape(replicas, own_rows, head_cols)
        attended_all = lax.all_to_all(attended_all, "head", split_axis=0, concat_axis=0, tiled=True)
        blocks = [attended_all[i] for i in range(replicas)]
    attended = jnp.concatenate(blocks, axis=1)

    branch = jnp.dot(attended, w_out_cat, preferred_element_type=F32)
    start_own = me * own_rows
    inputs_own = lax.dynamic_slice_in_dim(block_input, start_own, own_rows, 0).astype(F32)
    mixed = inputs_own + branch
    normed2_full, norm2_pull = jax.vjp(rms_norm, mixed, norm2_gain)
    normed2 = normed2_full.astype(BF)
    logits = jnp.dot(normed2, w_router, preferred_element_type=F32)
    expert_range = jnp.arange(experts, dtype=jnp.int32)
    chosen = (expert_ids[:, :, None] == expert_range[None, None, :]).astype(F32)
    gates = jax.nn.softmax(jnp.sum(chosen * logits[:, None, :], axis=2), axis=-1)

    def slot_gates_of(places, values):
        terms = sum(
            jnp.where(places[:, k : k + 1] == slot_range, values[:, k : k + 1], 0.0)
            for k in range(2)
        )
        return jnp.sum(terms, axis=0)

    rows_here = exchange(contract(both, normed2, 0, 0).astype(BF))
    gates_here = exchange(slot_gates_of(dest, gates))
    normed2_far = lax.ppermute(normed2, "head", far_perm)
    gates_far_own = lax.ppermute(gates, "head", far_perm)
    rows_far = exchange(contract(both_far, normed2_far, 0, 0).astype(BF))
    gates_far = exchange(slot_gates_of(dest_far, gates_far_own))

    hidden_here, ggp_here, gup_here = expert_forward(
        rows_here, gate_w, up_w, unscaled_here, gates_here
    )
    returned = jnp.dot(hidden_here, down_w, preferred_element_type=F32).astype(BF)
    came_back = exchange(returned)
    grad_routed = (contract(ggp_here, gate_w, 1, 1) + contract(gup_here, up_w, 1, 1)).astype(BF)
    grad_back = exchange(grad_routed)
    hidden_far, ggp_far, gup_far = expert_forward(rows_far, gate_w, up_w, unscaled_far, gates_far)
    scaled_here = (cot_here.astype(F32) * gates_here).astype(BF)
    scaled_far = (cot_far.astype(F32) * gates_far).astype(BF)

    low = me % far
    high = me // far

    def reduced(lefts, rights):
        rows = lefts[0].shape[1] // replicas

        def part(at):
            return sum(
                contract(lax.dynamic_slice_in_dim(left, at * rows, rows, 1), right, 0, 0)
                for left, right in zip(lefts, rights)
            )

        if far == 2:
            sent = hop(part(high * far + (1 - low)).astype(BF), 1)
            return (part(me) + sent.astype(F32))[None]
        whole = jnp.concatenate([part(high * far + i) for i in range(far)], axis=0).astype(BF)
        member = [[h * far + i for i in range(far)] for h in range(2)]
        return lax.psum_scatter(
            whole, "head", scatter_dimension=0, axis_index_groups=member, tiled=True
        ).astype(F32)[None]

    grad_down_w = reduced((hidden_here, hidden_far), (scaled_here, scaled_far))
    grad_gate_w = reduced((rows_here, rows_far), (ggp_here, ggp_far))
    grad_up_w = reduced((rows_here, rows_far), (gup_here, gup_far))

    chosen_rows = [jnp.dot(pick, came_back, preferred_element_type=F32) for pick in picks]
    output = mixed + sum(gates[:, k : k + 1] * chosen_rows[k] for k in range(2))
    grad_output = cotangent.astype(F32)
    grad_gates = jnp.stack([jnp.sum(grad_output * rows, axis=1) for rows in chosen_rows], axis=1)
    grad_normed2 = jnp.dot(both, grad_back, preferred_element_type=F32)
    grad_picked = gates * (grad_gates - jnp.sum(gates * grad_gates, axis=1, keepdims=True))
    grad_logits = jnp.sum(chosen * grad_picked[:, :, None], axis=1)
    grad_normed2 = grad_normed2 + contract(grad_logits, w_router.astype(F32), 1, 1, HIGH)
    grad_router = contract(normed2.astype(F32), grad_logits, 0, 0, HIGH)
    grad_mixed, grad_norm2 = norm2_pull(grad_normed2)
    grad_mixed = grad_mixed + grad_output
    grad_branch = grad_mixed.astype(BF)

    grad_wout = contract(attended, grad_branch, 0, 0).astype(BF)
    grad_wout = grad_wout.reshape(replicas, groups, out_rows, width)
    grad_wout = lax.psum_scatter(grad_wout, "dp", scatter_dimension=1, tiled=True)[:, 0]
    if stepwise:
        grad_wout = sum(
            (hop(grad_wout[r], r) if r else grad_wout[r]).astype(F32) for r in range(replicas)
        ).astype(BF)
    else:
        grad_wout = lax.psum_scatter(
            grad_wout.reshape(replicas * out_rows, width), "head", scatter_dimension=0, tiled=True
        )
    grad_out_proj = lax.all_gather(grad_wout, "dp", axis=0, tiled=True).astype(F32)

    grad_heads = contract(grad_branch, w_out_cat, 1, 1).astype(BF)
    sums = jnp.zeros((heads_here, TILE, 2 * length), F32)
    grad_blocks = [grad_heads[:, i * head_cols : (i + 1) * head_cols] for i in range(replicas)]
    grad_total = None
    weight_terms = []
    if stepwise:
        arrived = [hop(grad_blocks[r], r) if r else grad_blocks[0] for r in range(replicas)]
        for r in (0, 2, 3, 1):
            grad_qkv, sums = attend_bwd(order[r].reshape(1), qkv, arrived[r], kept[r], sums, length)
            normed_seq = lax.dynamic_slice_in_dim(normed, order[r] * length, length, 0)
            weight_terms.append(contract(normed_seq, grad_qkv, 0, 0))
            mine = hop(grad_qkv, r) if r else grad_qkv
            weight = lax.dynamic_index_in_dim(w_qkv_all, order[r], 0, keepdims=False)
            term = contract(mine, weight, 1, 1)
            grad_total = term if grad_total is None else grad_total + term
        grad_normed = grad_total
        grad_qkv_w = sum(weight_terms)
    else:
        stacked = jnp.stack(grad_blocks, axis=0)
        stacked = lax.all_to_all(stacked, "head", split_axis=0, concat_axis=0, tiled=True)
        stacked = stacked.reshape(group_rows, head_cols)
        seqs = []
        for s in range(sequences):
            grad_seq = stacked[s * length : (s + 1) * length]
            grad_qkv, sums = attend_bwd(
                jnp.full((1,), s, jnp.int32), qkv, grad_seq, kept[s], sums, length
            )
            seqs.append(grad_qkv)
        grad_qkv = jnp.concatenate(seqs, axis=0)
        grad_qkv_w = contract(normed, grad_qkv, 0, 0)
        grad_qkv = lax.all_to_all(
            grad_qkv.reshape(replicas, own_rows, 3 * head_cols),
            "head",
            split_axis=0,
            concat_axis=0,
            tiled=True,
        )
        grad_normed = sum(contract(grad_qkv[i], w_qkv_all[i], 1, 1) for i in range(replicas))

    _, norm1_pull = jax.vjp(rms_norm, inputs_own, norm1_gain)
    grad_first, grad_norm1 = norm1_pull(grad_normed)
    grad_input = grad_mixed + grad_first
    grad_bias = contract(unskew(sums), line, 1, 1, HIGH)
    grad_qkv_w, grad_bias = lax.psum((grad_qkv_w.astype(BF), grad_bias), "dp")
    grad_qkv_w = grad_qkv_w.astype(F32)
    grad_norm1, grad_norm2, grad_router = lax.psum(
        (grad_norm1, grad_norm2, grad_router), ("dp", "head")
    )
    return (
        output,
        grad_input,
        grad_norm1,
        grad_qkv_w[:, :head_cols],
        grad_qkv_w[:, head_cols : 2 * head_cols],
        grad_qkv_w[:, 2 * head_cols :],
        grad_out_proj,
        jnp.transpose(grad_bias),
        grad_norm2,
        grad_router,
        grad_gate_w,
        grad_up_w,
        grad_down_w,
    )


def body(*args):
    block_input, cotangent, rel_bucket, pos_bias, w_gate, w_router = (
        args[0],
        args[1],
        args[4],
        args[10],
        args[13],
        args[12],
    )
    own_rows = cotangent.shape[0]
    length = (rel_bucket.shape[0] + 1) // 2
    replicas, groups = lax.axis_size("head"), lax.axis_size("dp")
    experts = w_router.shape[1]
    capacity = 5 * 2 * own_rows // (4 * experts)
    stepwise = (
        own_rows == length
        and block_input.shape[0] == replicas * length
        and replicas == 4
        and groups == 8
        and experts == groups
        and capacity % 16 == 0
        and pos_bias.shape[1] % 2 == 0
        and w_gate.shape[2] % 256 == 0
    )
    return body_steps(*args) if stepwise else body_plain(*args)


def body_steps(
    block_input,
    cotangent,
    expert_ids,
    priority,
    rel_bucket,
    norm1_gain,
    w_query,
    w_key,
    w_value,
    w_out,
    pos_bias,
    norm2_gain,
    w_router,
    w_gate,
    w_up,
    w_down,
):
    group_rows, width = block_input.shape
    own_rows = cotangent.shape[0]
    buckets, heads_here = pos_bias.shape
    head_cols = w_query.shape[1]
    length = (rel_bucket.shape[0] + 1) // 2
    experts = w_router.shape[1]
    capacity = 5 * 2 * own_rows // (4 * experts)
    slot_count = experts * capacity
    replicas, groups = lax.axis_size("head"), lax.axis_size("dp")
    me, dp_at = lax.axis_index("head"), lax.axis_index("dp")
    far = replicas // 2
    far_perm = [(i, i ^ far) for i in range(replicas)]

    def hop(value, r):
        return lax.ppermute(value, "head", [(i, i ^ r) for i in range(replicas)])

    dest = route_slots(expert_ids, priority[0], experts, capacity)
    mixed_dest = jnp.where(
        dest < slot_count,
        ((dest // capacity) ^ dp_at) * capacity + dest % capacity,
        slot_count,
    )
    routing_far = hop(jnp.concatenate([dest, expert_ids], axis=1), far)
    slot_row = jnp.arange(slot_count, dtype=jnp.int32)[None, :]
    slot_col = jnp.arange(slot_count, dtype=jnp.int32)[:, None]
    expert_range = jnp.arange(experts, dtype=jnp.int32)
    lane_range = jnp.arange(TILE, dtype=jnp.int32)[None, :]

    def dispatch_of(places, ids):
        first = (slot_col == places[:, 0][None, :]).astype(BF)
        second = (slot_col == places[:, 1][None, :]).astype(BF)
        signs = (ids[:, 1:2] == lane_range).astype(BF) - (ids[:, 0:1] == lane_range).astype(BF)
        return first + second, contract(first - second, signs, 1, 0).astype(BF)

    both, signs = dispatch_of(mixed_dest, expert_ids)
    picks = [(mixed_dest[:, k : k + 1] == slot_row).astype(BF) for k in range(2)]
    router_wide = jnp.pad(w_router, ((0, 0), (0, TILE - experts)))
    cot_sent = jnp.concatenate([contract(both, cotangent, 1, 0).astype(BF), signs], axis=1)
    cot_sent = cot_sent.reshape(experts, capacity, width + TILE)
    cot_far_own = hop(cotangent, far)

    out_rows = head_cols // groups
    piece = lax.dynamic_slice_in_dim(w_out, dp_at * out_rows, out_rows, 0)
    w_out_all = lax.all_gather(piece, ("head", "dp"), axis=0, tiled=True)
    w_qkv = jnp.concatenate([w_query, w_key, w_value], axis=1)
    order = [me ^ r for r in range(replicas)]
    w_out_all = w_out_all.reshape(replicas, head_cols, width)
    w_out_cat = jnp.concatenate(
        [lax.dynamic_index_in_dim(w_out_all, o, 0, keepdims=False) for o in order], axis=0
    )

    inputs_all = block_input.astype(F32)
    normed = rms_norm(inputs_all, norm1_gain).astype(BF)
    qkv = jnp.dot(normed, w_qkv, preferred_element_type=F32).astype(BF)
    line = (rel_bucket[::-1][None, :] == jnp.arange(buckets, dtype=jnp.int32)[:, None]).astype(F32)
    line = jnp.pad(line, ((0, 0), (1, 0)))
    table = skew(contract(pos_bias, line, 0, 0, HIGH))
    attended, probs, cot_here = attend_all(qkv, table, cot_sent, length, replicas)

    branch = jnp.dot(attended, w_out_cat, preferred_element_type=F32)
    inputs_own = lax.dynamic_slice_in_dim(block_input, me * own_rows, own_rows, 0).astype(F32)
    mixed = inputs_own + branch
    normed2_full, norm2_pull = jax.vjp(rms_norm, mixed, norm2_gain)
    normed2 = normed2_full.astype(BF)

    gate_w, up_w, down_w = w_gate[0], w_up[0], w_down[0]
    normed2_far = hop(normed2, far)
    tile = 256
    (rows_here, hidden_here, ggp_here, gup_here, scaled_here, came_back, grad_back) = expert_stage(
        normed2, both, cot_here, router_wide, gate_w, up_w, down_w, groups, capacity, tile
    )
    rows_here = rows_here.reshape(slot_count, width)
    scaled_here = scaled_here.reshape(slot_count, width)
    came_back = came_back.reshape(slot_count, width)
    grad_back = grad_back.reshape(slot_count, width)

    both_far, signs_far = dispatch_of(routing_far[:, :2], routing_far[:, 2:])
    far_own = jnp.concatenate([normed2_far, cot_far_own], axis=1)
    far_sent = jnp.concatenate([contract(both_far, far_own, 1, 0).astype(BF), signs_far], axis=1)
    far_sent, grad_back = lax.optimization_barrier((far_sent, grad_back))
    far_came = lax.all_to_all(
        far_sent.reshape(experts, capacity, 2 * width + TILE),
        "dp",
        split_axis=0,
        concat_axis=0,
        tiled=True,
    ).reshape(slot_count, 2 * width + TILE)
    rows_far = far_came[:, :width]
    hidden_far, ggp_far, gup_far, scaled_far = far_stage(
        rows_far, far_came[:, width:], router_wide, gate_w, up_w, down_w, tile
    )

    low, high = me % far, me // far

    def part(lefts, rights, at):
        rows = lefts[0].shape[1] // replicas
        return sum(
            contract(lax.dynamic_slice_in_dim(left, at * rows, rows, 1), right, 0, 0)
            for left, right in zip(lefts, rights)
        )

    def sent(lefts, rights):
        return hop(part(lefts, rights, high * far + (1 - low)).astype(BF), 1)

    weight_args = (
        ((rows_here, rows_far), (ggp_here, ggp_far)),
        ((rows_here, rows_far), (gup_here, gup_far)),
        ((hidden_here, hidden_far), (scaled_here, scaled_far)),
    )
    came = [sent(*a) for a in weight_args]

    logits = jnp.dot(normed2, w_router, preferred_element_type=F32)
    chosen = (expert_ids[:, :, None] == expert_range[None, None, :]).astype(F32)
    gates = jax.nn.softmax(jnp.sum(chosen * logits[:, None, :], axis=2), axis=-1)
    chosen_rows = [jnp.dot(pick, came_back, preferred_element_type=F32) for pick in picks]
    output = mixed + sum(gates[:, k : k + 1] * chosen_rows[k] for k in range(2))
    grad_output = cotangent.astype(F32)
    grad_gates = jnp.stack([jnp.sum(grad_output * rows, axis=1) for rows in chosen_rows], axis=1)
    grad_normed2 = jnp.dot(picks[0] + picks[1], grad_back, preferred_element_type=F32)
    grad_picked = gates * (grad_gates - jnp.sum(gates * grad_gates, axis=1, keepdims=True))
    grad_logits = jnp.sum(chosen * grad_picked[:, :, None], axis=1)
    grad_normed2 = grad_normed2 + contract(grad_logits, w_router.astype(F32), 1, 1, HIGH)
    grad_router = contract(normed2.astype(F32), grad_logits, 0, 0, HIGH)
    grad_mixed, grad_norm2 = norm2_pull(grad_normed2)
    grad_mixed = grad_mixed + grad_output
    grad_branch = grad_mixed.astype(BF)

    grad_wout = contract(attended, grad_branch, 0, 0).astype(BF)
    grad_wout = grad_wout.reshape(replicas, groups, out_rows, width)
    grad_wout = lax.psum_scatter(grad_wout, "dp", scatter_dimension=1, tiled=True)[:, 0]
    grad_wout = sum(
        (hop(grad_wout[r], r) if r else grad_wout[r]).astype(F32) for r in range(replicas)
    ).astype(BF)
    grad_out_proj = lax.all_gather(grad_wout, "dp", axis=0, tiled=True).astype(F32)

    qkv_rows = width // groups
    piece = lax.dynamic_slice_in_dim(w_qkv, dp_at * qkv_rows, qkv_rows, 0)
    piece, _ = lax.optimization_barrier((piece, w_out_cat))
    w_qkv_all = lax.all_gather(piece, ("head", "dp"), axis=0, tiled=True)
    w_qkv_all = w_qkv_all.reshape(replicas, width, 3 * head_cols)
    grad_heads = contract(grad_branch, w_out_cat, 1, 1).astype(BF)
    sums = jnp.zeros((heads_here, TILE, 2 * length), F32)
    grad_blocks = [grad_heads[:, i * head_cols : (i + 1) * head_cols] for i in range(replicas)]
    grad_normed = None
    weight_terms = []
    arrived = [hop(grad_blocks[r], r) if r else grad_blocks[0] for r in range(replicas)]
    for r in (0, 2, 3, 1):
        grad_qkv, sums = attend_bwd(order[r].reshape(1), qkv, arrived[r], probs[r], sums, length)
        normed_seq = lax.dynamic_slice_in_dim(normed, order[r] * length, length, 0)
        weight_terms.append(contract(normed_seq, grad_qkv, 0, 0))
        mine = hop(grad_qkv, r) if r else grad_qkv
        weight = lax.dynamic_index_in_dim(w_qkv_all, order[r], 0, keepdims=False)
        term = contract(mine, weight, 1, 1)
        grad_normed = term if grad_normed is None else grad_normed + term
    grad_qkv_w = sum(weight_terms)

    _, norm1_pull = jax.vjp(rms_norm, inputs_own, norm1_gain)
    grad_first, grad_norm1 = norm1_pull(grad_normed)
    grad_input = grad_mixed + grad_first
    grad_bias = contract(unskew(sums), line, 1, 1, HIGH)
    grad_qkv_w, grad_bias = lax.psum((grad_qkv_w.astype(BF), grad_bias), "dp")
    grad_qkv_w = grad_qkv_w.astype(F32)
    grad_norm1, grad_norm2, grad_router = lax.psum(
        (grad_norm1, grad_norm2, grad_router), ("dp", "head")
    )
    came, _ = lax.optimization_barrier((came, grad_normed))
    grad_gate_w, grad_up_w, grad_down_w = (
        (part(*a, me) + piece.astype(F32))[None] for a, piece in zip(weight_args, came)
    )
    return (
        output,
        grad_input,
        grad_norm1,
        grad_qkv_w[:, :head_cols],
        grad_qkv_w[:, head_cols : 2 * head_cols],
        grad_qkv_w[:, 2 * head_cols :],
        grad_out_proj,
        jnp.transpose(grad_bias),
        grad_norm2,
        grad_router,
        grad_gate_w,
        grad_up_w,
        grad_down_w,
    )


def solution(mesh):
    placed = (
        P("dp", None),
        P(("dp", "head"), None),
        P(("dp", "head"), None),
        P(("dp", "head"), None),
        P(),
        P(),
        P(None, "head"),
        P(None, "head"),
        P(None, "head"),
        P("head", None),
        P(None, "head"),
        P(),
        P(),
        P("dp", None, None),
        P("dp", None, None),
        P("dp", None, None),
    )
    return jax.shard_map(
        body,
        mesh=mesh,
        in_specs=placed,
        out_specs=(
            P(("dp", "head"), None),
            P(("dp", "head"), None),
            P(),
            P(None, "head"),
            P(None, "head"),
            P(None, "head"),
            P("head", None),
            P(None, "head"),
            P(),
            P(),
            P("dp", "head", None),
            P("dp", "head", None),
            P("dp", "head", None),
        ),
        check_vma=False,
    )
```

```python
import functools

import jax
import jax.numpy as jnp
from jax import lax
from jax.experimental import pallas as pl
from jax.experimental.pallas import tpu as pltpu
from jax.sharding import PartitionSpec as P

EPS = 1e-06
SCALE = 0.125
HIGH = lax.Precision.HIGHEST
TILE = 128
BF = jnp.bfloat16
F32 = jnp.float32
VMEM_LIMIT = 48 << 20
VMEM_MOST = 60 << 20
GELU_A = 0.7978845608028654
GELU_B = 0.044715
PEERS = [2, 4, 3, 5, 6, 7, 1]


def rms_norm(value, gain):
    return value * lax.rsqrt(jnp.mean(value * value, axis=-1, keepdims=True) + EPS) * gain


def geglu(gate, up_part):
    return jax.nn.gelu(gate) * up_part


def contract(left, right, left_dim, right_dim, precision=None):
    return lax.dot_general(
        left,
        right,
        (((left_dim,), (right_dim,)), ((), ())),
        precision=precision,
        preferred_element_type=jnp.float32,
    )


def route_slots(chosen, ranks, experts, capacity):
    count = chosen.shape[0]
    keys = jnp.concatenate([ranks, ranks + count])
    wanted = jnp.concatenate([chosen[:, 0], chosen[:, 1]])
    smaller = (wanted[:, None] == wanted[None, :]) & (keys[None, :] < keys[:, None])
    place = jnp.sum(smaller.astype(jnp.int32), axis=1)
    dest = jnp.where(place < capacity, wanted * capacity + place, experts * capacity)
    return jnp.stack([dest[:count], dest[count:]], axis=1)


def skew_kernel(line_ref, table_ref):
    heads, rows, cols = table_ref.shape
    row = lax.broadcasted_iota(jnp.int32, (rows, cols), 0)
    for h in range(heads):
        value = jnp.broadcast_to(line_ref[h], (rows, cols))
        shift = 1
        while shift < rows:
            value = jnp.where((row & shift) != 0, pltpu.roll(value, shift, 1), value)
            shift *= 2
        table_ref[h] = value


def unskew_kernel(table_ref, line_ref):
    heads, rows, cols = table_ref.shape
    row = lax.broadcasted_iota(jnp.int32, (rows, cols), 0)
    for h in range(heads):
        value = table_ref[h]
        shift = 1
        while shift < rows:
            value = jnp.where((row & shift) != 0, pltpu.roll(value, cols - shift, 1), value)
            shift *= 2
        line_ref[h] = jnp.sum(value, axis=0, keepdims=True)


def skew(line):
    heads, cols = line.shape
    return pl.pallas_call(
        skew_kernel,
        out_shape=jax.ShapeDtypeStruct((heads, TILE, cols), F32),
        compiler_params=pltpu.CompilerParams(vmem_limit_bytes=VMEM_LIMIT),
        name="skew",
    )(line[:, None, :])


def unskew(table):
    heads, _, cols = table.shape
    return pl.pallas_call(
        unskew_kernel,
        out_shape=jax.ShapeDtypeStruct((heads, 1, cols), F32),
        compiler_params=pltpu.CompilerParams(vmem_limit_bytes=VMEM_LIMIT),
        name="unskew",
    )(table)[:, 0]


def lanes_of(shape, half, part):
    lane = lax.broadcasted_iota(jnp.int32, shape, 1)
    return (lane >= half) if part else (lane < half)


def attend_fwd_kernel(seq_ref, q_ref, k_ref, v_ref, table_ref, out_ref, probs_ref, acc_ref):
    del seq_ref
    length, lanes = q_ref.shape
    half = lanes // 2
    chunk = 2 * TILE
    key = k_ref[...]
    value_t = v_ref[...].T
    for part in range(2):
        query = jnp.where(lanes_of((length, lanes), half, part), q_ref[...] * SCALE, 0).astype(BF)
        for c in range(length // chunk):
            cols = slice(c * chunk, (c + 1) * chunk)
            scores = contract(key, query[cols], 1, 1)
            pieces = []
            for kb in range(length // TILE):
                at = length - TILE * kb + chunk * c
                pieces.append(
                    scores[kb * TILE : (kb + 1) * TILE] + table_ref[part, :, at : at + chunk]
                )
            scores = jnp.concatenate(pieces, axis=0)
            top = jnp.max(scores, axis=0, keepdims=True)
            shifted = jnp.exp(scores - top)
            total = jnp.sum(shifted, axis=0, keepdims=True)
            probs = (shifted * (1.0 / total)).astype(BF)
            probs_ref[part, :, cols] = probs
            acc_ref[part * half : (part + 1) * half, cols] = jnp.dot(
                value_t[part * half : (part + 1) * half], probs, preferred_element_type=F32
            )
    out_ref[...] = acc_ref[...].T.astype(BF)


def attend_fwd(seq, qkv, table, length):
    heads, _, width = table.shape
    columns = qkv.shape[1] // 3
    pairs = heads // 2
    lanes = columns // pairs
    spec = [
        pl.BlockSpec((length, lanes), lambda p, s, j=j: (s[0], j * pairs + p)) for j in range(3)
    ]
    return pl.pallas_call(
        attend_fwd_kernel,
        out_shape=(
            jax.ShapeDtypeStruct((length, columns), BF),
            jax.ShapeDtypeStruct((heads, length, length), BF),
        ),
        grid_spec=pltpu.PrefetchScalarGridSpec(
            num_scalar_prefetch=1,
            grid=(pairs,),
            in_specs=spec + [pl.BlockSpec((2, TILE, width), lambda p, s: (p, 0, 0))],
            out_specs=[
                pl.BlockSpec((length, lanes), lambda p, s: (0, p)),
                pl.BlockSpec((2, length, length), lambda p, s: (p, 0, 0)),
            ],
            scratch_shapes=[pltpu.VMEM((lanes, length), F32)],
        ),
        compiler_params=pltpu.CompilerParams(vmem_limit_bytes=VMEM_LIMIT),
        cost_estimate=pl.CostEstimate(
            flops=heads * 8 * length * length * lanes,
            bytes_accessed=heads * length * length * 2 + 8 * length * columns,
            transcendentals=heads * length * length,
        ),
        name="attend_fwd",
    )(seq, qkv, qkv, qkv, table)


def attend_bwd_kernel(
    seq_ref, q_ref, k_ref, v_ref, grad_ref, probs_ref, sums_in_ref, out_ref, sums_ref, acc_ref
):
    del seq_ref
    length, lanes = q_ref.shape
    half = lanes // 2
    chunk = 2 * TILE
    pair = pl.program_id(0)
    columns = out_ref.shape[1] // 3
    key_t = k_ref[...].T
    value = v_ref[...]
    sums_ref[...] = sums_in_ref[...]
    grad_keys, grad_values = [], []
    for part in range(2):
        mask = lanes_of((length, lanes), half, part)
        grad = jnp.where(mask, grad_ref[...], 0).astype(BF)
        grad_key = jnp.zeros((length, lanes), F32)
        grad_value = jnp.zeros((length, lanes), F32)
        for c in range(length // chunk):
            cols = slice(c * chunk, (c + 1) * chunk)
            grad_probs = contract(value, grad[cols], 1, 1)
            probs_low = probs_ref[part, :, cols]
            probs = probs_low.astype(F32)
            delta = jnp.sum(probs * grad_probs, axis=0, keepdims=True)
            grad_scores = (probs * (grad_probs - delta)).astype(BF)
            grad_value += jnp.dot(probs_low, grad_ref[cols, :], preferred_element_type=F32)
            grad_key += jnp.dot(grad_scores, q_ref[cols, :], preferred_element_type=F32)
            acc_ref[part * half : (part + 1) * half, cols] = jnp.dot(
                key_t[part * half : (part + 1) * half], grad_scores, preferred_element_type=F32
            )
            for kb in range(length // TILE):
                at = length - TILE * kb + chunk * c
                sums_ref[part, :, at : at + chunk] += grad_scores[
                    kb * TILE : (kb + 1) * TILE
                ].astype(F32)
        grad_keys.append(grad_key)
        grad_values.append(grad_value)
    first = lanes_of((length, lanes), half, 0)
    at = pl.multiple_of(pair * lanes, lanes)
    out_ref[:, pl.ds(at, lanes)] = (acc_ref[...].T * SCALE).astype(BF)
    at = pl.multiple_of(columns + pair * lanes, lanes)
    out_ref[:, pl.ds(at, lanes)] = (jnp.where(first, *grad_keys) * SCALE).astype(BF)
    at = pl.multiple_of(2 * columns + pair * lanes, lanes)
    out_ref[:, pl.ds(at, lanes)] = jnp.where(first, *grad_values).astype(BF)


def attend_bwd(seq, qkv, grad, probs, sums, length):
    heads, _, width = sums.shape
    columns = qkv.shape[1] // 3
    pairs = heads // 2
    lanes = columns // pairs
    spec = [
        pl.BlockSpec((length, lanes), lambda p, s, j=j: (s[0], j * pairs + p)) for j in range(3)
    ]
    sums_spec = pl.BlockSpec((2, TILE, width), lambda p, s: (p, 0, 0))
    return pl.pallas_call(
        attend_bwd_kernel,
        out_shape=(
            jax.ShapeDtypeStruct((length, 3 * columns), BF),
            jax.ShapeDtypeStruct(sums.shape, F32),
        ),
        grid_spec=pltpu.PrefetchScalarGridSpec(
            num_scalar_prefetch=1,
            grid=(pairs,),
            in_specs=spec
            + [
                pl.BlockSpec((length, lanes), lambda p, s: (0, p)),
                pl.BlockSpec((2, length, length), lambda p, s: (p, 0, 0)),
                sums_spec,
            ],
            out_specs=[pl.BlockSpec((length, 3 * columns), lambda p, s: (0, 0)), sums_spec],
            scratch_shapes=[pltpu.VMEM((lanes, length), F32)],
        ),
        compiler_params=pltpu.CompilerParams(vmem_limit_bytes=VMEM_LIMIT),
        cost_estimate=pl.CostEstimate(
            flops=heads * 16 * length * length * lanes,
            bytes_accessed=heads * length * length * 2 + 16 * length * columns,
            transcendentals=0,
        ),
        name="attend_bwd",
    )(seq, qkv, qkv, qkv, grad, probs, sums)


def flipped(index, bits):
    out, step = index, 1
    while step <= bits:
        if bits & step:
            out = out + step * (1 - 2 * lax.rem(index // step, 2))
        step *= 2
    return out


def greet(peers):
    barrier = pltpu.get_barrier_semaphore()
    for peer in peers:
        pl.semaphore_signal(barrier, inc=1, device_id=peer, device_id_type=pl.DeviceIdType.MESH)
    pl.semaphore_wait(barrier, len(peers))


def remote(source, target, send_sem, recv_sem, peer):
    return pltpu.make_async_remote_copy(
        src_ref=source,
        dst_ref=target,
        send_sem=send_sem,
        recv_sem=recv_sem,
        device_id=peer,
        device_id_type=pl.DeviceIdType.MESH,
    )


def attend_all_kernel(
    input_ref,
    gain_ref,
    query_ref,
    key_ref,
    value_ref,
    table_ref,
    sent_ref,
    out_ref,
    probs_ref,
    came_ref,
    normed_out,
    qkv_out,
    acc_ref,
    block_ref,
    hold_ref,
    normed_ref,
    qkv_ref,
    row_send,
    row_recv,
    hop_send,
    hop_recv,
    hold_sem,
    own_sem,
):
    z, d = lax.axis_index("head"), lax.axis_index("dp")
    heads, _, _ = table_ref.shape
    replicas, length, columns = block_ref.shape
    pairs = heads // 2
    lanes = columns // pairs
    half = lanes // 2
    chunk = 2 * TILE
    hops = range(1, replicas)
    greet([{"dp": flipped(d, o)} for o in PEERS] + [{"head": flipped(z, r)} for r in hops])
    copies = []
    for o in PEERS:
        copies.append(
            remote(
                sent_ref.at[o],
                came_ref.at[o],
                row_send.at[o],
                row_recv.at[o],
                {"dp": flipped(d, o)},
            )
        )
        copies[-1].start()
    own = pltpu.make_async_copy(sent_ref.at[0], came_ref.at[0], own_sem.at[0])
    own.start()

    moves = []
    for turn, r in enumerate(reversed(range(replicas))):
        start = flipped(z, r) * length
        slot = turn % 2
        if turn >= 2:
            for move in moves[turn - 2]:
                move.wait()

        def norm_step(i, carry, start=start, slot=slot):
            rows = pl.multiple_of(start + i * TILE, TILE)
            value = input_ref[pl.ds(rows, TILE), :].astype(F32)
            value = rms_norm(value, gain_ref[...])
            normed_ref[slot, pl.ds(pl.multiple_of(i * TILE, TILE), TILE), :] = value.astype(BF)
            return carry

        lax.fori_loop(0, length // TILE, norm_step, 0)
        for i, weight in enumerate((query_ref, key_ref, value_ref)):
            qkv_ref[slot, :, i * columns : (i + 1) * columns] = jnp.dot(
                normed_ref[slot], weight[...], preferred_element_type=F32
            ).astype(BF)

        def pair_step(pair, carry, slot=slot, r=r):
            def part_of(j):
                at = pl.multiple_of(j * columns + pair * lanes, lanes)
                return qkv_ref[slot, :, pl.ds(at, lanes)]

            key = part_of(1)
            value_t = part_of(2).T
            scaled = part_of(0) * SCALE
            for part in range(2):
                query = jnp.where(lanes_of((length, lanes), half, part), scaled, 0).astype(BF)
                for c in range(length // chunk):
                    cols = slice(c * chunk, (c + 1) * chunk)
                    scores = contract(key, query[cols], 1, 1)
                    pieces = []
                    for kb in range(length // TILE):
                        at = length - TILE * kb + chunk * c
                        pieces.append(
                            scores[kb * TILE : (kb + 1) * TILE]
                            + table_ref[pair * 2 + part, :, at : at + chunk]
                        )
                    scores = jnp.concatenate(pieces, axis=0)
                    top = jnp.max(scores, axis=0, keepdims=True)
                    shifted = jnp.exp(scores - top)
                    total = jnp.sum(shifted, axis=0, keepdims=True)
                    probs = (shifted * (1.0 / total)).astype(BF)
                    hold_ref[slot, pair * 2 + part, :, cols] = probs
                    acc_ref[part * half : (part + 1) * half, cols] = jnp.dot(
                        value_t[part * half : (part + 1) * half],
                        probs,
                        preferred_element_type=F32,
                    )
            at = pl.multiple_of(pair * lanes, lanes)
            block_ref[r, :, pl.ds(at, lanes)] = acc_ref[...].T.astype(BF)
            return carry

        lax.fori_loop(0, pairs, pair_step, 0)
        moves.append(
            [
                pltpu.make_async_copy(ref.at[slot], out.at[r], hold_sem.at[i, slot])
                for i, (ref, out) in enumerate(
                    ((hold_ref, probs_ref), (normed_ref, normed_out), (qkv_ref, qkv_out))
                )
            ]
        )
        for move in moves[-1]:
            move.start()
        target = out_ref.at[:, pl.ds(r * columns, columns)]
        if r:
            hop = remote(
                block_ref.at[r], target, hop_send.at[r], hop_recv.at[r], {"head": flipped(z, r)}
            )
            hop.start()
            copies.append(hop)
        else:
            last = pltpu.make_async_copy(block_ref.at[0], target, own_sem.at[1])
            last.start()
    for move in moves[-2] + moves[-1]:
        move.wait()
    own.wait()
    last.wait()
    for copy in copies:
        copy.wait()


def attend_all(inputs, gain, weights, table, sent, length, replicas):
    heads, _, _ = table.shape
    width = inputs.shape[1]
    columns = weights[0].shape[1]
    lanes = 2 * columns // heads
    groups = sent.shape[0]
    vmem = pl.BlockSpec(memory_space=pltpu.VMEM)
    hbm = pl.BlockSpec(memory_space=pl.ANY)
    return pl.pallas_call(
        attend_all_kernel,
        out_shape=(
            jax.ShapeDtypeStruct((length, replicas * columns), BF),
            jax.ShapeDtypeStruct((replicas, heads, length, length), BF),
            jax.ShapeDtypeStruct(sent.shape, BF),
            jax.ShapeDtypeStruct((replicas, length, width), BF),
            jax.ShapeDtypeStruct((replicas, length, 3 * columns), BF),
        ),
        in_specs=[vmem] * 6 + [hbm],
        out_specs=[hbm] * 5,
        scratch_shapes=[
            pltpu.VMEM((lanes, length), F32),
            pltpu.VMEM((replicas, length, columns), BF),
            pltpu.VMEM((2, heads, length, length), BF),
            pltpu.VMEM((2, length, width), BF),
            pltpu.VMEM((2, length, 3 * columns), BF),
            pltpu.SemaphoreType.DMA((groups,)),
            pltpu.SemaphoreType.DMA((groups,)),
            pltpu.SemaphoreType.DMA((replicas,)),
            pltpu.SemaphoreType.DMA((replicas,)),
            pltpu.SemaphoreType.DMA((3, 2)),
            pltpu.SemaphoreType.DMA((2,)),
        ],
        compiler_params=pltpu.CompilerParams(
            vmem_limit_bytes=VMEM_LIMIT, collective_id=1, has_side_effects=True
        ),
        cost_estimate=pl.CostEstimate(
            flops=replicas * heads * 8 * length * length * lanes,
            bytes_accessed=replicas * heads * length * length * 4,
            transcendentals=replicas * heads * length * length,
        ),
        name="attend_all",
    )(inputs, gain, *weights, table, sent)


def expert_tile(rows, scaled, gate_w, up_w, down_w):
    gate = jnp.dot(rows, gate_w, preferred_element_type=F32)
    up_part = jnp.dot(rows, up_w, preferred_element_type=F32)
    grad_hidden = contract(scaled, down_w, 1, 1)
    square = gate * gate
    bend = jnp.tanh(gate * (GELU_A + GELU_A * GELU_B * square))
    half = 0.5 + 0.5 * bend
    active = gate * half
    slope = half + 0.5 * gate * (1.0 - bend * bend) * (GELU_A + 3.0 * GELU_A * GELU_B * square)
    hidden = (active * up_part).astype(BF)
    grad_gate = (grad_hidden * up_part * slope).astype(BF)
    grad_up = (grad_hidden * active).astype(BF)
    return hidden, grad_gate, grad_up


def scaled_rows(rows, extended, router, width):
    logits = jnp.dot(rows, router, preferred_element_type=F32)
    sign = extended[:, width:].astype(F32)
    gap = jnp.sum(logits * sign, axis=1, keepdims=True)
    return (extended[:, :width].astype(F32) * (1.0 / (1.0 + jnp.exp(gap)))).astype(BF)


def expert_kernel(
    width,
    tile,
    normed_ref,
    both_ref,
    cot_ref,
    router_ref,
    gate_hbm,
    up_hbm,
    down_hbm,
    rows_out,
    hidden_out,
    grad_gate_out,
    grad_up_out,
    scaled_out,
    back_out,
    grad_back_out,
    gate_w,
    up_w,
    down_w,
    rows,
    sends,
    back,
    grad_back,
    hidden,
    grad_gate,
    grad_up,
    scaled,
    weight_sem,
    row_send,
    row_recv,
    back_send,
    back_recv,
    grad_send,
    grad_recv,
    unit_sem,
    keep_sem,
):
    d = lax.axis_index("dp")
    groups, capacity, _ = rows.shape
    units = gate_w.shape[1]
    tiles = units // tile
    count = 2 * capacity

    def weights_of(t):
        at = pl.multiple_of(t * tile, tile)
        return [
            pltpu.make_async_copy(
                gate_hbm.at[:, pl.ds(at, tile)], gate_w.at[:, pl.ds(at, tile)], weight_sem.at[0, t]
            ),
            pltpu.make_async_copy(
                up_hbm.at[:, pl.ds(at, tile)], up_w.at[:, pl.ds(at, tile)], weight_sem.at[1, t]
            ),
            pltpu.make_async_copy(
                down_hbm.at[pl.ds(at, tile), :], down_w.at[pl.ds(at, tile), :], weight_sem.at[2, t]
            ),
        ]

    def start_weights(t, carry):
        for copy in weights_of(t):
            copy.start()
        return carry

    lax.fori_loop(0, tiles, start_weights, 0)
    greet([{"dp": flipped(d, o)} for o in PEERS])
    pending = []
    arrivals = {}
    for o in PEERS:
        sends[o] = jnp.dot(
            both_ref[o * capacity : (o + 1) * capacity],
            normed_ref[...],
            preferred_element_type=F32,
        ).astype(BF)
        arrivals[o] = remote(
            sends.at[o], rows.at[o], row_send.at[o], row_recv.at[o], {"dp": flipped(d, o)}
        )
        arrivals[o].start()
    rows[0] = jnp.dot(
        both_ref[:capacity], normed_ref[...], preferred_element_type=F32
    ).astype(BF)

    unit_copies = {}
    for j in range(groups // 2):
        pair = (2 * j, 2 * j + 1)
        slot = j % 2
        for o in pair:
            if o:
                arrivals[o].wait_recv()
        if j >= 2:
            for copy in unit_copies[j - 2]:
                copy.wait()
        here = rows[2 * j : 2 * j + 2].reshape(count, width)
        extended = cot_ref[2 * j : 2 * j + 2].reshape(count, cot_ref.shape[2])
        scaled[2 * j : 2 * j + 2] = scaled_rows(here, extended, router_ref[...], width).reshape(
            2, capacity, width
        )

        def tile_step(t, carry, j=j, slot=slot):
            at = pl.multiple_of(t * tile, tile)
            if j == 0:
                for copy in weights_of(t):
                    copy.wait()
            values = expert_tile(
                rows[2 * j : 2 * j + 2].reshape(count, width),
                scaled[2 * j : 2 * j + 2].reshape(count, width),
                gate_w[:, pl.ds(at, tile)],
                up_w[:, pl.ds(at, tile)],
                down_w[pl.ds(at, tile), :],
            )
            for ref, value in zip((hidden, grad_gate, grad_up), values):
                ref[slot, :, pl.ds(at, tile)] = value
            return carry

        lax.fori_loop(0, tiles, tile_step, 0)
        span = pl.ds(j * count, count)
        unit_copies[j] = [
            pltpu.make_async_copy(ref.at[slot], out.at[span], unit_sem.at[slot, i])
            for i, (ref, out) in enumerate(
                ((hidden, hidden_out), (grad_gate, grad_gate_out), (grad_up, grad_up_out))
            )
        ]
        for copy in unit_copies[j]:
            copy.start()

        def back_step(t, carry, j=j, slot=slot):
            at = pl.multiple_of(t * tile, tile)
            value = jnp.dot(hidden[slot], down_w[:, pl.ds(at, tile)], preferred_element_type=F32)
            back[2 * j : 2 * j + 2, :, pl.ds(at, tile)] = value.astype(BF).reshape(
                2, capacity, tile
            )
            return carry

        def grad_step(t, carry, j=j, slot=slot):
            at = pl.multiple_of(t * tile, tile)
            value = contract(grad_gate[slot], gate_w[pl.ds(at, tile), :], 1, 1) + contract(
                grad_up[slot], up_w[pl.ds(at, tile), :], 1, 1
            )
            grad_back[2 * j : 2 * j + 2, :, pl.ds(at, tile)] = value.astype(BF).reshape(
                2, capacity, tile
            )
            return carry

        for step, buffer, out, send_sem, recv_sem in (
            (back_step, back, back_out, back_send, back_recv),
            (grad_step, grad_back, grad_back_out, grad_send, grad_recv),
        ):
            lax.fori_loop(0, width // tile, step, 0)
            for o in pair:
                if o:
                    copy = remote(
                        buffer.at[o],
                        out.at[o],
                        send_sem.at[o],
                        recv_sem.at[o],
                        {"dp": flipped(d, o)},
                    )
                else:
                    copy = pltpu.make_async_copy(buffer.at[0], out.at[0], send_sem.at[0])
                copy.start()
                pending.append(copy)

    keeps = [
        pltpu.make_async_copy(rows, rows_out, keep_sem.at[0]),
        pltpu.make_async_copy(scaled, scaled_out, keep_sem.at[1]),
    ]
    for copy in keeps:
        copy.start()
    for j in range(groups // 2 - 2, groups // 2):
        for copy in unit_copies[j]:
            copy.wait()
    for o in PEERS:
        arrivals[o].wait_send()
    for copy in pending + keeps:
        copy.wait()


def expert_stage(normed2, both, cot, router, gate_w, up_w, down_w, groups, capacity, tile):
    width, units = gate_w.shape
    slots = groups * capacity
    vmem = pl.BlockSpec(memory_space=pltpu.VMEM)
    hbm = pl.BlockSpec(memory_space=pl.ANY)
    row_shape = jax.ShapeDtypeStruct((groups, capacity, width), BF)
    unit_shape = jax.ShapeDtypeStruct((slots, units), BF)
    row_buffer = pltpu.VMEM((groups, capacity, width), BF)
    unit_buffer = pltpu.VMEM((2, 2 * capacity, units), BF)
    row_sem = pltpu.SemaphoreType.DMA((groups,))
    return pl.pallas_call(
        functools.partial(expert_kernel, width, tile),
        out_shape=(row_shape,) + (unit_shape,) * 3 + (row_shape,) * 3,
        in_specs=[vmem] * 4 + [hbm] * 3,
        out_specs=[hbm] * 7,
        scratch_shapes=[
            pltpu.VMEM((width, units), BF),
            pltpu.VMEM((width, units), BF),
            pltpu.VMEM((units, width), BF),
            row_buffer,
            row_buffer,
            row_buffer,
            row_buffer,
            unit_buffer,
            unit_buffer,
            unit_buffer,
            row_buffer,
            pltpu.SemaphoreType.DMA((3, units // tile)),
            row_sem,
            row_sem,
            row_sem,
            row_sem,
            row_sem,
            row_sem,
            pltpu.SemaphoreType.DMA((2, 3)),
            pltpu.SemaphoreType.DMA((2,)),
        ],
        compiler_params=pltpu.CompilerParams(
            vmem_limit_bytes=VMEM_MOST, collective_id=2, has_side_effects=True
        ),
        cost_estimate=pl.CostEstimate(
            flops=12 * slots * width * units,
            bytes_accessed=6 * width * units + 6 * slots * units,
            transcendentals=slots * units,
        ),
        name="expert_stage",
    )(normed2, both, cot, router, gate_w, up_w, down_w)


def attend_back_kernel(
    far_ref,
    both_ref,
    signs_ref,
    grad_ref,
    qkv_hbm,
    probs_hbm,
    query_w,
    key_w,
    value_w,
    far_out,
    grad_qkv_out,
    grad_normed_out,
    sums_ref,
    acc_ref,
    sends,
    grads,
    qkv_ref,
    probs_ref,
    grad_qkv_ref,
    parts,
    landed,
    far_send,
    far_recv,
    hop_send,
    hop_recv,
    part_send,
    part_recv,
    load_sem,
    store_sem,
    own_sem,
):
    z, d = lax.axis_index("head"), lax.axis_index("dp")
    replicas, length, columns = grads.shape
    groups, capacity, extent = sends.shape
    heads, _, width = sums_ref.shape
    pairs = heads // 2
    lanes = columns // pairs
    half = lanes // 2
    chunk = 2 * TILE
    hops = range(1, replicas)
    order = [0, 3, 2, 1]

    def loads(turn):
        r, slot = order[turn], turn % 2
        return [
            pltpu.make_async_copy(qkv_hbm.at[r], qkv_ref.at[slot], load_sem.at[0, slot]),
            pltpu.make_async_copy(probs_hbm.at[r], probs_ref.at[slot], load_sem.at[1, slot]),
        ]

    for copy in loads(0):
        copy.start()
    greet([{"dp": flipped(d, o)} for o in PEERS] + [{"head": flipped(z, r)} for r in hops])
    copies = []
    arrivals = {}
    for r in order[1:]:
        arrivals[r] = remote(
            grad_ref.at[:, pl.ds(r * columns, columns)],
            grads.at[r],
            hop_send.at[r],
            hop_recv.at[r],
            {"head": flipped(z, r)},
        )
        arrivals[r].start()
    model = extent - TILE
    for o in PEERS + [0]:
        span = slice(o * capacity, (o + 1) * capacity)
        sends[o, :, :model] = jnp.dot(
            both_ref[span], far_ref[...], preferred_element_type=F32
        ).astype(BF)
        sends[o, :, model:] = signs_ref[span]
        if o:
            copy = remote(
                sends.at[o],
                far_out.at[o],
                far_send.at[o],
                far_recv.at[o],
                {"dp": flipped(d, o)},
            )
        else:
            copy = pltpu.make_async_copy(sends.at[0], far_out.at[0], own_sem)
        copy.start()
        copies.append(copy)
    sums_ref[...] = jnp.zeros_like(sums_ref)
    grads[0] = grad_ref[:, :columns]

    stores = []
    for turn, r in enumerate(order):
        slot = turn % 2
        if turn + 1 < replicas:
            for copy in loads(turn + 1):
                copy.start()
        for copy in loads(turn):
            copy.wait()
        if r:
            arrivals[r].wait_recv()
        if turn >= 2:
            stores[turn - 2].wait()

        def pair_step(pair, carry, slot=slot, r=r):
            def part_of(j):
                at = pl.multiple_of(j * columns + pair * lanes, lanes)
                return qkv_ref[slot, :, pl.ds(at, lanes)]

            at = pl.multiple_of(pair * lanes, lanes)
            query, value = part_of(0), part_of(2)
            key_t = part_of(1).T
            grad_all = grads[r, :, pl.ds(at, lanes)]
            grad_keys, grad_values = [], []
            for part in range(2):
                mask = lanes_of((length, lanes), half, part)
                grad = jnp.where(mask, grad_all, 0).astype(BF)
                grad_key = jnp.zeros((length, lanes), F32)
                grad_value = jnp.zeros((length, lanes), F32)
                for c in range(length // chunk):
                    cols = slice(c * chunk, (c + 1) * chunk)
                    grad_probs = contract(value, grad[cols], 1, 1)
                    probs_low = probs_ref[slot, pair * 2 + part, :, cols]
                    probs = probs_low.astype(F32)
                    delta = jnp.sum(probs * grad_probs, axis=0, keepdims=True)
                    grad_scores = (probs * (grad_probs - delta)).astype(BF)
                    grad_value += jnp.dot(probs_low, grad_all[cols], preferred_element_type=F32)
                    grad_key += jnp.dot(grad_scores, query[cols], preferred_element_type=F32)
                    acc_ref[part * half : (part + 1) * half, cols] = jnp.dot(
                        key_t[part * half : (part + 1) * half],
                        grad_scores,
                        preferred_element_type=F32,
                    )
                    for kb in range(length // TILE):
                        to = length - TILE * kb + chunk * c
                        sums_ref[pair * 2 + part, :, to : to + chunk] += grad_scores[
                            kb * TILE : (kb + 1) * TILE
                        ].astype(F32)
                grad_keys.append(grad_key)
                grad_values.append(grad_value)
            first = lanes_of((length, lanes), half, 0)
            results = (
                acc_ref[...].T * SCALE,
                jnp.where(first, *grad_keys) * SCALE,
                jnp.where(first, *grad_values),
            )
            for j, result in enumerate(results):
                to = pl.multiple_of(j * columns + pair * lanes, lanes)
                grad_qkv_ref[slot, :, pl.ds(to, lanes)] = result.astype(BF)
            return carry

        lax.fori_loop(0, pairs, pair_step, 0)
        stores.append(
            pltpu.make_async_copy(grad_qkv_ref.at[slot], grad_qkv_out.at[r], store_sem.at[slot])
        )
        stores[-1].start()

        def part_step(i, carry, slot=slot, r=r):
            span = pl.ds(pl.multiple_of(i * TILE, TILE), TILE)
            total = sum(
                contract(
                    grad_qkv_ref[slot, :, j * columns : (j + 1) * columns], weight[span, :], 1, 1
                )
                for j, weight in enumerate((query_w, key_w, value_w))
            )
            parts[r, :, span] = total.astype(BF)
            return carry

        lax.fori_loop(0, parts.shape[2] // TILE, part_step, 0)
        if r:
            copy = remote(
                parts.at[r], landed.at[r], part_send.at[r], part_recv.at[r], {"head": flipped(z, r)}
            )
            copy.start()
            copies.append(copy)

    for r in order[1:]:
        arrivals[r].wait_send()
    stores[-2].wait()
    stores[-1].wait()
    for copy in copies:
        copy.wait()
    grad_normed_out[...] = parts[0].astype(F32) + sum(landed[r].astype(F32) for r in hops)


def attend_back(far_own, both_far, signs_far, grad_heads, qkv, probs, weights, groups):
    replicas, length, triple = qkv.shape
    heads = probs.shape[1]
    columns = triple // 3
    width = weights[0].shape[0]
    lanes = 2 * columns // heads
    capacity = both_far.shape[0] // groups
    extent = far_own.shape[1] + TILE
    vmem = pl.BlockSpec(memory_space=pltpu.VMEM)
    hbm = pl.BlockSpec(memory_space=pl.ANY)
    hop_sem = pltpu.SemaphoreType.DMA((replicas,))
    return pl.pallas_call(
        attend_back_kernel,
        out_shape=(
            jax.ShapeDtypeStruct((groups, capacity, extent), BF),
            jax.ShapeDtypeStruct((replicas, length, triple), BF),
            jax.ShapeDtypeStruct((length, width), F32),
            jax.ShapeDtypeStruct((heads, TILE, 2 * length), F32),
        ),
        in_specs=[vmem] * 4 + [hbm] * 2 + [vmem] * 3,
        out_specs=[hbm, hbm, vmem, vmem],
        scratch_shapes=[
            pltpu.VMEM((lanes, length), F32),
            pltpu.VMEM((groups, capacity, extent), BF),
            pltpu.VMEM((replicas, length, columns), BF),
            pltpu.VMEM((2, length, triple), BF),
            pltpu.VMEM((2, heads, length, length), BF),
            pltpu.VMEM((2, length, triple), BF),
            pltpu.VMEM((replicas, length, width), BF),
            pltpu.VMEM((replicas, length, width), BF),
            pltpu.SemaphoreType.DMA((groups,)),
            pltpu.SemaphoreType.DMA((groups,)),
            hop_sem,
            hop_sem,
            hop_sem,
            hop_sem,
            pltpu.SemaphoreType.DMA((2, 2)),
            pltpu.SemaphoreType.DMA((2,)),
            pltpu.SemaphoreType.DMA,
        ],
        compiler_params=pltpu.CompilerParams(
            vmem_limit_bytes=VMEM_LIMIT, collective_id=3, has_side_effects=True
        ),
        cost_estimate=pl.CostEstimate(
            flops=replicas * heads * 16 * length * length * lanes,
            bytes_accessed=replicas * heads * length * length * 4,
            transcendentals=0,
        ),
        name="attend_back",
    )(far_own, both_far, signs_far, grad_heads, qkv, probs, *weights)


def last_kernel(
    tile,
    far_ref,
    rows_here,
    scaled_here,
    router_ref,
    gate_hbm,
    up_hbm,
    down_hbm,
    grad_gate_hbm,
    grad_up_hbm,
    hidden_hbm,
    qkv_w_hbm,
    out_w_hbm,
    small_ref,
    gate_out,
    up_out,
    down_out,
    qkv_w_out,
    out_w_out,
    small_out,
    scaled,
    left,
    weights,
    downs,
    units,
    hidden,
    hidden_here,
    send_wide,
    came_wide,
    send_tall,
    came_tall,
    qkv_land,
    qkv_sum,
    out_land,
    out_sum,
    out_hop,
    out_last,
    small_land,
    small_sum,
    small_hop,
    stream_sem,
    hidden_sem,
    wide_send,
    wide_recv,
    tall_sem,
    first_send,
    first_recv,
    hop_send,
    hop_recv,
    third_send,
    third_recv,
    own_sem,
):
    z, d = lax.axis_index("head"), lax.axis_index("dp")
    groups, capacity, _ = far_ref.shape
    slots, width = scaled_here.shape
    rows, total_units = gate_out.shape
    half_units = hidden_here.shape[1]
    tiles = total_units // tile
    low, high = lax.rem(z, 2), z // 2
    keep_at = pl.multiple_of(low * rows, rows)
    send_at = pl.multiple_of((1 - low) * rows, rows)
    near = {"head": flipped(z, 1)}
    count = 2 * capacity
    hops = [3, 2, 1]

    def streams(t):
        slot = lax.rem(t, 2)
        at = pl.multiple_of(t * tile, tile)
        cols = pl.ds(at, tile)
        return [
            pltpu.make_async_copy(gate_hbm.at[:, cols], weights.at[slot, 0], stream_sem.at[0, slot]),
            pltpu.make_async_copy(up_hbm.at[:, cols], weights.at[slot, 1], stream_sem.at[1, slot]),
            pltpu.make_async_copy(down_hbm.at[cols, :], downs.at[slot], stream_sem.at[2, slot]),
            pltpu.make_async_copy(
                grad_gate_hbm.at[:, cols], units.at[slot, 0], stream_sem.at[3, slot]
            ),
            pltpu.make_async_copy(
                grad_up_hbm.at[:, cols], units.at[slot, 1], stream_sem.at[4, slot]
            ),
        ]

    for copy in streams(0):
        copy.start()
    half_copy = pltpu.make_async_copy(
        hidden_hbm.at[:, pl.ds(pl.multiple_of(high * half_units, TILE), half_units)],
        hidden_here,
        hidden_sem,
    )
    half_copy.start()
    greet([{"dp": flipped(d, o)} for o in PEERS] + [{"head": flipped(z, r)} for r in hops])

    first = []
    for o in PEERS:
        peer = flipped(d, o)
        for i, (source, target) in enumerate(
            (
                (qkv_w_hbm.at[peer], qkv_land.at[o]),
                (out_w_hbm.at[:, peer], out_land.at[o]),
                (small_ref, small_land.at[o]),
            )
        ):
            copy = remote(source, target, first_send.at[i, o], first_recv.at[i, o], {"dp": peer})
            copy.start()
            first.append(copy)
    own = [
        pltpu.make_async_copy(qkv_w_hbm.at[d], qkv_land.at[0], own_sem.at[0]),
        pltpu.make_async_copy(out_w_hbm.at[:, d], out_land.at[0], own_sem.at[1]),
    ]
    for copy in own:
        copy.start()

    for j in range(groups // 2):
        span = slice(j * count, (j + 1) * count)
        here = far_ref[2 * j : 2 * j + 2, :, :width].reshape(count, width)
        extended = far_ref[2 * j : 2 * j + 2, :, width:].reshape(count, width + TILE)
        scaled[span] = scaled_rows(here, extended, router_ref[...], width)

    wide = 2 * rows
    columns = pl.ds(pl.multiple_of(high * wide, wide), wide)

    def left_step(i, carry):
        at = pl.multiple_of(i * capacity, capacity)
        left[0, pl.ds(at, capacity), :] = rows_here[pl.ds(at, capacity), columns]
        left[1, pl.ds(at, capacity), :] = far_ref[i, :, columns]
        return carry

    lax.fori_loop(0, groups, left_step, 0)

    def wide_copy(i, t):
        at = pl.multiple_of(t * tile, tile)
        return remote(
            send_wide.at[i, :, pl.ds(at, tile)],
            came_wide.at[i, :, pl.ds(at, tile)],
            wide_send.at[i, t],
            wide_recv.at[i, t],
            near,
        )

    def tile_step(t, carry):
        slot = lax.rem(t, 2)
        at = pl.multiple_of(t * tile, tile)

        @pl.when(t + 1 < tiles)
        def _():
            for copy in streams(t + 1):
                copy.start()

        for copy in streams(t):
            copy.wait()

        def chunk_step(j, inner):
            span = pl.ds(pl.multiple_of(j * count, count), count)
            here = far_ref[pl.ds(2 * j, 2), :, :width].reshape(count, width)
            values = expert_tile(
                here, scaled[span], weights[slot, 0], weights[slot, 1], downs[slot]
            )
            hidden[span, pl.ds(at, tile)] = values[0]
            units[slot, 2, span, :] = values[1]
            units[slot, 3, span, :] = values[2]
            return inner

        lax.fori_loop(0, groups // 2, chunk_step, 0)
        for i, out in enumerate((gate_out, up_out)):
            value = contract(left[0], units[slot, i], 0, 0) + contract(
                left[1], units[slot, 2 + i], 0, 0
            )
            upper = low == 1
            send_wide[i, :, pl.ds(at, tile)] = jnp.where(
                upper, value[:rows], value[rows:]
            ).astype(BF)
            out[:, pl.ds(at, tile)] = jnp.where(upper, value[rows:], value[:rows])
            wide_copy(i, t).start()
        return carry

    middle = tiles // 2
    lax.fori_loop(0, middle, tile_step, 0)

    for copy in first:
        copy.wait()
    for copy in own:
        copy.wait()
    small_land[0] = small_ref[...]
    qkv_sum[...] = sum(qkv_land[o].astype(F32) for o in range(groups)).astype(BF)
    out_sum[...] = sum(out_land[o].astype(F32) for o in range(groups)).astype(BF)
    small_sum[...] = sum(small_land[o] for o in range(groups))
    second = []
    for o in PEERS:
        copy = remote(
            qkv_sum, qkv_w_out.at[d], third_send.at[0, o], third_recv.at[0, o], {"dp": flipped(d, o)}
        )
        copy.start()
        second.append(copy)
    mine = [pltpu.make_async_copy(qkv_sum, qkv_w_out.at[d], own_sem.at[0])]
    mine[0].start()
    over = []
    for r in hops:
        for i, (source, target) in enumerate(
            ((out_sum.at[r], out_hop.at[r]), (small_sum, small_hop.at[r]))
        ):
            copy = remote(
                source, target, hop_send.at[i, r], hop_recv.at[i, r], {"head": flipped(z, r)}
            )
            copy.start()
            over.append(copy)

    lax.fori_loop(middle, tiles, tile_step, 0)

    for copy in over:
        copy.wait()
    out_last[...] = (
        out_sum[0].astype(F32) + sum(out_hop[r].astype(F32) for r in hops)
    ).astype(BF)
    small_out[0] = small_sum[...]
    small_out[1] = small_sum[...] + sum(small_hop[r] for r in hops)
    for o in PEERS:
        copy = remote(
            out_last,
            out_w_out.at[d],
            third_send.at[1, o],
            third_recv.at[1, o],
            {"dp": flipped(d, o)},
        )
        copy.start()
        second.append(copy)
    mine.append(pltpu.make_async_copy(out_last, out_w_out.at[d], own_sem.at[1]))
    mine[1].start()

    half_copy.wait()
    share = half_units // 2
    halves = pl.ds(pl.multiple_of(high * half_units, TILE), half_units)

    def tall_step(i, carry):
        cols = pl.ds(pl.multiple_of(i * tile, tile), tile)
        value = contract(hidden_here[...], scaled_here[:, cols], 0, 0) + contract(
            hidden[:, halves], scaled[:, cols], 0, 0
        )
        upper = low == 1
        send_tall[:, cols] = jnp.where(upper, value[:share], value[share:]).astype(BF)
        down_out[:, cols] = jnp.where(upper, value[share:], value[:share])
        return carry

    lax.fori_loop(0, width // tile, tall_step, 0)
    tall = remote(send_tall, came_tall, tall_sem.at[0], tall_sem.at[1], near)
    tall.start()

    def wide_end(t, carry):
        at = pl.multiple_of(t * tile, tile)
        for i, out in enumerate((gate_out, up_out)):
            wide_copy(i, t).wait()
            out[:, pl.ds(at, tile)] += came_wide[i, :, pl.ds(at, tile)].astype(F32)
        return carry

    lax.fori_loop(0, tiles, wide_end, 0)
    for copy in second + mine:
        copy.wait()
    tall.wait()
    down_out[...] += came_tall[...].astype(F32)


def last_stage(
    far, rows_here, scaled_here, router, weights, grads_here, hidden_here, qkv_w, out_w, small, tile
):
    gate_w, up_w, down_w = weights
    width, units = gate_w.shape
    groups, capacity, extent = far.shape
    replicas, _, part_rows, _ = out_w.shape
    slots = groups * capacity
    vmem = pl.BlockSpec(memory_space=pltpu.VMEM)
    hbm = pl.BlockSpec(memory_space=pl.ANY)
    rows, share = width // replicas, units // replicas
    plane_sem = pltpu.SemaphoreType.DMA((3, groups))
    hop_sem = pltpu.SemaphoreType.DMA((2, replicas))
    return pl.pallas_call(
        functools.partial(last_kernel, tile),
        out_shape=(
            jax.ShapeDtypeStruct((rows, units), F32),
            jax.ShapeDtypeStruct((rows, units), F32),
            jax.ShapeDtypeStruct((share, width), F32),
            jax.ShapeDtypeStruct(qkv_w.shape, BF),
            jax.ShapeDtypeStruct(out_w.shape[1:], BF),
            jax.ShapeDtypeStruct((2,) + small.shape, F32),
        ),
        in_specs=[vmem] * 4 + [hbm] * 8 + [vmem],
        out_specs=[vmem, vmem, vmem, hbm, hbm, vmem],
        scratch_shapes=[
            pltpu.VMEM((slots, width), BF),
            pltpu.VMEM((2, slots, 2 * rows), BF),
            pltpu.VMEM((2, 2, width, tile), BF),
            pltpu.VMEM((2, tile, width), BF),
            pltpu.VMEM((2, 4, slots, tile), BF),
            pltpu.VMEM((slots, units), BF),
            pltpu.VMEM((slots, units // 2), BF),
            pltpu.VMEM((2, rows, units), BF),
            pltpu.VMEM((2, rows, units), BF),
            pltpu.VMEM((share, width), BF),
            pltpu.VMEM((share, width), BF),
            pltpu.VMEM(qkv_w.shape, BF),
            pltpu.VMEM(qkv_w.shape[1:], BF),
            pltpu.VMEM((groups, replicas, part_rows, width), BF),
            pltpu.VMEM((replicas, part_rows, width), BF),
            pltpu.VMEM((replicas, part_rows, width), BF),
            pltpu.VMEM((part_rows, width), BF),
            pltpu.VMEM((groups,) + small.shape, F32),
            pltpu.VMEM(small.shape, F32),
            pltpu.VMEM((replicas,) + small.shape, F32),
            pltpu.SemaphoreType.DMA((5, 2)),
            pltpu.SemaphoreType.DMA,
            pltpu.SemaphoreType.DMA((2, units // tile)),
            pltpu.SemaphoreType.DMA((2, units // tile)),
            pltpu.SemaphoreType.DMA((2,)),
            plane_sem,
            plane_sem,
            hop_sem,
            hop_sem,
            plane_sem,
            plane_sem,
            pltpu.SemaphoreType.DMA((2,)),
        ],
        compiler_params=pltpu.CompilerParams(
            vmem_limit_bytes=VMEM_MOST, collective_id=4, has_side_effects=True
        ),
        cost_estimate=pl.CostEstimate(
            flops=12 * slots * width * units,
            bytes_accessed=6 * width * units + 6 * slots * units,
            transcendentals=slots * units,
        ),
        name="last_stage",
    )(
        far,
        rows_here,
        scaled_here,
        router,
        gate_w,
        up_w,
        down_w,
        *grads_here,
        hidden_here,
        qkv_w,
        out_w,
        small,
    )


def expert_forward(rows, gate_w, up_w, grad_unscaled, slot_gates):
    gate_pre = jnp.dot(rows, gate_w, preferred_element_type=F32)
    up_pre = jnp.dot(rows, up_w, preferred_element_type=F32)
    hidden, pull = jax.vjp(geglu, gate_pre, up_pre)
    grad_gate_pre, grad_up_pre = pull(grad_unscaled * slot_gates)
    return hidden.astype(BF), grad_gate_pre.astype(BF), grad_up_pre.astype(BF)


def body_plain(
    block_input,
    cotangent,
    expert_ids,
    priority,
    rel_bucket,
    norm1_gain,
    w_query,
    w_key,
    w_value,
    w_out,
    pos_bias,
    norm2_gain,
    w_router,
    w_gate,
    w_up,
    w_down,
):
    group_rows, width = block_input.shape
    own_rows = cotangent.shape[0]
    buckets, heads_here = pos_bias.shape
    head_cols = w_query.shape[1]
    length = (rel_bucket.shape[0] + 1) // 2
    sequences = group_rows // length
    experts = w_router.shape[1]
    capacity = 5 * 2 * own_rows // (4 * experts)
    slot_count = experts * capacity
    replicas = lax.axis_size("head")
    groups = lax.axis_size("dp")
    me = lax.axis_index("head")
    far = replicas // 2
    far_perm = [(i, i ^ far) for i in range(replicas)]
    stepwise = own_rows == length and sequences == replicas

    def hop(value, r):
        return lax.ppermute(value, "head", [(i, i ^ r) for i in range(replicas)])

    def exchange(value):
        parts = value.reshape(experts, capacity, -1)
        return lax.all_to_all(parts, "dp", split_axis=0, concat_axis=0, tiled=True).reshape(
            slot_count, -1
        )

    dest = route_slots(expert_ids, priority[0], experts, capacity)
    dest_far = lax.ppermute(dest, "head", far_perm)
    slot_range = jnp.arange(slot_count, dtype=jnp.int32)[None, :]
    picks = [(dest[:, k : k + 1] == slot_range).astype(BF) for k in range(2)]
    both = picks[0] + picks[1]
    both_far = sum((dest_far[:, k : k + 1] == slot_range).astype(BF) for k in range(2))

    down_w, gate_w, up_w = w_down[0], w_gate[0], w_up[0]
    cot_here = exchange(contract(both, cotangent, 0, 0).astype(BF))
    cot_far_own = lax.ppermute(cotangent, "head", far_perm)
    cot_far = exchange(contract(both_far, cot_far_own, 0, 0).astype(BF))
    unscaled_here = contract(cot_here, down_w, 1, 1)
    unscaled_far = contract(cot_far, down_w, 1, 1)

    dp_at = lax.axis_index("dp")
    out_rows = head_cols // groups
    piece = lax.dynamic_slice_in_dim(w_out, dp_at * out_rows, out_rows, 0)
    w_out_all = lax.all_gather(piece, ("head", "dp"), axis=0, tiled=True)
    w_qkv = jnp.concatenate([w_query, w_key, w_value], axis=1)
    qkv_rows = width // groups
    piece = lax.dynamic_slice_in_dim(w_qkv, dp_at * qkv_rows, qkv_rows, 0)
    w_qkv_all = lax.all_gather(piece, ("head", "dp"), axis=0, tiled=True)
    if stepwise:
        order = [me ^ r for r in range(replicas)]
    else:
        order = list(range(replicas))
    w_out_all = w_out_all.reshape(replicas, head_cols, width)
    w_qkv_all = w_qkv_all.reshape(replicas, width, 3 * head_cols)
    w_out_cat = jnp.concatenate(
        [lax.dynamic_index_in_dim(w_out_all, o, 0, keepdims=False) for o in order], axis=0
    )

    inputs_all = block_input.astype(F32)
    normed = rms_norm(inputs_all, norm1_gain).astype(BF)
    qkv = jnp.dot(normed, w_qkv, preferred_element_type=F32).astype(BF)
    line = (rel_bucket[::-1][None, :] == jnp.arange(buckets, dtype=jnp.int32)[:, None]).astype(F32)
    line = jnp.pad(line, ((0, 0), (1, 0)))
    table = skew(contract(pos_bias, line, 0, 0, HIGH))
    kept = {}
    if stepwise:
        blocks = [None] * replicas
        for r in reversed(range(replicas)):
            attended_seq, probs = attend_fwd(order[r].reshape(1), qkv, table, length)
            kept[r] = probs
            blocks[r] = hop(attended_seq, r) if r else attended_seq
    else:
        seqs = []
        for s in range(sequences):
            attended_seq, kept[s] = attend_fwd(jnp.full((1,), s, jnp.int32), qkv, table, length)
            seqs.append(attended_seq)
        attended_all = jnp.concatenate(seqs, axis=0).reshape(replicas, own_rows, head_cols)
        attended_all = lax.all_to_all(attended_all, "head", split_axis=0, concat_axis=0, tiled=True)
        blocks = [attended_all[i] for i in range(replicas)]
    attended = jnp.concatenate(blocks, axis=1)

    branch = jnp.dot(attended, w_out_cat, preferred_element_type=F32)
    start_own = me * own_rows
    inputs_own = lax.dynamic_slice_in_dim(block_input, start_own, own_rows, 0).astype(F32)
    mixed = inputs_own + branch
    normed2_full, norm2_pull = jax.vjp(rms_norm, mixed, norm2_gain)
    normed2 = normed2_full.astype(BF)
    logits = jnp.dot(normed2, w_router, preferred_element_type=F32)
    expert_range = jnp.arange(experts, dtype=jnp.int32)
    chosen = (expert_ids[:, :, None] == expert_range[None, None, :]).astype(F32)
    gates = jax.nn.softmax(jnp.sum(chosen * logits[:, None, :], axis=2), axis=-1)

    def slot_gates_of(places, values):
        terms = sum(
            jnp.where(places[:, k : k + 1] == slot_range, values[:, k : k + 1], 0.0)
            for k in range(2)
        )
        return jnp.sum(terms, axis=0)

    rows_here = exchange(contract(both, normed2, 0, 0).astype(BF))
    gates_here = exchange(slot_gates_of(dest, gates))
    normed2_far = lax.ppermute(normed2, "head", far_perm)
    gates_far_own = lax.ppermute(gates, "head", far_perm)
    rows_far = exchange(contract(both_far, normed2_far, 0, 0).astype(BF))
    gates_far = exchange(slot_gates_of(dest_far, gates_far_own))

    hidden_here, ggp_here, gup_here = expert_forward(
        rows_here, gate_w, up_w, unscaled_here, gates_here
    )
    returned = jnp.dot(hidden_here, down_w, preferred_element_type=F32).astype(BF)
    came_back = exchange(returned)
    grad_routed = (contract(ggp_here, gate_w, 1, 1) + contract(gup_here, up_w, 1, 1)).astype(BF)
    grad_back = exchange(grad_routed)
    hidden_far, ggp_far, gup_far = expert_forward(rows_far, gate_w, up_w, unscaled_far, gates_far)
    scaled_here = (cot_here.astype(F32) * gates_here).astype(BF)
    scaled_far = (cot_far.astype(F32) * gates_far).astype(BF)

    low = me % far
    high = me // far

    def reduced(lefts, rights):
        rows = lefts[0].shape[1] // replicas

        def part(at):
            return sum(
                contract(lax.dynamic_slice_in_dim(left, at * rows, rows, 1), right, 0, 0)
                for left, right in zip(lefts, rights)
            )

        if far == 2:
            sent = hop(part(high * far + (1 - low)).astype(BF), 1)
            return (part(me) + sent.astype(F32))[None]
        whole = jnp.concatenate([part(high * far + i) for i in range(far)], axis=0).astype(BF)
        member = [[h * far + i for i in range(far)] for h in range(2)]
        return lax.psum_scatter(
            whole, "head", scatter_dimension=0, axis_index_groups=member, tiled=True
        ).astype(F32)[None]

    grad_down_w = reduced((hidden_here, hidden_far), (scaled_here, scaled_far))
    grad_gate_w = reduced((rows_here, rows_far), (ggp_here, ggp_far))
    grad_up_w = reduced((rows_here, rows_far), (gup_here, gup_far))

    chosen_rows = [jnp.dot(pick, came_back, preferred_element_type=F32) for pick in picks]
    output = mixed + sum(gates[:, k : k + 1] * chosen_rows[k] for k in range(2))
    grad_output = cotangent.astype(F32)
    grad_gates = jnp.stack([jnp.sum(grad_output * rows, axis=1) for rows in chosen_rows], axis=1)
    grad_normed2 = jnp.dot(both, grad_back, preferred_element_type=F32)
    grad_picked = gates * (grad_gates - jnp.sum(gates * grad_gates, axis=1, keepdims=True))
    grad_logits = jnp.sum(chosen * grad_picked[:, :, None], axis=1)
    grad_normed2 = grad_normed2 + contract(grad_logits, w_router.astype(F32), 1, 1, HIGH)
    grad_router = contract(normed2.astype(F32), grad_logits, 0, 0, HIGH)
    grad_mixed, grad_norm2 = norm2_pull(grad_normed2)
    grad_mixed = grad_mixed + grad_output
    grad_branch = grad_mixed.astype(BF)

    grad_wout = contract(attended, grad_branch, 0, 0).astype(BF)
    grad_wout = grad_wout.reshape(replicas, groups, out_rows, width)
    grad_wout = lax.psum_scatter(grad_wout, "dp", scatter_dimension=1, tiled=True)[:, 0]
    if stepwise:
        grad_wout = sum(
            (hop(grad_wout[r], r) if r else grad_wout[r]).astype(F32) for r in range(replicas)
        ).astype(BF)
    else:
        grad_wout = lax.psum_scatter(
            grad_wout.reshape(replicas * out_rows, width), "head", scatter_dimension=0, tiled=True
        )
    grad_out_proj = lax.all_gather(grad_wout, "dp", axis=0, tiled=True).astype(F32)

    grad_heads = contract(grad_branch, w_out_cat, 1, 1).astype(BF)
    sums = jnp.zeros((heads_here, TILE, 2 * length), F32)
    grad_blocks = [grad_heads[:, i * head_cols : (i + 1) * head_cols] for i in range(replicas)]
    grad_total = None
    weight_terms = []
    if stepwise:
        arrived = [hop(grad_blocks[r], r) if r else grad_blocks[0] for r in range(replicas)]
        for r in (0, 2, 3, 1):
            grad_qkv, sums = attend_bwd(order[r].reshape(1), qkv, arrived[r], kept[r], sums, length)
            normed_seq = lax.dynamic_slice_in_dim(normed, order[r] * length, length, 0)
            weight_terms.append(contract(normed_seq, grad_qkv, 0, 0))
            mine = hop(grad_qkv, r) if r else grad_qkv
            weight = lax.dynamic_index_in_dim(w_qkv_all, order[r], 0, keepdims=False)
            term = contract(mine, weight, 1, 1)
            grad_total = term if grad_total is None else grad_total + term
        grad_normed = grad_total
        grad_qkv_w = sum(weight_terms)
    else:
        stacked = jnp.stack(grad_blocks, axis=0)
        stacked = lax.all_to_all(stacked, "head", split_axis=0, concat_axis=0, tiled=True)
        stacked = stacked.reshape(group_rows, head_cols)
        seqs = []
        for s in range(sequences):
            grad_seq = stacked[s * length : (s + 1) * length]
            grad_qkv, sums = attend_bwd(
                jnp.full((1,), s, jnp.int32), qkv, grad_seq, kept[s], sums, length
            )
            seqs.append(grad_qkv)
        grad_qkv = jnp.concatenate(seqs, axis=0)
        grad_qkv_w = contract(normed, grad_qkv, 0, 0)
        grad_qkv = lax.all_to_all(
            grad_qkv.reshape(replicas, own_rows, 3 * head_cols),
            "head",
            split_axis=0,
            concat_axis=0,
            tiled=True,
        )
        grad_normed = sum(contract(grad_qkv[i], w_qkv_all[i], 1, 1) for i in range(replicas))

    _, norm1_pull = jax.vjp(rms_norm, inputs_own, norm1_gain)
    grad_first, grad_norm1 = norm1_pull(grad_normed)
    grad_input = grad_mixed + grad_first
    grad_bias = contract(unskew(sums), line, 1, 1, HIGH)
    grad_qkv_w, grad_bias = lax.psum((grad_qkv_w.astype(BF), grad_bias), "dp")
    grad_qkv_w = grad_qkv_w.astype(F32)
    grad_norm1, grad_norm2, grad_router = lax.psum(
        (grad_norm1, grad_norm2, grad_router), ("dp", "head")
    )
    return (
        output,
        grad_input,
        grad_norm1,
        grad_qkv_w[:, :head_cols],
        grad_qkv_w[:, head_cols : 2 * head_cols],
        grad_qkv_w[:, 2 * head_cols :],
        grad_out_proj,
        jnp.transpose(grad_bias),
        grad_norm2,
        grad_router,
        grad_gate_w,
        grad_up_w,
        grad_down_w,
    )


def body(*args):
    block_input, cotangent, rel_bucket, pos_bias, w_gate, w_router = (
        args[0],
        args[1],
        args[4],
        args[10],
        args[13],
        args[12],
    )
    own_rows = cotangent.shape[0]
    length = (rel_bucket.shape[0] + 1) // 2
    replicas, groups = lax.axis_size("head"), lax.axis_size("dp")
    experts = w_router.shape[1]
    capacity = 5 * 2 * own_rows // (4 * experts)
    stepwise = (
        own_rows == length
        and block_input.shape[0] == replicas * length
        and replicas == 4
        and groups == 8
        and experts == groups
        and capacity % 16 == 0
        and pos_bias.shape[1] % 2 == 0
        and w_gate.shape[2] % 256 == 0
    )
    return body_steps(*args) if stepwise else body_plain(*args)


def body_steps(
    block_input,
    cotangent,
    expert_ids,
    priority,
    rel_bucket,
    norm1_gain,
    w_query,
    w_key,
    w_value,
    w_out,
    pos_bias,
    norm2_gain,
    w_router,
    w_gate,
    w_up,
    w_down,
):
    group_rows, width = block_input.shape
    own_rows = cotangent.shape[0]
    buckets, heads_here = pos_bias.shape
    head_cols = w_query.shape[1]
    length = (rel_bucket.shape[0] + 1) // 2
    experts = w_router.shape[1]
    capacity = 5 * 2 * own_rows // (4 * experts)
    slot_count = experts * capacity
    replicas, groups = lax.axis_size("head"), lax.axis_size("dp")
    me, dp_at = lax.axis_index("head"), lax.axis_index("dp")
    far = replicas // 2
    far_perm = [(i, i ^ far) for i in range(replicas)]

    def hop(value, r):
        return lax.ppermute(value, "head", [(i, i ^ r) for i in range(replicas)])

    dest = route_slots(expert_ids, priority[0], experts, capacity)
    mixed_dest = jnp.where(
        dest < slot_count,
        ((dest // capacity) ^ dp_at) * capacity + dest % capacity,
        slot_count,
    )
    routing_far = hop(jnp.concatenate([mixed_dest, expert_ids], axis=1), far)
    slot_row = jnp.arange(slot_count, dtype=jnp.int32)[None, :]
    slot_col = jnp.arange(slot_count, dtype=jnp.int32)[:, None]
    expert_range = jnp.arange(experts, dtype=jnp.int32)
    lane_range = jnp.arange(TILE, dtype=jnp.int32)[None, :]

    def dispatch_of(places, ids):
        first = (slot_col == places[:, 0][None, :]).astype(BF)
        second = (slot_col == places[:, 1][None, :]).astype(BF)
        signs = (ids[:, 1:2] == lane_range).astype(BF) - (ids[:, 0:1] == lane_range).astype(BF)
        return first + second, contract(first - second, signs, 1, 0).astype(BF)

    both, signs = dispatch_of(mixed_dest, expert_ids)
    both_far, signs_far = dispatch_of(routing_far[:, :2], routing_far[:, 2:])
    picks = [(mixed_dest[:, k : k + 1] == slot_row).astype(BF) for k in range(2)]
    router_wide = jnp.pad(w_router, ((0, 0), (0, TILE - experts)))
    cot_sent = jnp.concatenate([contract(both, cotangent, 1, 0).astype(BF), signs], axis=1)
    cot_sent = cot_sent.reshape(experts, capacity, width + TILE)
    cot_far_own = hop(cotangent, far)

    out_rows = head_cols // groups
    piece = lax.dynamic_slice_in_dim(w_out, dp_at * out_rows, out_rows, 0)
    w_out_all = lax.all_gather(piece, ("head", "dp"), axis=0, tiled=True)
    order = [me ^ r for r in range(replicas)]
    w_out_all = w_out_all.reshape(replicas, head_cols, width)
    w_out_cat = jnp.concatenate(
        [lax.dynamic_index_in_dim(w_out_all, o, 0, keepdims=False) for o in order], axis=0
    )

    line = (rel_bucket[::-1][None, :] == jnp.arange(buckets, dtype=jnp.int32)[:, None]).astype(F32)
    line = jnp.pad(line, ((0, 0), (1, 0)))
    table = skew(contract(pos_bias, line, 0, 0, HIGH))
    input_weights = (w_query, w_key, w_value)
    attended, probs, cot_here, normed, qkv = attend_all(
        block_input, norm1_gain[None, :], input_weights, table, cot_sent, length, replicas
    )

    branch = jnp.dot(attended, w_out_cat, preferred_element_type=F32)
    inputs_own = lax.dynamic_slice_in_dim(block_input, me * own_rows, own_rows, 0).astype(F32)
    mixed = inputs_own + branch
    normed2_full, norm2_pull = jax.vjp(rms_norm, mixed, norm2_gain)
    normed2 = normed2_full.astype(BF)

    gate_w, up_w, down_w = w_gate[0], w_up[0], w_down[0]
    normed2_far = hop(normed2, far)
    tile = 256
    (rows_here, hidden_here, ggp_here, gup_here, scaled_here, came_back, grad_back) = expert_stage(
        normed2, both, cot_here, router_wide, gate_w, up_w, down_w, groups, capacity, tile
    )
    rows_here = rows_here.reshape(slot_count, width)
    scaled_here = scaled_here.reshape(slot_count, width)
    came_back = came_back.reshape(slot_count, width)
    grad_back = grad_back.reshape(slot_count, width)

    logits = jnp.dot(normed2, w_router, preferred_element_type=F32)
    chosen = (expert_ids[:, :, None] == expert_range[None, None, :]).astype(F32)
    gates = jax.nn.softmax(jnp.sum(chosen * logits[:, None, :], axis=2), axis=-1)
    chosen_rows = [jnp.dot(pick, came_back, preferred_element_type=F32) for pick in picks]
    output = mixed + sum(gates[:, k : k + 1] * chosen_rows[k] for k in range(2))
    grad_output = cotangent.astype(F32)
    grad_gates = jnp.stack([jnp.sum(grad_output * rows, axis=1) for rows in chosen_rows], axis=1)
    grad_normed2 = jnp.dot(picks[0] + picks[1], grad_back, preferred_element_type=F32)
    grad_picked = gates * (grad_gates - jnp.sum(gates * grad_gates, axis=1, keepdims=True))
    grad_logits = jnp.sum(chosen * grad_picked[:, :, None], axis=1)
    grad_normed2 = grad_normed2 + contract(grad_logits, w_router.astype(F32), 1, 1, HIGH)
    grad_router = contract(normed2.astype(F32), grad_logits, 0, 0, HIGH)
    grad_mixed, grad_norm2 = norm2_pull(grad_normed2)
    grad_mixed = grad_mixed + grad_output
    grad_branch = grad_mixed.astype(BF)
    grad_wout = contract(attended, grad_branch, 0, 0).astype(BF)
    grad_heads = contract(grad_branch, w_out_cat, 1, 1).astype(BF)

    far_own = jnp.concatenate([normed2_far, cot_far_own], axis=1)
    far_came, grad_qkv, grad_normed, sums = attend_back(
        far_own, both_far, signs_far, grad_heads, qkv, probs, input_weights, groups
    )
    grad_qkv_w = lax.dot_general(
        normed, grad_qkv, (((0, 1), (0, 1)), ((), ())), preferred_element_type=F32
    ).astype(BF)
    _, norm1_pull = jax.vjp(rms_norm, inputs_own, norm1_gain)
    grad_first, grad_norm1 = norm1_pull(grad_normed)
    grad_input = grad_mixed + grad_first
    grad_bias = contract(line, unskew(sums), 1, 1, HIGH)

    flat = jnp.concatenate(
        [grad_norm1, grad_norm2, grad_router.reshape(-1), grad_bias.reshape(-1)]
    )
    small_rows = -(-flat.shape[0] // (8 * TILE)) * 8
    small = jnp.pad(flat, (0, small_rows * TILE - flat.shape[0])).reshape(small_rows, TILE)

    grad_gate_w, grad_up_w, grad_down_w, grad_qkv_w, grad_out_proj, summed = last_stage(
        far_came,
        rows_here,
        scaled_here,
        router_wide,
        (gate_w, up_w, down_w),
        (ggp_here, gup_here),
        hidden_here,
        grad_qkv_w.reshape(groups, width // groups, 3 * head_cols),
        grad_wout.reshape(replicas, groups, out_rows, width),
        small,
        tile,
    )
    grad_qkv_w = grad_qkv_w.reshape(width, 3 * head_cols).astype(F32)
    grad_out_proj = grad_out_proj.reshape(head_cols, width).astype(F32)
    summed = summed.reshape(2, -1)
    ends = [width, 2 * width, 2 * width + width * experts]
    grad_bias = summed[0, ends[2] : ends[2] + buckets * heads_here].reshape(buckets, heads_here)
    return (
        output,
        grad_input,
        summed[1, : ends[0]],
        grad_qkv_w[:, :head_cols],
        grad_qkv_w[:, head_cols : 2 * head_cols],
        grad_qkv_w[:, 2 * head_cols :],
        grad_out_proj,
        grad_bias,
        summed[1, ends[0] : ends[1]],
        summed[1, ends[1] : ends[2]].reshape(width, experts),
        grad_gate_w[None],
        grad_up_w[None],
        grad_down_w[None],
    )


def solution(mesh):
    placed = (
        P("dp", None),
        P(("dp", "head"), None),
        P(("dp", "head"), None),
        P(("dp", "head"), None),
        P(),
        P(),
        P(None, "head"),
        P(None, "head"),
        P(None, "head"),
        P("head", None),
        P(None, "head"),
        P(),
        P(),
        P("dp", None, None),
        P("dp", None, None),
        P("dp", None, None),
    )
    return jax.shard_map(
        body,
        mesh=mesh,
        in_specs=placed,
        out_specs=(
            P(("dp", "head"), None),
            P(("dp", "head"), None),
            P(),
            P(None, "head"),
            P(None, "head"),
            P(None, "head"),
            P("head", None),
            P(None, "head"),
            P(),
            P(),
            P("dp", "head", None),
            P("dp", "head", None),
            P("dp", "head", None),
        ),
        check_vma=False,
    )
```

```python
import functools

import jax
import jax.numpy as jnp
from jax import lax
from jax.experimental import pallas as pl
from jax.experimental.pallas import tpu as pltpu
from jax.sharding import PartitionSpec as P

EPS = 1e-06
SCALE = 0.125
HIGH = lax.Precision.HIGHEST
TILE = 128
BF = jnp.bfloat16
F32 = jnp.float32
VMEM_LIMIT = 48 << 20
VMEM_MOST = 60 << 20
GELU_A = 0.7978845608028654
GELU_B = 0.044715
PEERS = [2, 4, 3, 5, 6, 7, 1]
ROW_PEERS = [6, 7, 2, 3, 4, 5, 1]


def rms_norm(value, gain):
    return value * lax.rsqrt(jnp.mean(value * value, axis=-1, keepdims=True) + EPS) * gain


def geglu(gate, up_part):
    return jax.nn.gelu(gate) * up_part


def contract(left, right, left_dim, right_dim, precision=None):
    return lax.dot_general(
        left,
        right,
        (((left_dim,), (right_dim,)), ((), ())),
        precision=precision,
        preferred_element_type=jnp.float32,
    )


def route_slots(chosen, ranks, experts, capacity):
    count = chosen.shape[0]
    keys = jnp.concatenate([ranks, ranks + count])
    wanted = jnp.concatenate([chosen[:, 0], chosen[:, 1]])
    smaller = (wanted[:, None] == wanted[None, :]) & (keys[None, :] < keys[:, None])
    place = jnp.sum(smaller.astype(jnp.int32), axis=1)
    dest = jnp.where(place < capacity, wanted * capacity + place, experts * capacity)
    return jnp.stack([dest[:count], dest[count:]], axis=1)


def skew_kernel(line_ref, table_ref):
    heads, rows, cols = table_ref.shape
    row = lax.broadcasted_iota(jnp.int32, (rows, cols), 0)
    for h in range(heads):
        value = jnp.broadcast_to(line_ref[h], (rows, cols))
        shift = 1
        while shift < rows:
            value = jnp.where((row & shift) != 0, pltpu.roll(value, shift, 1), value)
            shift *= 2
        table_ref[h] = value


def unskew_kernel(table_ref, line_ref):
    heads, rows, cols = table_ref.shape
    row = lax.broadcasted_iota(jnp.int32, (rows, cols), 0)
    for h in range(heads):
        value = table_ref[h]
        shift = 1
        while shift < rows:
            value = jnp.where((row & shift) != 0, pltpu.roll(value, cols - shift, 1), value)
            shift *= 2
        line_ref[h] = jnp.sum(value, axis=0, keepdims=True)


def skew(line):
    heads, cols = line.shape
    return pl.pallas_call(
        skew_kernel,
        out_shape=jax.ShapeDtypeStruct((heads, TILE, cols), F32),
        compiler_params=pltpu.CompilerParams(vmem_limit_bytes=VMEM_LIMIT),
        name="skew",
    )(line[:, None, :])


def unskew(table):
    heads, _, cols = table.shape
    return pl.pallas_call(
        unskew_kernel,
        out_shape=jax.ShapeDtypeStruct((heads, 1, cols), F32),
        compiler_params=pltpu.CompilerParams(vmem_limit_bytes=VMEM_LIMIT),
        name="unskew",
    )(table)[:, 0]


def lanes_of(shape, half, part):
    lane = lax.broadcasted_iota(jnp.int32, shape, 1)
    return (lane >= half) if part else (lane < half)


def attend_fwd_kernel(seq_ref, q_ref, k_ref, v_ref, table_ref, out_ref, probs_ref, acc_ref):
    del seq_ref
    length, lanes = q_ref.shape
    half = lanes // 2
    chunk = 2 * TILE
    key = k_ref[...]
    value_t = v_ref[...].T
    for part in range(2):
        query = jnp.where(lanes_of((length, lanes), half, part), q_ref[...] * SCALE, 0).astype(BF)
        for c in range(length // chunk):
            cols = slice(c * chunk, (c + 1) * chunk)
            scores = contract(key, query[cols], 1, 1)
            pieces = []
            for kb in range(length // TILE):
                at = length - TILE * kb + chunk * c
                pieces.append(
                    scores[kb * TILE : (kb + 1) * TILE] + table_ref[part, :, at : at + chunk]
                )
            scores = jnp.concatenate(pieces, axis=0)
            top = jnp.max(scores, axis=0, keepdims=True)
            shifted = jnp.exp(scores - top)
            total = jnp.sum(shifted, axis=0, keepdims=True)
            probs = (shifted * (1.0 / total)).astype(BF)
            probs_ref[part, :, cols] = probs
            acc_ref[part * half : (part + 1) * half, cols] = jnp.dot(
                value_t[part * half : (part + 1) * half], probs, preferred_element_type=F32
            )
    out_ref[...] = acc_ref[...].T.astype(BF)


def attend_fwd(seq, qkv, table, length):
    heads, _, width = table.shape
    columns = qkv.shape[1] // 3
    pairs = heads // 2
    lanes = columns // pairs
    spec = [
        pl.BlockSpec((length, lanes), lambda p, s, j=j: (s[0], j * pairs + p)) for j in range(3)
    ]
    return pl.pallas_call(
        attend_fwd_kernel,
        out_shape=(
            jax.ShapeDtypeStruct((length, columns), BF),
            jax.ShapeDtypeStruct((heads, length, length), BF),
        ),
        grid_spec=pltpu.PrefetchScalarGridSpec(
            num_scalar_prefetch=1,
            grid=(pairs,),
            in_specs=spec + [pl.BlockSpec((2, TILE, width), lambda p, s: (p, 0, 0))],
            out_specs=[
                pl.BlockSpec((length, lanes), lambda p, s: (0, p)),
                pl.BlockSpec((2, length, length), lambda p, s: (p, 0, 0)),
            ],
            scratch_shapes=[pltpu.VMEM((lanes, length), F32)],
        ),
        compiler_params=pltpu.CompilerParams(vmem_limit_bytes=VMEM_LIMIT),
        cost_estimate=pl.CostEstimate(
            flops=heads * 8 * length * length * lanes,
            bytes_accessed=heads * length * length * 2 + 8 * length * columns,
            transcendentals=heads * length * length,
        ),
        name="attend_fwd",
    )(seq, qkv, qkv, qkv, table)


def attend_bwd_kernel(
    seq_ref, q_ref, k_ref, v_ref, grad_ref, probs_ref, sums_in_ref, out_ref, sums_ref, acc_ref
):
    del seq_ref
    length, lanes = q_ref.shape
    half = lanes // 2
    chunk = 2 * TILE
    pair = pl.program_id(0)
    columns = out_ref.shape[1] // 3
    key_t = k_ref[...].T
    value = v_ref[...]
    sums_ref[...] = sums_in_ref[...]
    grad_keys, grad_values = [], []
    for part in range(2):
        mask = lanes_of((length, lanes), half, part)
        grad = jnp.where(mask, grad_ref[...], 0).astype(BF)
        grad_key = jnp.zeros((length, lanes), F32)
        grad_value = jnp.zeros((length, lanes), F32)
        for c in range(length // chunk):
            cols = slice(c * chunk, (c + 1) * chunk)
            grad_probs = contract(value, grad[cols], 1, 1)
            probs_low = probs_ref[part, :, cols]
            probs = probs_low.astype(F32)
            delta = jnp.sum(probs * grad_probs, axis=0, keepdims=True)
            grad_scores = (probs * (grad_probs - delta)).astype(BF)
            grad_value += jnp.dot(probs_low, grad_ref[cols, :], preferred_element_type=F32)
            grad_key += jnp.dot(grad_scores, q_ref[cols, :], preferred_element_type=F32)
            acc_ref[part * half : (part + 1) * half, cols] = jnp.dot(
                key_t[part * half : (part + 1) * half], grad_scores, preferred_element_type=F32
            )
            for kb in range(length // TILE):
                at = length - TILE * kb + chunk * c
                sums_ref[part, :, at : at + chunk] += grad_scores[
                    kb * TILE : (kb + 1) * TILE
                ].astype(F32)
        grad_keys.append(grad_key)
        grad_values.append(grad_value)
    first = lanes_of((length, lanes), half, 0)
    at = pl.multiple_of(pair * lanes, lanes)
    out_ref[:, pl.ds(at, lanes)] = (acc_ref[...].T * SCALE).astype(BF)
    at = pl.multiple_of(columns + pair * lanes, lanes)
    out_ref[:, pl.ds(at, lanes)] = (jnp.where(first, *grad_keys) * SCALE).astype(BF)
    at = pl.multiple_of(2 * columns + pair * lanes, lanes)
    out_ref[:, pl.ds(at, lanes)] = jnp.where(first, *grad_values).astype(BF)


def attend_bwd(seq, qkv, grad, probs, sums, length):
    heads, _, width = sums.shape
    columns = qkv.shape[1] // 3
    pairs = heads // 2
    lanes = columns // pairs
    spec = [
        pl.BlockSpec((length, lanes), lambda p, s, j=j: (s[0], j * pairs + p)) for j in range(3)
    ]
    sums_spec = pl.BlockSpec((2, TILE, width), lambda p, s: (p, 0, 0))
    return pl.pallas_call(
        attend_bwd_kernel,
        out_shape=(
            jax.ShapeDtypeStruct((length, 3 * columns), BF),
            jax.ShapeDtypeStruct(sums.shape, F32),
        ),
        grid_spec=pltpu.PrefetchScalarGridSpec(
            num_scalar_prefetch=1,
            grid=(pairs,),
            in_specs=spec
            + [
                pl.BlockSpec((length, lanes), lambda p, s: (0, p)),
                pl.BlockSpec((2, length, length), lambda p, s: (p, 0, 0)),
                sums_spec,
            ],
            out_specs=[pl.BlockSpec((length, 3 * columns), lambda p, s: (0, 0)), sums_spec],
            scratch_shapes=[pltpu.VMEM((lanes, length), F32)],
        ),
        compiler_params=pltpu.CompilerParams(vmem_limit_bytes=VMEM_LIMIT),
        cost_estimate=pl.CostEstimate(
            flops=heads * 16 * length * length * lanes,
            bytes_accessed=heads * length * length * 2 + 16 * length * columns,
            transcendentals=0,
        ),
        name="attend_bwd",
    )(seq, qkv, qkv, qkv, grad, probs, sums)


def flipped(index, bits):
    out, step = index, 1
    while step <= bits:
        if bits & step:
            out = out + step * (1 - 2 * lax.rem(index // step, 2))
        step *= 2
    return out


def greet(peers):
    barrier = pltpu.get_barrier_semaphore()
    for peer in peers:
        pl.semaphore_signal(barrier, inc=1, device_id=peer, device_id_type=pl.DeviceIdType.MESH)
    pl.semaphore_wait(barrier, len(peers))


def remote(source, target, send_sem, recv_sem, peer):
    return pltpu.make_async_remote_copy(
        src_ref=source,
        dst_ref=target,
        send_sem=send_sem,
        recv_sem=recv_sem,
        device_id=peer,
        device_id_type=pl.DeviceIdType.MESH,
    )


def attend_all_kernel(
    input_ref,
    gain_ref,
    query_ref,
    key_ref,
    value_ref,
    line_ref,
    both_ref,
    signs_ref,
    cot_ref,
    routing_hbm,
    w_out_ref,
    gain2_ref,
    attended_out,
    probs_out,
    came_out,
    normed_out,
    qkv_out,
    w_cat_out,
    cot_far_out,
    routing_far_out,
    mixed_ref,
    normed2_ref,
    table_ref,
    sends,
    acc_ref,
    block_ref,
    hold_ref,
    normed_ref,
    qkv_ref,
    attended_ref,
    w_cat,
    w_land,
    row_send,
    row_recv,
    hop_send,
    hop_recv,
    w_send,
    w_recv,
    plane_send,
    plane_recv,
    far_send,
    far_recv,
    hold_sem,
    own_sem,
):
    z, d = lax.axis_index("head"), lax.axis_index("dp")
    heads, _, _ = table_ref.shape
    replicas, length, columns = block_ref.shape
    groups, capacity, _ = sends.shape
    width = input_ref.shape[1]
    part_rows = w_land.shape[1]
    pairs = heads // 2
    lanes = columns // pairs
    half = lanes // 2
    chunk = 2 * TILE
    hops = [3, 2, 1]
    greet([{"dp": flipped(d, o)} for o in PEERS] + [{"head": flipped(z, r)} for r in hops])
    copies = []

    def launch(*what):
        copy = remote(*what)
        copy.start()
        copies.append(copy)
        return copy

    piece = w_out_ref.at[pl.ds(pl.multiple_of(d * part_rows, part_rows), part_rows), :]
    w_hops = {}
    for r in hops:
        w_hops[r] = remote(piece, w_land.at[r], w_send.at[r], w_recv.at[r], {"head": flipped(z, r)})
        w_hops[r].start()
    for o in PEERS + [0]:
        span = slice(o * capacity, (o + 1) * capacity)
        sends[o, :, :width] = jnp.dot(
            both_ref[span], cot_ref[...], preferred_element_type=F32
        ).astype(BF)
        sends[o, :, width:] = signs_ref[span]
        if o:
            launch(
                sends.at[o], came_out.at[o], row_send.at[o], row_recv.at[o], {"dp": flipped(d, o)}
            )
    own = pltpu.make_async_copy(sends.at[0], came_out.at[0], own_sem.at[0])
    own.start()
    far = {"head": flipped(z, 2)}
    launch(routing_hbm, routing_far_out, far_send.at[0], far_recv.at[0], far)
    early = pl.ds(0, length // 2)
    launch(cot_ref.at[early], cot_far_out, far_send.at[1], far_recv.at[1], far)
    skew_kernel(line_ref, table_ref)
    w_cat[:columns, :] = w_out_ref[...]

    moves = []
    for turn, r in enumerate(reversed(range(replicas))):
        start = flipped(z, r) * length
        slot = turn % 2
        if turn >= 2:
            for move in moves[turn - 2]:
                move.wait()

        def norm_step(i, carry, start=start, slot=slot):
            rows = pl.multiple_of(start + i * TILE, TILE)
            value = input_ref[pl.ds(rows, TILE), :].astype(F32)
            value = rms_norm(value, gain_ref[...])
            normed_ref[slot, pl.ds(pl.multiple_of(i * TILE, TILE), TILE), :] = value.astype(BF)
            return carry

        lax.fori_loop(0, length // TILE, norm_step, 0)
        for i, weight in enumerate((query_ref, key_ref, value_ref)):
            qkv_ref[slot, :, i * columns : (i + 1) * columns] = jnp.dot(
                normed_ref[slot], weight[...], preferred_element_type=F32
            ).astype(BF)

        def pair_step(pair, carry, slot=slot, r=r):
            def part_of(j):
                at = pl.multiple_of(j * columns + pair * lanes, lanes)
                return qkv_ref[slot, :, pl.ds(at, lanes)]

            key = part_of(1)
            value_t = part_of(2).T
            scaled = part_of(0) * SCALE
            for part in range(2):
                query = jnp.where(lanes_of((length, lanes), half, part), scaled, 0).astype(BF)
                for c in range(length // chunk):
                    cols = slice(c * chunk, (c + 1) * chunk)
                    scores = contract(key, query[cols], 1, 1)
                    pieces = []
                    for kb in range(length // TILE):
                        at = length - TILE * kb + chunk * c
                        pieces.append(
                            scores[kb * TILE : (kb + 1) * TILE]
                            + table_ref[pair * 2 + part, :, at : at + chunk]
                        )
                    scores = jnp.concatenate(pieces, axis=0)
                    top = jnp.max(scores, axis=0, keepdims=True)
                    shifted = jnp.exp(scores - top)
                    total = jnp.sum(shifted, axis=0, keepdims=True)
                    probs = (shifted * (1.0 / total)).astype(BF)
                    hold_ref[slot, pair * 2 + part, :, cols] = probs
                    acc_ref[part * half : (part + 1) * half, cols] = jnp.dot(
                        value_t[part * half : (part + 1) * half],
                        probs,
                        preferred_element_type=F32,
                    )
            at = pl.multiple_of(pair * lanes, lanes)
            block_ref[r, :, pl.ds(at, lanes)] = acc_ref[...].T.astype(BF)
            return carry

        lax.fori_loop(0, pairs, pair_step, 0)
        moves.append(
            [
                pltpu.make_async_copy(ref.at[slot], out.at[r], hold_sem.at[i, slot])
                for i, (ref, out) in enumerate(
                    ((hold_ref, probs_out), (normed_ref, normed_out), (qkv_ref, qkv_out))
                )
            ]
        )
        for move in moves[-1]:
            move.start()
        if r:
            launch(
                block_ref.at[r],
                attended_ref.at[:, pl.ds(r * columns, columns)],
                hop_send.at[r],
                hop_recv.at[r],
                {"head": flipped(z, r)},
            )
        else:
            attended_ref[:, :columns] = block_ref[0]
        if turn == 0:
            for s in hops:
                w_hops[s].wait()
                at = pl.multiple_of(s * columns + d * part_rows, part_rows)
                w_cat[pl.ds(at, part_rows), :] = w_land[s]
                for o in PEERS:
                    launch(
                        w_land.at[s],
                        w_cat.at[pl.ds(at, part_rows), :],
                        plane_send.at[s, o],
                        plane_recv.at[s, o],
                        {"dp": flipped(d, o)},
                    )
    for copy in copies:
        copy.wait()
    outs = [
        pltpu.make_async_copy(attended_ref, attended_out, own_sem.at[1]),
        pltpu.make_async_copy(w_cat, w_cat_out, own_sem.at[2]),
    ]
    for copy in outs:
        copy.start()

    def branch_step(i, carry):
        cols = pl.ds(pl.multiple_of(i * chunk, chunk), chunk)
        mixed_ref[:, cols] = jnp.dot(
            attended_ref[...], w_cat[:, cols], preferred_element_type=F32
        )
        return carry

    lax.fori_loop(0, width // chunk, branch_step, 0)

    def mixed_step(i, carry):
        at = pl.multiple_of(i * TILE, TILE)
        span = pl.ds(at, TILE)
        rows = pl.multiple_of(z * length + at, TILE)
        value = mixed_ref[span, :] + input_ref[pl.ds(rows, TILE), :].astype(F32)
        mixed_ref[span, :] = value
        normed2_ref[span, :] = rms_norm(value, gain2_ref[...]).astype(BF)
        return carry

    lax.fori_loop(0, length // TILE, mixed_step, 0)
    for move in moves[-2] + moves[-1] + outs + [own]:
        move.wait()


def attend_all(inputs, gain, weights, line, both, signs, cot, routing, w_out, gain2, groups):
    heads, _, table_width = line.shape
    width = inputs.shape[1]
    length = cot.shape[0]
    replicas = inputs.shape[0] // length
    columns = weights[0].shape[1]
    lanes = 2 * columns // heads
    capacity = both.shape[0] // groups
    part_rows = columns // groups
    vmem = pl.BlockSpec(memory_space=pltpu.VMEM)
    hbm = pl.BlockSpec(memory_space=pl.ANY)
    came_shape = (groups, capacity, width + TILE)
    plane_sem = pltpu.SemaphoreType.DMA((groups,))
    hop_sem = pltpu.SemaphoreType.DMA((replicas,))
    both_sem = pltpu.SemaphoreType.DMA((replicas, groups))
    two_sem = pltpu.SemaphoreType.DMA((2,))
    return pl.pallas_call(
        attend_all_kernel,
        out_shape=(
            jax.ShapeDtypeStruct((length, replicas * columns), BF),
            jax.ShapeDtypeStruct((replicas, heads, length, length), BF),
            jax.ShapeDtypeStruct(came_shape, BF),
            jax.ShapeDtypeStruct((replicas, length, width), BF),
            jax.ShapeDtypeStruct((replicas, length, 3 * columns), BF),
            jax.ShapeDtypeStruct((replicas * columns, width), BF),
            jax.ShapeDtypeStruct((length // 2, width), BF),
            jax.ShapeDtypeStruct(routing.shape, routing.dtype),
            jax.ShapeDtypeStruct((length, width), F32),
            jax.ShapeDtypeStruct((length, width), BF),
        ),
        in_specs=[vmem] * 9 + [hbm] + [vmem] * 2,
        out_specs=[hbm] * 8 + [vmem] * 2,
        scratch_shapes=[
            pltpu.VMEM((heads, TILE, table_width), F32),
            pltpu.VMEM(came_shape, BF),
            pltpu.VMEM((lanes, length), F32),
            pltpu.VMEM((replicas, length, columns), BF),
            pltpu.VMEM((2, heads, length, length), BF),
            pltpu.VMEM((2, length, width), BF),
            pltpu.VMEM((2, length, 3 * columns), BF),
            pltpu.VMEM((length, replicas * columns), BF),
            pltpu.VMEM((replicas * columns, width), BF),
            pltpu.VMEM((replicas, part_rows, width), BF),
            plane_sem,
            plane_sem,
            hop_sem,
            hop_sem,
            hop_sem,
            hop_sem,
            both_sem,
            both_sem,
            two_sem,
            two_sem,
            pltpu.SemaphoreType.DMA((3, 2)),
            pltpu.SemaphoreType.DMA((3,)),
        ],
        compiler_params=pltpu.CompilerParams(
            vmem_limit_bytes=VMEM_LIMIT, collective_id=1, has_side_effects=True
        ),
        cost_estimate=pl.CostEstimate(
            flops=replicas * heads * 8 * length * length * lanes,
            bytes_accessed=replicas * heads * length * length * 4,
            transcendentals=replicas * heads * length * length,
        ),
        name="attend_all",
    )(inputs, gain, *weights, line, both, signs, cot, routing, w_out, gain2)


def expert_tile(rows, scaled, gate_w, up_w, down_w):
    gate = jnp.dot(rows, gate_w, preferred_element_type=F32)
    up_part = jnp.dot(rows, up_w, preferred_element_type=F32)
    grad_hidden = contract(scaled, down_w, 1, 1)
    square = gate * gate
    bend = jnp.tanh(gate * (GELU_A + GELU_A * GELU_B * square))
    half = 0.5 + 0.5 * bend
    active = gate * half
    slope = half + 0.5 * gate * (1.0 - bend * bend) * (GELU_A + 3.0 * GELU_A * GELU_B * square)
    hidden = (active * up_part).astype(BF)
    grad_gate = (grad_hidden * up_part * slope).astype(BF)
    grad_up = (grad_hidden * active).astype(BF)
    return hidden, grad_gate, grad_up


def scaled_rows(rows, extended, router, width):
    logits = jnp.dot(rows, router, preferred_element_type=F32)
    sign = extended[:, width:].astype(F32)
    gap = jnp.sum(logits * sign, axis=1, keepdims=True)
    return (extended[:, :width].astype(F32) * (1.0 / (1.0 + jnp.exp(gap)))).astype(BF)


def expert_kernel(
    width,
    tile,
    normed_ref,
    both_ref,
    cot_ref,
    router_ref,
    gate_hbm,
    up_hbm,
    down_hbm,
    cot_hbm,
    rows_out,
    hidden_out,
    grad_gate_out,
    grad_up_out,
    scaled_out,
    back_out,
    grad_back_out,
    far_out,
    cot_far_out,
    gate_w,
    up_w,
    down_w,
    rows,
    sends,
    back,
    grad_back,
    hidden,
    grad_gate,
    grad_up,
    scaled,
    weight_sem,
    row_send,
    row_recv,
    back_send,
    back_recv,
    grad_send,
    grad_recv,
    unit_sem,
    keep_sem,
    far_sem,
):
    z, d = lax.axis_index("head"), lax.axis_index("dp")
    far = {"head": flipped(z, 2)}
    groups, capacity, _ = rows.shape
    units = gate_w.shape[1]
    tiles = units // tile
    count = 2 * capacity

    def weights_of(t):
        at = pl.multiple_of(t * tile, tile)
        return [
            pltpu.make_async_copy(
                gate_hbm.at[:, pl.ds(at, tile)], gate_w.at[:, pl.ds(at, tile)], weight_sem.at[0, t]
            ),
            pltpu.make_async_copy(
                up_hbm.at[:, pl.ds(at, tile)], up_w.at[:, pl.ds(at, tile)], weight_sem.at[1, t]
            ),
            pltpu.make_async_copy(
                down_hbm.at[pl.ds(at, tile), :], down_w.at[pl.ds(at, tile), :], weight_sem.at[2, t]
            ),
        ]

    def start_weights(t, carry):
        for copy in weights_of(t):
            copy.start()
        return carry

    lax.fori_loop(0, tiles, start_weights, 0)
    greet([{"dp": flipped(d, o)} for o in ROW_PEERS] + [far])
    pending = []
    arrivals = {}
    for o in ROW_PEERS:
        sends[o] = jnp.dot(
            both_ref[o * capacity : (o + 1) * capacity],
            normed_ref[...],
            preferred_element_type=F32,
        ).astype(BF)
        arrivals[o] = remote(
            sends.at[o], rows.at[o], row_send.at[o], row_recv.at[o], {"dp": flipped(d, o)}
        )
        arrivals[o].start()
    over = [
        remote(normed_ref, far_out, far_sem.at[0, 0], far_sem.at[0, 1], far),
        remote(
            cot_hbm.at[pl.ds(cot_far_out.shape[0], cot_far_out.shape[0])],
            cot_far_out,
            far_sem.at[1, 0],
            far_sem.at[1, 1],
            far,
        ),
    ]
    for copy in over:
        copy.start()
    rows[0] = jnp.dot(
        both_ref[:capacity], normed_ref[...], preferred_element_type=F32
    ).astype(BF)

    unit_copies = {}
    order = [0, 3, 1, 2]
    for turn, j in enumerate(order):
        pair = (2 * j, 2 * j + 1)
        slot = turn % 2
        for o in pair:
            if o:
                arrivals[o].wait_recv()
        if turn >= 2:
            for copy in unit_copies[order[turn - 2]]:
                copy.wait()
        here = rows[2 * j : 2 * j + 2].reshape(count, width)
        extended = cot_ref[2 * j : 2 * j + 2].reshape(count, cot_ref.shape[2])
        scaled[2 * j : 2 * j + 2] = scaled_rows(here, extended, router_ref[...], width).reshape(
            2, capacity, width
        )

        def tile_step(t, carry, j=j, slot=slot):
            at = pl.multiple_of(t * tile, tile)
            if j == 0:
                for copy in weights_of(t):
                    copy.wait()
            values = expert_tile(
                rows[2 * j : 2 * j + 2].reshape(count, width),
                scaled[2 * j : 2 * j + 2].reshape(count, width),
                gate_w[:, pl.ds(at, tile)],
                up_w[:, pl.ds(at, tile)],
                down_w[pl.ds(at, tile), :],
            )
            for ref, value in zip((hidden, grad_gate, grad_up), values):
                ref[slot, :, pl.ds(at, tile)] = value
            return carry

        lax.fori_loop(0, tiles, tile_step, 0)
        span = pl.ds(j * count, count)
        unit_copies[j] = [
            pltpu.make_async_copy(ref.at[slot], out.at[span], unit_sem.at[slot, i])
            for i, (ref, out) in enumerate(
                ((hidden, hidden_out), (grad_gate, grad_gate_out), (grad_up, grad_up_out))
            )
        ]
        for copy in unit_copies[j]:
            copy.start()

        def back_step(t, carry, j=j, slot=slot):
            at = pl.multiple_of(t * tile, tile)
            value = jnp.dot(hidden[slot], down_w[:, pl.ds(at, tile)], preferred_element_type=F32)
            back[2 * j : 2 * j + 2, :, pl.ds(at, tile)] = value.astype(BF).reshape(
                2, capacity, tile
            )
            return carry

        def grad_step(t, carry, j=j, slot=slot):
            at = pl.multiple_of(t * tile, tile)
            value = contract(grad_gate[slot], gate_w[pl.ds(at, tile), :], 1, 1) + contract(
                grad_up[slot], up_w[pl.ds(at, tile), :], 1, 1
            )
            grad_back[2 * j : 2 * j + 2, :, pl.ds(at, tile)] = value.astype(BF).reshape(
                2, capacity, tile
            )
            return carry

        for step, buffer, out, send_sem, recv_sem in (
            (back_step, back, back_out, back_send, back_recv),
            (grad_step, grad_back, grad_back_out, grad_send, grad_recv),
        ):
            lax.fori_loop(0, width // tile, step, 0)
            for o in pair:
                if o:
                    copy = remote(
                        buffer.at[o],
                        out.at[o],
                        send_sem.at[o],
                        recv_sem.at[o],
                        {"dp": flipped(d, o)},
                    )
                else:
                    copy = pltpu.make_async_copy(buffer.at[0], out.at[0], send_sem.at[0])
                copy.start()
                pending.append(copy)

    keeps = [
        pltpu.make_async_copy(rows, rows_out, keep_sem.at[0]),
        pltpu.make_async_copy(scaled, scaled_out, keep_sem.at[1]),
    ]
    for copy in keeps:
        copy.start()
    for j in order[-2:]:
        for copy in unit_copies[j]:
            copy.wait()
    for o in ROW_PEERS:
        arrivals[o].wait_send()
    for copy in pending + keeps + over:
        copy.wait()


def expert_stage(
    normed2, both, cot, router, gate_w, up_w, down_w, cot_own, groups, capacity, tile
):
    width, units = gate_w.shape
    slots = groups * capacity
    vmem = pl.BlockSpec(memory_space=pltpu.VMEM)
    hbm = pl.BlockSpec(memory_space=pl.ANY)
    row_shape = jax.ShapeDtypeStruct((groups, capacity, width), BF)
    unit_shape = jax.ShapeDtypeStruct((slots, units), BF)
    row_buffer = pltpu.VMEM((groups, capacity, width), BF)
    unit_buffer = pltpu.VMEM((2, 2 * capacity, units), BF)
    row_sem = pltpu.SemaphoreType.DMA((groups,))
    return pl.pallas_call(
        functools.partial(expert_kernel, width, tile),
        out_shape=(row_shape,)
        + (unit_shape,) * 3
        + (row_shape,) * 3
        + (
            jax.ShapeDtypeStruct(normed2.shape, BF),
            jax.ShapeDtypeStruct((normed2.shape[0] // 2, width), BF),
        ),
        in_specs=[vmem] * 4 + [hbm] * 4,
        out_specs=[hbm] * 9,
        scratch_shapes=[
            pltpu.VMEM((width, units), BF),
            pltpu.VMEM((width, units), BF),
            pltpu.VMEM((units, width), BF),
            row_buffer,
            row_buffer,
            row_buffer,
            row_buffer,
            unit_buffer,
            unit_buffer,
            unit_buffer,
            row_buffer,
            pltpu.SemaphoreType.DMA((3, units // tile)),
            row_sem,
            row_sem,
            row_sem,
            row_sem,
            row_sem,
            row_sem,
            pltpu.SemaphoreType.DMA((2, 3)),
            pltpu.SemaphoreType.DMA((2,)),
            pltpu.SemaphoreType.DMA((2, 2)),
        ],
        compiler_params=pltpu.CompilerParams(
            vmem_limit_bytes=VMEM_MOST, collective_id=2, has_side_effects=True
        ),
        cost_estimate=pl.CostEstimate(
            flops=12 * slots * width * units,
            bytes_accessed=6 * width * units + 6 * slots * units,
            transcendentals=slots * units,
        ),
        name="expert_stage",
    )(normed2, both, cot, router, gate_w, up_w, down_w, cot_own)


def split_parts(value):
    first = value.astype(BF)
    rest = value - first.astype(F32)
    second = rest.astype(BF)
    return first, second, (rest - second.astype(F32)).astype(BF)


def combine_kernel(
    back_ref,
    grad_back_ref,
    first_ref,
    second_ref,
    mixed_ref,
    normed2_ref,
    cot_ref,
    signs_ref,
    router_ref,
    gain_ref,
    w_cat_ref,
    output_ref,
    grad_mixed_ref,
    grad_branch_ref,
    grad_heads_ref,
    grad_router_ref,
    grad_norm2_ref,
    picked,
    slopes,
):
    length, width = mixed_ref.shape
    chunk = 2 * TILE

    def pick_step(i, carry):
        cols = pl.ds(pl.multiple_of(i * chunk, chunk), chunk)
        for k, (pick, source) in enumerate(((first_ref, back_ref), (second_ref, back_ref))):
            picked[k, :, cols] = jnp.dot(pick[...], source[:, cols], preferred_element_type=F32)
        picked[2, :, cols] = jnp.dot(
            first_ref[...] + second_ref[...], grad_back_ref[:, cols], preferred_element_type=F32
        )
        return carry

    lax.fori_loop(0, width // chunk, pick_step, 0)

    def row_step(i, total):
        span = pl.ds(pl.multiple_of(i * TILE, TILE), TILE)
        sign = signs_ref[span, :].astype(F32)
        logits = jnp.dot(normed2_ref[span, :], router_ref[...], preferred_element_type=F32)
        gap = jnp.sum(logits * sign, axis=1, keepdims=True)
        gate0, gate1 = 1.0 / (1.0 + jnp.exp(gap)), 1.0 / (1.0 + jnp.exp(-gap))
        cot = cot_ref[span, :].astype(F32)
        mixed = mixed_ref[span, :]
        row0, row1 = picked[0, span, :], picked[1, span, :]
        output_ref[span, :] = mixed + (gate0 * row0 + gate1 * row1)
        grad_gap = jnp.sum(cot * (row1 - row0), axis=1, keepdims=True)
        slope = gate0 * gate1 * grad_gap * sign
        slopes[span, :] = slope
        grad_normed2 = picked[2, span, :] + sum(
            contract(part, router_ref[...], 1, 1) for part in split_parts(slope)
        )
        scale = lax.rsqrt(jnp.mean(mixed * mixed, axis=1, keepdims=True) + EPS)
        inner = grad_normed2 * gain_ref[...]
        mean = jnp.mean(inner * mixed, axis=1, keepdims=True)
        grad_mixed = cot + scale * inner - mixed * (scale * scale * scale * mean)
        grad_mixed_ref[span, :] = grad_mixed
        grad_branch_ref[span, :] = grad_mixed.astype(BF)
        return total + jnp.sum(grad_normed2 * mixed * scale, axis=0, keepdims=True)

    grad_norm2_ref[...] = lax.fori_loop(
        0, length // TILE, row_step, jnp.zeros((1, width), F32)
    )

    def head_step(i, carry):
        cols = pl.ds(pl.multiple_of(i * chunk, chunk), chunk)
        grad_heads_ref[:, cols] = contract(grad_branch_ref[...], w_cat_ref[cols, :], 1, 1).astype(BF)
        return carry

    lax.fori_loop(0, w_cat_ref.shape[0] // chunk, head_step, 0)
    experts = grad_router_ref.shape[0]
    grad_router_ref[...] = sum(
        contract(part, normed2_ref[...], 0, 0) for part in split_parts(slopes[...])
    )[:experts]


def combine(back, grad_back, picks, mixed, normed2, cot, signs, router, gain, w_cat, experts):
    length, width = mixed.shape
    vmem = pl.BlockSpec(memory_space=pltpu.VMEM)
    return pl.pallas_call(
        combine_kernel,
        out_shape=(
            jax.ShapeDtypeStruct((length, width), F32),
            jax.ShapeDtypeStruct((length, width), F32),
            jax.ShapeDtypeStruct((length, width), BF),
            jax.ShapeDtypeStruct((length, w_cat.shape[0]), BF),
            jax.ShapeDtypeStruct((experts, width), F32),
            jax.ShapeDtypeStruct((1, width), F32),
        ),
        in_specs=[vmem] * 11,
        out_specs=[vmem] * 6,
        scratch_shapes=[pltpu.VMEM((3, length, width), F32), pltpu.VMEM((length, TILE), F32)],
        compiler_params=pltpu.CompilerParams(vmem_limit_bytes=VMEM_LIMIT),
        cost_estimate=pl.CostEstimate(
            flops=6 * length * back.shape[0] * width,
            bytes_accessed=4 * back.shape[0] * width,
            transcendentals=0,
        ),
        name="combine",
    )(back, grad_back, *picks, mixed, normed2, cot, signs, router, gain, w_cat)


def attend_back_kernel(
    normed2_far,
    cot_far,
    cot_rest,
    both_ref,
    signs_ref,
    grad_ref,
    qkv_hbm,
    probs_hbm,
    normed_hbm,
    query_w,
    key_w,
    value_w,
    attended_ref,
    grad_branch_ref,
    grad_mixed_ref,
    input_ref,
    gain_ref,
    far_out,
    qkv_w_ref,
    out_w_ref,
    grad_input_ref,
    norm1_ref,
    lines_ref,
    sums_ref,
    acc_ref,
    sends,
    grads,
    qkv_ref,
    probs_ref,
    normed_ref,
    grad_qkv_ref,
    weight_sum,
    parts,
    landed,
    far_send,
    far_recv,
    hop_send,
    hop_recv,
    part_send,
    part_recv,
    load_sem,
    own_sem,
):
    z, d = lax.axis_index("head"), lax.axis_index("dp")
    replicas, length, columns = grads.shape
    groups, capacity, extent = sends.shape
    width = input_ref.shape[1]
    heads = sums_ref.shape[0]
    pairs = heads // 2
    lanes = columns // pairs
    half = lanes // 2
    chunk = 2 * TILE
    hops = [3, 2, 1]
    order = [0, 3, 2, 1]

    def loads(turn):
        r, slot = order[turn], turn % 2
        return [
            pltpu.make_async_copy(source.at[r], target.at[slot], load_sem.at[i, slot])
            for i, (source, target) in enumerate(
                ((qkv_hbm, qkv_ref), (probs_hbm, probs_ref), (normed_hbm, normed_ref))
            )
        ]

    for copy in loads(0):
        copy.start()
    greet([{"dp": flipped(d, o)} for o in PEERS] + [{"head": flipped(z, r)} for r in hops])
    copies = []
    arrivals = {}
    for r in hops:
        arrivals[r] = remote(
            grad_ref.at[:, pl.ds(r * columns, columns)],
            grads.at[r],
            hop_send.at[r],
            hop_recv.at[r],
            {"head": flipped(z, r)},
        )
        arrivals[r].start()
    for o in PEERS + [0]:
        span = slice(o * capacity, (o + 1) * capacity)
        sends[o, :, :width] = jnp.dot(
            both_ref[span], normed2_far[...], preferred_element_type=F32
        ).astype(BF)
        early = cot_far.shape[0]
        sends[o, :, width : 2 * width] = (
            jnp.dot(both_ref[span, :early], cot_far[...], preferred_element_type=F32)
            + jnp.dot(both_ref[span, early:], cot_rest[...], preferred_element_type=F32)
        ).astype(BF)
        sends[o, :, 2 * width :] = signs_ref[span]
        if o:
            copy = remote(
                sends.at[o],
                far_out.at[o],
                far_send.at[o],
                far_recv.at[o],
                {"dp": flipped(d, o)},
            )
        else:
            copy = pltpu.make_async_copy(sends.at[0], far_out.at[0], own_sem)
        copy.start()
        copies.append(copy)
    sums_ref[...] = jnp.zeros_like(sums_ref)
    grads[0] = grad_ref[:, :columns]

    near, over = {"head": flipped(z, 1)}, {"head": flipped(z, 2)}
    steps = length // 2

    def half_copy(i, source, target, h, peer):
        span = pl.ds(h * steps, steps)
        return remote(
            parts.at[source, span], landed.at[target, span], part_send.at[i, h], part_recv.at[i, h], peer
        )

    inner = [half_copy(0, 3, 2, h, near) for h in range(2)]
    outer = [half_copy(1, 2, 0, h, over) for h in range(2)]
    direct = [half_copy(2, 1, 1, h, near) for h in range(2)]

    for turn, r in enumerate(order):
        slot = turn % 2
        if turn + 1 < replicas:
            for copy in loads(turn + 1):
                copy.start()
        for copy in loads(turn):
            copy.wait()
        if r:
            arrivals[r].wait_recv()

        def pair_step(pair, carry, slot=slot, r=r):
            def part_of(j):
                at = pl.multiple_of(j * columns + pair * lanes, lanes)
                return qkv_ref[slot, :, pl.ds(at, lanes)]

            at = pl.multiple_of(pair * lanes, lanes)
            query, value = part_of(0), part_of(2)
            key_t = part_of(1).T
            grad_all = grads[r, :, pl.ds(at, lanes)]
            grad_keys, grad_values = [], []
            for part in range(2):
                mask = lanes_of((length, lanes), half, part)
                grad = jnp.where(mask, grad_all, 0).astype(BF)
                grad_key = jnp.zeros((length, lanes), F32)
                grad_value = jnp.zeros((length, lanes), F32)
                for c in range(length // chunk):
                    cols = slice(c * chunk, (c + 1) * chunk)
                    grad_probs = contract(value, grad[cols], 1, 1)
                    probs_low = probs_ref[slot, pair * 2 + part, :, cols]
                    probs = probs_low.astype(F32)
                    delta = jnp.sum(probs * grad_probs, axis=0, keepdims=True)
                    grad_scores = (probs * (grad_probs - delta)).astype(BF)
                    grad_value += jnp.dot(probs_low, grad_all[cols], preferred_element_type=F32)
                    grad_key += jnp.dot(grad_scores, query[cols], preferred_element_type=F32)
                    acc_ref[part * half : (part + 1) * half, cols] = jnp.dot(
                        key_t[part * half : (part + 1) * half],
                        grad_scores,
                        preferred_element_type=F32,
                    )
                    for kb in range(length // TILE):
                        to = length - TILE * kb + chunk * c
                        sums_ref[pair * 2 + part, :, to : to + chunk] += grad_scores[
                            kb * TILE : (kb + 1) * TILE
                        ].astype(F32)
                grad_keys.append(grad_key)
                grad_values.append(grad_value)
            first = lanes_of((length, lanes), half, 0)
            results = (
                acc_ref[...].T * SCALE,
                jnp.where(first, *grad_keys) * SCALE,
                jnp.where(first, *grad_values),
            )
            for j, result in enumerate(results):
                to = pl.multiple_of(j * columns + pair * lanes, lanes)
                grad_qkv_ref[slot, :, pl.ds(to, lanes)] = result.astype(BF)
            return carry

        lax.fori_loop(0, pairs, pair_step, 0)

        def part_step(i, carry, slot=slot, r=r):
            span = pl.ds(pl.multiple_of(i * chunk, chunk), chunk)
            total = sum(
                contract(
                    grad_qkv_ref[slot, :, j * columns : (j + 1) * columns], weight[span, :], 1, 1
                )
                for j, weight in enumerate((query_w, key_w, value_w))
            )
            parts[r, :, span] = total.astype(BF)
            return carry

        lax.fori_loop(0, width // chunk, part_step, 0)
        if r == 3:
            for copy in inner:
                copy.start()
        if r == 1:
            for copy in direct:
                copy.start()

        def weight_step(i, carry, slot=slot, turn=turn):
            cols = pl.ds(pl.multiple_of(i * chunk, chunk), chunk)
            value = contract(normed_ref[slot, :, cols], grad_qkv_ref[slot], 0, 0)
            if turn:
                value = value + weight_sum[cols, :]
            if turn + 1 < replicas:
                weight_sum[cols, :] = value
            else:
                qkv_w_ref[cols, :] = value.astype(BF)
            return carry

        def relay(h):
            inner[h].wait_recv()
            span = slice(h * steps, (h + 1) * steps)
            parts[2, span, :] = (
                parts[2, span, :].astype(F32) + landed[2, span, :].astype(F32)
            ).astype(BF)
            outer[h].start()

        if turn == replicas - 1:
            relay(0)
        lax.fori_loop(0, width // chunk, weight_step, 0)
    relay(1)

    def wout_step(i, carry):
        rows = pl.ds(pl.multiple_of(i * chunk, chunk), chunk)
        out_w_ref[rows, :] = contract(attended_ref[:, rows], grad_branch_ref[...], 0, 0).astype(BF)
        return carry

    lax.fori_loop(0, out_w_ref.shape[0] // chunk, wout_step, 0)
    unskew_kernel(sums_ref, lines_ref)

    for copy in direct + outer:
        copy.wait()

    def end_step(i, total):
        span = pl.ds(pl.multiple_of(i * TILE, TILE), TILE)
        grad_normed = (
            parts[0, span, :].astype(F32)
            + landed[0, span, :].astype(F32)
            + landed[1, span, :].astype(F32)
        )
        value = input_ref[span, :].astype(F32)
        scale = lax.rsqrt(jnp.mean(value * value, axis=1, keepdims=True) + EPS)
        inner_grad = grad_normed * gain_ref[...]
        mean = jnp.mean(inner_grad * value, axis=1, keepdims=True)
        grad_input_ref[span, :] = (
            grad_mixed_ref[span, :] + scale * inner_grad - value * (scale * scale * scale * mean)
        )
        return total + jnp.sum(grad_normed * value * scale, axis=0, keepdims=True)

    norm1_ref[...] = lax.fori_loop(0, length // TILE, end_step, jnp.zeros((1, width), F32))
    for r in hops:
        arrivals[r].wait_send()
    for copy in inner:
        copy.wait_send()
    for copy in copies:
        copy.wait()


def attend_back(
    normed2_far,
    cot_far,
    cot_rest,
    both_far,
    signs_far,
    grad_heads,
    qkv,
    probs,
    normed,
    weights,
    attended,
    grad_branch,
    grad_mixed,
    inputs,
    gain,
    groups,
):
    replicas, length, triple = qkv.shape
    heads = probs.shape[1]
    columns = triple // 3
    width = inputs.shape[1]
    lanes = 2 * columns // heads
    capacity = both_far.shape[0] // groups
    extent = 2 * width + TILE
    vmem = pl.BlockSpec(memory_space=pltpu.VMEM)
    hbm = pl.BlockSpec(memory_space=pl.ANY)
    hop_sem = pltpu.SemaphoreType.DMA((replicas,))
    plane_sem = pltpu.SemaphoreType.DMA((groups,))
    part_sem = pltpu.SemaphoreType.DMA((3, 2))
    return pl.pallas_call(
        attend_back_kernel,
        out_shape=(
            jax.ShapeDtypeStruct((groups, capacity, extent), BF),
            jax.ShapeDtypeStruct((width, triple), BF),
            jax.ShapeDtypeStruct((replicas * columns, width), BF),
            jax.ShapeDtypeStruct((length, width), F32),
            jax.ShapeDtypeStruct((1, width), F32),
            jax.ShapeDtypeStruct((heads, 1, 2 * length), F32),
        ),
        in_specs=[vmem] * 6 + [hbm] * 3 + [vmem] * 8,
        out_specs=[hbm] + [vmem] * 5,
        scratch_shapes=[
            pltpu.VMEM((heads, TILE, 2 * length), F32),
            pltpu.VMEM((lanes, length), F32),
            pltpu.VMEM((groups, capacity, extent), BF),
            pltpu.VMEM((replicas, length, columns), BF),
            pltpu.VMEM((2, length, triple), BF),
            pltpu.VMEM((2, heads, length, length), BF),
            pltpu.VMEM((2, length, width), BF),
            pltpu.VMEM((2, length, triple), BF),
            pltpu.VMEM((width, triple), F32),
            pltpu.VMEM((replicas, length, width), BF),
            pltpu.VMEM((3, length, width), BF),
            plane_sem,
            plane_sem,
            hop_sem,
            hop_sem,
            part_sem,
            part_sem,
            pltpu.SemaphoreType.DMA((3, 2)),
            pltpu.SemaphoreType.DMA,
        ],
        compiler_params=pltpu.CompilerParams(
            vmem_limit_bytes=VMEM_MOST, collective_id=3, has_side_effects=True
        ),
        cost_estimate=pl.CostEstimate(
            flops=replicas * heads * 16 * length * length * lanes,
            bytes_accessed=replicas * heads * length * length * 4,
            transcendentals=0,
        ),
        name="attend_back",
    )(
        normed2_far,
        cot_far,
        cot_rest,
        both_far,
        signs_far,
        grad_heads,
        qkv,
        probs,
        normed,
        *weights,
        attended,
        grad_branch,
        grad_mixed,
        inputs,
        gain,
    )


def last_kernel(
    tile,
    far_ref,
    rows_here,
    scaled_here,
    router_ref,
    gate_hbm,
    up_hbm,
    down_hbm,
    grad_gate_hbm,
    grad_up_hbm,
    hidden_hbm,
    qkv_w_hbm,
    out_w_hbm,
    norm1_ref,
    norm2_ref,
    router_grad_ref,
    lines_ref,
    gate_out,
    up_out,
    down_out,
    qkv_w_out,
    out_w_out,
    small_out,
    scaled,
    left,
    weights,
    downs,
    units,
    hidden,
    hidden_here,
    send_wide,
    came_wide,
    send_tall,
    came_tall,
    qkv_land,
    qkv_sum,
    out_land,
    out_sum,
    out_hop,
    out_last,
    small_own,
    small_land,
    small_sum,
    small_hop,
    stream_sem,
    hidden_sem,
    wide_send,
    wide_recv,
    tall_sem,
    first_send,
    first_recv,
    hop_send,
    hop_recv,
    third_send,
    third_recv,
    own_sem,
):
    z, d = lax.axis_index("head"), lax.axis_index("dp")
    groups, capacity, _ = far_ref.shape
    slots, width = scaled_here.shape
    rows, total_units = gate_out.shape
    half_units = hidden_here.shape[1]
    tiles = total_units // tile
    low, high = lax.rem(z, 2), z // 2
    keep_at = pl.multiple_of(low * rows, rows)
    send_at = pl.multiple_of((1 - low) * rows, rows)
    near = {"head": flipped(z, 1)}
    count = 2 * capacity
    hops = [3, 2, 1]

    def streams(t):
        slot = lax.rem(t, 2)
        at = pl.multiple_of(t * tile, tile)
        cols = pl.ds(at, tile)
        return [
            pltpu.make_async_copy(gate_hbm.at[:, cols], weights.at[slot, 0], stream_sem.at[0, slot]),
            pltpu.make_async_copy(up_hbm.at[:, cols], weights.at[slot, 1], stream_sem.at[1, slot]),
            pltpu.make_async_copy(down_hbm.at[cols, :], downs.at[slot], stream_sem.at[2, slot]),
            pltpu.make_async_copy(
                grad_gate_hbm.at[:, cols], units.at[slot, 0], stream_sem.at[3, slot]
            ),
            pltpu.make_async_copy(
                grad_up_hbm.at[:, cols], units.at[slot, 1], stream_sem.at[4, slot]
            ),
        ]

    for copy in streams(0):
        copy.start()
    half_copy = pltpu.make_async_copy(
        hidden_hbm.at[:, pl.ds(pl.multiple_of(high * half_units, TILE), half_units)],
        hidden_here,
        hidden_sem,
    )
    half_copy.start()
    greet([{"dp": flipped(d, o)} for o in PEERS] + [{"head": flipped(z, r)} for r in hops])

    heads = lines_ref.shape[0]
    small_own[...] = jnp.zeros_like(small_own)
    small_own[0:1] = norm1_ref[...]
    small_own[1:2] = norm2_ref[...]
    for h in range(heads):
        small_own[2 + h : 3 + h] = lines_ref[h]
    small_own[8:] = router_grad_ref[...]

    first = []
    for o in PEERS:
        peer = flipped(d, o)
        for i, (source, target) in enumerate(
            (
                (qkv_w_hbm.at[peer], qkv_land.at[o]),
                (out_w_hbm.at[:, peer], out_land.at[o]),
                (small_own, small_land.at[o]),
            )
        ):
            copy = remote(source, target, first_send.at[i, o], first_recv.at[i, o], {"dp": peer})
            copy.start()
            first.append(copy)
    own = [
        pltpu.make_async_copy(qkv_w_hbm.at[d], qkv_land.at[0], own_sem.at[0]),
        pltpu.make_async_copy(out_w_hbm.at[:, d], out_land.at[0], own_sem.at[1]),
    ]
    for copy in own:
        copy.start()

    for j in range(groups // 2):
        span = slice(j * count, (j + 1) * count)
        here = far_ref[2 * j : 2 * j + 2, :, :width].reshape(count, width)
        extended = far_ref[2 * j : 2 * j + 2, :, width:].reshape(count, width + TILE)
        scaled[span] = scaled_rows(here, extended, router_ref[...], width)

    wide = 2 * rows
    columns = pl.ds(pl.multiple_of(high * wide, wide), wide)

    def left_step(i, carry):
        at = pl.multiple_of(i * capacity, capacity)
        left[0, pl.ds(at, capacity), :] = rows_here[pl.ds(at, capacity), columns]
        left[1, pl.ds(at, capacity), :] = far_ref[i, :, columns]
        return carry

    lax.fori_loop(0, groups, left_step, 0)

    def wide_copy(i, t):
        at = pl.multiple_of(t * tile, tile)
        return remote(
            send_wide.at[i, :, pl.ds(at, tile)],
            came_wide.at[i, :, pl.ds(at, tile)],
            wide_send.at[i, t],
            wide_recv.at[i, t],
            near,
        )

    def tile_step(t, carry):
        slot = lax.rem(t, 2)
        at = pl.multiple_of(t * tile, tile)

        @pl.when(t + 1 < tiles)
        def _():
            for copy in streams(t + 1):
                copy.start()

        for copy in streams(t):
            copy.wait()

        def chunk_step(j, inner):
            span = pl.ds(pl.multiple_of(j * count, count), count)
            here = far_ref[pl.ds(2 * j, 2), :, :width].reshape(count, width)
            values = expert_tile(
                here, scaled[span], weights[slot, 0], weights[slot, 1], downs[slot]
            )
            hidden[span, pl.ds(at, tile)] = values[0]
            units[slot, 2, span, :] = values[1]
            units[slot, 3, span, :] = values[2]
            return inner

        lax.fori_loop(0, groups // 2, chunk_step, 0)
        for i, out in enumerate((gate_out, up_out)):
            value = contract(left[0], units[slot, i], 0, 0) + contract(
                left[1], units[slot, 2 + i], 0, 0
            )
            upper = low == 1
            send_wide[i, :, pl.ds(at, tile)] = jnp.where(
                upper, value[:rows], value[rows:]
            ).astype(BF)
            out[:, pl.ds(at, tile)] = jnp.where(upper, value[rows:], value[:rows])
            wide_copy(i, t).start()
        return carry

    lax.fori_loop(0, tiles, tile_step, 0)

    for copy in first:
        copy.wait()
    for copy in own:
        copy.wait()
    small_land[0] = small_own[...]
    qkv_sum[...] = sum(qkv_land[o].astype(F32) for o in range(groups)).astype(BF)
    out_sum[...] = sum(out_land[o].astype(F32) for o in range(groups)).astype(BF)
    small_sum[...] = sum(small_land[o] for o in range(groups))
    second = []
    for o in PEERS:
        copy = remote(
            qkv_sum, qkv_w_out.at[d], third_send.at[0, o], third_recv.at[0, o], {"dp": flipped(d, o)}
        )
        copy.start()
        second.append(copy)
    mine = [pltpu.make_async_copy(qkv_sum, qkv_w_out.at[d], own_sem.at[0])]
    mine[0].start()
    over = []
    for r in hops:
        for i, (source, target) in enumerate(
            ((out_sum.at[r], out_hop.at[r]), (small_sum, small_hop.at[r]))
        ):
            copy = remote(
                source, target, hop_send.at[i, r], hop_recv.at[i, r], {"head": flipped(z, r)}
            )
            copy.start()
            over.append(copy)

    half_copy.wait()
    share = half_units // 2
    halves = pl.ds(pl.multiple_of(high * half_units, TILE), half_units)

    def tall_step(i, carry):
        cols = pl.ds(pl.multiple_of(i * tile, tile), tile)
        value = contract(hidden_here[...], scaled_here[:, cols], 0, 0) + contract(
            hidden[:, halves], scaled[:, cols], 0, 0
        )
        upper = low == 1
        send_tall[:, cols] = jnp.where(upper, value[:share], value[share:]).astype(BF)
        down_out[:, cols] = jnp.where(upper, value[share:], value[:share])
        return carry

    lax.fori_loop(0, width // tile, tall_step, 0)
    tall = remote(send_tall, came_tall, tall_sem.at[0], tall_sem.at[1], near)
    tall.start()

    for copy in over:
        copy.wait()
    out_last[...] = (
        out_sum[0].astype(F32) + sum(out_hop[r].astype(F32) for r in hops)
    ).astype(BF)
    small_out[0] = small_sum[...]
    small_out[1] = small_sum[...] + sum(small_hop[r] for r in hops)
    for o in PEERS:
        copy = remote(
            out_last,
            out_w_out.at[d],
            third_send.at[1, o],
            third_recv.at[1, o],
            {"dp": flipped(d, o)},
        )
        copy.start()
        second.append(copy)
    mine.append(pltpu.make_async_copy(out_last, out_w_out.at[d], own_sem.at[1]))
    mine[1].start()

    def wide_end(t, carry):
        at = pl.multiple_of(t * tile, tile)
        for i, out in enumerate((gate_out, up_out)):
            wide_copy(i, t).wait()
            out[:, pl.ds(at, tile)] += came_wide[i, :, pl.ds(at, tile)].astype(F32)
        return carry

    lax.fori_loop(0, tiles, wide_end, 0)
    for copy in second + mine:
        copy.wait()
    tall.wait()
    down_out[...] += came_tall[...].astype(F32)


def last_stage(
    far, rows_here, scaled_here, router, weights, grads_here, hidden_here, qkv_w, out_w, small, tile
):
    gate_w, up_w, down_w = weights
    width, units = gate_w.shape
    groups, capacity, extent = far.shape
    replicas, _, part_rows, _ = out_w.shape
    slots = groups * capacity
    vmem = pl.BlockSpec(memory_space=pltpu.VMEM)
    hbm = pl.BlockSpec(memory_space=pl.ANY)
    rows, share = width // replicas, units // replicas
    small_shape = (8 + groups, width)
    plane_sem = pltpu.SemaphoreType.DMA((3, groups))
    hop_sem = pltpu.SemaphoreType.DMA((2, replicas))
    return pl.pallas_call(
        functools.partial(last_kernel, tile),
        out_shape=(
            jax.ShapeDtypeStruct((rows, units), F32),
            jax.ShapeDtypeStruct((rows, units), F32),
            jax.ShapeDtypeStruct((share, width), F32),
            jax.ShapeDtypeStruct(qkv_w.shape, BF),
            jax.ShapeDtypeStruct(out_w.shape[1:], BF),
            jax.ShapeDtypeStruct((2,) + small_shape, F32),
        ),
        in_specs=[vmem] * 4 + [hbm] * 8 + [vmem] * 4,
        out_specs=[vmem, vmem, vmem, hbm, hbm, vmem],
        scratch_shapes=[
            pltpu.VMEM((slots, width), BF),
            pltpu.VMEM((2, slots, 2 * rows), BF),
            pltpu.VMEM((2, 2, width, tile), BF),
            pltpu.VMEM((2, tile, width), BF),
            pltpu.VMEM((2, 4, slots, tile), BF),
            pltpu.VMEM((slots, units), BF),
            pltpu.VMEM((slots, units // 2), BF),
            pltpu.VMEM((2, rows, units), BF),
            pltpu.VMEM((2, rows, units), BF),
            pltpu.VMEM((share, width), BF),
            pltpu.VMEM((share, width), BF),
            pltpu.VMEM(qkv_w.shape, BF),
            pltpu.VMEM(qkv_w.shape[1:], BF),
            pltpu.VMEM((groups, replicas, part_rows, width), BF),
            pltpu.VMEM((replicas, part_rows, width), BF),
            pltpu.VMEM((replicas, part_rows, width), BF),
            pltpu.VMEM((part_rows, width), BF),
            pltpu.VMEM(small_shape, F32),
            pltpu.VMEM((groups,) + small_shape, F32),
            pltpu.VMEM(small_shape, F32),
            pltpu.VMEM((replicas,) + small_shape, F32),
            pltpu.SemaphoreType.DMA((5, 2)),
            pltpu.SemaphoreType.DMA,
            pltpu.SemaphoreType.DMA((2, units // tile)),
            pltpu.SemaphoreType.DMA((2, units // tile)),
            pltpu.SemaphoreType.DMA((2,)),
            plane_sem,
            plane_sem,
            hop_sem,
            hop_sem,
            plane_sem,
            plane_sem,
            pltpu.SemaphoreType.DMA((2,)),
        ],
        compiler_params=pltpu.CompilerParams(
            vmem_limit_bytes=VMEM_MOST, collective_id=4, has_side_effects=True
        ),
        cost_estimate=pl.CostEstimate(
            flops=12 * slots * width * units,
            bytes_accessed=6 * width * units + 6 * slots * units,
            transcendentals=slots * units,
        ),
        name="last_stage",
    )(
        far,
        rows_here,
        scaled_here,
        router,
        gate_w,
        up_w,
        down_w,
        *grads_here,
        hidden_here,
        qkv_w,
        out_w,
        *small,
    )


def expert_forward(rows, gate_w, up_w, grad_unscaled, slot_gates):
    gate_pre = jnp.dot(rows, gate_w, preferred_element_type=F32)
    up_pre = jnp.dot(rows, up_w, preferred_element_type=F32)
    hidden, pull = jax.vjp(geglu, gate_pre, up_pre)
    grad_gate_pre, grad_up_pre = pull(grad_unscaled * slot_gates)
    return hidden.astype(BF), grad_gate_pre.astype(BF), grad_up_pre.astype(BF)


def body_plain(
    block_input,
    cotangent,
    expert_ids,
    priority,
    rel_bucket,
    norm1_gain,
    w_query,
    w_key,
    w_value,
    w_out,
    pos_bias,
    norm2_gain,
    w_router,
    w_gate,
    w_up,
    w_down,
):
    group_rows, width = block_input.shape
    own_rows = cotangent.shape[0]
    buckets, heads_here = pos_bias.shape
    head_cols = w_query.shape[1]
    length = (rel_bucket.shape[0] + 1) // 2
    sequences = group_rows // length
    experts = w_router.shape[1]
    capacity = 5 * 2 * own_rows // (4 * experts)
    slot_count = experts * capacity
    replicas = lax.axis_size("head")
    groups = lax.axis_size("dp")
    me = lax.axis_index("head")
    far = replicas // 2
    far_perm = [(i, i ^ far) for i in range(replicas)]
    stepwise = own_rows == length and sequences == replicas

    def hop(value, r):
        return lax.ppermute(value, "head", [(i, i ^ r) for i in range(replicas)])

    def exchange(value):
        parts = value.reshape(experts, capacity, -1)
        return lax.all_to_all(parts, "dp", split_axis=0, concat_axis=0, tiled=True).reshape(
            slot_count, -1
        )

    dest = route_slots(expert_ids, priority[0], experts, capacity)
    dest_far = lax.ppermute(dest, "head", far_perm)
    slot_range = jnp.arange(slot_count, dtype=jnp.int32)[None, :]
    picks = [(dest[:, k : k + 1] == slot_range).astype(BF) for k in range(2)]
    both = picks[0] + picks[1]
    both_far = sum((dest_far[:, k : k + 1] == slot_range).astype(BF) for k in range(2))

    down_w, gate_w, up_w = w_down[0], w_gate[0], w_up[0]
    cot_here = exchange(contract(both, cotangent, 0, 0).astype(BF))
    cot_far_own = lax.ppermute(cotangent, "head", far_perm)
    cot_far = exchange(contract(both_far, cot_far_own, 0, 0).astype(BF))
    unscaled_here = contract(cot_here, down_w, 1, 1)
    unscaled_far = contract(cot_far, down_w, 1, 1)

    dp_at = lax.axis_index("dp")
    out_rows = head_cols // groups
    piece = lax.dynamic_slice_in_dim(w_out, dp_at * out_rows, out_rows, 0)
    w_out_all = lax.all_gather(piece, ("head", "dp"), axis=0, tiled=True)
    w_qkv = jnp.concatenate([w_query, w_key, w_value], axis=1)
    qkv_rows = width // groups
    piece = lax.dynamic_slice_in_dim(w_qkv, dp_at * qkv_rows, qkv_rows, 0)
    w_qkv_all = lax.all_gather(piece, ("head", "dp"), axis=0, tiled=True)
    if stepwise:
        order = [me ^ r for r in range(replicas)]
    else:
        order = list(range(replicas))
    w_out_all = w_out_all.reshape(replicas, head_cols, width)
    w_qkv_all = w_qkv_all.reshape(replicas, width, 3 * head_cols)
    w_out_cat = jnp.concatenate(
        [lax.dynamic_index_in_dim(w_out_all, o, 0, keepdims=False) for o in order], axis=0
    )

    inputs_all = block_input.astype(F32)
    normed = rms_norm(inputs_all, norm1_gain).astype(BF)
    qkv = jnp.dot(normed, w_qkv, preferred_element_type=F32).astype(BF)
    line = (rel_bucket[::-1][None, :] == jnp.arange(buckets, dtype=jnp.int32)[:, None]).astype(F32)
    line = jnp.pad(line, ((0, 0), (1, 0)))
    table = skew(contract(pos_bias, line, 0, 0, HIGH))
    kept = {}
    if stepwise:
        blocks = [None] * replicas
        for r in reversed(range(replicas)):
            attended_seq, probs = attend_fwd(order[r].reshape(1), qkv, table, length)
            kept[r] = probs
            blocks[r] = hop(attended_seq, r) if r else attended_seq
    else:
        seqs = []
        for s in range(sequences):
            attended_seq, kept[s] = attend_fwd(jnp.full((1,), s, jnp.int32), qkv, table, length)
            seqs.append(attended_seq)
        attended_all = jnp.concatenate(seqs, axis=0).reshape(replicas, own_rows, head_cols)
        attended_all = lax.all_to_all(attended_all, "head", split_axis=0, concat_axis=0, tiled=True)
        blocks = [attended_all[i] for i in range(replicas)]
    attended = jnp.concatenate(blocks, axis=1)

    branch = jnp.dot(attended, w_out_cat, preferred_element_type=F32)
    start_own = me * own_rows
    inputs_own = lax.dynamic_slice_in_dim(block_input, start_own, own_rows, 0).astype(F32)
    mixed = inputs_own + branch
    normed2_full, norm2_pull = jax.vjp(rms_norm, mixed, norm2_gain)
    normed2 = normed2_full.astype(BF)
    logits = jnp.dot(normed2, w_router, preferred_element_type=F32)
    expert_range = jnp.arange(experts, dtype=jnp.int32)
    chosen = (expert_ids[:, :, None] == expert_range[None, None, :]).astype(F32)
    gates = jax.nn.softmax(jnp.sum(chosen * logits[:, None, :], axis=2), axis=-1)

    def slot_gates_of(places, values):
        terms = sum(
            jnp.where(places[:, k : k + 1] == slot_range, values[:, k : k + 1], 0.0)
            for k in range(2)
        )
        return jnp.sum(terms, axis=0)

    rows_here = exchange(contract(both, normed2, 0, 0).astype(BF))
    gates_here = exchange(slot_gates_of(dest, gates))
    normed2_far = lax.ppermute(normed2, "head", far_perm)
    gates_far_own = lax.ppermute(gates, "head", far_perm)
    rows_far = exchange(contract(both_far, normed2_far, 0, 0).astype(BF))
    gates_far = exchange(slot_gates_of(dest_far, gates_far_own))

    hidden_here, ggp_here, gup_here = expert_forward(
        rows_here, gate_w, up_w, unscaled_here, gates_here
    )
    returned = jnp.dot(hidden_here, down_w, preferred_element_type=F32).astype(BF)
    came_back = exchange(returned)
    grad_routed = (contract(ggp_here, gate_w, 1, 1) + contract(gup_here, up_w, 1, 1)).astype(BF)
    grad_back = exchange(grad_routed)
    hidden_far, ggp_far, gup_far = expert_forward(rows_far, gate_w, up_w, unscaled_far, gates_far)
    scaled_here = (cot_here.astype(F32) * gates_here).astype(BF)
    scaled_far = (cot_far.astype(F32) * gates_far).astype(BF)

    low = me % far
    high = me // far

    def reduced(lefts, rights):
        rows = lefts[0].shape[1] // replicas

        def part(at):
            return sum(
                contract(lax.dynamic_slice_in_dim(left, at * rows, rows, 1), right, 0, 0)
                for left, right in zip(lefts, rights)
            )

        if far == 2:
            sent = hop(part(high * far + (1 - low)).astype(BF), 1)
            return (part(me) + sent.astype(F32))[None]
        whole = jnp.concatenate([part(high * far + i) for i in range(far)], axis=0).astype(BF)
        member = [[h * far + i for i in range(far)] for h in range(2)]
        return lax.psum_scatter(
            whole, "head", scatter_dimension=0, axis_index_groups=member, tiled=True
        ).astype(F32)[None]

    grad_down_w = reduced((hidden_here, hidden_far), (scaled_here, scaled_far))
    grad_gate_w = reduced((rows_here, rows_far), (ggp_here, ggp_far))
    grad_up_w = reduced((rows_here, rows_far), (gup_here, gup_far))

    chosen_rows = [jnp.dot(pick, came_back, preferred_element_type=F32) for pick in picks]
    output = mixed + sum(gates[:, k : k + 1] * chosen_rows[k] for k in range(2))
    grad_output = cotangent.astype(F32)
    grad_gates = jnp.stack([jnp.sum(grad_output * rows, axis=1) for rows in chosen_rows], axis=1)
    grad_normed2 = jnp.dot(both, grad_back, preferred_element_type=F32)
    grad_picked = gates * (grad_gates - jnp.sum(gates * grad_gates, axis=1, keepdims=True))
    grad_logits = jnp.sum(chosen * grad_picked[:, :, None], axis=1)
    grad_normed2 = grad_normed2 + contract(grad_logits, w_router.astype(F32), 1, 1, HIGH)
    grad_router = contract(normed2.astype(F32), grad_logits, 0, 0, HIGH)
    grad_mixed, grad_norm2 = norm2_pull(grad_normed2)
    grad_mixed = grad_mixed + grad_output
    grad_branch = grad_mixed.astype(BF)

    grad_wout = contract(attended, grad_branch, 0, 0).astype(BF)
    grad_wout = grad_wout.reshape(replicas, groups, out_rows, width)
    grad_wout = lax.psum_scatter(grad_wout, "dp", scatter_dimension=1, tiled=True)[:, 0]
    if stepwise:
        grad_wout = sum(
            (hop(grad_wout[r], r) if r else grad_wout[r]).astype(F32) for r in range(replicas)
        ).astype(BF)
    else:
        grad_wout = lax.psum_scatter(
            grad_wout.reshape(replicas * out_rows, width), "head", scatter_dimension=0, tiled=True
        )
    grad_out_proj = lax.all_gather(grad_wout, "dp", axis=0, tiled=True).astype(F32)

    grad_heads = contract(grad_branch, w_out_cat, 1, 1).astype(BF)
    sums = jnp.zeros((heads_here, TILE, 2 * length), F32)
    grad_blocks = [grad_heads[:, i * head_cols : (i + 1) * head_cols] for i in range(replicas)]
    grad_total = None
    weight_terms = []
    if stepwise:
        arrived = [hop(grad_blocks[r], r) if r else grad_blocks[0] for r in range(replicas)]
        for r in (0, 2, 3, 1):
            grad_qkv, sums = attend_bwd(order[r].reshape(1), qkv, arrived[r], kept[r], sums, length)
            normed_seq = lax.dynamic_slice_in_dim(normed, order[r] * length, length, 0)
            weight_terms.append(contract(normed_seq, grad_qkv, 0, 0))
            mine = hop(grad_qkv, r) if r else grad_qkv
            weight = lax.dynamic_index_in_dim(w_qkv_all, order[r], 0, keepdims=False)
            term = contract(mine, weight, 1, 1)
            grad_total = term if grad_total is None else grad_total + term
        grad_normed = grad_total
        grad_qkv_w = sum(weight_terms)
    else:
        stacked = jnp.stack(grad_blocks, axis=0)
        stacked = lax.all_to_all(stacked, "head", split_axis=0, concat_axis=0, tiled=True)
        stacked = stacked.reshape(group_rows, head_cols)
        seqs = []
        for s in range(sequences):
            grad_seq = stacked[s * length : (s + 1) * length]
            grad_qkv, sums = attend_bwd(
                jnp.full((1,), s, jnp.int32), qkv, grad_seq, kept[s], sums, length
            )
            seqs.append(grad_qkv)
        grad_qkv = jnp.concatenate(seqs, axis=0)
        grad_qkv_w = contract(normed, grad_qkv, 0, 0)
        grad_qkv = lax.all_to_all(
            grad_qkv.reshape(replicas, own_rows, 3 * head_cols),
            "head",
            split_axis=0,
            concat_axis=0,
            tiled=True,
        )
        grad_normed = sum(contract(grad_qkv[i], w_qkv_all[i], 1, 1) for i in range(replicas))

    _, norm1_pull = jax.vjp(rms_norm, inputs_own, norm1_gain)
    grad_first, grad_norm1 = norm1_pull(grad_normed)
    grad_input = grad_mixed + grad_first
    grad_bias = contract(unskew(sums), line, 1, 1, HIGH)
    grad_qkv_w, grad_bias = lax.psum((grad_qkv_w.astype(BF), grad_bias), "dp")
    grad_qkv_w = grad_qkv_w.astype(F32)
    grad_norm1, grad_norm2, grad_router = lax.psum(
        (grad_norm1, grad_norm2, grad_router), ("dp", "head")
    )
    return (
        output,
        grad_input,
        grad_norm1,
        grad_qkv_w[:, :head_cols],
        grad_qkv_w[:, head_cols : 2 * head_cols],
        grad_qkv_w[:, 2 * head_cols :],
        grad_out_proj,
        jnp.transpose(grad_bias),
        grad_norm2,
        grad_router,
        grad_gate_w,
        grad_up_w,
        grad_down_w,
    )


def body(*args):
    block_input, cotangent, rel_bucket, pos_bias, w_gate, w_router = (
        args[0],
        args[1],
        args[4],
        args[10],
        args[13],
        args[12],
    )
    own_rows = cotangent.shape[0]
    length = (rel_bucket.shape[0] + 1) // 2
    replicas, groups = lax.axis_size("head"), lax.axis_size("dp")
    experts = w_router.shape[1]
    capacity = 5 * 2 * own_rows // (4 * experts)
    stepwise = (
        own_rows == length
        and block_input.shape[0] == replicas * length
        and replicas == 4
        and groups == 8
        and experts == groups
        and capacity % 16 == 0
        and pos_bias.shape[1] in (2, 4, 6)
        and w_gate.shape[2] % 256 == 0
    )
    return body_steps(*args) if stepwise else body_plain(*args)


def body_steps(
    block_input,
    cotangent,
    expert_ids,
    priority,
    rel_bucket,
    norm1_gain,
    w_query,
    w_key,
    w_value,
    w_out,
    pos_bias,
    norm2_gain,
    w_router,
    w_gate,
    w_up,
    w_down,
):
    group_rows, width = block_input.shape
    own_rows = cotangent.shape[0]
    buckets, heads_here = pos_bias.shape
    head_cols = w_query.shape[1]
    length = (rel_bucket.shape[0] + 1) // 2
    experts = w_router.shape[1]
    capacity = 5 * 2 * own_rows // (4 * experts)
    slot_count = experts * capacity
    replicas, groups = lax.axis_size("head"), lax.axis_size("dp")
    me, dp_at = lax.axis_index("head"), lax.axis_index("dp")

    dest = route_slots(expert_ids, priority[0], experts, capacity)
    mixed_dest = jnp.where(
        dest < slot_count,
        ((dest // capacity) ^ dp_at) * capacity + dest % capacity,
        slot_count,
    )
    routing = jnp.concatenate([mixed_dest, expert_ids], axis=1)
    slot_row = jnp.arange(slot_count, dtype=jnp.int32)[None, :]
    slot_col = jnp.arange(slot_count, dtype=jnp.int32)[:, None]
    lane_range = jnp.arange(TILE, dtype=jnp.int32)[None, :]

    def token_signs(ids):
        return (ids[:, 1:2] == lane_range).astype(BF) - (ids[:, 0:1] == lane_range).astype(BF)

    def dispatch_of(places, ids):
        first = (slot_col == places[:, 0][None, :]).astype(BF)
        second = (slot_col == places[:, 1][None, :]).astype(BF)
        return first + second, contract(first - second, token_signs(ids), 1, 0).astype(BF)

    both, signs = dispatch_of(mixed_dest, expert_ids)
    picks = [(mixed_dest[:, k : k + 1] == slot_row).astype(BF) for k in range(2)]
    router_wide = jnp.pad(w_router, ((0, 0), (0, TILE - experts)))
    line = (rel_bucket[::-1][None, :] == jnp.arange(buckets, dtype=jnp.int32)[:, None]).astype(F32)
    line = jnp.pad(line, ((0, 0), (1, 0)))
    input_weights = (w_query, w_key, w_value)
    (
        attended,
        probs,
        cot_here,
        normed,
        qkv,
        w_cat,
        cot_far,
        routing_far,
        mixed,
        normed2,
    ) = attend_all(
        block_input,
        norm1_gain[None, :],
        input_weights,
        contract(pos_bias, line, 0, 0, HIGH)[:, None, :],
        both,
        signs,
        cotangent,
        routing,
        w_out,
        norm2_gain[None, :],
        groups,
    )

    gate_w, up_w, down_w = w_gate[0], w_up[0], w_down[0]
    tile = 256
    (
        rows_here,
        hidden_here,
        ggp_here,
        gup_here,
        scaled_here,
        came_back,
        grad_back,
        normed2_far,
        cot_far_rest,
    ) = expert_stage(
        normed2,
        both,
        cot_here,
        router_wide,
        gate_w,
        up_w,
        down_w,
        cotangent,
        groups,
        capacity,
        tile,
    )
    rows_here = rows_here.reshape(slot_count, width)
    scaled_here = scaled_here.reshape(slot_count, width)

    output, grad_mixed, grad_branch, grad_heads, grad_router, grad_norm2 = combine(
        came_back.reshape(slot_count, width),
        grad_back.reshape(slot_count, width),
        picks,
        mixed,
        normed2,
        cotangent,
        token_signs(expert_ids),
        router_wide,
        norm2_gain[None, :],
        w_cat,
        experts,
    )

    both_far, signs_far = dispatch_of(routing_far[:, :2], routing_far[:, 2:])
    inputs_own = lax.dynamic_slice_in_dim(block_input, me * own_rows, own_rows, 0)
    far_came, grad_qkv_w, grad_wout, grad_input, grad_norm1, lines = attend_back(
        normed2_far,
        cot_far,
        cot_far_rest,
        both_far,
        signs_far,
        grad_heads,
        qkv,
        probs,
        normed,
        input_weights,
        attended,
        grad_branch,
        grad_mixed,
        inputs_own,
        norm1_gain[None, :],
        groups,
    )

    grad_gate_w, grad_up_w, grad_down_w, grad_qkv_w, grad_out_proj, summed = last_stage(
        far_came,
        rows_here,
        scaled_here,
        router_wide,
        (gate_w, up_w, down_w),
        (ggp_here, gup_here),
        hidden_here,
        grad_qkv_w.reshape(groups, width // groups, 3 * head_cols),
        grad_wout.reshape(replicas, groups, head_cols // groups, width),
        (grad_norm1, grad_norm2, grad_router, lines),
        tile,
    )
    grad_qkv_w = grad_qkv_w.reshape(width, 3 * head_cols).astype(F32)
    grad_out_proj = grad_out_proj.reshape(head_cols, width).astype(F32)
    return (
        output,
        grad_input,
        summed[1, 0],
        grad_qkv_w[:, :head_cols],
        grad_qkv_w[:, head_cols : 2 * head_cols],
        grad_qkv_w[:, 2 * head_cols :],
        grad_out_proj,
        contract(line, summed[0, 2 : 2 + heads_here], 1, 1, HIGH),
        summed[1, 1],
        jnp.transpose(summed[1, 8 : 8 + experts]),
        grad_gate_w[None],
        grad_up_w[None],
        grad_down_w[None],
    )


def solution(mesh):
    placed = (
        P("dp", None),
        P(("dp", "head"), None),
        P(("dp", "head"), None),
        P(("dp", "head"), None),
        P(),
        P(),
        P(None, "head"),
        P(None, "head"),
        P(None, "head"),
        P("head", None),
        P(None, "head"),
        P(),
        P(),
        P("dp", None, None),
        P("dp", None, None),
        P("dp", None, None),
    )
    return jax.shard_map(
        body,
        mesh=mesh,
        in_specs=placed,
        out_specs=(
            P(("dp", "head"), None),
            P(("dp", "head"), None),
            P(),
            P(None, "head"),
            P(None, "head"),
            P(None, "head"),
            P("head", None),
            P(None, "head"),
            P(),
            P(),
            P("dp", "head", None),
            P("dp", "head", None),
            P("dp", "head", None),
        ),
        check_vma=False,
    )
```

```python
import functools

import jax
import jax.numpy as jnp
from jax import lax
from jax.experimental import pallas as pl
from jax.experimental.pallas import tpu as pltpu
from jax.sharding import PartitionSpec as P

EPS = 1e-06
SCALE = 0.125
HIGH = lax.Precision.HIGHEST
TILE = 128
BF = jnp.bfloat16
F32 = jnp.float32
VMEM_LIMIT = 48 << 20
VMEM_MOST = 60 << 20
GELU_A = 0.7978845608028654
GELU_B = 0.044715
OFFSETS = [0, 1, 6, 7, 2, 4, 3, 5]
PEERS = [4, 5, 6, 7, 2, 3, 1]
ROW_PEERS = [2, 3, 4, 5, 6, 7, 1]


def rms_norm(value, gain):
    return value * lax.rsqrt(jnp.mean(value * value, axis=-1, keepdims=True) + EPS) * gain


def geglu(gate, up_part):
    return jax.nn.gelu(gate) * up_part


def contract(left, right, left_dim, right_dim, precision=None):
    return lax.dot_general(
        left,
        right,
        (((left_dim,), (right_dim,)), ((), ())),
        precision=precision,
        preferred_element_type=jnp.float32,
    )


def route_slots(chosen, ranks, experts, capacity):
    count = chosen.shape[0]
    keys = jnp.concatenate([ranks, ranks + count])
    wanted = jnp.concatenate([chosen[:, 0], chosen[:, 1]])
    smaller = (wanted[:, None] == wanted[None, :]) & (keys[None, :] < keys[:, None])
    place = jnp.sum(smaller.astype(jnp.int32), axis=1)
    dest = jnp.where(place < capacity, wanted * capacity + place, experts * capacity)
    return jnp.stack([dest[:count], dest[count:]], axis=1)


def skew_kernel(line_ref, table_ref):
    heads, rows, cols = table_ref.shape
    row = lax.broadcasted_iota(jnp.int32, (rows, cols), 0)
    for h in range(heads):
        value = jnp.broadcast_to(line_ref[h], (rows, cols))
        shift = 1
        while shift < rows:
            value = jnp.where((row & shift) != 0, pltpu.roll(value, shift, 1), value)
            shift *= 2
        table_ref[h] = value


def unskew_kernel(table_ref, line_ref):
    heads, rows, cols = table_ref.shape
    row = lax.broadcasted_iota(jnp.int32, (rows, cols), 0)
    for h in range(heads):
        value = table_ref[h]
        shift = 1
        while shift < rows:
            value = jnp.where((row & shift) != 0, pltpu.roll(value, cols - shift, 1), value)
            shift *= 2
        line_ref[h] = jnp.sum(value, axis=0, keepdims=True)


def skew(line):
    heads, cols = line.shape
    return pl.pallas_call(
        skew_kernel,
        out_shape=jax.ShapeDtypeStruct((heads, TILE, cols), F32),
        compiler_params=pltpu.CompilerParams(vmem_limit_bytes=VMEM_LIMIT),
        name="skew",
    )(line[:, None, :])


def unskew(table):
    heads, _, cols = table.shape
    return pl.pallas_call(
        unskew_kernel,
        out_shape=jax.ShapeDtypeStruct((heads, 1, cols), F32),
        compiler_params=pltpu.CompilerParams(vmem_limit_bytes=VMEM_LIMIT),
        name="unskew",
    )(table)[:, 0]


def lanes_of(shape, half, part):
    lane = lax.broadcasted_iota(jnp.int32, shape, 1)
    return (lane >= half) if part else (lane < half)


def attend_fwd_kernel(seq_ref, q_ref, k_ref, v_ref, table_ref, out_ref, probs_ref, acc_ref):
    del seq_ref
    length, lanes = q_ref.shape
    half = lanes // 2
    chunk = 2 * TILE
    key = k_ref[...]
    value_t = v_ref[...].T
    for part in range(2):
        query = jnp.where(lanes_of((length, lanes), half, part), q_ref[...] * SCALE, 0).astype(BF)
        for c in range(length // chunk):
            cols = slice(c * chunk, (c + 1) * chunk)
            scores = contract(key, query[cols], 1, 1)
            pieces = []
            for kb in range(length // TILE):
                at = length - TILE * kb + chunk * c
                pieces.append(
                    scores[kb * TILE : (kb + 1) * TILE] + table_ref[part, :, at : at + chunk]
                )
            scores = jnp.concatenate(pieces, axis=0)
            top = jnp.max(scores, axis=0, keepdims=True)
            shifted = jnp.exp(scores - top)
            total = jnp.sum(shifted, axis=0, keepdims=True)
            probs = (shifted * (1.0 / total)).astype(BF)
            probs_ref[part, :, cols] = probs
            acc_ref[part * half : (part + 1) * half, cols] = jnp.dot(
                value_t[part * half : (part + 1) * half], probs, preferred_element_type=F32
            )
    out_ref[...] = acc_ref[...].T.astype(BF)


def attend_fwd(seq, qkv, table, length):
    heads, _, width = table.shape
    columns = qkv.shape[1] // 3
    pairs = heads // 2
    lanes = columns // pairs
    spec = [
        pl.BlockSpec((length, lanes), lambda p, s, j=j: (s[0], j * pairs + p)) for j in range(3)
    ]
    return pl.pallas_call(
        attend_fwd_kernel,
        out_shape=(
            jax.ShapeDtypeStruct((length, columns), BF),
            jax.ShapeDtypeStruct((heads, length, length), BF),
        ),
        grid_spec=pltpu.PrefetchScalarGridSpec(
            num_scalar_prefetch=1,
            grid=(pairs,),
            in_specs=spec + [pl.BlockSpec((2, TILE, width), lambda p, s: (p, 0, 0))],
            out_specs=[
                pl.BlockSpec((length, lanes), lambda p, s: (0, p)),
                pl.BlockSpec((2, length, length), lambda p, s: (p, 0, 0)),
            ],
            scratch_shapes=[pltpu.VMEM((lanes, length), F32)],
        ),
        compiler_params=pltpu.CompilerParams(vmem_limit_bytes=VMEM_LIMIT),
        cost_estimate=pl.CostEstimate(
            flops=heads * 8 * length * length * lanes,
            bytes_accessed=heads * length * length * 2 + 8 * length * columns,
            transcendentals=heads * length * length,
        ),
        name="attend_fwd",
    )(seq, qkv, qkv, qkv, table)


def attend_bwd_kernel(
    seq_ref, q_ref, k_ref, v_ref, grad_ref, probs_ref, sums_in_ref, out_ref, sums_ref, acc_ref
):
    del seq_ref
    length, lanes = q_ref.shape
    half = lanes // 2
    chunk = 2 * TILE
    pair = pl.program_id(0)
    columns = out_ref.shape[1] // 3
    key_t = k_ref[...].T
    value = v_ref[...]
    sums_ref[...] = sums_in_ref[...]
    grad_keys, grad_values = [], []
    for part in range(2):
        mask = lanes_of((length, lanes), half, part)
        grad = jnp.where(mask, grad_ref[...], 0).astype(BF)
        grad_key = jnp.zeros((length, lanes), F32)
        grad_value = jnp.zeros((length, lanes), F32)
        for c in range(length // chunk):
            cols = slice(c * chunk, (c + 1) * chunk)
            grad_probs = contract(value, grad[cols], 1, 1)
            probs_low = probs_ref[part, :, cols]
            probs = probs_low.astype(F32)
            delta = jnp.sum(probs * grad_probs, axis=0, keepdims=True)
            grad_scores = (probs * (grad_probs - delta)).astype(BF)
            grad_value += jnp.dot(probs_low, grad_ref[cols, :], preferred_element_type=F32)
            grad_key += jnp.dot(grad_scores, q_ref[cols, :], preferred_element_type=F32)
            acc_ref[part * half : (part + 1) * half, cols] = jnp.dot(
                key_t[part * half : (part + 1) * half], grad_scores, preferred_element_type=F32
            )
            for kb in range(length // TILE):
                at = length - TILE * kb + chunk * c
                sums_ref[part, :, at : at + chunk] += grad_scores[
                    kb * TILE : (kb + 1) * TILE
                ].astype(F32)
        grad_keys.append(grad_key)
        grad_values.append(grad_value)
    first = lanes_of((length, lanes), half, 0)
    at = pl.multiple_of(pair * lanes, lanes)
    out_ref[:, pl.ds(at, lanes)] = (acc_ref[...].T * SCALE).astype(BF)
    at = pl.multiple_of(columns + pair * lanes, lanes)
    out_ref[:, pl.ds(at, lanes)] = (jnp.where(first, *grad_keys) * SCALE).astype(BF)
    at = pl.multiple_of(2 * columns + pair * lanes, lanes)
    out_ref[:, pl.ds(at, lanes)] = jnp.where(first, *grad_values).astype(BF)


def attend_bwd(seq, qkv, grad, probs, sums, length):
    heads, _, width = sums.shape
    columns = qkv.shape[1] // 3
    pairs = heads // 2
    lanes = columns // pairs
    spec = [
        pl.BlockSpec((length, lanes), lambda p, s, j=j: (s[0], j * pairs + p)) for j in range(3)
    ]
    sums_spec = pl.BlockSpec((2, TILE, width), lambda p, s: (p, 0, 0))
    return pl.pallas_call(
        attend_bwd_kernel,
        out_shape=(
            jax.ShapeDtypeStruct((length, 3 * columns), BF),
            jax.ShapeDtypeStruct(sums.shape, F32),
        ),
        grid_spec=pltpu.PrefetchScalarGridSpec(
            num_scalar_prefetch=1,
            grid=(pairs,),
            in_specs=spec
            + [
                pl.BlockSpec((length, lanes), lambda p, s: (0, p)),
                pl.BlockSpec((2, length, length), lambda p, s: (p, 0, 0)),
                sums_spec,
            ],
            out_specs=[pl.BlockSpec((length, 3 * columns), lambda p, s: (0, 0)), sums_spec],
            scratch_shapes=[pltpu.VMEM((lanes, length), F32)],
        ),
        compiler_params=pltpu.CompilerParams(vmem_limit_bytes=VMEM_LIMIT),
        cost_estimate=pl.CostEstimate(
            flops=heads * 16 * length * length * lanes,
            bytes_accessed=heads * length * length * 2 + 16 * length * columns,
            transcendentals=0,
        ),
        name="attend_bwd",
    )(seq, qkv, qkv, qkv, grad, probs, sums)


def flipped(index, bits):
    out, step = index, 1
    while step <= bits:
        if bits & step:
            out = out + step * (1 - 2 * lax.rem(index // step, 2))
        step *= 2
    return out


def plane(d, position):
    return flipped(d, OFFSETS[position])


def greet(peers):
    barrier = pltpu.get_barrier_semaphore()
    for peer in peers:
        pl.semaphore_signal(barrier, inc=1, device_id=peer, device_id_type=pl.DeviceIdType.MESH)
    pl.semaphore_wait(barrier, len(peers))


def remote(source, target, send_sem, recv_sem, peer):
    return pltpu.make_async_remote_copy(
        src_ref=source,
        dst_ref=target,
        send_sem=send_sem,
        recv_sem=recv_sem,
        device_id=peer,
        device_id_type=pl.DeviceIdType.MESH,
    )


def attend_all_kernel(
    input_hbm,
    gain_ref,
    query_hbm,
    key_hbm,
    value_hbm,
    line_ref,
    cot_hbm,
    routing_ref,
    w_out_hbm,
    gain2_ref,
    attended_out,
    probs_out,
    came_out,
    normed_out,
    qkv_out,
    w_cat_out,
    cot_far_out,
    routing_far_out,
    mixed_ref,
    normed2_ref,
    input_ref,
    weight_ref,
    cot_ref,
    w_out_ref,
    table_ref,
    sends,
    acc_ref,
    block_ref,
    hold_ref,
    normed_ref,
    qkv_ref,
    attended_ref,
    w_cat,
    w_land,
    row_send,
    row_recv,
    hop_send,
    hop_recv,
    w_send,
    w_recv,
    plane_send,
    plane_recv,
    far_send,
    far_recv,
    hold_sem,
    own_sem,
    load_sem,
):
    z, d = lax.axis_index("head"), lax.axis_index("dp")
    heads, _, _ = table_ref.shape
    replicas, length, columns = block_ref.shape
    groups, capacity, _ = sends.shape
    width = input_ref.shape[1]
    part_rows = w_land.shape[1]
    pairs = heads // 2
    lanes = columns // pairs
    half = lanes // 2
    chunk = 2 * TILE
    hops = [3, 2, 1]
    cot_load = pltpu.make_async_copy(cot_hbm, cot_ref, load_sem.at[0])
    w_out_load = pltpu.make_async_copy(w_out_hbm, w_out_ref, load_sem.at[1])
    weight_loads = [
        pltpu.make_async_copy(source, weight_ref.at[i], load_sem.at[2 + i])
        for i, source in enumerate((query_hbm, key_hbm, value_hbm))
    ]
    input_loads = {}
    for r in [3, 2, 1, 0]:
        span = pl.ds(pl.multiple_of(flipped(z, r) * length, length), length)
        input_loads[r] = pltpu.make_async_copy(
            input_hbm.at[span], input_ref.at[span], load_sem.at[5 + r]
        )
    for copy in [cot_load, input_loads[3]] + weight_loads:
        copy.start()
    for copy in [input_loads[2], input_loads[1], input_loads[0], w_out_load]:
        copy.start()
    greet([{"dp": plane(d, o)} for o in PEERS] + [{"head": flipped(z, r)} for r in hops])
    copies = []

    def launch(*what):
        copy = remote(*what)
        copy.start()
        copies.append(copy)
        return copy

    piece = w_out_hbm.at[pl.ds(pl.multiple_of(d * part_rows, part_rows), part_rows), :]
    w_hops = {}
    for r in hops:
        w_hops[r] = remote(piece, w_land.at[r], w_send.at[r], w_recv.at[r], {"head": flipped(z, r)})
        w_hops[r].start()
    cot_load.wait()
    for o in PEERS + [0]:
        first, second = selector(routing_ref, o * capacity, capacity)
        sends[o, :, :width] = jnp.dot(
            (first + second).astype(BF), cot_ref[...], preferred_element_type=F32
        ).astype(BF)
        sends[o, :, width:] = slot_signs(routing_ref, first, second)
        if o:
            launch(
                sends.at[o], came_out.at[o], row_send.at[o], row_recv.at[o], {"dp": plane(d, o)}
            )
    own = pltpu.make_async_copy(sends.at[0], came_out.at[0], own_sem.at[0])
    own.start()
    far = {"head": flipped(z, 2)}
    launch(routing_ref, routing_far_out, far_send.at[0], far_recv.at[0], far)
    early = pl.ds(0, length // 2)
    launch(cot_hbm.at[early], cot_far_out, far_send.at[1], far_recv.at[1], far)
    skew_kernel(line_ref, table_ref)
    w_out_load.wait()
    w_cat[:columns, :] = w_out_ref[...]

    moves = []
    for turn, r in enumerate(reversed(range(replicas))):
        start = flipped(z, r) * length
        slot = turn % 2
        if turn >= 2:
            for move in moves[turn - 2]:
                move.wait()

        input_loads[r].wait()

        def norm_step(i, carry, start=start, slot=slot):
            rows = pl.multiple_of(start + i * TILE, TILE)
            value = input_ref[pl.ds(rows, TILE), :].astype(F32)
            value = rms_norm(value, gain_ref[...])
            normed_ref[slot, pl.ds(pl.multiple_of(i * TILE, TILE), TILE), :] = value.astype(BF)
            return carry

        lax.fori_loop(0, length // TILE, norm_step, 0)
        for i in range(3):
            if turn == 0:
                weight_loads[i].wait()
            qkv_ref[slot, :, i * columns : (i + 1) * columns] = jnp.dot(
                normed_ref[slot], weight_ref[i], preferred_element_type=F32
            ).astype(BF)

        def pair_step(pair, carry, slot=slot, r=r):
            def part_of(j):
                at = pl.multiple_of(j * columns + pair * lanes, lanes)
                return qkv_ref[slot, :, pl.ds(at, lanes)]

            key = part_of(1)
            value_t = part_of(2).T
            scaled = part_of(0) * SCALE
            for part in range(2):
                query = jnp.where(lanes_of((length, lanes), half, part), scaled, 0).astype(BF)
                for c in range(length // chunk):
                    cols = slice(c * chunk, (c + 1) * chunk)
                    scores = contract(key, query[cols], 1, 1)
                    pieces = []
                    for kb in range(length // TILE):
                        at = length - TILE * kb + chunk * c
                        pieces.append(
                            scores[kb * TILE : (kb + 1) * TILE]
                            + table_ref[pair * 2 + part, :, at : at + chunk]
                        )
                    scores = jnp.concatenate(pieces, axis=0)
                    top = jnp.max(scores, axis=0, keepdims=True)
                    shifted = jnp.exp(scores - top)
                    total = jnp.sum(shifted, axis=0, keepdims=True)
                    probs = (shifted * (1.0 / total)).astype(BF)
                    hold_ref[slot, pair * 2 + part, :, cols] = probs
                    acc_ref[part * half : (part + 1) * half, cols] = jnp.dot(
                        value_t[part * half : (part + 1) * half],
                        probs,
                        preferred_element_type=F32,
                    )
            at = pl.multiple_of(pair * lanes, lanes)
            block_ref[r, :, pl.ds(at, lanes)] = acc_ref[...].T.astype(BF)
            return carry

        lax.fori_loop(0, pairs, pair_step, 0)
        moves.append(
            [
                pltpu.make_async_copy(ref.at[slot], out.at[r], hold_sem.at[i, slot])
                for i, (ref, out) in enumerate(
                    ((hold_ref, probs_out), (normed_ref, normed_out), (qkv_ref, qkv_out))
                )
            ]
        )
        for move in moves[-1]:
            move.start()
        if r:
            launch(
                block_ref.at[r],
                attended_ref.at[:, pl.ds(r * columns, columns)],
                hop_send.at[r],
                hop_recv.at[r],
                {"head": flipped(z, r)},
            )
        else:
            attended_ref[:, :columns] = block_ref[0]
        if turn == 0:
            for s in hops:
                w_hops[s].wait()
                at = pl.multiple_of(s * columns + d * part_rows, part_rows)
                w_cat[pl.ds(at, part_rows), :] = w_land[s]
                for o in PEERS:
                    launch(
                        w_land.at[s],
                        w_cat.at[pl.ds(at, part_rows), :],
                        plane_send.at[s, o],
                        plane_recv.at[s, o],
                        {"dp": plane(d, o)},
                    )
    for copy in copies:
        copy.wait()
    outs = [
        pltpu.make_async_copy(attended_ref, attended_out, own_sem.at[1]),
        pltpu.make_async_copy(w_cat, w_cat_out, own_sem.at[2]),
    ]
    for copy in outs:
        copy.start()

    def branch_step(i, carry):
        cols = pl.ds(pl.multiple_of(i * chunk, chunk), chunk)
        mixed_ref[:, cols] = jnp.dot(
            attended_ref[...], w_cat[:, cols], preferred_element_type=F32
        )
        return carry

    lax.fori_loop(0, width // chunk, branch_step, 0)

    def mixed_step(i, carry):
        at = pl.multiple_of(i * TILE, TILE)
        span = pl.ds(at, TILE)
        rows = pl.multiple_of(z * length + at, TILE)
        value = mixed_ref[span, :] + input_ref[pl.ds(rows, TILE), :].astype(F32)
        mixed_ref[span, :] = value
        normed2_ref[span, :] = rms_norm(value, gain2_ref[...]).astype(BF)
        return carry

    lax.fori_loop(0, length // TILE, mixed_step, 0)
    for move in moves[-2] + moves[-1] + outs + [own]:
        move.wait()


def attend_all(inputs, gain, weights, line, cot, routing, w_out, gain2, groups, capacity):
    heads, _, table_width = line.shape
    width = inputs.shape[1]
    length = cot.shape[0]
    replicas = inputs.shape[0] // length
    columns = weights[0].shape[1]
    lanes = 2 * columns // heads
    part_rows = columns // groups
    vmem = pl.BlockSpec(memory_space=pltpu.VMEM)
    hbm = pl.BlockSpec(memory_space=pl.ANY)
    came_shape = (groups, capacity, width + TILE)
    plane_sem = pltpu.SemaphoreType.DMA((groups,))
    hop_sem = pltpu.SemaphoreType.DMA((replicas,))
    both_sem = pltpu.SemaphoreType.DMA((replicas, groups))
    two_sem = pltpu.SemaphoreType.DMA((2,))
    return pl.pallas_call(
        attend_all_kernel,
        out_shape=(
            jax.ShapeDtypeStruct((length, replicas * columns), BF),
            jax.ShapeDtypeStruct((replicas, heads, length, length), BF),
            jax.ShapeDtypeStruct(came_shape, BF),
            jax.ShapeDtypeStruct((replicas, length, width), BF),
            jax.ShapeDtypeStruct((replicas, length, 3 * columns), BF),
            jax.ShapeDtypeStruct((replicas * columns, width), BF),
            jax.ShapeDtypeStruct((length // 2, width), BF),
            jax.ShapeDtypeStruct(routing.shape, routing.dtype),
            jax.ShapeDtypeStruct((length, width), F32),
            jax.ShapeDtypeStruct((length, width), BF),
        ),
        in_specs=[hbm, vmem, hbm, hbm, hbm, vmem, hbm, vmem, hbm, vmem],
        out_specs=[hbm] * 8 + [vmem] * 2,
        scratch_shapes=[
            pltpu.VMEM(inputs.shape, BF),
            pltpu.VMEM((3,) + weights[0].shape, BF),
            pltpu.VMEM(cot.shape, BF),
            pltpu.VMEM(w_out.shape, BF),
            pltpu.VMEM((heads, TILE, table_width), F32),
            pltpu.VMEM(came_shape, BF),
            pltpu.VMEM((lanes, length), F32),
            pltpu.VMEM((replicas, length, columns), BF),
            pltpu.VMEM((2, heads, length, length), BF),
            pltpu.VMEM((2, length, width), BF),
            pltpu.VMEM((2, length, 3 * columns), BF),
            pltpu.VMEM((length, replicas * columns), BF),
            pltpu.VMEM((replicas * columns, width), BF),
            pltpu.VMEM((replicas, part_rows, width), BF),
            plane_sem,
            plane_sem,
            hop_sem,
            hop_sem,
            hop_sem,
            hop_sem,
            both_sem,
            both_sem,
            two_sem,
            two_sem,
            pltpu.SemaphoreType.DMA((3, 2)),
            pltpu.SemaphoreType.DMA((3,)),
            pltpu.SemaphoreType.DMA((9,)),
        ],
        compiler_params=pltpu.CompilerParams(
            vmem_limit_bytes=VMEM_LIMIT, collective_id=1, has_side_effects=True
        ),
        cost_estimate=pl.CostEstimate(
            flops=replicas * heads * 8 * length * length * lanes,
            bytes_accessed=replicas * heads * length * length * 4,
            transcendentals=replicas * heads * length * length,
        ),
        name="attend_all",
    )(inputs, gain, *weights, line, cot, routing, w_out, gain2)


def selector(routing, start, count):
    slot = lax.broadcasted_iota(jnp.int32, (count, routing.shape[1]), 0) + start
    return [jnp.where(slot == routing[k : k + 1], 1.0, 0.0) for k in range(2)]


def slot_signs(routing, first, second):
    lane = lax.broadcasted_iota(jnp.int32, (TILE, routing.shape[1]), 0)
    signs = jnp.where(lane == routing[3:4], 1.0, 0.0) - jnp.where(lane == routing[2:3], 1.0, 0.0)
    return contract((first - second).astype(BF), signs.astype(BF), 1, 1).astype(BF)


def token_selector(routing, slots):
    slot = lax.broadcasted_iota(jnp.int32, (routing.shape[0], slots), 1)
    return [jnp.where(slot == routing[:, k : k + 1], 1.0, 0.0) for k in range(2)]


def expert_tile(rows, scaled, gate_w, up_w, down_w):
    gate = jnp.dot(rows, gate_w, preferred_element_type=F32)
    up_part = jnp.dot(rows, up_w, preferred_element_type=F32)
    grad_hidden = contract(scaled, down_w, 1, 1)
    square = gate * gate
    bend = jnp.tanh(gate * (GELU_A + GELU_A * GELU_B * square))
    half = 0.5 + 0.5 * bend
    active = gate * half
    slope = half + 0.5 * gate * (1.0 - bend * bend) * (GELU_A + 3.0 * GELU_A * GELU_B * square)
    hidden = (active * up_part).astype(BF)
    grad_gate = (grad_hidden * up_part * slope).astype(BF)
    grad_up = (grad_hidden * active).astype(BF)
    return hidden, grad_gate, grad_up


def scaled_rows(rows, extended, router, width):
    logits = jnp.dot(rows, router, preferred_element_type=F32)
    sign = extended[:, width:].astype(F32)
    gap = jnp.sum(logits * sign, axis=1, keepdims=True)
    return (extended[:, :width].astype(F32) * (1.0 / (1.0 + jnp.exp(gap)))).astype(BF)


def expert_kernel(
    width,
    tile,
    normed_ref,
    routing_ref,
    cot_ref,
    router_ref,
    gate_hbm,
    up_hbm,
    down_hbm,
    cot_hbm,
    rows_out,
    hidden_out,
    grad_gate_out,
    grad_up_out,
    scaled_out,
    back_out,
    grad_back_out,
    slope_out,
    far_out,
    cot_far_out,
    gate_w,
    up_w,
    down_w,
    rows,
    sends,
    back,
    grad_back,
    slopes,
    hidden,
    grad_gate,
    grad_up,
    scaled,
    weight_sem,
    row_send,
    row_recv,
    slope_send,
    slope_recv,
    grad_send,
    grad_recv,
    unit_sem,
    keep_sem,
    far_sem,
):
    z, d = lax.axis_index("head"), lax.axis_index("dp")
    far = {"head": flipped(z, 2)}
    groups, capacity, _ = rows.shape
    units = gate_w.shape[1]
    tiles = units // tile
    count = 2 * capacity

    def weights_of(t):
        at = pl.multiple_of(t * tile, tile)
        return [
            pltpu.make_async_copy(
                gate_hbm.at[:, pl.ds(at, tile)], gate_w.at[:, pl.ds(at, tile)], weight_sem.at[0, t]
            ),
            pltpu.make_async_copy(
                up_hbm.at[:, pl.ds(at, tile)], up_w.at[:, pl.ds(at, tile)], weight_sem.at[1, t]
            ),
            pltpu.make_async_copy(
                down_hbm.at[pl.ds(at, tile), :], down_w.at[pl.ds(at, tile), :], weight_sem.at[2, t]
            ),
        ]

    def start_weights(t, carry):
        for copy in weights_of(t):
            copy.start()
        return carry

    lax.fori_loop(0, tiles, start_weights, 0)
    greet([{"dp": plane(d, o)} for o in ROW_PEERS] + [far])
    pending = []
    arrivals = {}

    def picked(o):
        first, second = selector(routing_ref, o * capacity, capacity)
        return jnp.dot(
            (first + second).astype(BF), normed_ref[...], preferred_element_type=F32
        ).astype(BF)

    for o in ROW_PEERS:
        sends[o] = picked(o)
        arrivals[o] = remote(
            sends.at[o], rows.at[o], row_send.at[o], row_recv.at[o], {"dp": plane(d, o)}
        )
        arrivals[o].start()
    over = [
        remote(normed_ref, far_out, far_sem.at[0, 0], far_sem.at[0, 1], far),
        remote(
            cot_hbm.at[pl.ds(cot_far_out.shape[0], cot_far_out.shape[0])],
            cot_far_out,
            far_sem.at[1, 0],
            far_sem.at[1, 1],
            far,
        ),
    ]
    for copy in over:
        copy.start()
    rows[0] = picked(0)

    unit_copies = {}
    order = list(range(groups // 2))
    for turn, j in enumerate(order):
        pair = (2 * j, 2 * j + 1)
        slot = turn % 2
        for o in pair:
            if o:
                arrivals[o].wait_recv()
        if turn >= 2:
            for copy in unit_copies[order[turn - 2]]:
                copy.wait()
        here = rows[2 * j : 2 * j + 2].reshape(count, width)
        extended = cot_ref[2 * j : 2 * j + 2].reshape(count, cot_ref.shape[2])
        scaled[2 * j : 2 * j + 2] = scaled_rows(here, extended, router_ref[...], width).reshape(
            2, capacity, width
        )

        def tile_step(t, carry, j=j, slot=slot):
            at = pl.multiple_of(t * tile, tile)
            if j == 0:
                for copy in weights_of(t):
                    copy.wait()
            values = expert_tile(
                rows[2 * j : 2 * j + 2].reshape(count, width),
                scaled[2 * j : 2 * j + 2].reshape(count, width),
                gate_w[:, pl.ds(at, tile)],
                up_w[:, pl.ds(at, tile)],
                down_w[pl.ds(at, tile), :],
            )
            for ref, value in zip((hidden, grad_gate, grad_up), values):
                ref[slot, :, pl.ds(at, tile)] = value
            return carry

        lax.fori_loop(0, tiles, tile_step, 0)
        span = pl.ds(j * count, count)
        unit_copies[j] = [
            pltpu.make_async_copy(ref.at[slot], out.at[span], unit_sem.at[slot, i])
            for i, (ref, out) in enumerate(
                ((hidden, hidden_out), (grad_gate, grad_gate_out), (grad_up, grad_up_out))
            )
        ]
        for copy in unit_copies[j]:
            copy.start()

        def back_step(t, carry, j=j, slot=slot):
            at = pl.multiple_of(t * tile, tile)
            value = jnp.dot(hidden[slot], down_w[:, pl.ds(at, tile)], preferred_element_type=F32)
            back[2 * j : 2 * j + 2, :, pl.ds(at, tile)] = value.astype(BF).reshape(
                2, capacity, tile
            )
            return carry

        def grad_step(t, carry, j=j, slot=slot):
            at = pl.multiple_of(t * tile, tile)
            value = contract(grad_gate[slot], gate_w[pl.ds(at, tile), :], 1, 1) + contract(
                grad_up[slot], up_w[pl.ds(at, tile), :], 1, 1
            )
            grad_back[2 * j : 2 * j + 2, :, pl.ds(at, tile)] = value.astype(BF).reshape(
                2, capacity, tile
            )
            return carry

        def give(buffer, out, send_sem, recv_sem, pair=pair):
            for o in pair:
                if o:
                    copy = remote(
                        buffer.at[o],
                        out.at[o],
                        send_sem.at[o],
                        recv_sem.at[o],
                        {"dp": plane(d, o)},
                    )
                else:
                    copy = pltpu.make_async_copy(buffer.at[0], out.at[0], send_sem.at[0])
                copy.start()
                pending.append(copy)

        lax.fori_loop(0, width // tile, grad_step, 0)
        give(grad_back, grad_back_out, grad_send, grad_recv)
        lax.fori_loop(0, width // tile, back_step, 0)
        product = jnp.sum(
            cot_ref[2 * j : 2 * j + 2, :, :width].reshape(count, width).astype(F32)
            * back[2 * j : 2 * j + 2].reshape(count, width).astype(F32),
            axis=1,
            keepdims=True,
        )
        lane = lax.broadcasted_iota(jnp.int32, (count, TILE), 1)
        spread = jnp.zeros((count, TILE), F32)
        for k, term in enumerate(split_parts(product)):
            spread = jnp.where(lane == k, term.astype(F32), spread)
        slopes[2 * j : 2 * j + 2] = spread.astype(BF).reshape(2, capacity, TILE)
        give(slopes, slope_out, slope_send, slope_recv)

    keeps = [
        pltpu.make_async_copy(rows, rows_out, keep_sem.at[0]),
        pltpu.make_async_copy(scaled, scaled_out, keep_sem.at[1]),
        pltpu.make_async_copy(back, back_out, keep_sem.at[2]),
    ]
    for copy in keeps:
        copy.start()
    for j in order[-2:]:
        for copy in unit_copies[j]:
            copy.wait()
    for o in ROW_PEERS:
        arrivals[o].wait_send()
    for copy in pending + keeps + over:
        copy.wait()


def expert_stage(
    normed2, routing, cot, router, gate_w, up_w, down_w, cot_own, groups, capacity, tile
):
    width, units = gate_w.shape
    slots = groups * capacity
    vmem = pl.BlockSpec(memory_space=pltpu.VMEM)
    hbm = pl.BlockSpec(memory_space=pl.ANY)
    row_shape = jax.ShapeDtypeStruct((groups, capacity, width), BF)
    unit_shape = jax.ShapeDtypeStruct((slots, units), BF)
    row_buffer = pltpu.VMEM((groups, capacity, width), BF)
    unit_buffer = pltpu.VMEM((2, 2 * capacity, units), BF)
    row_sem = pltpu.SemaphoreType.DMA((groups,))
    return pl.pallas_call(
        functools.partial(expert_kernel, width, tile),
        out_shape=(row_shape,)
        + (unit_shape,) * 3
        + (row_shape,) * 3
        + (
            jax.ShapeDtypeStruct((groups, capacity, TILE), BF),
            jax.ShapeDtypeStruct(normed2.shape, BF),
            jax.ShapeDtypeStruct((normed2.shape[0] // 2, width), BF),
        ),
        in_specs=[vmem] * 4 + [hbm] * 4,
        out_specs=[hbm] * 10,
        scratch_shapes=[
            pltpu.VMEM((width, units), BF),
            pltpu.VMEM((width, units), BF),
            pltpu.VMEM((units, width), BF),
            row_buffer,
            row_buffer,
            row_buffer,
            row_buffer,
            pltpu.VMEM((groups, capacity, TILE), BF),
            unit_buffer,
            unit_buffer,
            unit_buffer,
            row_buffer,
            pltpu.SemaphoreType.DMA((3, units // tile)),
            row_sem,
            row_sem,
            row_sem,
            row_sem,
            row_sem,
            row_sem,
            pltpu.SemaphoreType.DMA((2, 3)),
            pltpu.SemaphoreType.DMA((3,)),
            pltpu.SemaphoreType.DMA((2, 2)),
        ],
        compiler_params=pltpu.CompilerParams(
            vmem_limit_bytes=VMEM_MOST, collective_id=2, has_side_effects=True
        ),
        cost_estimate=pl.CostEstimate(
            flops=12 * slots * width * units,
            bytes_accessed=6 * width * units + 6 * slots * units,
            transcendentals=slots * units,
        ),
        name="expert_stage",
    )(normed2, routing, cot, router, gate_w, up_w, down_w, cot_own)


def split_parts(value):
    first = value.astype(BF)
    rest = value - first.astype(F32)
    second = rest.astype(BF)
    return first, second, (rest - second.astype(F32)).astype(BF)


def combine_kernel(
    grad_back_ref,
    slot_slope_ref,
    routing_ref,
    mixed_ref,
    normed2_ref,
    cot_ref,
    router_ref,
    gain_ref,
    w_cat_ref,
    gates_ref,
    grad_mixed_ref,
    grad_branch_ref,
    grad_heads_ref,
    grad_router_ref,
    grad_norm2_ref,
    picked,
    slopes,
    gaps,
    pick,
):
    length, width = mixed_ref.shape
    chunk = 2 * TILE

    slots = grad_back_ref.shape[0]
    first, second = token_selector(routing_ref, slots)
    gaps[...] = jnp.dot(
        (second - first).astype(BF), slot_slope_ref[...], preferred_element_type=F32
    )
    pick[...] = (first + second).astype(BF)

    def pick_step(i, carry):
        cols = pl.ds(pl.multiple_of(i * chunk, chunk), chunk)
        picked[:, cols] = jnp.dot(pick[...], grad_back_ref[:, cols], preferred_element_type=F32)
        return carry

    lax.fori_loop(0, width // chunk, pick_step, 0)
    lane = lax.broadcasted_iota(jnp.int32, (TILE, TILE), 1)

    def row_step(i, total):
        span = pl.ds(pl.multiple_of(i * TILE, TILE), TILE)
        ids = routing_ref[span, :]
        sign = jnp.where(lane == ids[:, 3:4], 1.0, 0.0) - jnp.where(lane == ids[:, 2:3], 1.0, 0.0)
        logits = jnp.dot(normed2_ref[span, :], router_ref[...], preferred_element_type=F32)
        gap = jnp.sum(logits * sign, axis=1, keepdims=True)
        gate0, gate1 = 1.0 / (1.0 + jnp.exp(gap)), 1.0 / (1.0 + jnp.exp(-gap))
        cot = cot_ref[span, :].astype(F32)
        mixed = mixed_ref[span, :]
        gates_ref[span, :] = jnp.where(lane == 0, gate0, gate1)
        grad_gap = jnp.sum(gaps[span, :], axis=1, keepdims=True)
        slope = gate0 * gate1 * grad_gap * sign
        slopes[span, :] = slope
        grad_normed2 = picked[span, :] + sum(
            contract(part, router_ref[...], 1, 1) for part in split_parts(slope)
        )
        scale = lax.rsqrt(jnp.mean(mixed * mixed, axis=1, keepdims=True) + EPS)
        inner = grad_normed2 * gain_ref[...]
        mean = jnp.mean(inner * mixed, axis=1, keepdims=True)
        grad_mixed = cot + scale * inner - mixed * (scale * scale * scale * mean)
        grad_mixed_ref[span, :] = grad_mixed
        grad_branch_ref[span, :] = grad_mixed.astype(BF)
        return total + jnp.sum(grad_normed2 * mixed * scale, axis=0, keepdims=True)

    grad_norm2_ref[...] = lax.fori_loop(
        0, length // TILE, row_step, jnp.zeros((1, width), F32)
    )

    def head_step(i, carry):
        cols = pl.ds(pl.multiple_of(i * chunk, chunk), chunk)
        grad_heads_ref[:, cols] = contract(grad_branch_ref[...], w_cat_ref[cols, :], 1, 1).astype(BF)
        return carry

    lax.fori_loop(0, w_cat_ref.shape[0] // chunk, head_step, 0)
    experts = grad_router_ref.shape[0]
    grad_router_ref[...] = sum(
        contract(part, normed2_ref[...], 0, 0) for part in split_parts(slopes[...])
    )[:experts]


def combine(grad_back, slot_slope, routing, mixed, normed2, cot, router, gain, w_cat, experts):
    length, width = mixed.shape
    vmem = pl.BlockSpec(memory_space=pltpu.VMEM)
    return pl.pallas_call(
        combine_kernel,
        out_shape=(
            jax.ShapeDtypeStruct((length, TILE), F32),
            jax.ShapeDtypeStruct((length, width), F32),
            jax.ShapeDtypeStruct((length, width), BF),
            jax.ShapeDtypeStruct((length, w_cat.shape[0]), BF),
            jax.ShapeDtypeStruct((experts, width), F32),
            jax.ShapeDtypeStruct((1, width), F32),
        ),
        in_specs=[vmem] * 9,
        out_specs=[vmem] * 6,
        scratch_shapes=[
            pltpu.VMEM((length, width), F32),
            pltpu.VMEM((length, TILE), F32),
            pltpu.VMEM((length, TILE), F32),
            pltpu.VMEM((length, grad_back.shape[0]), BF),
        ],
        compiler_params=pltpu.CompilerParams(vmem_limit_bytes=VMEM_LIMIT),
        cost_estimate=pl.CostEstimate(
            flops=3 * length * grad_back.shape[0] * width,
            bytes_accessed=4 * grad_back.shape[0] * width,
            transcendentals=0,
        ),
        name="combine",
    )(grad_back, slot_slope, routing, mixed, normed2, cot, router, gain, w_cat)


def attend_back_kernel(
    normed2_far,
    cot_far,
    cot_rest,
    routing_ref,
    router_ref,
    grad_ref,
    qkv_hbm,
    probs_hbm,
    normed_hbm,
    query_w,
    key_w,
    value_w,
    attended_ref,
    grad_branch_ref,
    far_rows_ref,
    far_scaled_ref,
    carry_ref,
    part_sum_ref,
    qkv_w_ref,
    out_w_ref,
    lines_ref,
    sums_ref,
    acc_ref,
    sends,
    far_land,
    grads,
    qkv_ref,
    probs_ref,
    normed_ref,
    grad_qkv_ref,
    weight_sum,
    parts,
    landed,
    far_send,
    far_recv,
    hop_send,
    hop_recv,
    part_send,
    part_recv,
    load_sem,
    own_sem,
):
    z, d = lax.axis_index("head"), lax.axis_index("dp")
    replicas, length, columns = grads.shape
    groups, capacity, extent = sends.shape
    width = normed2_far.shape[1]
    heads = sums_ref.shape[0]
    pairs = heads // 2
    lanes = columns // pairs
    half = lanes // 2
    chunk = 2 * TILE
    hops = [3, 2, 1]
    order = [3, 0, 1, 2]

    def loads(turn):
        r, slot = order[turn], turn % 2
        return [
            pltpu.make_async_copy(source.at[r], target.at[slot], load_sem.at[i, slot])
            for i, (source, target) in enumerate(
                ((qkv_hbm, qkv_ref), (probs_hbm, probs_ref), (normed_hbm, normed_ref))
            )
        ]

    for copy in loads(0):
        copy.start()
    greet([{"dp": plane(d, o)} for o in PEERS] + [{"head": flipped(z, r)} for r in hops])
    copies = []
    arrivals = {}
    for r in hops:
        arrivals[r] = remote(
            grad_ref.at[:, pl.ds(r * columns, columns)],
            grads.at[r],
            hop_send.at[r],
            hop_recv.at[r],
            {"head": flipped(z, r)},
        )
        arrivals[r].start()
    for o in PEERS + [0]:
        first, second = selector(routing_ref, o * capacity, capacity)
        both = (first + second).astype(BF)
        early = cot_far.shape[0]
        sends[o, :, :width] = jnp.dot(
            both, normed2_far[...], preferred_element_type=F32
        ).astype(BF)
        sends[o, :, width : 2 * width] = (
            jnp.dot(both[:, :early], cot_far[...], preferred_element_type=F32)
            + jnp.dot(both[:, early:], cot_rest[...], preferred_element_type=F32)
        ).astype(BF)
        sends[o, :, 2 * width :] = slot_signs(routing_ref, first, second)
        if o:
            copy = remote(
                sends.at[o],
                far_land.at[o],
                far_send.at[o],
                far_recv.at[o],
                {"dp": plane(d, o)},
            )
        else:
            copy = pltpu.make_async_copy(sends.at[0], far_land.at[0], own_sem)
        copy.start()
        copies.append(copy)
    sums_ref[...] = jnp.zeros_like(sums_ref)
    grads[0] = grad_ref[:, :columns]

    near = {"head": flipped(z, 1)}

    def part_copy(i, source, target, peer):
        return remote(parts.at[source], landed.at[target], part_send.at[i], part_recv.at[i], peer)

    inner = part_copy(0, 3, 0, near)
    direct = part_copy(1, 1, 1, near)

    for turn, r in enumerate(order):
        slot = turn % 2
        if turn + 1 < replicas:
            for copy in loads(turn + 1):
                copy.start()
        for copy in loads(turn):
            copy.wait()
        if r:
            arrivals[r].wait_recv()

        def pair_step(pair, carry, slot=slot, r=r):
            def part_of(j):
                at = pl.multiple_of(j * columns + pair * lanes, lanes)
                return qkv_ref[slot, :, pl.ds(at, lanes)]

            at = pl.multiple_of(pair * lanes, lanes)
            query, value = part_of(0), part_of(2)
            key_t = part_of(1).T
            grad_all = grads[r, :, pl.ds(at, lanes)]
            grad_keys, grad_values = [], []
            for part in range(2):
                mask = lanes_of((length, lanes), half, part)
                grad = jnp.where(mask, grad_all, 0).astype(BF)
                grad_key = jnp.zeros((length, lanes), F32)
                grad_value = jnp.zeros((length, lanes), F32)
                for c in range(length // chunk):
                    cols = slice(c * chunk, (c + 1) * chunk)
                    grad_probs = contract(value, grad[cols], 1, 1)
                    probs_low = probs_ref[slot, pair * 2 + part, :, cols]
                    probs = probs_low.astype(F32)
                    delta = jnp.sum(probs * grad_probs, axis=0, keepdims=True)
                    grad_scores = (probs * (grad_probs - delta)).astype(BF)
                    grad_value += jnp.dot(probs_low, grad_all[cols], preferred_element_type=F32)
                    grad_key += jnp.dot(grad_scores, query[cols], preferred_element_type=F32)
                    acc_ref[part * half : (part + 1) * half, cols] = jnp.dot(
                        key_t[part * half : (part + 1) * half],
                        grad_scores,
                        preferred_element_type=F32,
                    )
                    for kb in range(length // TILE):
                        to = length - TILE * kb + chunk * c
                        sums_ref[pair * 2 + part, :, to : to + chunk] += grad_scores[
                            kb * TILE : (kb + 1) * TILE
                        ].astype(F32)
                grad_keys.append(grad_key)
                grad_values.append(grad_value)
            first = lanes_of((length, lanes), half, 0)
            results = (
                acc_ref[...].T * SCALE,
                jnp.where(first, *grad_keys) * SCALE,
                jnp.where(first, *grad_values),
            )
            for j, result in enumerate(results):
                to = pl.multiple_of(j * columns + pair * lanes, lanes)
                grad_qkv_ref[slot, :, pl.ds(to, lanes)] = result.astype(BF)
            return carry

        lax.fori_loop(0, pairs, pair_step, 0)

        def part_step(i, carry, slot=slot, r=r):
            span = pl.ds(pl.multiple_of(i * chunk, chunk), chunk)
            total = sum(
                contract(
                    grad_qkv_ref[slot, :, j * columns : (j + 1) * columns], weight[span, :], 1, 1
                )
                for j, weight in enumerate((query_w, key_w, value_w))
            )
            parts[r, :, span] = total.astype(BF)
            return carry

        lax.fori_loop(0, width // chunk, part_step, 0)
        if r == 3:
            inner.start()
        if r == 1:
            direct.start()

        def weight_step(i, carry, slot=slot, turn=turn):
            cols = pl.ds(pl.multiple_of(i * chunk, chunk), chunk)
            value = contract(normed_ref[slot, :, cols], grad_qkv_ref[slot], 0, 0)
            if turn:
                value = value + weight_sum[cols, :]
            if turn + 1 < replicas:
                weight_sum[cols, :] = value
            else:
                qkv_w_ref[cols, :] = value.astype(BF)
            return carry

        lax.fori_loop(0, width // chunk, weight_step, 0)

    def wout_step(i, carry):
        rows = pl.ds(pl.multiple_of(i * chunk, chunk), chunk)
        out_w_ref[rows, :] = contract(attended_ref[:, rows], grad_branch_ref[...], 0, 0).astype(BF)
        return carry

    lax.fori_loop(0, out_w_ref.shape[0] // chunk, wout_step, 0)
    unskew_kernel(sums_ref, lines_ref)

    for r in hops:
        arrivals[r].wait_send()
    for copy in copies:
        copy.wait()
    count = 2 * capacity
    for j in range(groups // 2):
        pair, span = slice(2 * j, 2 * j + 2), slice(j * count, (j + 1) * count)
        rows = far_land[pair, :, :width].reshape(count, width)
        far_rows_ref[span] = rows
        far_scaled_ref[span] = scaled_rows(
            rows, far_land[pair, :, width:].reshape(count, width + TILE), router_ref[...], width
        )
    inner.wait()
    carry_ref[...] = (parts[2].astype(F32) + landed[0].astype(F32)).astype(BF)
    direct.wait()
    part_sum_ref[...] = parts[0].astype(F32) + landed[1].astype(F32)


def attend_back(
    normed2_far,
    cot_far,
    cot_rest,
    routing_far,
    router,
    grad_heads,
    qkv,
    probs,
    normed,
    weights,
    attended,
    grad_branch,
    groups,
    capacity,
):
    replicas, length, triple = qkv.shape
    heads = probs.shape[1]
    columns = triple // 3
    width = normed.shape[2]
    lanes = 2 * columns // heads
    slots = groups * capacity
    extent = 2 * width + TILE
    vmem = pl.BlockSpec(memory_space=pltpu.VMEM)
    hbm = pl.BlockSpec(memory_space=pl.ANY)
    hop_sem = pltpu.SemaphoreType.DMA((replicas,))
    plane_sem = pltpu.SemaphoreType.DMA((groups,))
    part_sem = pltpu.SemaphoreType.DMA((2,))
    return pl.pallas_call(
        attend_back_kernel,
        out_shape=(
            jax.ShapeDtypeStruct((slots, width), BF),
            jax.ShapeDtypeStruct((slots, width), BF),
            jax.ShapeDtypeStruct((length, width), BF),
            jax.ShapeDtypeStruct((length, width), F32),
            jax.ShapeDtypeStruct((width, triple), BF),
            jax.ShapeDtypeStruct((replicas * columns, width), BF),
            jax.ShapeDtypeStruct((heads, 1, 2 * length), F32),
        ),
        in_specs=[vmem] * 6 + [hbm] * 3 + [vmem] * 5,
        out_specs=[vmem] * 7,
        scratch_shapes=[
            pltpu.VMEM((heads, TILE, 2 * length), F32),
            pltpu.VMEM((lanes, length), F32),
            pltpu.VMEM((groups, capacity, extent), BF),
            pltpu.VMEM((groups, capacity, extent), BF),
            pltpu.VMEM((replicas, length, columns), BF),
            pltpu.VMEM((2, length, triple), BF),
            pltpu.VMEM((2, heads, length, length), BF),
            pltpu.VMEM((2, length, width), BF),
            pltpu.VMEM((2, length, triple), BF),
            pltpu.VMEM((width, triple), F32),
            pltpu.VMEM((replicas, length, width), BF),
            pltpu.VMEM((2, length, width), BF),
            plane_sem,
            plane_sem,
            hop_sem,
            hop_sem,
            part_sem,
            part_sem,
            pltpu.SemaphoreType.DMA((3, 2)),
            pltpu.SemaphoreType.DMA,
        ],
        compiler_params=pltpu.CompilerParams(
            vmem_limit_bytes=VMEM_MOST, collective_id=3, has_side_effects=True
        ),
        cost_estimate=pl.CostEstimate(
            flops=replicas * heads * 16 * length * length * lanes,
            bytes_accessed=replicas * heads * length * length * 4,
            transcendentals=0,
        ),
        name="attend_back",
    )(
        normed2_far,
        cot_far,
        cot_rest,
        routing_far,
        router,
        grad_heads,
        qkv,
        probs,
        normed,
        *weights,
        attended,
        grad_branch,
    )


def last_kernel(
    tile,
    far_ref,
    scaled,
    scaled_here,
    gates_ref,
    routing_ref,
    gain_ref,
    gate_hbm,
    up_hbm,
    down_hbm,
    grad_gate_hbm,
    grad_up_hbm,
    hidden_hbm,
    qkv_w_hbm,
    out_w_hbm,
    rows_hbm,
    carry_hbm,
    part_sum_hbm,
    input_hbm,
    back_hbm,
    norm2_ref,
    router_grad_ref,
    lines_ref,
    wide_out,
    wide_came,
    tall_out,
    tall_came,
    qkv_w_out,
    out_w_out,
    small_out,
    grad_input_out,
    output_out,
    back_out,
    left,
    weights,
    downs,
    units,
    hidden,
    hidden_here,
    send_wide,
    keep_wide,
    send_tall,
    keep_tall,
    qkv_land,
    qkv_sum,
    out_land,
    out_sum,
    out_hop,
    out_last,
    small_own,
    small_land,
    small_sum,
    small_hop,
    work,
    own_input,
    carried,
    stream_sem,
    hidden_sem,
    wide_send,
    wide_recv,
    keep_sem,
    tall_send,
    tall_recv,
    tall_keep,
    first_send,
    first_recv,
    hop_send,
    hop_recv,
    third_send,
    third_recv,
    carry_sem,
    back_send,
    back_recv,
    own_sem,
):
    z, d = lax.axis_index("head"), lax.axis_index("dp")
    slots, width = scaled_here.shape
    groups = qkv_land.shape[0]
    capacity = slots // groups
    length = own_input.shape[0]
    chunk = 2 * TILE
    _, rows, total_units = send_wide.shape
    half_units = hidden_here.shape[1]
    tiles = total_units // tile
    low, high = lax.rem(z, 2), z // 2
    keep_at = pl.multiple_of(low * rows, rows)
    send_at = pl.multiple_of((1 - low) * rows, rows)
    near = {"head": flipped(z, 1)}
    count = 2 * capacity
    hops = [3, 2, 1]

    def streams(t):
        slot = lax.rem(t, 2)
        at = pl.multiple_of(t * tile, tile)
        cols = pl.ds(at, tile)
        return [
            pltpu.make_async_copy(gate_hbm.at[:, cols], weights.at[slot, 0], stream_sem.at[0, slot]),
            pltpu.make_async_copy(up_hbm.at[:, cols], weights.at[slot, 1], stream_sem.at[1, slot]),
            pltpu.make_async_copy(down_hbm.at[cols, :], downs.at[slot], stream_sem.at[2, slot]),
            pltpu.make_async_copy(
                grad_gate_hbm.at[:, cols], units.at[slot, 0], stream_sem.at[3, slot]
            ),
            pltpu.make_async_copy(
                grad_up_hbm.at[:, cols], units.at[slot, 1], stream_sem.at[4, slot]
            ),
        ]

    for copy in streams(0):
        copy.start()
    half_copy = pltpu.make_async_copy(
        hidden_hbm.at[:, pl.ds(pl.multiple_of(high * half_units, TILE), half_units)],
        hidden_here,
        hidden_sem,
    )
    half_copy.start()
    greet([{"dp": plane(d, o)} for o in PEERS] + [{"head": flipped(z, r)} for r in hops])

    carry = remote(
        carry_hbm, carried, carry_sem.at[0], carry_sem.at[1], {"head": flipped(z, 2)}
    )
    carry.start()
    wide = 2 * rows
    loads = [
        pltpu.make_async_copy(
            rows_hbm.at[:, pl.ds(pl.multiple_of(high * wide, wide), wide)], left, own_sem.at[2]
        ),
        pltpu.make_async_copy(part_sum_hbm, work.at[0], own_sem.at[3]),
        pltpu.make_async_copy(
            input_hbm.at[pl.ds(pl.multiple_of(z * length, length), length)], own_input, own_sem.at[5]
        ),
    ]
    for copy in loads:
        copy.start()

    first = []
    for o in PEERS:
        peer = plane(d, o)
        for i, (source, target) in enumerate(
            (
                (qkv_w_hbm.at[peer], qkv_land.at[o]),
                (out_w_hbm.at[:, peer], out_land.at[o]),
            )
        ):
            copy = remote(source, target, first_send.at[i, o], first_recv.at[i, o], {"dp": peer})
            copy.start()
            first.append(copy)
    own = [
        pltpu.make_async_copy(qkv_w_hbm.at[d], qkv_land.at[0], own_sem.at[0]),
        pltpu.make_async_copy(out_w_hbm.at[:, d], out_land.at[0], own_sem.at[1]),
    ]
    for copy in own:
        copy.start()

    backs = []
    for o in ROW_PEERS:
        copy = remote(
            back_hbm.at[o], back_out.at[o], back_send.at[o], back_recv.at[o], {"dp": plane(d, o)}
        )
        copy.start()
        backs.append(copy)
    backs.append(pltpu.make_async_copy(back_hbm.at[0], back_out.at[0], back_send.at[0]))
    backs[-1].start()
    loads[0].wait()
    columns = pl.ds(pl.multiple_of(high * wide, wide), wide)

    def wide_copy(i, t):
        at = pl.multiple_of(t * tile, tile)
        return remote(
            send_wide.at[i, :, pl.ds(at, tile)],
            wide_came.at[i, :, pl.ds(at, tile)],
            wide_send.at[i, t],
            wide_recv.at[i, t],
            near,
        )

    def keep_copy(i, t):
        at = pl.multiple_of(t * tile, tile)
        slot = lax.rem(t, 2)
        return pltpu.make_async_copy(
            keep_wide.at[i, slot], wide_out.at[i, :, pl.ds(at, tile)], keep_sem.at[i, slot]
        )

    def tile_step(t, carry):
        slot = lax.rem(t, 2)
        at = pl.multiple_of(t * tile, tile)

        @pl.when(t + 1 < tiles)
        def _():
            for copy in streams(t + 1):
                copy.start()

        for copy in streams(t):
            copy.wait()

        def chunk_step(j, inner):
            span = pl.ds(pl.multiple_of(j * count, count), count)
            values = expert_tile(
                far_ref[span], scaled[span], weights[slot, 0], weights[slot, 1], downs[slot]
            )
            hidden[span, pl.ds(at, tile)] = values[0]
            units[slot, 2, span, :] = values[1]
            units[slot, 3, span, :] = values[2]
            return inner

        lax.fori_loop(0, groups // 2, chunk_step, 0)
        @pl.when(t >= 2)
        def _():
            for i in range(2):
                keep_copy(i, t - 2).wait()

        for i in range(2):
            value = contract(left[...], units[slot, i], 0, 0) + contract(
                far_ref[:, columns], units[slot, 2 + i], 0, 0
            )
            upper = low == 1
            send_wide[i, :, pl.ds(at, tile)] = jnp.where(
                upper, value[:rows], value[rows:]
            ).astype(BF)
            keep_wide[i, slot] = jnp.where(upper, value[rows:], value[:rows])
            wide_copy(i, t).start()
            keep_copy(i, t).start()
        return carry

    lax.fori_loop(0, tiles, tile_step, 0)

    carry.wait()
    for copy in loads[1:]:
        copy.wait()

    def norm_step(i, total):
        span = pl.ds(pl.multiple_of(i * TILE, TILE), TILE)
        grad_normed = work[0, span, :] + carried[span, :].astype(F32)
        value = own_input[span, :].astype(F32)
        scale = lax.rsqrt(jnp.mean(value * value, axis=1, keepdims=True) + EPS)
        inner = grad_normed * gain_ref[...]
        mean = jnp.mean(inner * value, axis=1, keepdims=True)
        work[1, span, :] = scale * inner - value * (scale * scale * scale * mean)
        return total + jnp.sum(grad_normed * value * scale, axis=0, keepdims=True)

    heads = lines_ref.shape[0]
    small_own[...] = jnp.zeros_like(small_own)
    small_own[0:1] = lax.fori_loop(0, length // TILE, norm_step, jnp.zeros((1, width), F32))
    small_own[1:2] = norm2_ref[...]
    for h in range(heads):
        small_own[2 + h : 3 + h] = lines_ref[h]
    small_own[8:] = router_grad_ref[...]
    ends = [pltpu.make_async_copy(work.at[1], grad_input_out, own_sem.at[4])]
    for copy in ends:
        copy.start()
    small = []
    for o in PEERS:
        copy = remote(
            small_own, small_land.at[o], first_send.at[2, o], first_recv.at[2, o], {"dp": plane(d, o)}
        )
        copy.start()
        small.append(copy)
    small_land[0] = small_own[...]

    for copy in first:
        copy.wait()
    for copy in own:
        copy.wait()
    qkv_sum[...] = sum(qkv_land[o].astype(F32) for o in range(groups)).astype(BF)
    out_sum[...] = sum(out_land[o].astype(F32) for o in range(groups)).astype(BF)
    second = []
    for o in PEERS:
        copy = remote(
            qkv_sum, qkv_w_out.at[d], third_send.at[0, o], third_recv.at[0, o], {"dp": plane(d, o)}
        )
        copy.start()
        second.append(copy)
    mine = [pltpu.make_async_copy(qkv_sum, qkv_w_out.at[d], own_sem.at[0])]
    mine[0].start()
    over = []
    for r in hops:
        copy = remote(
            out_sum.at[r], out_hop.at[r], hop_send.at[0, r], hop_recv.at[0, r], {"head": flipped(z, r)}
        )
        copy.start()
        over.append(copy)

    half_copy.wait()
    share = half_units // 2
    halves = pl.ds(pl.multiple_of(high * half_units, TILE), half_units)

    def tall_copies(i):
        cols = pl.ds(pl.multiple_of(i * tile, tile), tile)
        return [
            remote(
                send_tall.at[:, cols], tall_came.at[:, cols], tall_send.at[i], tall_recv.at[i], near
            ),
            pltpu.make_async_copy(keep_tall.at[:, cols], tall_out.at[:, cols], tall_keep.at[i]),
        ]

    def tall_step(i, carry):
        cols = pl.ds(pl.multiple_of(i * tile, tile), tile)
        value = contract(hidden_here[...], scaled_here[:, cols], 0, 0) + contract(
            hidden[:, halves], scaled[:, cols], 0, 0
        )
        upper = low == 1
        send_tall[:, cols] = jnp.where(upper, value[:share], value[share:]).astype(BF)
        keep_tall[:, cols] = jnp.where(upper, value[share:], value[:share])
        for copy in tall_copies(i):
            copy.start()
        return carry

    lax.fori_loop(0, width // tile, tall_step, 0)
    for copy in small:
        copy.wait()
    small_sum[...] = sum(small_land[o] for o in range(groups))
    small_over = []
    for r in hops:
        copy = remote(
            small_sum, small_hop.at[r], hop_send.at[1, r], hop_recv.at[1, r], {"head": flipped(z, r)}
        )
        copy.start()
        small_over.append(copy)

    for copy in over:
        copy.wait()
    out_last[...] = (
        out_sum[0].astype(F32) + sum(out_hop[r].astype(F32) for r in hops)
    ).astype(BF)
    for o in PEERS:
        copy = remote(
            out_last,
            out_w_out.at[d],
            third_send.at[1, o],
            third_recv.at[1, o],
            {"dp": plane(d, o)},
        )
        copy.start()
        second.append(copy)
    mine.append(pltpu.make_async_copy(out_last, out_w_out.at[d], own_sem.at[1]))
    mine[1].start()

    for copy in backs:
        copy.wait()
    rows_back = [
        pltpu.make_async_copy(
            back_out.at[o], hidden.at[o * capacity : (o + 1) * capacity, :width], back_recv.at[o]
        )
        for o in range(groups)
    ]
    for copy in rows_back:
        copy.start()
    for k, pick in enumerate(token_selector(routing_ref, slots)):
        hidden_here[k * length : (k + 1) * length, :slots] = pick.astype(BF)
    for copy in rows_back:
        copy.wait()

    def output_step(i, carry):
        cols = pl.ds(pl.multiple_of(i * chunk, chunk), chunk)
        work[0, :, cols] = sum(
            gates_ref[:, k : k + 1]
            * jnp.dot(
                hidden_here[k * length : (k + 1) * length, :slots],
                hidden[:, cols],
                preferred_element_type=F32,
            )
            for k in range(2)
        )
        return carry

    lax.fori_loop(0, width // chunk, output_step, 0)
    ends.append(pltpu.make_async_copy(work.at[0], output_out, own_sem.at[3]))
    ends[1].start()

    for i in range(2):
        for t in (tiles - 2, tiles - 1):
            keep_copy(i, t).wait()

    def wide_end(t, carry):
        for i in range(2):
            wide_copy(i, t).wait()
        return carry

    lax.fori_loop(0, tiles, wide_end, 0)
    for copy in second + mine + ends + small_over:
        copy.wait()
    small_out[0] = small_sum[...]
    small_out[1] = small_sum[...] + sum(small_hop[r] for r in hops)

    def tall_end(i, carry):
        for copy in tall_copies(i):
            copy.wait()
        return carry

    lax.fori_loop(0, width // tile, tall_end, 0)


def last_stage(
    far, here, tokens, weights, grads_here, hidden_here, sums, finish, small, tile
):
    gate_w, up_w, down_w = weights
    width, units = gate_w.shape
    qkv_w, out_w = sums
    replicas, groups, part_rows, _ = out_w.shape
    slots = far[0].shape[0]
    length = tokens[0].shape[0]
    back = finish[-1]
    vmem = pl.BlockSpec(memory_space=pltpu.VMEM)
    hbm = pl.BlockSpec(memory_space=pl.ANY)
    rows, share = width // replicas, units // replicas
    small_shape = (8 + groups, width)
    plane_sem = pltpu.SemaphoreType.DMA((3, groups))
    hop_sem = pltpu.SemaphoreType.DMA((2, replicas))
    return pl.pallas_call(
        functools.partial(last_kernel, tile),
        out_shape=(
            jax.ShapeDtypeStruct((2, rows, units), F32),
            jax.ShapeDtypeStruct((2, rows, units), BF),
            jax.ShapeDtypeStruct((share, width), F32),
            jax.ShapeDtypeStruct((share, width), BF),
            jax.ShapeDtypeStruct(qkv_w.shape, BF),
            jax.ShapeDtypeStruct(out_w.shape[1:], BF),
            jax.ShapeDtypeStruct((2,) + small_shape, F32),
            jax.ShapeDtypeStruct((length, width), F32),
            jax.ShapeDtypeStruct((length, width), F32),
            jax.ShapeDtypeStruct(back.shape, BF),
        ),
        in_specs=[vmem] * 6 + [hbm] * 13 + [vmem] * 3,
        out_specs=[hbm] * 6 + [vmem] + [hbm] * 3,
        scratch_shapes=[
            pltpu.VMEM((slots, 2 * rows), BF),
            pltpu.VMEM((2, 2, width, tile), BF),
            pltpu.VMEM((2, tile, width), BF),
            pltpu.VMEM((2, 4, slots, tile), BF),
            pltpu.VMEM((slots, units), BF),
            pltpu.VMEM((slots, units // 2), BF),
            pltpu.VMEM((2, rows, units), BF),
            pltpu.VMEM((2, 2, rows, tile), F32),
            pltpu.VMEM((share, width), BF),
            pltpu.VMEM((share, width), F32),
            pltpu.VMEM(qkv_w.shape, BF),
            pltpu.VMEM(qkv_w.shape[1:], BF),
            pltpu.VMEM((groups, replicas, part_rows, width), BF),
            pltpu.VMEM((replicas, part_rows, width), BF),
            pltpu.VMEM((replicas, part_rows, width), BF),
            pltpu.VMEM((part_rows, width), BF),
            pltpu.VMEM(small_shape, F32),
            pltpu.VMEM((groups,) + small_shape, F32),
            pltpu.VMEM(small_shape, F32),
            pltpu.VMEM((replicas,) + small_shape, F32),
            pltpu.VMEM((2, length, width), F32),
            pltpu.VMEM((length, width), BF),
            pltpu.VMEM((length, width), BF),
            pltpu.SemaphoreType.DMA((5, 2)),
            pltpu.SemaphoreType.DMA,
            pltpu.SemaphoreType.DMA((2, units // tile)),
            pltpu.SemaphoreType.DMA((2, units // tile)),
            pltpu.SemaphoreType.DMA((2, 2)),
            pltpu.SemaphoreType.DMA((width // tile,)),
            pltpu.SemaphoreType.DMA((width // tile,)),
            pltpu.SemaphoreType.DMA((width // tile,)),
            plane_sem,
            plane_sem,
            hop_sem,
            hop_sem,
            plane_sem,
            plane_sem,
            pltpu.SemaphoreType.DMA((2,)),
            pltpu.SemaphoreType.DMA((groups,)),
            pltpu.SemaphoreType.DMA((groups,)),
            pltpu.SemaphoreType.DMA((6,)),
        ],
        compiler_params=pltpu.CompilerParams(
            vmem_limit_bytes=VMEM_MOST, collective_id=4, has_side_effects=True
        ),
        cost_estimate=pl.CostEstimate(
            flops=12 * slots * width * units,
            bytes_accessed=6 * width * units + 6 * slots * units,
            transcendentals=slots * units,
        ),
        name="last_stage",
    )(
        *far,
        here[1],
        *tokens,
        gate_w,
        up_w,
        down_w,
        *grads_here,
        hidden_here,
        qkv_w,
        out_w,
        here[0],
        *finish,
        *small,
    )


def expert_forward(rows, gate_w, up_w, grad_unscaled, slot_gates):
    gate_pre = jnp.dot(rows, gate_w, preferred_element_type=F32)
    up_pre = jnp.dot(rows, up_w, preferred_element_type=F32)
    hidden, pull = jax.vjp(geglu, gate_pre, up_pre)
    grad_gate_pre, grad_up_pre = pull(grad_unscaled * slot_gates)
    return hidden.astype(BF), grad_gate_pre.astype(BF), grad_up_pre.astype(BF)


def body_plain(
    block_input,
    cotangent,
    expert_ids,
    priority,
    rel_bucket,
    norm1_gain,
    w_query,
    w_key,
    w_value,
    w_out,
    pos_bias,
    norm2_gain,
    w_router,
    w_gate,
    w_up,
    w_down,
):
    group_rows, width = block_input.shape
    own_rows = cotangent.shape[0]
    buckets, heads_here = pos_bias.shape
    head_cols = w_query.shape[1]
    length = (rel_bucket.shape[0] + 1) // 2
    sequences = group_rows // length
    experts = w_router.shape[1]
    capacity = 5 * 2 * own_rows // (4 * experts)
    slot_count = experts * capacity
    replicas = lax.axis_size("head")
    groups = lax.axis_size("dp")
    me = lax.axis_index("head")
    far = replicas // 2
    far_perm = [(i, i ^ far) for i in range(replicas)]
    stepwise = own_rows == length and sequences == replicas

    def hop(value, r):
        return lax.ppermute(value, "head", [(i, i ^ r) for i in range(replicas)])

    def exchange(value):
        parts = value.reshape(experts, capacity, -1)
        return lax.all_to_all(parts, "dp", split_axis=0, concat_axis=0, tiled=True).reshape(
            slot_count, -1
        )

    dest = route_slots(expert_ids, priority[0], experts, capacity)
    dest_far = lax.ppermute(dest, "head", far_perm)
    slot_range = jnp.arange(slot_count, dtype=jnp.int32)[None, :]
    picks = [(dest[:, k : k + 1] == slot_range).astype(BF) for k in range(2)]
    both = picks[0] + picks[1]
    both_far = sum((dest_far[:, k : k + 1] == slot_range).astype(BF) for k in range(2))

    down_w, gate_w, up_w = w_down[0], w_gate[0], w_up[0]
    cot_here = exchange(contract(both, cotangent, 0, 0).astype(BF))
    cot_far_own = lax.ppermute(cotangent, "head", far_perm)
    cot_far = exchange(contract(both_far, cot_far_own, 0, 0).astype(BF))
    unscaled_here = contract(cot_here, down_w, 1, 1)
    unscaled_far = contract(cot_far, down_w, 1, 1)

    dp_at = lax.axis_index("dp")
    out_rows = head_cols // groups
    piece = lax.dynamic_slice_in_dim(w_out, dp_at * out_rows, out_rows, 0)
    w_out_all = lax.all_gather(piece, ("head", "dp"), axis=0, tiled=True)
    w_qkv = jnp.concatenate([w_query, w_key, w_value], axis=1)
    qkv_rows = width // groups
    piece = lax.dynamic_slice_in_dim(w_qkv, dp_at * qkv_rows, qkv_rows, 0)
    w_qkv_all = lax.all_gather(piece, ("head", "dp"), axis=0, tiled=True)
    if stepwise:
        order = [me ^ r for r in range(replicas)]
    else:
        order = list(range(replicas))
    w_out_all = w_out_all.reshape(replicas, head_cols, width)
    w_qkv_all = w_qkv_all.reshape(replicas, width, 3 * head_cols)
    w_out_cat = jnp.concatenate(
        [lax.dynamic_index_in_dim(w_out_all, o, 0, keepdims=False) for o in order], axis=0
    )

    inputs_all = block_input.astype(F32)
    normed = rms_norm(inputs_all, norm1_gain).astype(BF)
    qkv = jnp.dot(normed, w_qkv, preferred_element_type=F32).astype(BF)
    line = (rel_bucket[::-1][None, :] == jnp.arange(buckets, dtype=jnp.int32)[:, None]).astype(F32)
    line = jnp.pad(line, ((0, 0), (1, 0)))
    table = skew(contract(pos_bias, line, 0, 0, HIGH))
    kept = {}
    if stepwise:
        blocks = [None] * replicas
        for r in reversed(range(replicas)):
            attended_seq, probs = attend_fwd(order[r].reshape(1), qkv, table, length)
            kept[r] = probs
            blocks[r] = hop(attended_seq, r) if r else attended_seq
    else:
        seqs = []
        for s in range(sequences):
            attended_seq, kept[s] = attend_fwd(jnp.full((1,), s, jnp.int32), qkv, table, length)
            seqs.append(attended_seq)
        attended_all = jnp.concatenate(seqs, axis=0).reshape(replicas, own_rows, head_cols)
        attended_all = lax.all_to_all(attended_all, "head", split_axis=0, concat_axis=0, tiled=True)
        blocks = [attended_all[i] for i in range(replicas)]
    attended = jnp.concatenate(blocks, axis=1)

    branch = jnp.dot(attended, w_out_cat, preferred_element_type=F32)
    start_own = me * own_rows
    inputs_own = lax.dynamic_slice_in_dim(block_input, start_own, own_rows, 0).astype(F32)
    mixed = inputs_own + branch
    normed2_full, norm2_pull = jax.vjp(rms_norm, mixed, norm2_gain)
    normed2 = normed2_full.astype(BF)
    logits = jnp.dot(normed2, w_router, preferred_element_type=F32)
    expert_range = jnp.arange(experts, dtype=jnp.int32)
    chosen = (expert_ids[:, :, None] == expert_range[None, None, :]).astype(F32)
    gates = jax.nn.softmax(jnp.sum(chosen * logits[:, None, :], axis=2), axis=-1)

    def slot_gates_of(places, values):
        terms = sum(
            jnp.where(places[:, k : k + 1] == slot_range, values[:, k : k + 1], 0.0)
            for k in range(2)
        )
        return jnp.sum(terms, axis=0)

    rows_here = exchange(contract(both, normed2, 0, 0).astype(BF))
    gates_here = exchange(slot_gates_of(dest, gates))
    normed2_far = lax.ppermute(normed2, "head", far_perm)
    gates_far_own = lax.ppermute(gates, "head", far_perm)
    rows_far = exchange(contract(both_far, normed2_far, 0, 0).astype(BF))
    gates_far = exchange(slot_gates_of(dest_far, gates_far_own))

    hidden_here, ggp_here, gup_here = expert_forward(
        rows_here, gate_w, up_w, unscaled_here, gates_here
    )
    returned = jnp.dot(hidden_here, down_w, preferred_element_type=F32).astype(BF)
    came_back = exchange(returned)
    grad_routed = (contract(ggp_here, gate_w, 1, 1) + contract(gup_here, up_w, 1, 1)).astype(BF)
    grad_back = exchange(grad_routed)
    hidden_far, ggp_far, gup_far = expert_forward(rows_far, gate_w, up_w, unscaled_far, gates_far)
    scaled_here = (cot_here.astype(F32) * gates_here).astype(BF)
    scaled_far = (cot_far.astype(F32) * gates_far).astype(BF)

    low = me % far
    high = me // far

    def reduced(lefts, rights):
        rows = lefts[0].shape[1] // replicas

        def part(at):
            return sum(
                contract(lax.dynamic_slice_in_dim(left, at * rows, rows, 1), right, 0, 0)
                for left, right in zip(lefts, rights)
            )

        if far == 2:
            sent = hop(part(high * far + (1 - low)).astype(BF), 1)
            return (part(me) + sent.astype(F32))[None]
        whole = jnp.concatenate([part(high * far + i) for i in range(far)], axis=0).astype(BF)
        member = [[h * far + i for i in range(far)] for h in range(2)]
        return lax.psum_scatter(
            whole, "head", scatter_dimension=0, axis_index_groups=member, tiled=True
        ).astype(F32)[None]

    grad_down_w = reduced((hidden_here, hidden_far), (scaled_here, scaled_far))
    grad_gate_w = reduced((rows_here, rows_far), (ggp_here, ggp_far))
    grad_up_w = reduced((rows_here, rows_far), (gup_here, gup_far))

    chosen_rows = [jnp.dot(pick, came_back, preferred_element_type=F32) for pick in picks]
    output = mixed + sum(gates[:, k : k + 1] * chosen_rows[k] for k in range(2))
    grad_output = cotangent.astype(F32)
    grad_gates = jnp.stack([jnp.sum(grad_output * rows, axis=1) for rows in chosen_rows], axis=1)
    grad_normed2 = jnp.dot(both, grad_back, preferred_element_type=F32)
    grad_picked = gates * (grad_gates - jnp.sum(gates * grad_gates, axis=1, keepdims=True))
    grad_logits = jnp.sum(chosen * grad_picked[:, :, None], axis=1)
    grad_normed2 = grad_normed2 + contract(grad_logits, w_router.astype(F32), 1, 1, HIGH)
    grad_router = contract(normed2.astype(F32), grad_logits, 0, 0, HIGH)
    grad_mixed, grad_norm2 = norm2_pull(grad_normed2)
    grad_mixed = grad_mixed + grad_output
    grad_branch = grad_mixed.astype(BF)

    grad_wout = contract(attended, grad_branch, 0, 0).astype(BF)
    grad_wout = grad_wout.reshape(replicas, groups, out_rows, width)
    grad_wout = lax.psum_scatter(grad_wout, "dp", scatter_dimension=1, tiled=True)[:, 0]
    if stepwise:
        grad_wout = sum(
            (hop(grad_wout[r], r) if r else grad_wout[r]).astype(F32) for r in range(replicas)
        ).astype(BF)
    else:
        grad_wout = lax.psum_scatter(
            grad_wout.reshape(replicas * out_rows, width), "head", scatter_dimension=0, tiled=True
        )
    grad_out_proj = lax.all_gather(grad_wout, "dp", axis=0, tiled=True).astype(F32)

    grad_heads = contract(grad_branch, w_out_cat, 1, 1).astype(BF)
    sums = jnp.zeros((heads_here, TILE, 2 * length), F32)
    grad_blocks = [grad_heads[:, i * head_cols : (i + 1) * head_cols] for i in range(replicas)]
    grad_total = None
    weight_terms = []
    if stepwise:
        arrived = [hop(grad_blocks[r], r) if r else grad_blocks[0] for r in range(replicas)]
        for r in (0, 2, 3, 1):
            grad_qkv, sums = attend_bwd(order[r].reshape(1), qkv, arrived[r], kept[r], sums, length)
            normed_seq = lax.dynamic_slice_in_dim(normed, order[r] * length, length, 0)
            weight_terms.append(contract(normed_seq, grad_qkv, 0, 0))
            mine = hop(grad_qkv, r) if r else grad_qkv
            weight = lax.dynamic_index_in_dim(w_qkv_all, order[r], 0, keepdims=False)
            term = contract(mine, weight, 1, 1)
            grad_total = term if grad_total is None else grad_total + term
        grad_normed = grad_total
        grad_qkv_w = sum(weight_terms)
    else:
        stacked = jnp.stack(grad_blocks, axis=0)
        stacked = lax.all_to_all(stacked, "head", split_axis=0, concat_axis=0, tiled=True)
        stacked = stacked.reshape(group_rows, head_cols)
        seqs = []
        for s in range(sequences):
            grad_seq = stacked[s * length : (s + 1) * length]
            grad_qkv, sums = attend_bwd(
                jnp.full((1,), s, jnp.int32), qkv, grad_seq, kept[s], sums, length
            )
            seqs.append(grad_qkv)
        grad_qkv = jnp.concatenate(seqs, axis=0)
        grad_qkv_w = contract(normed, grad_qkv, 0, 0)
        grad_qkv = lax.all_to_all(
            grad_qkv.reshape(replicas, own_rows, 3 * head_cols),
            "head",
            split_axis=0,
            concat_axis=0,
            tiled=True,
        )
        grad_normed = sum(contract(grad_qkv[i], w_qkv_all[i], 1, 1) for i in range(replicas))

    _, norm1_pull = jax.vjp(rms_norm, inputs_own, norm1_gain)
    grad_first, grad_norm1 = norm1_pull(grad_normed)
    grad_input = grad_mixed + grad_first
    grad_bias = contract(unskew(sums), line, 1, 1, HIGH)
    grad_qkv_w, grad_bias = lax.psum((grad_qkv_w.astype(BF), grad_bias), "dp")
    grad_qkv_w = grad_qkv_w.astype(F32)
    grad_norm1, grad_norm2, grad_router = lax.psum(
        (grad_norm1, grad_norm2, grad_router), ("dp", "head")
    )
    return (
        output,
        grad_input,
        grad_norm1,
        grad_qkv_w[:, :head_cols],
        grad_qkv_w[:, head_cols : 2 * head_cols],
        grad_qkv_w[:, 2 * head_cols :],
        grad_out_proj,
        jnp.transpose(grad_bias),
        grad_norm2,
        grad_router,
        grad_gate_w,
        grad_up_w,
        grad_down_w,
    )


def body(*args):
    block_input, cotangent, rel_bucket, pos_bias, w_gate, w_router = (
        args[0],
        args[1],
        args[4],
        args[10],
        args[13],
        args[12],
    )
    own_rows = cotangent.shape[0]
    length = (rel_bucket.shape[0] + 1) // 2
    replicas, groups = lax.axis_size("head"), lax.axis_size("dp")
    experts = w_router.shape[1]
    capacity = 5 * 2 * own_rows // (4 * experts)
    stepwise = (
        own_rows == length
        and block_input.shape[0] == replicas * length
        and replicas == 4
        and groups == 8
        and experts == groups
        and capacity % 16 == 0
        and pos_bias.shape[1] in (2, 4, 6)
        and w_gate.shape[2] % 256 == 0
    )
    return body_steps(*args) if stepwise else body_plain(*args)


def body_steps(
    block_input,
    cotangent,
    expert_ids,
    priority,
    rel_bucket,
    norm1_gain,
    w_query,
    w_key,
    w_value,
    w_out,
    pos_bias,
    norm2_gain,
    w_router,
    w_gate,
    w_up,
    w_down,
):
    group_rows, width = block_input.shape
    own_rows = cotangent.shape[0]
    buckets, heads_here = pos_bias.shape
    head_cols = w_query.shape[1]
    length = (rel_bucket.shape[0] + 1) // 2
    experts = w_router.shape[1]
    capacity = 5 * 2 * own_rows // (4 * experts)
    slot_count = experts * capacity
    replicas, groups = lax.axis_size("head"), lax.axis_size("dp")
    me, dp_at = lax.axis_index("head"), lax.axis_index("dp")

    dest = route_slots(expert_ids, priority[0], experts, capacity)
    bits = (dest // capacity) ^ dp_at
    position = sum(p * (bits == offset).astype(jnp.int32) for p, offset in enumerate(OFFSETS))
    mixed_dest = jnp.where(
        dest < slot_count,
        position * capacity + dest % capacity,
        slot_count,
    )
    routing = jnp.concatenate([mixed_dest, expert_ids], axis=1)
    routing_rows = jnp.pad(routing.T, ((0, 4), (0, 0)))
    routing_cols = jnp.pad(routing, ((0, 0), (0, 4)))
    router_wide = jnp.pad(w_router, ((0, 0), (0, TILE - experts)))
    line = (rel_bucket[::-1][None, :] == jnp.arange(buckets, dtype=jnp.int32)[:, None]).astype(F32)
    line = jnp.pad(line, ((0, 0), (1, 0)))
    input_weights = (w_query, w_key, w_value)
    (
        attended,
        probs,
        cot_here,
        normed,
        qkv,
        w_cat,
        cot_far,
        routing_far,
        mixed,
        normed2,
    ) = attend_all(
        block_input,
        norm1_gain[None, :],
        input_weights,
        contract(pos_bias, line, 0, 0, HIGH)[:, None, :],
        cotangent,
        routing_rows,
        w_out,
        norm2_gain[None, :],
        groups,
        capacity,
    )

    gate_w, up_w, down_w = w_gate[0], w_up[0], w_down[0]
    tile = 256
    (
        rows_here,
        hidden_here,
        ggp_here,
        gup_here,
        scaled_here,
        back,
        grad_back,
        slot_slope,
        normed2_far,
        cot_far_rest,
    ) = expert_stage(
        normed2,
        routing_rows,
        cot_here,
        router_wide,
        gate_w,
        up_w,
        down_w,
        cotangent,
        groups,
        capacity,
        tile,
    )

    gates, grad_mixed, grad_branch, grad_heads, grad_router, grad_norm2 = combine(
        grad_back.reshape(slot_count, width),
        slot_slope.reshape(slot_count, TILE),
        routing_cols,
        mixed,
        normed2,
        cotangent,
        router_wide,
        norm2_gain[None, :],
        w_cat,
        experts,
    )

    far_rows, far_scaled, carry, part_sum, grad_qkv_w, grad_wout, lines = attend_back(
        normed2_far,
        cot_far,
        cot_far_rest,
        routing_far,
        router_wide,
        grad_heads,
        qkv,
        probs,
        normed,
        input_weights,
        attended,
        grad_branch,
        groups,
        capacity,
    )

    (
        wide_kept,
        wide_came,
        tall_kept,
        tall_came,
        grad_qkv_w,
        grad_out_proj,
        summed,
        grad_first,
        expert_sum,
        _,
    ) = last_stage(
        (far_rows, far_scaled),
        (rows_here.reshape(slot_count, width), scaled_here.reshape(slot_count, width)),
        (gates, routing_cols, norm1_gain[None, :]),
        (gate_w, up_w, down_w),
        (ggp_here, gup_here),
        hidden_here,
        (
            grad_qkv_w.reshape(groups, width // groups, 3 * head_cols),
            grad_wout.reshape(replicas, groups, head_cols // groups, width),
        ),
        (carry, part_sum, block_input, back),
        (grad_norm2, grad_router, lines),
        tile,
    )
    grad_qkv_w = grad_qkv_w.reshape(width, 3 * head_cols).astype(F32)
    grad_out_proj = grad_out_proj.reshape(head_cols, width).astype(F32)
    return (
        mixed + expert_sum,
        grad_mixed + grad_first,
        summed[1, 0],
        grad_qkv_w[:, :head_cols],
        grad_qkv_w[:, head_cols : 2 * head_cols],
        grad_qkv_w[:, 2 * head_cols :],
        grad_out_proj,
        contract(line, summed[0, 2 : 2 + heads_here], 1, 1, HIGH),
        summed[1, 1],
        jnp.transpose(summed[1, 8 : 8 + experts]),
        (wide_kept[0] + wide_came[0].astype(F32))[None],
        (wide_kept[1] + wide_came[1].astype(F32))[None],
        (tall_kept + tall_came.astype(F32))[None],
    )


def solution(mesh):
    placed = (
        P("dp", None),
        P(("dp", "head"), None),
        P(("dp", "head"), None),
        P(("dp", "head"), None),
        P(),
        P(),
        P(None, "head"),
        P(None, "head"),
        P(None, "head"),
        P("head", None),
        P(None, "head"),
        P(),
        P(),
        P("dp", None, None),
        P("dp", None, None),
        P("dp", None, None),
    )
    return jax.shard_map(
        body,
        mesh=mesh,
        in_specs=placed,
        out_specs=(
            P(("dp", "head"), None),
            P(("dp", "head"), None),
            P(),
            P(None, "head"),
            P(None, "head"),
            P(None, "head"),
            P("head", None),
            P(None, "head"),
            P(),
            P(),
            P("dp", "head", None),
            P("dp", "head", None),
            P("dp", "head", None),
        ),
        check_vma=False,
    )
```

```python
import functools

import jax
import jax.numpy as jnp
from jax import lax
from jax.experimental import pallas as pl
from jax.experimental.pallas import tpu as pltpu
from jax.sharding import PartitionSpec as P

EPS = 1e-06
SCALE = 0.125
HIGH = lax.Precision.HIGHEST
TILE = 128
BF = jnp.bfloat16
F32 = jnp.float32
VMEM_LIMIT = 48 << 20
VMEM_MOST = 60 << 20
GELU_A = 0.7978845608028654
GELU_B = 0.044715
OFFSETS = [0, 1, 6, 7, 2, 4, 3, 5]
PEERS = [4, 5, 6, 7, 2, 3, 1]


def rms_norm(value, gain):
    return value * lax.rsqrt(jnp.mean(value * value, axis=-1, keepdims=True) + EPS) * gain


def geglu(gate, up_part):
    return jax.nn.gelu(gate) * up_part


def contract(left, right, left_dim, right_dim, precision=None):
    return lax.dot_general(
        left,
        right,
        (((left_dim,), (right_dim,)), ((), ())),
        precision=precision,
        preferred_element_type=jnp.float32,
    )


def route_slots(chosen, ranks, experts, capacity):
    count = chosen.shape[0]
    keys = jnp.concatenate([ranks, ranks + count])
    wanted = jnp.concatenate([chosen[:, 0], chosen[:, 1]])
    smaller = (wanted[:, None] == wanted[None, :]) & (keys[None, :] < keys[:, None])
    place = jnp.sum(smaller.astype(jnp.int32), axis=1)
    dest = jnp.where(place < capacity, wanted * capacity + place, experts * capacity)
    return jnp.stack([dest[:count], dest[count:]], axis=1)


def skew_kernel(line_ref, table_ref):
    heads, rows, cols = table_ref.shape
    row = lax.broadcasted_iota(jnp.int32, (8, cols), 0)
    for h in range(heads):
        value = jnp.broadcast_to(line_ref[h], (8, cols))
        for shift in (1, 2, 4):
            value = jnp.where((row & shift) != 0, pltpu.roll(value, shift, 1), value)
        table_ref[h, :8] = value
        done = 8
        while done < rows:
            table_ref[h, done : 2 * done] = pltpu.roll(table_ref[h, :done], done, 1)
            done *= 2


def unskew_kernel(table_ref, line_ref):
    heads, rows, cols = table_ref.shape
    row = lax.broadcasted_iota(jnp.int32, (8, cols), 0)
    for h in range(heads):
        value, left = table_ref[h], rows // 2
        while left >= 8:
            value = value[:left] + pltpu.roll(value[left:], cols - left, 1)
            left //= 2
        for shift in (1, 2, 4):
            value = jnp.where((row & shift) != 0, pltpu.roll(value, cols - shift, 1), value)
        line_ref[h] = jnp.sum(value, axis=0, keepdims=True)


def skew(line):
    heads, cols = line.shape
    return pl.pallas_call(
        skew_kernel,
        out_shape=jax.ShapeDtypeStruct((heads, TILE, cols), F32),
        compiler_params=pltpu.CompilerParams(vmem_limit_bytes=VMEM_LIMIT),
        name="skew",
    )(line[:, None, :])


def unskew(table):
    heads, _, cols = table.shape
    return pl.pallas_call(
        unskew_kernel,
        out_shape=jax.ShapeDtypeStruct((heads, 1, cols), F32),
        compiler_params=pltpu.CompilerParams(vmem_limit_bytes=VMEM_LIMIT),
        name="unskew",
    )(table)[:, 0]


def lanes_of(shape, half, part):
    lane = lax.broadcasted_iota(jnp.int32, shape, 1)
    return (lane >= half) if part else (lane < half)


def attend_fwd_kernel(seq_ref, q_ref, k_ref, v_ref, table_ref, out_ref, probs_ref, acc_ref):
    del seq_ref
    length, lanes = q_ref.shape
    half = lanes // 2
    chunk = 2 * TILE
    key = k_ref[...]
    value_t = v_ref[...].T
    for part in range(2):
        query = jnp.where(lanes_of((length, lanes), half, part), q_ref[...] * SCALE, 0).astype(BF)
        for c in range(length // chunk):
            cols = slice(c * chunk, (c + 1) * chunk)
            scores = contract(key, query[cols], 1, 1)
            pieces = []
            for kb in range(length // TILE):
                at = length - TILE * kb + chunk * c
                pieces.append(
                    scores[kb * TILE : (kb + 1) * TILE] + table_ref[part, :, at : at + chunk]
                )
            scores = jnp.concatenate(pieces, axis=0)
            top = jnp.max(scores, axis=0, keepdims=True)
            shifted = jnp.exp(scores - top)
            total = jnp.sum(shifted, axis=0, keepdims=True)
            probs = (shifted * (1.0 / total)).astype(BF)
            probs_ref[part, :, cols] = probs
            acc_ref[part * half : (part + 1) * half, cols] = jnp.dot(
                value_t[part * half : (part + 1) * half], probs, preferred_element_type=F32
            )
    out_ref[...] = acc_ref[...].T.astype(BF)


def attend_fwd(seq, qkv, table, length):
    heads, _, width = table.shape
    columns = qkv.shape[1] // 3
    pairs = heads // 2
    lanes = columns // pairs
    spec = [
        pl.BlockSpec((length, lanes), lambda p, s, j=j: (s[0], j * pairs + p)) for j in range(3)
    ]
    return pl.pallas_call(
        attend_fwd_kernel,
        out_shape=(
            jax.ShapeDtypeStruct((length, columns), BF),
            jax.ShapeDtypeStruct((heads, length, length), BF),
        ),
        grid_spec=pltpu.PrefetchScalarGridSpec(
            num_scalar_prefetch=1,
            grid=(pairs,),
            in_specs=spec + [pl.BlockSpec((2, TILE, width), lambda p, s: (p, 0, 0))],
            out_specs=[
                pl.BlockSpec((length, lanes), lambda p, s: (0, p)),
                pl.BlockSpec((2, length, length), lambda p, s: (p, 0, 0)),
            ],
            scratch_shapes=[pltpu.VMEM((lanes, length), F32)],
        ),
        compiler_params=pltpu.CompilerParams(vmem_limit_bytes=VMEM_LIMIT),
        cost_estimate=pl.CostEstimate(
            flops=heads * 8 * length * length * lanes,
            bytes_accessed=heads * length * length * 2 + 8 * length * columns,
            transcendentals=heads * length * length,
        ),
        name="attend_fwd",
    )(seq, qkv, qkv, qkv, table)


def attend_bwd_kernel(
    seq_ref, q_ref, k_ref, v_ref, grad_ref, probs_ref, sums_in_ref, out_ref, sums_ref, acc_ref
):
    del seq_ref
    length, lanes = q_ref.shape
    half = lanes // 2
    chunk = 2 * TILE
    pair = pl.program_id(0)
    columns = out_ref.shape[1] // 3
    key_t = k_ref[...].T
    value = v_ref[...]
    sums_ref[...] = sums_in_ref[...]
    grad_keys, grad_values = [], []
    for part in range(2):
        mask = lanes_of((length, lanes), half, part)
        grad = jnp.where(mask, grad_ref[...], 0).astype(BF)
        grad_key = jnp.zeros((length, lanes), F32)
        grad_value = jnp.zeros((length, lanes), F32)
        for c in range(length // chunk):
            cols = slice(c * chunk, (c + 1) * chunk)
            grad_probs = contract(value, grad[cols], 1, 1)
            probs_low = probs_ref[part, :, cols]
            probs = probs_low.astype(F32)
            delta = jnp.sum(probs * grad_probs, axis=0, keepdims=True)
            grad_scores = (probs * (grad_probs - delta)).astype(BF)
            grad_value += jnp.dot(probs_low, grad_ref[cols, :], preferred_element_type=F32)
            grad_key += jnp.dot(grad_scores, q_ref[cols, :], preferred_element_type=F32)
            acc_ref[part * half : (part + 1) * half, cols] = jnp.dot(
                key_t[part * half : (part + 1) * half], grad_scores, preferred_element_type=F32
            )
            for kb in range(length // TILE):
                at = length - TILE * kb + chunk * c
                sums_ref[part, :, at : at + chunk] += grad_scores[
                    kb * TILE : (kb + 1) * TILE
                ].astype(F32)
        grad_keys.append(grad_key)
        grad_values.append(grad_value)
    first = lanes_of((length, lanes), half, 0)
    at = pl.multiple_of(pair * lanes, lanes)
    out_ref[:, pl.ds(at, lanes)] = (acc_ref[...].T * SCALE).astype(BF)
    at = pl.multiple_of(columns + pair * lanes, lanes)
    out_ref[:, pl.ds(at, lanes)] = (jnp.where(first, *grad_keys) * SCALE).astype(BF)
    at = pl.multiple_of(2 * columns + pair * lanes, lanes)
    out_ref[:, pl.ds(at, lanes)] = jnp.where(first, *grad_values).astype(BF)


def attend_bwd(seq, qkv, grad, probs, sums, length):
    heads, _, width = sums.shape
    columns = qkv.shape[1] // 3
    pairs = heads // 2
    lanes = columns // pairs
    spec = [
        pl.BlockSpec((length, lanes), lambda p, s, j=j: (s[0], j * pairs + p)) for j in range(3)
    ]
    sums_spec = pl.BlockSpec((2, TILE, width), lambda p, s: (p, 0, 0))
    return pl.pallas_call(
        attend_bwd_kernel,
        out_shape=(
            jax.ShapeDtypeStruct((length, 3 * columns), BF),
            jax.ShapeDtypeStruct(sums.shape, F32),
        ),
        grid_spec=pltpu.PrefetchScalarGridSpec(
            num_scalar_prefetch=1,
            grid=(pairs,),
            in_specs=spec
            + [
                pl.BlockSpec((length, lanes), lambda p, s: (0, p)),
                pl.BlockSpec((2, length, length), lambda p, s: (p, 0, 0)),
                sums_spec,
            ],
            out_specs=[pl.BlockSpec((length, 3 * columns), lambda p, s: (0, 0)), sums_spec],
            scratch_shapes=[pltpu.VMEM((lanes, length), F32)],
        ),
        compiler_params=pltpu.CompilerParams(vmem_limit_bytes=VMEM_LIMIT),
        cost_estimate=pl.CostEstimate(
            flops=heads * 16 * length * length * lanes,
            bytes_accessed=heads * length * length * 2 + 16 * length * columns,
            transcendentals=0,
        ),
        name="attend_bwd",
    )(seq, qkv, qkv, qkv, grad, probs, sums)


def flipped(index, bits):
    out, step = index, 1
    while step <= bits:
        if bits & step:
            out = out + step * (1 - 2 * lax.rem(index // step, 2))
        step *= 2
    return out


def plane(d, position):
    return flipped(d, OFFSETS[position])


def greet(peers):
    barrier = pltpu.get_barrier_semaphore()
    for peer in peers:
        pl.semaphore_signal(barrier, inc=1, device_id=peer, device_id_type=pl.DeviceIdType.MESH)
    pl.semaphore_wait(barrier, len(peers))


def remote(source, target, send_sem, recv_sem, peer):
    return pltpu.make_async_remote_copy(
        src_ref=source,
        dst_ref=target,
        send_sem=send_sem,
        recv_sem=recv_sem,
        device_id=peer,
        device_id_type=pl.DeviceIdType.MESH,
    )


def attend_all_kernel(
    input_hbm,
    gain_ref,
    query_hbm,
    key_hbm,
    value_hbm,
    line_ref,
    cot_hbm,
    routing_ref,
    w_out_hbm,
    gain2_ref,
    attended_out,
    probs_out,
    came_out,
    normed_out,
    qkv_out,
    w_cat_out,
    cot_far_out,
    routing_far_out,
    mixed_ref,
    normed2_ref,
    input_ref,
    weight_ref,
    cot_ref,
    w_out_ref,
    table_ref,
    sends,
    acc_ref,
    block_ref,
    hold_ref,
    normed_ref,
    qkv_ref,
    attended_ref,
    w_cat,
    w_land,
    row_send,
    row_recv,
    hop_send,
    hop_recv,
    w_send,
    w_recv,
    plane_send,
    plane_recv,
    core_send,
    core_recv,
    far_send,
    far_recv,
    hold_sem,
    own_sem,
    load_sem,
):
    z, d = lax.axis_index("head"), lax.axis_index("dp")
    heads, _, _ = table_ref.shape
    replicas, length, columns = block_ref.shape
    groups, capacity, _ = sends.shape
    width = input_ref.shape[1]
    part_rows = w_land.shape[1]
    pairs = heads // 2
    lanes = columns // pairs
    half = lanes // 2
    chunk = 2 * TILE
    hops = [3, 2, 1]
    cot_load = pltpu.make_async_copy(cot_hbm, cot_ref, load_sem.at[0])
    w_out_load = pltpu.make_async_copy(w_out_hbm, w_out_ref, load_sem.at[1])
    weight_loads = [
        pltpu.make_async_copy(
            source, weight_ref.at[:, pl.ds(i * columns, columns)], load_sem.at[2 + i]
        )
        for i, source in enumerate((query_hbm, key_hbm, value_hbm))
    ]
    input_loads = {}
    for r in [3, 2, 1, 0]:
        span = pl.ds(pl.multiple_of(flipped(z, r) * length, length), length)
        input_loads[r] = pltpu.make_async_copy(
            input_hbm.at[span], input_ref.at[span], load_sem.at[5 + r]
        )
    for copy in [cot_load, input_loads[3]] + weight_loads:
        copy.start()
    for copy in [input_loads[2], input_loads[1], input_loads[0], w_out_load]:
        copy.start()
    greet([{"dp": plane(d, o)} for o in PEERS] + [{"head": flipped(z, r)} for r in hops])
    copies = []

    def launch(*what):
        copy = remote(*what)
        copy.start()
        copies.append(copy)
        return copy

    piece = w_out_hbm.at[pl.ds(pl.multiple_of(d * part_rows, part_rows), part_rows), :]
    w_hops = {}
    for r in hops:
        w_hops[r] = remote(piece, w_land.at[r], w_send.at[r], w_recv.at[r], {"head": flipped(z, r)})
        w_hops[r].start()
    cot_load.wait()
    half_plane = groups // 2

    def dispatch(start):
        span = slice(start, start + half_plane)
        first, second = selector(routing_ref, start * capacity, half_plane * capacity)
        sends[span, :, :width] = (
            jnp.dot((first + second).astype(BF), cot_ref[...], preferred_element_type=F32)
            .astype(BF)
            .reshape(half_plane, capacity, width)
        )
        sends[span, :, width:] = slot_signs(routing_ref, first, second).reshape(
            half_plane, capacity, TILE
        )

    def send_rows(start):
        for o in range(start, start + half_plane):
            if o:
                launch(
                    sends.at[o], came_out.at[o], row_send.at[o], row_recv.at[o], {"dp": plane(d, o)}
                )

    chips = [o for o, bits in enumerate(OFFSETS) if o and bits % 2 == 0]
    plane_copies = {}

    def w_rows(s, o):
        at = s * columns + plane(d, o) * part_rows
        return pl.ds(pl.multiple_of(at, part_rows), part_rows)

    dispatch(half_plane)
    for s in hops:
        w_hops[s].wait()
        at = w_rows(s, 0)
        w_cat[at, :] = w_land[s]
        for o in chips:
            plane_copies[s, o] = remote(
                w_land.at[s],
                w_cat.at[at, :],
                plane_send.at[s, o],
                plane_recv.at[s, o],
                {"dp": plane(d, o)},
            )
            plane_copies[s, o].start()
    send_rows(half_plane)
    dispatch(0)
    send_rows(0)
    own = pltpu.make_async_copy(sends.at[0], came_out.at[0], own_sem.at[0])
    own.start()
    far = {"head": flipped(z, 2)}
    launch(routing_ref, routing_far_out, far_send.at[0], far_recv.at[0], far)
    early = pl.ds(0, cot_far_out.shape[0])
    launch(cot_hbm.at[early], cot_far_out, far_send.at[1], far_recv.at[1], far)
    skew_kernel(line_ref, table_ref)
    w_out_load.wait()
    w_cat[:columns, :] = w_out_ref[...]

    moves = []
    for turn, r in enumerate(reversed(range(replicas))):
        start = flipped(z, r) * length
        slot = turn % 2
        if turn >= 2:
            for move in moves[turn - 2]:
                move.wait()

        input_loads[r].wait()

        def norm_step(i, carry, start=start, slot=slot):
            rows = pl.multiple_of(start + i * TILE, TILE)
            value = input_ref[pl.ds(rows, TILE), :].astype(F32)
            value = rms_norm(value, gain_ref[...])
            normed_ref[slot, pl.ds(pl.multiple_of(i * TILE, TILE), TILE), :] = value.astype(BF)
            return carry

        lax.fori_loop(0, length // TILE, norm_step, 0)
        if turn == 0:
            for copy in weight_loads:
                copy.wait()
        qkv_ref[slot] = jnp.dot(
            normed_ref[slot], weight_ref[...], preferred_element_type=F32
        ).astype(BF)

        def pair_step(pair, carry, slot=slot, r=r):
            def part_of(j):
                at = pl.multiple_of(j * columns + pair * lanes, lanes)
                return qkv_ref[slot, :, pl.ds(at, lanes)]

            key = part_of(1)
            value_t = part_of(2).T
            scaled = part_of(0) * SCALE
            for part in range(2):
                query = jnp.where(lanes_of((length, lanes), half, part), scaled, 0).astype(BF)
                for c in range(length // chunk):
                    cols = slice(c * chunk, (c + 1) * chunk)
                    scores = contract(key, query[cols], 1, 1)
                    pieces = []
                    for kb in range(length // TILE):
                        at = length - TILE * kb + chunk * c
                        pieces.append(
                            scores[kb * TILE : (kb + 1) * TILE]
                            + table_ref[pair * 2 + part, :, at : at + chunk]
                        )
                    scores = jnp.concatenate(pieces, axis=0)
                    top = jnp.max(scores, axis=0, keepdims=True)
                    shifted = jnp.exp(scores - top)
                    total = jnp.sum(shifted, axis=0, keepdims=True)
                    probs = (shifted * (1.0 / total)).astype(BF)
                    hold_ref[slot, pair * 2 + part, :, cols] = probs
                    acc_ref[part * half : (part + 1) * half, cols] = jnp.dot(
                        value_t[part * half : (part + 1) * half],
                        probs,
                        preferred_element_type=F32,
                    )
            at = pl.multiple_of(pair * lanes, lanes)
            block_ref[r, :, pl.ds(at, lanes)] = acc_ref[...].T.astype(BF)
            return carry

        lax.fori_loop(0, pairs, pair_step, 0)
        moves.append(
            [
                pltpu.make_async_copy(ref.at[slot], out.at[r], hold_sem.at[i, slot])
                for i, (ref, out) in enumerate(
                    ((hold_ref, probs_out), (normed_ref, normed_out), (qkv_ref, qkv_out))
                )
            ]
        )
        for move in moves[-1]:
            move.start()
        if r:
            launch(
                block_ref.at[r],
                attended_ref.at[:, pl.ds(r * columns, columns)],
                hop_send.at[r],
                hop_recv.at[r],
                {"head": flipped(z, r)},
            )
        else:
            attended_ref[:, :columns] = block_ref[0]
        if turn == 1:
            for s in hops:
                for o in [0] + chips:
                    if o:
                        plane_copies[s, o].wait_recv()
                    piece = w_cat.at[w_rows(s, o), :]
                    launch(piece, piece, core_send.at[s, o], core_recv.at[s, o], {"dp": plane(d, 1)})
    for copy in plane_copies.values():
        copy.wait_send()
    for copy in copies:
        copy.wait()
    outs = [
        pltpu.make_async_copy(attended_ref, attended_out, own_sem.at[1]),
        pltpu.make_async_copy(w_cat, w_cat_out, own_sem.at[2]),
    ]
    for copy in outs:
        copy.start()

    mixed_ref[...] = jnp.dot(attended_ref[...], w_cat[...], preferred_element_type=F32)

    def mixed_step(i, carry):
        at = pl.multiple_of(i * TILE, TILE)
        span = pl.ds(at, TILE)
        rows = pl.multiple_of(z * length + at, TILE)
        value = mixed_ref[span, :] + input_ref[pl.ds(rows, TILE), :].astype(F32)
        mixed_ref[span, :] = value
        normed2_ref[span, :] = rms_norm(value, gain2_ref[...]).astype(BF)
        return carry

    lax.fori_loop(0, length // TILE, mixed_step, 0)
    for move in moves[-2] + moves[-1] + outs + [own]:
        move.wait()


def attend_all(inputs, gain, weights, line, cot, routing, w_out, gain2, groups, capacity):
    heads, _, table_width = line.shape
    width = inputs.shape[1]
    length = cot.shape[0]
    replicas = inputs.shape[0] // length
    columns = weights[0].shape[1]
    lanes = 2 * columns // heads
    part_rows = columns // groups
    vmem = pl.BlockSpec(memory_space=pltpu.VMEM)
    hbm = pl.BlockSpec(memory_space=pl.ANY)
    came_shape = (groups, capacity, width + TILE)
    plane_sem = pltpu.SemaphoreType.DMA((groups,))
    hop_sem = pltpu.SemaphoreType.DMA((replicas,))
    both_sem = pltpu.SemaphoreType.DMA((replicas, groups))
    two_sem = pltpu.SemaphoreType.DMA((2,))
    return pl.pallas_call(
        attend_all_kernel,
        out_shape=(
            jax.ShapeDtypeStruct((length, replicas * columns), BF),
            jax.ShapeDtypeStruct((replicas, heads, length, length), BF),
            jax.ShapeDtypeStruct(came_shape, BF),
            jax.ShapeDtypeStruct((replicas, length, width), BF),
            jax.ShapeDtypeStruct((replicas, length, 3 * columns), BF),
            jax.ShapeDtypeStruct((replicas * columns, width), BF),
            jax.ShapeDtypeStruct((length // 4, width), BF),
            jax.ShapeDtypeStruct(routing.shape, routing.dtype),
            jax.ShapeDtypeStruct((length, width), F32),
            jax.ShapeDtypeStruct((length, width), BF),
        ),
        in_specs=[hbm, vmem, hbm, hbm, hbm, vmem, hbm, vmem, hbm, vmem],
        out_specs=[hbm] * 8 + [vmem] * 2,
        scratch_shapes=[
            pltpu.VMEM(inputs.shape, BF),
            pltpu.VMEM((width, 3 * columns), BF),
            pltpu.VMEM(cot.shape, BF),
            pltpu.VMEM(w_out.shape, BF),
            pltpu.VMEM((heads, TILE, table_width), F32),
            pltpu.VMEM(came_shape, BF),
            pltpu.VMEM((lanes, length), F32),
            pltpu.VMEM((replicas, length, columns), BF),
            pltpu.VMEM((2, heads, length, length), BF),
            pltpu.VMEM((2, length, width), BF),
            pltpu.VMEM((2, length, 3 * columns), BF),
            pltpu.VMEM((length, replicas * columns), BF),
            pltpu.VMEM((replicas * columns, width), BF),
            pltpu.VMEM((replicas, part_rows, width), BF),
            plane_sem,
            plane_sem,
            hop_sem,
            hop_sem,
            hop_sem,
            hop_sem,
            both_sem,
            both_sem,
            both_sem,
            both_sem,
            two_sem,
            two_sem,
            pltpu.SemaphoreType.DMA((3, 2)),
            pltpu.SemaphoreType.DMA((3,)),
            pltpu.SemaphoreType.DMA((9,)),
        ],
        compiler_params=pltpu.CompilerParams(
            vmem_limit_bytes=VMEM_MOST, collective_id=1, has_side_effects=True
        ),
        cost_estimate=pl.CostEstimate(
            flops=replicas * heads * 8 * length * length * lanes,
            bytes_accessed=replicas * heads * length * length * 4,
            transcendentals=replicas * heads * length * length,
        ),
        name="attend_all",
    )(inputs, gain, *weights, line, cot, routing, w_out, gain2)


def selector(routing, start, count):
    slot = lax.broadcasted_iota(jnp.int32, (count, routing.shape[1]), 0) + start
    return [jnp.where(slot == routing[k : k + 1], 1.0, 0.0) for k in range(2)]


def slot_signs(routing, first, second):
    lane = lax.broadcasted_iota(jnp.int32, (TILE, routing.shape[1]), 0)
    signs = jnp.where(lane == routing[3:4], 1.0, 0.0) - jnp.where(lane == routing[2:3], 1.0, 0.0)
    return contract((first - second).astype(BF), signs.astype(BF), 1, 1).astype(BF)


def token_selector(routing, slots):
    slot = lax.broadcasted_iota(jnp.int32, (routing.shape[0], slots), 1)
    return [jnp.where(slot == routing[:, k : k + 1], 1.0, 0.0) for k in range(2)]


def expert_tile(rows, scaled, gate_w, up_w, down_w):
    gate = jnp.dot(rows, gate_w, preferred_element_type=F32)
    up_part = jnp.dot(rows, up_w, preferred_element_type=F32)
    grad_hidden = contract(scaled, down_w, 1, 1)
    square = gate * gate
    bend = jnp.tanh(gate * (GELU_A + GELU_A * GELU_B * square))
    half = 0.5 + 0.5 * bend
    active = gate * half
    slope = half + 0.5 * gate * (1.0 - bend * bend) * (GELU_A + 3.0 * GELU_A * GELU_B * square)
    hidden = (active * up_part).astype(BF)
    grad_gate = (grad_hidden * up_part * slope).astype(BF)
    grad_up = (grad_hidden * active).astype(BF)
    return hidden, grad_gate, grad_up


def scaled_rows(rows, extended, router, width):
    logits = jnp.dot(rows, router, preferred_element_type=F32)
    sign = extended[:, width:].astype(F32)
    gap = jnp.sum(logits * sign, axis=1, keepdims=True)
    return (extended[:, :width].astype(F32) * (1.0 / (1.0 + jnp.exp(gap)))).astype(BF)


def expert_kernel(
    width,
    tile,
    normed_ref,
    routing_ref,
    cot_ref,
    router_ref,
    gate_hbm,
    up_hbm,
    down_hbm,
    cot_hbm,
    rows_out,
    hidden_out,
    grad_gate_out,
    grad_up_out,
    scaled_out,
    back_out,
    grad_back_out,
    slope_out,
    far_out,
    cot_far_out,
    gate_w,
    up_w,
    down_w,
    rows,
    sends,
    back,
    grad_back,
    slopes,
    hidden,
    grad_gate,
    grad_up,
    scaled,
    weight_sem,
    row_send,
    row_recv,
    slope_send,
    slope_recv,
    grad_send,
    grad_recv,
    unit_sem,
    keep_sem,
    far_sem,
):
    z, d = lax.axis_index("head"), lax.axis_index("dp")
    far = {"head": flipped(z, 2)}
    groups, capacity, _ = rows.shape
    units = gate_w.shape[1]
    tiles = units // tile
    count = 2 * capacity

    def weights_of(t):
        at = t * tile if isinstance(t, int) else pl.multiple_of(t * tile, tile)
        return [
            pltpu.make_async_copy(
                gate_hbm.at[:, pl.ds(at, tile)], gate_w.at[:, pl.ds(at, tile)], weight_sem.at[0, t]
            ),
            pltpu.make_async_copy(
                up_hbm.at[:, pl.ds(at, tile)], up_w.at[:, pl.ds(at, tile)], weight_sem.at[1, t]
            ),
            pltpu.make_async_copy(
                down_hbm.at[pl.ds(at, tile), :], down_w.at[pl.ds(at, tile), :], weight_sem.at[2, t]
            ),
        ]

    def start_weights(t, carry):
        for copy in weights_of(t):
            copy.start()
        return carry

    lax.fori_loop(0, tiles, start_weights, 0)
    greet([{"dp": plane(d, o)} for o in PEERS] + [far])
    pending = []
    arrivals = {}

    for start, number in ((2, 2), (4, groups - 4), (0, 2)):
        first, second = selector(routing_ref, start * capacity, number * capacity)
        sends[start : start + number] = (
            jnp.dot((first + second).astype(BF), normed_ref[...], preferred_element_type=F32)
            .astype(BF)
            .reshape(number, capacity, width)
        )
        for o in range(start, start + number):
            if o:
                arrivals[o] = remote(
                    sends.at[o], rows.at[o], row_send.at[o], row_recv.at[o], {"dp": plane(d, o)}
                )
                arrivals[o].start()
    over = [
        remote(normed_ref, far_out, far_sem.at[0, 0], far_sem.at[0, 1], far),
        remote(
            cot_hbm.at[pl.ds(cot_far_out.shape[0] // 2, cot_far_out.shape[0])],
            cot_far_out,
            far_sem.at[1, 0],
            far_sem.at[1, 1],
            far,
        ),
    ]
    for copy in over:
        copy.start()
    rows[0] = sends[0]

    unit_copies = {}
    order = list(range(groups // 2))
    for turn, j in enumerate(order):
        pair = (2 * j, 2 * j + 1)
        slot = turn % 2
        for o in pair:
            if o:
                arrivals[o].wait_recv()
        if turn >= 2:
            for copy in unit_copies[order[turn - 2]]:
                copy.wait()
        here = rows[2 * j : 2 * j + 2].reshape(count, width)
        extended = cot_ref[2 * j : 2 * j + 2].reshape(count, cot_ref.shape[2])
        scaled[2 * j : 2 * j + 2] = scaled_rows(here, extended, router_ref[...], width).reshape(
            2, capacity, width
        )

        def wide_tile(at, size, j=j, slot=slot):
            values = expert_tile(
                rows[2 * j : 2 * j + 2].reshape(count, width),
                scaled[2 * j : 2 * j + 2].reshape(count, width),
                gate_w[:, pl.ds(at, size)],
                up_w[:, pl.ds(at, size)],
                down_w[pl.ds(at, size), :],
            )
            for ref, value in zip((hidden, grad_gate, grad_up), values):
                ref[slot, :, pl.ds(at, size)] = value

        def tile_step(t, carry, j=j):
            if j == 0:
                for i in range(2):
                    for copy in weights_of(2 * t + i):
                        copy.wait()
            wide_tile(pl.multiple_of(2 * t * tile, tile), 2 * tile)
            return carry

        lax.fori_loop(0, tiles // 2, tile_step, 0)
        if tiles % 2:
            if j == 0:
                for copy in weights_of(tiles - 1):
                    copy.wait()
            wide_tile((tiles - 1) * tile, tile)
        span = pl.ds(j * count, count)
        unit_copies[j] = [
            pltpu.make_async_copy(ref.at[slot], out.at[span], unit_sem.at[slot, i])
            for i, (ref, out) in enumerate(
                ((hidden, hidden_out), (grad_gate, grad_gate_out), (grad_up, grad_up_out))
            )
        ]
        for copy in unit_copies[j]:
            copy.start()

        def back_step(t, carry, j=j, slot=slot):
            cols = pl.ds(pl.multiple_of(t * 2 * tile, 2 * tile), 2 * tile)
            value = jnp.dot(hidden[slot], down_w[:, cols], preferred_element_type=F32)
            back[2 * j : 2 * j + 2, :, cols] = value.astype(BF).reshape(2, capacity, 2 * tile)
            return carry

        def grad_step(t, carry, j=j, slot=slot):
            cols = pl.ds(pl.multiple_of(t * 2 * tile, 2 * tile), 2 * tile)
            value = contract(grad_gate[slot], gate_w[cols, :], 1, 1) + contract(
                grad_up[slot], up_w[cols, :], 1, 1
            )
            grad_back[2 * j : 2 * j + 2, :, cols] = value.astype(BF).reshape(2, capacity, 2 * tile)
            return carry

        def give(buffer, out, send_sem, recv_sem, pair=pair):
            for o in pair:
                if o:
                    copy = remote(
                        buffer.at[o],
                        out.at[o],
                        send_sem.at[o],
                        recv_sem.at[o],
                        {"dp": plane(d, o)},
                    )
                else:
                    copy = pltpu.make_async_copy(buffer.at[0], out.at[0], send_sem.at[0])
                copy.start()
                pending.append(copy)

        lax.fori_loop(0, width // (2 * tile), grad_step, 0)
        give(grad_back, grad_back_out, grad_send, grad_recv)
        lax.fori_loop(0, width // (2 * tile), back_step, 0)
        product = jnp.sum(
            cot_ref[2 * j : 2 * j + 2, :, :width].reshape(count, width).astype(F32)
            * back[2 * j : 2 * j + 2].reshape(count, width).astype(F32),
            axis=1,
            keepdims=True,
        )
        lane = lax.broadcasted_iota(jnp.int32, (count, TILE), 1)
        spread = jnp.zeros((count, TILE), F32)
        for k, term in enumerate(split_parts(product)):
            spread = jnp.where(lane == k, term.astype(F32), spread)
        slopes[2 * j : 2 * j + 2] = spread.astype(BF).reshape(2, capacity, TILE)
        give(slopes, slope_out, slope_send, slope_recv)

    keeps = [
        pltpu.make_async_copy(rows, rows_out, keep_sem.at[0]),
        pltpu.make_async_copy(scaled, scaled_out, keep_sem.at[1]),
        pltpu.make_async_copy(back, back_out, keep_sem.at[2]),
    ]
    for copy in keeps:
        copy.start()
    for j in order[-2:]:
        for copy in unit_copies[j]:
            copy.wait()
    for o in PEERS:
        arrivals[o].wait_send()
    for copy in pending + keeps + over:
        copy.wait()


def expert_stage(
    normed2, routing, cot, router, gate_w, up_w, down_w, cot_own, groups, capacity, tile
):
    width, units = gate_w.shape
    slots = groups * capacity
    vmem = pl.BlockSpec(memory_space=pltpu.VMEM)
    hbm = pl.BlockSpec(memory_space=pl.ANY)
    row_shape = jax.ShapeDtypeStruct((groups, capacity, width), BF)
    unit_shape = jax.ShapeDtypeStruct((slots, units), BF)
    row_buffer = pltpu.VMEM((groups, capacity, width), BF)
    unit_buffer = pltpu.VMEM((2, 2 * capacity, units), BF)
    row_sem = pltpu.SemaphoreType.DMA((groups,))
    return pl.pallas_call(
        functools.partial(expert_kernel, width, tile),
        out_shape=(row_shape,)
        + (unit_shape,) * 3
        + (row_shape,) * 3
        + (
            jax.ShapeDtypeStruct((groups, capacity, TILE), BF),
            jax.ShapeDtypeStruct(normed2.shape, BF),
            jax.ShapeDtypeStruct((normed2.shape[0] // 2, width), BF),
        ),
        in_specs=[vmem] * 4 + [hbm] * 4,
        out_specs=[hbm] * 10,
        scratch_shapes=[
            pltpu.VMEM((width, units), BF),
            pltpu.VMEM((width, units), BF),
            pltpu.VMEM((units, width), BF),
            row_buffer,
            row_buffer,
            row_buffer,
            row_buffer,
            pltpu.VMEM((groups, capacity, TILE), BF),
            unit_buffer,
            unit_buffer,
            unit_buffer,
            row_buffer,
            pltpu.SemaphoreType.DMA((3, units // tile)),
            row_sem,
            row_sem,
            row_sem,
            row_sem,
            row_sem,
            row_sem,
            pltpu.SemaphoreType.DMA((2, 3)),
            pltpu.SemaphoreType.DMA((3,)),
            pltpu.SemaphoreType.DMA((2, 2)),
        ],
        compiler_params=pltpu.CompilerParams(
            vmem_limit_bytes=VMEM_MOST, collective_id=2, has_side_effects=True
        ),
        cost_estimate=pl.CostEstimate(
            flops=12 * slots * width * units,
            bytes_accessed=6 * width * units + 6 * slots * units,
            transcendentals=slots * units,
        ),
        name="expert_stage",
    )(normed2, routing, cot, router, gate_w, up_w, down_w, cot_own)


def split_parts(value):
    first = value.astype(BF)
    rest = value - first.astype(F32)
    second = rest.astype(BF)
    return first, second, (rest - second.astype(F32)).astype(BF)


def combine_kernel(
    grad_back_ref,
    slot_slope_ref,
    routing_ref,
    mixed_ref,
    normed2_ref,
    cot_ref,
    router_ref,
    gain_ref,
    w_cat_ref,
    gates_ref,
    grad_mixed_ref,
    grad_branch_ref,
    grad_heads_ref,
    grad_router_ref,
    grad_norm2_ref,
    cot_far_out,
    picked,
    slopes,
    gaps,
    pick,
    far_sem,
):
    length, width = mixed_ref.shape

    slots = grad_back_ref.shape[0]
    far = {"head": flipped(lax.axis_index("head"), 2)}
    greet([far])
    last = cot_far_out.shape[0]
    over = remote(
        cot_ref.at[pl.ds(length - last, last)], cot_far_out, far_sem.at[0], far_sem.at[1], far
    )
    over.start()
    first, second = token_selector(routing_ref, slots)
    gaps[...] = jnp.dot(
        (second - first).astype(BF), slot_slope_ref[...], preferred_element_type=F32
    )
    pick[...] = (first + second).astype(BF)

    picked[...] = jnp.dot(pick[...], grad_back_ref[...], preferred_element_type=F32)
    lane = lax.broadcasted_iota(jnp.int32, (TILE, TILE), 1)

    def row_step(i, total):
        span = pl.ds(pl.multiple_of(i * TILE, TILE), TILE)
        ids = routing_ref[span, :]
        sign = jnp.where(lane == ids[:, 3:4], 1.0, 0.0) - jnp.where(lane == ids[:, 2:3], 1.0, 0.0)
        logits = jnp.dot(normed2_ref[span, :], router_ref[...], preferred_element_type=F32)
        gap = jnp.sum(logits * sign, axis=1, keepdims=True)
        gate0, gate1 = 1.0 / (1.0 + jnp.exp(gap)), 1.0 / (1.0 + jnp.exp(-gap))
        cot = cot_ref[span, :].astype(F32)
        mixed = mixed_ref[span, :]
        gates_ref[span, :] = jnp.where(lane == 0, gate0, gate1)
        grad_gap = jnp.sum(gaps[span, :], axis=1, keepdims=True)
        slope = gate0 * gate1 * grad_gap * sign
        slopes[span, :] = slope
        grad_normed2 = picked[span, :] + sum(
            contract(part, router_ref[...], 1, 1) for part in split_parts(slope)
        )
        scale = lax.rsqrt(jnp.mean(mixed * mixed, axis=1, keepdims=True) + EPS)
        inner = grad_normed2 * gain_ref[...]
        mean = jnp.mean(inner * mixed, axis=1, keepdims=True)
        grad_mixed = cot + scale * inner - mixed * (scale * scale * scale * mean)
        grad_mixed_ref[span, :] = grad_mixed
        grad_branch_ref[span, :] = grad_mixed.astype(BF)
        return total + jnp.sum(grad_normed2 * mixed * scale, axis=0, keepdims=True)

    grad_norm2_ref[...] = lax.fori_loop(
        0, length // TILE, row_step, jnp.zeros((1, width), F32)
    )

    grad_heads_ref[...] = contract(grad_branch_ref[...], w_cat_ref[...], 1, 1).astype(BF)
    experts = grad_router_ref.shape[0]
    grad_router_ref[...] = sum(
        contract(part, normed2_ref[...], 0, 0) for part in split_parts(slopes[...])
    )[:experts]
    over.wait()


def combine(grad_back, slot_slope, routing, mixed, normed2, cot, router, gain, w_cat, experts):
    length, width = mixed.shape
    vmem = pl.BlockSpec(memory_space=pltpu.VMEM)
    return pl.pallas_call(
        combine_kernel,
        out_shape=(
            jax.ShapeDtypeStruct((length, TILE), F32),
            jax.ShapeDtypeStruct((length, width), F32),
            jax.ShapeDtypeStruct((length, width), BF),
            jax.ShapeDtypeStruct((length, w_cat.shape[0]), BF),
            jax.ShapeDtypeStruct((experts, width), F32),
            jax.ShapeDtypeStruct((1, width), F32),
            jax.ShapeDtypeStruct((length // 4, width), BF),
        ),
        in_specs=[vmem] * 9,
        out_specs=[vmem] * 6 + [pl.BlockSpec(memory_space=pl.ANY)],
        scratch_shapes=[
            pltpu.VMEM((length, width), F32),
            pltpu.VMEM((length, TILE), F32),
            pltpu.VMEM((length, TILE), F32),
            pltpu.VMEM((length, grad_back.shape[0]), BF),
            pltpu.SemaphoreType.DMA((2,)),
        ],
        compiler_params=pltpu.CompilerParams(
            vmem_limit_bytes=VMEM_MOST, collective_id=5, has_side_effects=True
        ),
        cost_estimate=pl.CostEstimate(
            flops=3 * length * grad_back.shape[0] * width,
            bytes_accessed=4 * grad_back.shape[0] * width,
            transcendentals=0,
        ),
        name="combine",
    )(grad_back, slot_slope, routing, mixed, normed2, cot, router, gain, w_cat)


def attend_back_kernel(
    normed2_far,
    cot_first,
    cot_middle,
    cot_last,
    routing_ref,
    router_ref,
    grad_ref,
    qkv_hbm,
    probs_hbm,
    normed_hbm,
    query_hbm,
    key_hbm,
    value_hbm,
    attended_ref,
    grad_branch_ref,
    far_rows_ref,
    far_scaled_ref,
    carry_ref,
    part_sum_ref,
    qkv_w_ref,
    out_w_ref,
    lines_ref,
    sums_ref,
    acc_ref,
    sends,
    cot_far,
    grads,
    qkv_ref,
    probs_ref,
    normed_ref,
    grad_qkv_ref,
    weight_ref,
    weight_sum,
    parts,
    landed,
    far_send,
    far_recv,
    hop_send,
    hop_recv,
    part_send,
    part_recv,
    load_sem,
    weight_sem,
    own_sem,
):
    z, d = lax.axis_index("head"), lax.axis_index("dp")
    replicas, length, columns = grads.shape
    _, groups, capacity, _ = sends.shape
    width = normed2_far.shape[1]
    heads = sums_ref.shape[0]
    pairs = heads // 2
    lanes = columns // pairs
    half = lanes // 2
    chunk = 2 * TILE
    hops = [3, 2, 1]
    order = [3, 0, 1, 2]

    def loads(turn):
        r, slot = order[turn], turn % 2
        return [
            pltpu.make_async_copy(source.at[r], target.at[slot], load_sem.at[i, slot])
            for i, (source, target) in enumerate(
                ((qkv_hbm, qkv_ref), (probs_hbm, probs_ref), (normed_hbm, normed_ref))
            )
        ]

    weight_loads = [
        pltpu.make_async_copy(
            source, weight_ref.at[:, pl.ds(i * columns, columns)], weight_sem.at[i]
        )
        for i, source in enumerate((query_hbm, key_hbm, value_hbm))
    ]
    for copy in loads(0) + weight_loads:
        copy.start()
    greet([{"dp": plane(d, o)} for o in PEERS] + [{"head": flipped(z, r)} for r in hops])
    copies = []
    arrivals = {}
    for r in hops:
        arrivals[r] = remote(
            grad_ref.at[:, pl.ds(r * columns, columns)],
            grads.at[r],
            hop_send.at[r],
            hop_recv.at[r],
            {"head": flipped(z, r)},
        )
        arrivals[r].start()
    half_plane = groups // 2
    at = 0
    for piece in (cot_first, cot_middle, cot_last):
        cot_far[at : at + piece.shape[0]] = piece[...]
        at += piece.shape[0]
    logits = contract(router_ref[...], normed2_far[...], 0, 1)
    expert = lax.broadcasted_iota(jnp.int32, logits.shape, 0)
    routing = routing_ref[...]
    sign = jnp.where(expert == routing[3:4], 1.0, 0.0) - jnp.where(expert == routing[2:3], 1.0, 0.0)
    gap = jnp.sum(logits * sign, axis=0, keepdims=True)
    gate0, gate1 = 1.0 / (1.0 + jnp.exp(gap)), 1.0 / (1.0 + jnp.exp(-gap))

    def dispatch(start):
        span = slice(start, start + half_plane)
        first, second = selector(routing_ref, start * capacity, half_plane * capacity)
        gate = jnp.sum(first * gate0 + second * gate1, axis=1, keepdims=True)
        both = (first + second).astype(BF)
        shape = (half_plane, capacity, width)
        sends[0, span] = (
            jnp.dot(both, normed2_far[...], preferred_element_type=F32).astype(BF).reshape(shape)
        )
        sends[1, span] = (
            (jnp.dot(both, cot_far[...], preferred_element_type=F32) * gate)
            .astype(BF)
            .reshape(shape)
        )
        for o in range(start, start + half_plane):
            for i, out in enumerate((far_rows_ref, far_scaled_ref)):
                if o:
                    copy = remote(
                        sends.at[i, o],
                        out.at[o],
                        far_send.at[i, o],
                        far_recv.at[i, o],
                        {"dp": plane(d, o)},
                    )
                else:
                    copy = pltpu.make_async_copy(sends.at[i, 0], out.at[0], own_sem.at[i])
                copy.start()
                copies.append(copy)

    dispatch(half_plane)
    sums_ref[...] = jnp.zeros_like(sums_ref)
    grads[0] = grad_ref[:, :columns]

    near = {"head": flipped(z, 1)}

    def part_copy(i, source, target, peer):
        return remote(parts.at[source], landed.at[target], part_send.at[i], part_recv.at[i], peer)

    inner = part_copy(0, 3, 0, near)
    direct = part_copy(1, 1, 1, near)

    for copy in weight_loads:
        copy.wait()
    for turn, r in enumerate(order):
        slot = turn % 2
        if turn + 1 < replicas:
            for copy in loads(turn + 1):
                copy.start()
        for copy in loads(turn):
            copy.wait()
        if r:
            arrivals[r].wait_recv()

        def pair_step(pair, carry, slot=slot, r=r):
            def part_of(j):
                at = pl.multiple_of(j * columns + pair * lanes, lanes)
                return qkv_ref[slot, :, pl.ds(at, lanes)]

            at = pl.multiple_of(pair * lanes, lanes)
            query, value = part_of(0), part_of(2)
            key_t = part_of(1).T
            grad_all = grads[r, :, pl.ds(at, lanes)]
            grad_keys, grad_values = [], []
            for part in range(2):
                mask = lanes_of((length, lanes), half, part)
                grad = jnp.where(mask, grad_all, 0).astype(BF)
                grad_key = jnp.zeros((length, lanes), F32)
                grad_value = jnp.zeros((length, lanes), F32)
                for c in range(length // chunk):
                    cols = slice(c * chunk, (c + 1) * chunk)
                    grad_probs = contract(value, grad[cols], 1, 1)
                    probs_low = probs_ref[slot, pair * 2 + part, :, cols]
                    probs = probs_low.astype(F32)
                    delta = jnp.sum(probs * grad_probs, axis=0, keepdims=True)
                    grad_scores = (probs * (grad_probs - delta)).astype(BF)
                    grad_value += jnp.dot(probs_low, grad_all[cols], preferred_element_type=F32)
                    grad_key += jnp.dot(grad_scores, query[cols], preferred_element_type=F32)
                    acc_ref[part * half : (part + 1) * half, cols] = jnp.dot(
                        key_t[part * half : (part + 1) * half],
                        grad_scores,
                        preferred_element_type=F32,
                    )
                    for kb in range(length // TILE):
                        to = length - TILE * kb + chunk * c
                        sums_ref[pair * 2 + part, :, to : to + chunk] += grad_scores[
                            kb * TILE : (kb + 1) * TILE
                        ].astype(F32)
                grad_keys.append(grad_key)
                grad_values.append(grad_value)
            first = lanes_of((length, lanes), half, 0)
            results = (
                acc_ref[...].T * SCALE,
                jnp.where(first, *grad_keys) * SCALE,
                jnp.where(first, *grad_values),
            )
            for j, result in enumerate(results):
                to = pl.multiple_of(j * columns + pair * lanes, lanes)
                grad_qkv_ref[slot, :, pl.ds(to, lanes)] = result.astype(BF)
            return carry

        lax.fori_loop(0, pairs, pair_step, 0)

        parts[r] = contract(grad_qkv_ref[slot], weight_ref[...], 1, 1).astype(BF)
        if r == 3:
            inner.start()
            dispatch(0)
        if r == 1:
            direct.start()

        def weight_step(i, carry, slot=slot, turn=turn):
            cols = pl.ds(pl.multiple_of(i * 2 * chunk, 2 * chunk), 2 * chunk)
            value = contract(normed_ref[slot, :, cols], grad_qkv_ref[slot], 0, 0)
            if turn:
                value = value + weight_sum[cols, :]
            if turn + 1 < replicas:
                weight_sum[cols, :] = value
            else:
                qkv_w_ref[cols, :] = value.astype(BF)
            return carry

        lax.fori_loop(0, width // (2 * chunk), weight_step, 0)

    out_w_ref[...] = contract(attended_ref[...], grad_branch_ref[...], 0, 0).astype(BF)
    unskew_kernel(sums_ref, lines_ref)

    for r in hops:
        arrivals[r].wait_send()
    for copy in copies:
        copy.wait()
    inner.wait()
    carry_ref[...] = (parts[2].astype(F32) + landed[0].astype(F32)).astype(BF)
    direct.wait()
    part_sum_ref[...] = parts[0].astype(F32) + landed[1].astype(F32)


def attend_back(
    normed2_far,
    cot_pieces,
    routing_far,
    router,
    grad_heads,
    qkv,
    probs,
    normed,
    weights,
    attended,
    grad_branch,
    groups,
    capacity,
):
    replicas, length, triple = qkv.shape
    heads = probs.shape[1]
    columns = triple // 3
    width = normed.shape[2]
    lanes = 2 * columns // heads
    far_shape = jax.ShapeDtypeStruct((groups, capacity, width), BF)
    vmem = pl.BlockSpec(memory_space=pltpu.VMEM)
    hbm = pl.BlockSpec(memory_space=pl.ANY)
    hop_sem = pltpu.SemaphoreType.DMA((replicas,))
    plane_sem = pltpu.SemaphoreType.DMA((2, groups))
    part_sem = pltpu.SemaphoreType.DMA((2,))
    return pl.pallas_call(
        attend_back_kernel,
        out_shape=(
            far_shape,
            far_shape,
            jax.ShapeDtypeStruct((length, width), BF),
            jax.ShapeDtypeStruct((length, width), F32),
            jax.ShapeDtypeStruct((width, triple), BF),
            jax.ShapeDtypeStruct((replicas * columns, width), BF),
            jax.ShapeDtypeStruct((heads, 1, 2 * length), F32),
        ),
        in_specs=[vmem] * 7 + [hbm] * 6 + [vmem] * 2,
        out_specs=[hbm] * 2 + [vmem] * 5,
        scratch_shapes=[
            pltpu.VMEM((heads, TILE, 2 * length), F32),
            pltpu.VMEM((lanes, length), F32),
            pltpu.VMEM((2, groups, capacity, width), BF),
            pltpu.VMEM((length, width), BF),
            pltpu.VMEM((replicas, length, columns), BF),
            pltpu.VMEM((2, length, triple), BF),
            pltpu.VMEM((2, heads, length, length), BF),
            pltpu.VMEM((2, length, width), BF),
            pltpu.VMEM((2, length, triple), BF),
            pltpu.VMEM((width, triple), BF),
            pltpu.VMEM((width, triple), F32),
            pltpu.VMEM((replicas, length, width), BF),
            pltpu.VMEM((2, length, width), BF),
            plane_sem,
            plane_sem,
            hop_sem,
            hop_sem,
            part_sem,
            part_sem,
            pltpu.SemaphoreType.DMA((3, 2)),
            pltpu.SemaphoreType.DMA((3,)),
            pltpu.SemaphoreType.DMA((2,)),
        ],
        compiler_params=pltpu.CompilerParams(
            vmem_limit_bytes=VMEM_MOST, collective_id=3, has_side_effects=True
        ),
        cost_estimate=pl.CostEstimate(
            flops=replicas * heads * 16 * length * length * lanes,
            bytes_accessed=replicas * heads * length * length * 4,
            transcendentals=0,
        ),
        name="attend_back",
    )(
        normed2_far,
        *cot_pieces,
        routing_far,
        router,
        grad_heads,
        qkv,
        probs,
        normed,
        *weights,
        attended,
        grad_branch,
    )


def last_kernel(
    tile,
    far_hbm,
    scaled_hbm,
    scaled_here_hbm,
    gates_ref,
    routing_ref,
    gain_ref,
    gate_hbm,
    up_hbm,
    down_hbm,
    grad_gate_hbm,
    grad_up_hbm,
    hidden_hbm,
    qkv_w_hbm,
    out_w_hbm,
    rows_hbm,
    carry_hbm,
    part_sum_hbm,
    input_hbm,
    back_hbm,
    norm2_ref,
    router_grad_ref,
    lines_ref,
    wide_out,
    wide_came,
    tall_out,
    tall_came,
    qkv_w_out,
    out_w_out,
    small_out,
    grad_input_out,
    output_out,
    back_out,
    far_ref,
    scaled,
    scaled_here,
    left,
    weights,
    downs,
    units,
    hidden,
    hidden_here,
    send_wide,
    keep_wide,
    send_tall,
    keep_tall,
    qkv_land,
    qkv_sum,
    out_land,
    out_sum,
    out_hop,
    out_last,
    small_own,
    small_land,
    small_sum,
    small_hop,
    small_last,
    work,
    own_input,
    carried,
    stream_sem,
    hidden_sem,
    wide_send,
    wide_recv,
    keep_sem,
    tall_send,
    tall_recv,
    tall_keep,
    first_send,
    first_recv,
    hop_send,
    hop_recv,
    third_send,
    third_recv,
    carry_sem,
    back_send,
    back_recv,
    own_sem,
):
    z, d = lax.axis_index("head"), lax.axis_index("dp")
    slots, width = scaled_here.shape
    groups = qkv_land.shape[0]
    capacity = slots // groups
    length = own_input.shape[0]
    chunk = 2 * TILE
    _, rows, total_units = send_wide.shape
    half_units = hidden_here.shape[1]
    tiles = total_units // tile
    low, high = lax.rem(z, 2), z // 2
    keep_at = pl.multiple_of(low * rows, rows)
    send_at = pl.multiple_of((1 - low) * rows, rows)
    near = {"head": flipped(z, 1)}
    count = 2 * capacity
    hops = [3, 2, 1]

    def streams(t):
        slot = lax.rem(t, 2)
        at = pl.multiple_of(t * tile, tile)
        cols = pl.ds(at, tile)
        return [
            pltpu.make_async_copy(gate_hbm.at[:, cols], weights.at[slot, 0], stream_sem.at[0, slot]),
            pltpu.make_async_copy(up_hbm.at[:, cols], weights.at[slot, 1], stream_sem.at[1, slot]),
            pltpu.make_async_copy(down_hbm.at[cols, :], downs.at[slot], stream_sem.at[2, slot]),
            pltpu.make_async_copy(
                grad_gate_hbm.at[:, cols], units.at[slot, 0], stream_sem.at[3, slot]
            ),
            pltpu.make_async_copy(
                grad_up_hbm.at[:, cols], units.at[slot, 1], stream_sem.at[4, slot]
            ),
        ]

    wide = 2 * rows
    for copy in streams(0):
        copy.start()
    far_loads = [
        pltpu.make_async_copy(source, target, own_sem.at[6 + i])
        for i, (source, target) in enumerate(
            ((far_hbm, far_ref), (scaled_hbm, scaled), (scaled_here_hbm, scaled_here))
        )
    ]
    for copy in far_loads:
        copy.start()
    loads = [
        pltpu.make_async_copy(
            rows_hbm.at[:, pl.ds(pl.multiple_of(high * wide, wide), wide)], left, own_sem.at[2]
        ),
        pltpu.make_async_copy(part_sum_hbm, work.at[0], own_sem.at[3]),
        pltpu.make_async_copy(
            input_hbm.at[pl.ds(pl.multiple_of(z * length, length), length)], own_input, own_sem.at[5]
        ),
    ]
    for copy in loads:
        copy.start()

    half_copy = pltpu.make_async_copy(
        hidden_hbm.at[:, pl.ds(pl.multiple_of(high * half_units, TILE), half_units)],
        hidden_here,
        hidden_sem,
    )
    half_copy.start()
    greet([{"dp": plane(d, o)} for o in PEERS] + [{"head": flipped(z, r)} for r in hops])

    carry = remote(
        carry_hbm, carried, carry_sem.at[0], carry_sem.at[1], {"head": flipped(z, 2)}
    )
    carry.start()
    for copy in far_loads[:2] + loads[:1]:
        copy.wait()
    columns = pl.ds(pl.multiple_of(high * wide, wide), wide)

    def wide_copy(i, t):
        at = pl.multiple_of(t * tile, tile)
        return remote(
            send_wide.at[i, :, pl.ds(at, tile)],
            wide_came.at[i, :, pl.ds(at, tile)],
            wide_send.at[i, t],
            wide_recv.at[i, t],
            near,
        )

    def keep_copy(i, t):
        at = pl.multiple_of(t * tile, tile)
        slot = lax.rem(t, 2)
        return pltpu.make_async_copy(
            keep_wide.at[i, slot], wide_out.at[i, :, pl.ds(at, tile)], keep_sem.at[i, slot]
        )

    def tile_step(t, carry):
        slot = lax.rem(t, 2)
        at = pl.multiple_of(t * tile, tile)

        @pl.when(t + 1 < tiles)
        def _():
            for copy in streams(t + 1):
                copy.start()

        for copy in streams(t):
            copy.wait()

        def chunk_step(j, inner):
            span = pl.ds(pl.multiple_of(j * count, count), count)
            values = expert_tile(
                far_ref[span], scaled[span], weights[slot, 0], weights[slot, 1], downs[slot]
            )
            hidden[span, pl.ds(at, tile)] = values[0]
            units[slot, 2, span, :] = values[1]
            units[slot, 3, span, :] = values[2]
            return inner

        lax.fori_loop(0, groups // 2, chunk_step, 0)
        @pl.when(t >= 2)
        def _():
            for i in range(2):
                keep_copy(i, t - 2).wait()

        for i in range(2):
            value = contract(left[...], units[slot, i], 0, 0) + contract(
                far_ref[:, columns], units[slot, 2 + i], 0, 0
            )
            upper = low == 1
            send_wide[i, :, pl.ds(at, tile)] = jnp.where(
                upper, value[:rows], value[rows:]
            ).astype(BF)
            keep_wide[i, slot] = jnp.where(upper, value[rows:], value[:rows])
            wide_copy(i, t).start()
            keep_copy(i, t).start()
        return carry

    tile_step(jnp.int32(0), 0)

    first = []
    for o in PEERS:
        peer = plane(d, o)
        for i, (source, target) in enumerate(
            (
                (qkv_w_hbm.at[peer], qkv_land.at[o]),
                (out_w_hbm.at[:, peer], out_land.at[o]),
            )
        ):
            copy = remote(source, target, first_send.at[i, o], first_recv.at[i, o], {"dp": peer})
            copy.start()
            first.append(copy)
    own = [
        pltpu.make_async_copy(qkv_w_hbm.at[d], qkv_land.at[0], own_sem.at[0]),
        pltpu.make_async_copy(out_w_hbm.at[:, d], out_land.at[0], own_sem.at[1]),
    ]
    for copy in own:
        copy.start()

    backs = []
    for o in PEERS:
        copy = remote(
            back_hbm.at[o], back_out.at[o], back_send.at[o], back_recv.at[o], {"dp": plane(d, o)}
        )
        copy.start()
        backs.append(copy)
    backs.append(pltpu.make_async_copy(back_hbm.at[0], back_out.at[0], back_send.at[0]))
    backs[-1].start()
    lax.fori_loop(1, tiles, tile_step, 0)

    carry.wait()
    for copy in loads[1:]:
        copy.wait()

    def norm_step(i, total):
        span = pl.ds(pl.multiple_of(i * TILE, TILE), TILE)
        grad_normed = work[0, span, :] + carried[span, :].astype(F32)
        value = own_input[span, :].astype(F32)
        scale = lax.rsqrt(jnp.mean(value * value, axis=1, keepdims=True) + EPS)
        inner = grad_normed * gain_ref[...]
        mean = jnp.mean(inner * value, axis=1, keepdims=True)
        work[1, span, :] = scale * inner - value * (scale * scale * scale * mean)
        return total + jnp.sum(grad_normed * value * scale, axis=0, keepdims=True)

    heads = lines_ref.shape[0]
    small_own[...] = jnp.zeros_like(small_own)
    small_own[0:1] = lax.fori_loop(0, length // TILE, norm_step, jnp.zeros((1, width), F32))
    small_own[1:2] = norm2_ref[...]
    for h in range(heads):
        small_own[2 + h : 3 + h] = lines_ref[h]
    small_own[8:] = router_grad_ref[...]
    ends = [pltpu.make_async_copy(work.at[1], grad_input_out, own_sem.at[4])]
    for copy in ends:
        copy.start()
    small = []

    def lanes(index):
        return pl.ds(pl.multiple_of(index * TILE, TILE), TILE)

    for o in PEERS:
        peer = plane(d, o)
        copy = remote(
            small_own.at[:, lanes(peer)],
            small_land.at[o],
            first_send.at[2, o],
            first_recv.at[2, o],
            {"dp": peer},
        )
        copy.start()
        small.append(copy)
    small_land[0] = small_own[:, lanes(d)]

    for copy in first:
        copy.wait()
    for copy in own:
        copy.wait()
    qkv_sum[...] = sum(qkv_land[o].astype(F32) for o in range(groups)).astype(BF)
    out_sum[...] = sum(out_land[o].astype(F32) for o in range(groups)).astype(BF)
    second = []
    for o in PEERS:
        copy = remote(
            qkv_sum, qkv_w_out.at[d], third_send.at[0, o], third_recv.at[0, o], {"dp": plane(d, o)}
        )
        copy.start()
        second.append(copy)
    mine = [pltpu.make_async_copy(qkv_sum, qkv_w_out.at[d], own_sem.at[0])]
    mine[0].start()
    over = []
    for r in hops:
        copy = remote(
            out_sum.at[r], out_hop.at[r], hop_send.at[0, r], hop_recv.at[0, r], {"head": flipped(z, r)}
        )
        copy.start()
        over.append(copy)

    half_copy.wait()
    far_loads[2].wait()
    share = half_units // 2
    halves = pl.ds(pl.multiple_of(high * half_units, TILE), half_units)

    def tall_copies(i):
        cols = pl.ds(pl.multiple_of(i * tile, tile), tile)
        return [
            remote(
                send_tall.at[:, cols], tall_came.at[:, cols], tall_send.at[i], tall_recv.at[i], near
            ),
            pltpu.make_async_copy(keep_tall.at[:, cols], tall_out.at[:, cols], tall_keep.at[i]),
        ]

    def tall_step(i, carry):
        cols = pl.ds(pl.multiple_of(i * tile, tile), tile)
        value = contract(hidden_here[...], scaled_here[:, cols], 0, 0) + contract(
            hidden[:, halves], scaled[:, cols], 0, 0
        )
        upper = low == 1
        send_tall[:, cols] = jnp.where(upper, value[:share], value[share:]).astype(BF)
        keep_tall[:, cols] = jnp.where(upper, value[share:], value[:share])
        for copy in tall_copies(i):
            copy.start()
        return carry

    lax.fori_loop(0, width // tile, tall_step, 0)
    for copy in small:
        copy.wait()
    small_sum[...] = sum(small_land[o] for o in range(groups))
    small_over = []
    for r in hops:
        copy = remote(
            small_sum, small_hop.at[r], hop_send.at[1, r], hop_recv.at[1, r], {"head": flipped(z, r)}
        )
        copy.start()
        small_over.append(copy)

    for copy in backs:
        copy.wait()
    rows_back = [
        pltpu.make_async_copy(
            back_out.at[o], hidden.at[o * capacity : (o + 1) * capacity, :width], back_recv.at[o]
        )
        for o in range(groups)
    ]
    for copy in rows_back:
        copy.start()
    for k, pick in enumerate(token_selector(routing_ref, slots)):
        hidden_here[k * length : (k + 1) * length, :slots] = pick.astype(BF)
    for copy in rows_back:
        copy.wait()

    def output_step(i, carry):
        cols = pl.ds(pl.multiple_of(i * chunk, chunk), chunk)
        work[0, :, cols] = sum(
            gates_ref[:, k : k + 1]
            * jnp.dot(
                hidden_here[k * length : (k + 1) * length, :slots],
                hidden[:, cols],
                preferred_element_type=F32,
            )
            for k in range(2)
        )
        return carry

    lax.fori_loop(0, width // chunk, output_step, 0)
    ends.append(pltpu.make_async_copy(work.at[0], output_out, own_sem.at[3]))
    ends[1].start()

    for copy in small_over:
        copy.wait()
    small_last[0] = small_sum[...]
    small_last[1] = small_sum[...] + sum(small_hop[r] for r in hops)
    small_out[:, :, lanes(d)] = small_last[...]
    for o in PEERS:
        copy = remote(
            small_last,
            small_out.at[:, :, lanes(d)],
            third_send.at[2, o],
            third_recv.at[2, o],
            {"dp": plane(d, o)},
        )
        copy.start()
        second.append(copy)
    for copy in over:
        copy.wait()
    out_last[...] = (
        out_sum[0].astype(F32) + sum(out_hop[r].astype(F32) for r in hops)
    ).astype(BF)
    for o in PEERS:
        copy = remote(
            out_last,
            out_w_out.at[d],
            third_send.at[1, o],
            third_recv.at[1, o],
            {"dp": plane(d, o)},
        )
        copy.start()
        second.append(copy)
    mine.append(pltpu.make_async_copy(out_last, out_w_out.at[d], own_sem.at[1]))
    mine[1].start()

    for i in range(2):
        for t in (tiles - 2, tiles - 1):
            keep_copy(i, t).wait()

    def wide_end(t, carry):
        for i in range(2):
            wide_copy(i, t).wait()
        return carry

    lax.fori_loop(0, tiles, wide_end, 0)
    for copy in second + mine + ends:
        copy.wait()

    def tall_end(i, carry):
        for copy in tall_copies(i):
            copy.wait()
        return carry

    lax.fori_loop(0, width // tile, tall_end, 0)


def last_stage(
    far, here, tokens, weights, grads_here, hidden_here, sums, finish, small, tile
):
    gate_w, up_w, down_w = weights
    width, units = gate_w.shape
    qkv_w, out_w = sums
    replicas, groups, part_rows, _ = out_w.shape
    slots = far[0].shape[0]
    length = tokens[0].shape[0]
    back = finish[-1]
    vmem = pl.BlockSpec(memory_space=pltpu.VMEM)
    hbm = pl.BlockSpec(memory_space=pl.ANY)
    rows, share = width // replicas, units // replicas
    small_shape = (8 + groups, width)
    plane_sem = pltpu.SemaphoreType.DMA((3, groups))
    hop_sem = pltpu.SemaphoreType.DMA((2, replicas))
    return pl.pallas_call(
        functools.partial(last_kernel, tile),
        out_shape=(
            jax.ShapeDtypeStruct((2, rows, units), F32),
            jax.ShapeDtypeStruct((2, rows, units), BF),
            jax.ShapeDtypeStruct((share, width), F32),
            jax.ShapeDtypeStruct((share, width), BF),
            jax.ShapeDtypeStruct(qkv_w.shape, BF),
            jax.ShapeDtypeStruct(out_w.shape[1:], BF),
            jax.ShapeDtypeStruct((2,) + small_shape, F32),
            jax.ShapeDtypeStruct((length, width), F32),
            jax.ShapeDtypeStruct((length, width), F32),
            jax.ShapeDtypeStruct(back.shape, BF),
        ),
        in_specs=[hbm] * 3 + [vmem] * 3 + [hbm] * 13 + [vmem] * 3,
        out_specs=[hbm] * 6 + [vmem] + [hbm] * 3,
        scratch_shapes=[
            pltpu.VMEM((slots, width), BF),
            pltpu.VMEM((slots, width), BF),
            pltpu.VMEM((slots, width), BF),
            pltpu.VMEM((slots, 2 * rows), BF),
            pltpu.VMEM((2, 2, width, tile), BF),
            pltpu.VMEM((2, tile, width), BF),
            pltpu.VMEM((2, 4, slots, tile), BF),
            pltpu.VMEM((slots, units), BF),
            pltpu.VMEM((slots, units // 2), BF),
            pltpu.VMEM((2, rows, units), BF),
            pltpu.VMEM((2, 2, rows, tile), F32),
            pltpu.VMEM((share, width), BF),
            pltpu.VMEM((share, width), F32),
            pltpu.VMEM(qkv_w.shape, BF),
            pltpu.VMEM(qkv_w.shape[1:], BF),
            pltpu.VMEM((groups, replicas, part_rows, width), BF),
            pltpu.VMEM((replicas, part_rows, width), BF),
            pltpu.VMEM((replicas, part_rows, width), BF),
            pltpu.VMEM((part_rows, width), BF),
            pltpu.VMEM(small_shape, F32),
            pltpu.VMEM((groups, small_shape[0], TILE), F32),
            pltpu.VMEM((small_shape[0], TILE), F32),
            pltpu.VMEM((replicas, small_shape[0], TILE), F32),
            pltpu.VMEM((2, small_shape[0], TILE), F32),
            pltpu.VMEM((2, length, width), F32),
            pltpu.VMEM((length, width), BF),
            pltpu.VMEM((length, width), BF),
            pltpu.SemaphoreType.DMA((5, 2)),
            pltpu.SemaphoreType.DMA,
            pltpu.SemaphoreType.DMA((2, units // tile)),
            pltpu.SemaphoreType.DMA((2, units // tile)),
            pltpu.SemaphoreType.DMA((2, 2)),
            pltpu.SemaphoreType.DMA((width // tile,)),
            pltpu.SemaphoreType.DMA((width // tile,)),
            pltpu.SemaphoreType.DMA((width // tile,)),
            plane_sem,
            plane_sem,
            hop_sem,
            hop_sem,
            plane_sem,
            plane_sem,
            pltpu.SemaphoreType.DMA((2,)),
            pltpu.SemaphoreType.DMA((groups,)),
            pltpu.SemaphoreType.DMA((groups,)),
            pltpu.SemaphoreType.DMA((9,)),
        ],
        compiler_params=pltpu.CompilerParams(
            vmem_limit_bytes=VMEM_MOST, collective_id=4, has_side_effects=True
        ),
        cost_estimate=pl.CostEstimate(
            flops=12 * slots * width * units,
            bytes_accessed=6 * width * units + 6 * slots * units,
            transcendentals=slots * units,
        ),
        name="last_stage",
    )(
        *far,
        here[1],
        *tokens,
        gate_w,
        up_w,
        down_w,
        *grads_here,
        hidden_here,
        qkv_w,
        out_w,
        here[0],
        *finish,
        *small,
    )


def finish_kernel(
    wide_kept,
    wide_came,
    tall_kept,
    tall_came,
    qkv_ref,
    out_ref,
    mixed_ref,
    expert_ref,
    grad_mixed_ref,
    grad_first_ref,
    summed_ref,
    line_ref,
    output_ref,
    grad_input_ref,
    query_out,
    key_out,
    value_out,
    out_out,
    gate_out,
    up_out,
    down_out,
    norm1_out,
    norm2_out,
    bias_out,
    router_out,
):
    output_ref[...] = mixed_ref[...] + expert_ref[...]
    grad_input_ref[...] = grad_mixed_ref[...] + grad_first_ref[...]
    gate_out[...] = wide_kept[0] + wide_came[0].astype(F32)
    up_out[...] = wide_kept[1] + wide_came[1].astype(F32)
    down_out[...] = tall_kept[...] + tall_came[...].astype(F32)
    columns = query_out.shape[1]
    for i, out in enumerate((query_out, key_out, value_out)):
        value = qkv_ref[:, :, i * columns : (i + 1) * columns].astype(F32)
        out[...] = value.reshape(out.shape)
    out_out[...] = out_ref[...].astype(F32).reshape(out_out.shape)

    @pl.when(pl.program_id(0) == 0)
    def _():
        norm1_out[...] = summed_ref[1, :1]
        norm2_out[...] = summed_ref[1, 1:2]
        heads = bias_out.shape[0]
        total = sum(contract(term, line_ref[...], 1, 1) for term in split_parts(summed_ref[0, :8]))
        bias_out[...] = total[2 : 2 + heads]
        router_out[...] = summed_ref[1, 8:]


def finish(wide, tall, qkv_w, out_w, tokens, summed, line, heads):
    steps = 4
    groups, part_rows, triple = qkv_w.shape
    _, out_rows, width = out_w.shape
    _, rows, units = wide[0].shape
    share = tall[0].shape[0]
    length = tokens[0].shape[0]
    columns = triple // 3
    experts = summed.shape[1] - 8

    def cut(shape, axis=0):
        block = tuple(n // steps if i == axis else n for i, n in enumerate(shape))
        return pl.BlockSpec(block, lambda t: tuple(t if i == axis else 0 for i in range(len(shape))))

    def whole(shape):
        return pl.BlockSpec(shape, lambda t: (0,) * len(shape))

    outs = [
        (length, width),
        (length, width),
        (groups * part_rows, columns),
        (groups * part_rows, columns),
        (groups * part_rows, columns),
        (groups * out_rows, width),
        (rows, units),
        (rows, units),
        (share, width),
    ]
    small = [(1, width), (1, width), (heads, line.shape[0]), (experts, width)]
    return pl.pallas_call(
        finish_kernel,
        out_shape=[jax.ShapeDtypeStruct(shape, F32) for shape in outs + small],
        grid=(steps,),
        in_specs=[cut(value.shape, 1) for value in wide]
        + [cut(value.shape) for value in tall]
        + [cut(qkv_w.shape), cut(out_w.shape)]
        + [cut(value.shape) for value in tokens]
        + [whole(summed.shape), whole(line.shape)],
        out_specs=[cut(shape) for shape in outs] + [whole(shape) for shape in small],
        compiler_params=pltpu.CompilerParams(vmem_limit_bytes=VMEM_MOST),
        cost_estimate=pl.CostEstimate(
            flops=4 * rows * units, bytes_accessed=48 * rows * units, transcendentals=0
        ),
        name="finish",
    )(*wide, *tall, qkv_w, out_w, *tokens, summed, line)


def expert_forward(rows, gate_w, up_w, grad_unscaled, slot_gates):
    gate_pre = jnp.dot(rows, gate_w, preferred_element_type=F32)
    up_pre = jnp.dot(rows, up_w, preferred_element_type=F32)
    hidden, pull = jax.vjp(geglu, gate_pre, up_pre)
    grad_gate_pre, grad_up_pre = pull(grad_unscaled * slot_gates)
    return hidden.astype(BF), grad_gate_pre.astype(BF), grad_up_pre.astype(BF)


def body_plain(
    block_input,
    cotangent,
    expert_ids,
    priority,
    rel_bucket,
    norm1_gain,
    w_query,
    w_key,
    w_value,
    w_out,
    pos_bias,
    norm2_gain,
    w_router,
    w_gate,
    w_up,
    w_down,
):
    group_rows, width = block_input.shape
    own_rows = cotangent.shape[0]
    buckets, heads_here = pos_bias.shape
    head_cols = w_query.shape[1]
    length = (rel_bucket.shape[0] + 1) // 2
    sequences = group_rows // length
    experts = w_router.shape[1]
    capacity = 5 * 2 * own_rows // (4 * experts)
    slot_count = experts * capacity
    replicas = lax.axis_size("head")
    groups = lax.axis_size("dp")
    me = lax.axis_index("head")
    far = replicas // 2
    far_perm = [(i, i ^ far) for i in range(replicas)]
    stepwise = own_rows == length and sequences == replicas

    def hop(value, r):
        return lax.ppermute(value, "head", [(i, i ^ r) for i in range(replicas)])

    def exchange(value):
        parts = value.reshape(experts, capacity, -1)
        return lax.all_to_all(parts, "dp", split_axis=0, concat_axis=0, tiled=True).reshape(
            slot_count, -1
        )

    dest = route_slots(expert_ids, priority[0], experts, capacity)
    dest_far = lax.ppermute(dest, "head", far_perm)
    slot_range = jnp.arange(slot_count, dtype=jnp.int32)[None, :]
    picks = [(dest[:, k : k + 1] == slot_range).astype(BF) for k in range(2)]
    both = picks[0] + picks[1]
    both_far = sum((dest_far[:, k : k + 1] == slot_range).astype(BF) for k in range(2))

    down_w, gate_w, up_w = w_down[0], w_gate[0], w_up[0]
    cot_here = exchange(contract(both, cotangent, 0, 0).astype(BF))
    cot_far_own = lax.ppermute(cotangent, "head", far_perm)
    cot_far = exchange(contract(both_far, cot_far_own, 0, 0).astype(BF))
    unscaled_here = contract(cot_here, down_w, 1, 1)
    unscaled_far = contract(cot_far, down_w, 1, 1)

    dp_at = lax.axis_index("dp")
    out_rows = head_cols // groups
    piece = lax.dynamic_slice_in_dim(w_out, dp_at * out_rows, out_rows, 0)
    w_out_all = lax.all_gather(piece, ("head", "dp"), axis=0, tiled=True)
    w_qkv = jnp.concatenate([w_query, w_key, w_value], axis=1)
    qkv_rows = width // groups
    piece = lax.dynamic_slice_in_dim(w_qkv, dp_at * qkv_rows, qkv_rows, 0)
    w_qkv_all = lax.all_gather(piece, ("head", "dp"), axis=0, tiled=True)
    if stepwise:
        order = [me ^ r for r in range(replicas)]
    else:
        order = list(range(replicas))
    w_out_all = w_out_all.reshape(replicas, head_cols, width)
    w_qkv_all = w_qkv_all.reshape(replicas, width, 3 * head_cols)
    w_out_cat = jnp.concatenate(
        [lax.dynamic_index_in_dim(w_out_all, o, 0, keepdims=False) for o in order], axis=0
    )

    inputs_all = block_input.astype(F32)
    normed = rms_norm(inputs_all, norm1_gain).astype(BF)
    qkv = jnp.dot(normed, w_qkv, preferred_element_type=F32).astype(BF)
    line = (rel_bucket[::-1][None, :] == jnp.arange(buckets, dtype=jnp.int32)[:, None]).astype(F32)
    line = jnp.pad(line, ((0, 0), (1, 0)))
    table = skew(contract(pos_bias, line, 0, 0, HIGH))
    kept = {}
    if stepwise:
        blocks = [None] * replicas
        for r in reversed(range(replicas)):
            attended_seq, probs = attend_fwd(order[r].reshape(1), qkv, table, length)
            kept[r] = probs
            blocks[r] = hop(attended_seq, r) if r else attended_seq
    else:
        seqs = []
        for s in range(sequences):
            attended_seq, kept[s] = attend_fwd(jnp.full((1,), s, jnp.int32), qkv, table, length)
            seqs.append(attended_seq)
        attended_all = jnp.concatenate(seqs, axis=0).reshape(replicas, own_rows, head_cols)
        attended_all = lax.all_to_all(attended_all, "head", split_axis=0, concat_axis=0, tiled=True)
        blocks = [attended_all[i] for i in range(replicas)]
    attended = jnp.concatenate(blocks, axis=1)

    branch = jnp.dot(attended, w_out_cat, preferred_element_type=F32)
    start_own = me * own_rows
    inputs_own = lax.dynamic_slice_in_dim(block_input, start_own, own_rows, 0).astype(F32)
    mixed = inputs_own + branch
    normed2_full, norm2_pull = jax.vjp(rms_norm, mixed, norm2_gain)
    normed2 = normed2_full.astype(BF)
    logits = jnp.dot(normed2, w_router, preferred_element_type=F32)
    expert_range = jnp.arange(experts, dtype=jnp.int32)
    chosen = (expert_ids[:, :, None] == expert_range[None, None, :]).astype(F32)
    gates = jax.nn.softmax(jnp.sum(chosen * logits[:, None, :], axis=2), axis=-1)

    def slot_gates_of(places, values):
        terms = sum(
            jnp.where(places[:, k : k + 1] == slot_range, values[:, k : k + 1], 0.0)
            for k in range(2)
        )
        return jnp.sum(terms, axis=0)

    rows_here = exchange(contract(both, normed2, 0, 0).astype(BF))
    gates_here = exchange(slot_gates_of(dest, gates))
    normed2_far = lax.ppermute(normed2, "head", far_perm)
    gates_far_own = lax.ppermute(gates, "head", far_perm)
    rows_far = exchange(contract(both_far, normed2_far, 0, 0).astype(BF))
    gates_far = exchange(slot_gates_of(dest_far, gates_far_own))

    hidden_here, ggp_here, gup_here = expert_forward(
        rows_here, gate_w, up_w, unscaled_here, gates_here
    )
    returned = jnp.dot(hidden_here, down_w, preferred_element_type=F32).astype(BF)
    came_back = exchange(returned)
    grad_routed = (contract(ggp_here, gate_w, 1, 1) + contract(gup_here, up_w, 1, 1)).astype(BF)
    grad_back = exchange(grad_routed)
    hidden_far, ggp_far, gup_far = expert_forward(rows_far, gate_w, up_w, unscaled_far, gates_far)
    scaled_here = (cot_here.astype(F32) * gates_here).astype(BF)
    scaled_far = (cot_far.astype(F32) * gates_far).astype(BF)

    low = me % far
    high = me // far

    def reduced(lefts, rights):
        rows = lefts[0].shape[1] // replicas

        def part(at):
            return sum(
                contract(lax.dynamic_slice_in_dim(left, at * rows, rows, 1), right, 0, 0)
                for left, right in zip(lefts, rights)
            )

        if far == 2:
            sent = hop(part(high * far + (1 - low)).astype(BF), 1)
            return (part(me) + sent.astype(F32))[None]
        whole = jnp.concatenate([part(high * far + i) for i in range(far)], axis=0).astype(BF)
        member = [[h * far + i for i in range(far)] for h in range(2)]
        return lax.psum_scatter(
            whole, "head", scatter_dimension=0, axis_index_groups=member, tiled=True
        ).astype(F32)[None]

    grad_down_w = reduced((hidden_here, hidden_far), (scaled_here, scaled_far))
    grad_gate_w = reduced((rows_here, rows_far), (ggp_here, ggp_far))
    grad_up_w = reduced((rows_here, rows_far), (gup_here, gup_far))

    chosen_rows = [jnp.dot(pick, came_back, preferred_element_type=F32) for pick in picks]
    output = mixed + sum(gates[:, k : k + 1] * chosen_rows[k] for k in range(2))
    grad_output = cotangent.astype(F32)
    grad_gates = jnp.stack([jnp.sum(grad_output * rows, axis=1) for rows in chosen_rows], axis=1)
    grad_normed2 = jnp.dot(both, grad_back, preferred_element_type=F32)
    grad_picked = gates * (grad_gates - jnp.sum(gates * grad_gates, axis=1, keepdims=True))
    grad_logits = jnp.sum(chosen * grad_picked[:, :, None], axis=1)
    grad_normed2 = grad_normed2 + contract(grad_logits, w_router.astype(F32), 1, 1, HIGH)
    grad_router = contract(normed2.astype(F32), grad_logits, 0, 0, HIGH)
    grad_mixed, grad_norm2 = norm2_pull(grad_normed2)
    grad_mixed = grad_mixed + grad_output
    grad_branch = grad_mixed.astype(BF)

    grad_wout = contract(attended, grad_branch, 0, 0).astype(BF)
    grad_wout = grad_wout.reshape(replicas, groups, out_rows, width)
    grad_wout = lax.psum_scatter(grad_wout, "dp", scatter_dimension=1, tiled=True)[:, 0]
    if stepwise:
        grad_wout = sum(
            (hop(grad_wout[r], r) if r else grad_wout[r]).astype(F32) for r in range(replicas)
        ).astype(BF)
    else:
        grad_wout = lax.psum_scatter(
            grad_wout.reshape(replicas * out_rows, width), "head", scatter_dimension=0, tiled=True
        )
    grad_out_proj = lax.all_gather(grad_wout, "dp", axis=0, tiled=True).astype(F32)

    grad_heads = contract(grad_branch, w_out_cat, 1, 1).astype(BF)
    sums = jnp.zeros((heads_here, TILE, 2 * length), F32)
    grad_blocks = [grad_heads[:, i * head_cols : (i + 1) * head_cols] for i in range(replicas)]
    grad_total = None
    weight_terms = []
    if stepwise:
        arrived = [hop(grad_blocks[r], r) if r else grad_blocks[0] for r in range(replicas)]
        for r in (0, 2, 3, 1):
            grad_qkv, sums = attend_bwd(order[r].reshape(1), qkv, arrived[r], kept[r], sums, length)
            normed_seq = lax.dynamic_slice_in_dim(normed, order[r] * length, length, 0)
            weight_terms.append(contract(normed_seq, grad_qkv, 0, 0))
            mine = hop(grad_qkv, r) if r else grad_qkv
            weight = lax.dynamic_index_in_dim(w_qkv_all, order[r], 0, keepdims=False)
            term = contract(mine, weight, 1, 1)
            grad_total = term if grad_total is None else grad_total + term
        grad_normed = grad_total
        grad_qkv_w = sum(weight_terms)
    else:
        stacked = jnp.stack(grad_blocks, axis=0)
        stacked = lax.all_to_all(stacked, "head", split_axis=0, concat_axis=0, tiled=True)
        stacked = stacked.reshape(group_rows, head_cols)
        seqs = []
        for s in range(sequences):
            grad_seq = stacked[s * length : (s + 1) * length]
            grad_qkv, sums = attend_bwd(
                jnp.full((1,), s, jnp.int32), qkv, grad_seq, kept[s], sums, length
            )
            seqs.append(grad_qkv)
        grad_qkv = jnp.concatenate(seqs, axis=0)
        grad_qkv_w = contract(normed, grad_qkv, 0, 0)
        grad_qkv = lax.all_to_all(
            grad_qkv.reshape(replicas, own_rows, 3 * head_cols),
            "head",
            split_axis=0,
            concat_axis=0,
            tiled=True,
        )
        grad_normed = sum(contract(grad_qkv[i], w_qkv_all[i], 1, 1) for i in range(replicas))

    _, norm1_pull = jax.vjp(rms_norm, inputs_own, norm1_gain)
    grad_first, grad_norm1 = norm1_pull(grad_normed)
    grad_input = grad_mixed + grad_first
    grad_bias = contract(unskew(sums), line, 1, 1, HIGH)
    grad_qkv_w, grad_bias = lax.psum((grad_qkv_w.astype(BF), grad_bias), "dp")
    grad_qkv_w = grad_qkv_w.astype(F32)
    grad_norm1, grad_norm2, grad_router = lax.psum(
        (grad_norm1, grad_norm2, grad_router), ("dp", "head")
    )
    return (
        output,
        grad_input,
        grad_norm1,
        grad_qkv_w[:, :head_cols],
        grad_qkv_w[:, head_cols : 2 * head_cols],
        grad_qkv_w[:, 2 * head_cols :],
        grad_out_proj,
        jnp.transpose(grad_bias),
        grad_norm2,
        grad_router,
        grad_gate_w,
        grad_up_w,
        grad_down_w,
    )


def body(*args):
    block_input, cotangent, rel_bucket, pos_bias, w_gate, w_router = (
        args[0],
        args[1],
        args[4],
        args[10],
        args[13],
        args[12],
    )
    own_rows = cotangent.shape[0]
    length = (rel_bucket.shape[0] + 1) // 2
    replicas, groups = lax.axis_size("head"), lax.axis_size("dp")
    experts = w_router.shape[1]
    capacity = 5 * 2 * own_rows // (4 * experts)
    stepwise = (
        own_rows == length
        and block_input.shape[0] == replicas * length
        and replicas == 4
        and groups == 8
        and experts == groups
        and capacity % 16 == 0
        and pos_bias.shape[1] in (2, 4, 6)
        and w_gate.shape[2] % 256 == 0
    )
    return body_steps(*args) if stepwise else body_plain(*args)


def body_steps(
    block_input,
    cotangent,
    expert_ids,
    priority,
    rel_bucket,
    norm1_gain,
    w_query,
    w_key,
    w_value,
    w_out,
    pos_bias,
    norm2_gain,
    w_router,
    w_gate,
    w_up,
    w_down,
):
    group_rows, width = block_input.shape
    own_rows = cotangent.shape[0]
    buckets, heads_here = pos_bias.shape
    head_cols = w_query.shape[1]
    length = (rel_bucket.shape[0] + 1) // 2
    experts = w_router.shape[1]
    capacity = 5 * 2 * own_rows // (4 * experts)
    slot_count = experts * capacity
    replicas, groups = lax.axis_size("head"), lax.axis_size("dp")
    me, dp_at = lax.axis_index("head"), lax.axis_index("dp")

    dest = route_slots(expert_ids, priority[0], experts, capacity)
    bits = (dest // capacity) ^ dp_at
    position = sum(p * (bits == offset).astype(jnp.int32) for p, offset in enumerate(OFFSETS))
    mixed_dest = jnp.where(
        dest < slot_count,
        position * capacity + dest % capacity,
        slot_count,
    )
    routing = jnp.concatenate([mixed_dest, expert_ids], axis=1)
    routing_rows = jnp.pad(routing.T, ((0, 4), (0, 0)))
    routing_cols = jnp.pad(routing, ((0, 0), (0, 4)))
    router_wide = jnp.pad(w_router, ((0, 0), (0, TILE - experts)))
    line = (rel_bucket[::-1][None, :] == jnp.arange(buckets, dtype=jnp.int32)[:, None]).astype(F32)
    line = jnp.pad(line, ((0, 0), (1, 0)))
    input_weights = (w_query, w_key, w_value)
    (
        attended,
        probs,
        cot_here,
        normed,
        qkv,
        w_cat,
        cot_far,
        routing_far,
        mixed,
        normed2,
    ) = attend_all(
        block_input,
        norm1_gain[None, :],
        input_weights,
        contract(pos_bias, line, 0, 0, HIGH)[:, None, :],
        cotangent,
        routing_rows,
        w_out,
        norm2_gain[None, :],
        groups,
        capacity,
    )

    gate_w, up_w, down_w = w_gate[0], w_up[0], w_down[0]
    tile = 256
    (
        rows_here,
        hidden_here,
        ggp_here,
        gup_here,
        scaled_here,
        back,
        grad_back,
        slot_slope,
        normed2_far,
        cot_far_rest,
    ) = expert_stage(
        normed2,
        routing_rows,
        cot_here,
        router_wide,
        gate_w,
        up_w,
        down_w,
        cotangent,
        groups,
        capacity,
        tile,
    )

    gates, grad_mixed, grad_branch, grad_heads, grad_router, grad_norm2, cot_far_last = combine(
        grad_back.reshape(slot_count, width),
        slot_slope.reshape(slot_count, TILE),
        routing_cols,
        mixed,
        normed2,
        cotangent,
        router_wide,
        norm2_gain[None, :],
        w_cat,
        experts,
    )

    far_rows, far_scaled, carry, part_sum, grad_qkv_w, grad_wout, lines = attend_back(
        normed2_far,
        (cot_far, cot_far_rest, cot_far_last),
        routing_far,
        router_wide,
        grad_heads,
        qkv,
        probs,
        normed,
        input_weights,
        attended,
        grad_branch,
        groups,
        capacity,
    )

    (
        wide_kept,
        wide_came,
        tall_kept,
        tall_came,
        grad_qkv_w,
        grad_out_proj,
        summed,
        grad_first,
        expert_sum,
        _,
    ) = last_stage(
        (far_rows.reshape(slot_count, width), far_scaled.reshape(slot_count, width)),
        (rows_here.reshape(slot_count, width), scaled_here.reshape(slot_count, width)),
        (gates, routing_cols, norm1_gain[None, :]),
        (gate_w, up_w, down_w),
        (ggp_here, gup_here),
        hidden_here,
        (
            grad_qkv_w.reshape(groups, width // groups, 3 * head_cols),
            grad_wout.reshape(replicas, groups, head_cols // groups, width),
        ),
        (carry, part_sum, block_input, back),
        (grad_norm2, grad_router, lines),
        tile,
    )
    results = finish(
        (wide_kept, wide_came),
        (tall_kept, tall_came),
        grad_qkv_w,
        grad_out_proj,
        (mixed, expert_sum, grad_mixed, grad_first),
        summed,
        line.astype(BF),
        heads_here,
    )
    output, grad_input, grad_query_w, grad_key_w, grad_value_w, grad_out_proj = results[:6]
    grad_gate_w, grad_up_w, grad_down_w, grad_norm1, grad_norm2, grad_bias, grad_router = results[6:]
    return (
        output,
        grad_input,
        grad_norm1[0],
        grad_query_w,
        grad_key_w,
        grad_value_w,
        grad_out_proj,
        jnp.transpose(grad_bias),
        grad_norm2[0],
        jnp.transpose(grad_router),
        grad_gate_w[None],
        grad_up_w[None],
        grad_down_w[None],
    )


def solution(mesh):
    placed = (
        P("dp", None),
        P(("dp", "head"), None),
        P(("dp", "head"), None),
        P(("dp", "head"), None),
        P(),
        P(),
        P(None, "head"),
        P(None, "head"),
        P(None, "head"),
        P("head", None),
        P(None, "head"),
        P(),
        P(),
        P("dp", None, None),
        P("dp", None, None),
        P("dp", None, None),
    )
    return jax.shard_map(
        body,
        mesh=mesh,
        in_specs=placed,
        out_specs=(
            P(("dp", "head"), None),
            P(("dp", "head"), None),
            P(),
            P(None, "head"),
            P(None, "head"),
            P(None, "head"),
            P("head", None),
            P(None, "head"),
            P(),
            P(),
            P("dp", "head", None),
            P("dp", "head", None),
            P("dp", "head", None),
        ),
        check_vma=False,
    )
```

```python
import functools

import jax
import jax.numpy as jnp
from jax import lax
from jax.experimental import pallas as pl
from jax.experimental.pallas import tpu as pltpu
from jax.sharding import PartitionSpec as P

EPS = 1e-06
SCALE = 0.125
HIGH = lax.Precision.HIGHEST
TILE = 128
BF = jnp.bfloat16
F32 = jnp.float32
VMEM_LIMIT = 48 << 20
VMEM_MOST = 60 << 20
GELU_A = 0.7978845608028654
GELU_B = 0.044715
OFFSETS = [0, 1, 6, 7, 2, 4, 3, 5]
PEERS = [4, 5, 6, 7, 2, 3, 1]


def rms_norm(value, gain):
    return value * lax.rsqrt(jnp.mean(value * value, axis=-1, keepdims=True) + EPS) * gain


def geglu(gate, up_part):
    return jax.nn.gelu(gate) * up_part


def contract(left, right, left_dim, right_dim, precision=None):
    return lax.dot_general(
        left,
        right,
        (((left_dim,), (right_dim,)), ((), ())),
        precision=precision,
        preferred_element_type=jnp.float32,
    )


def route_slots(chosen, ranks, experts, capacity):
    count = chosen.shape[0]
    keys = jnp.concatenate([ranks, ranks + count])
    wanted = jnp.concatenate([chosen[:, 0], chosen[:, 1]])
    smaller = (wanted[:, None] == wanted[None, :]) & (keys[None, :] < keys[:, None])
    place = jnp.sum(smaller.astype(jnp.int32), axis=1)
    dest = jnp.where(place < capacity, wanted * capacity + place, experts * capacity)
    return jnp.stack([dest[:count], dest[count:]], axis=1)


def skew_kernel(line_ref, table_ref):
    heads, rows, cols = table_ref.shape
    row = lax.broadcasted_iota(jnp.int32, (8, cols), 0)
    for h in range(heads):
        value = jnp.broadcast_to(line_ref[h], (8, cols))
        for shift in (1, 2, 4):
            value = jnp.where((row & shift) != 0, pltpu.roll(value, shift, 1), value)
        table_ref[h, :8] = value
        done = 8
        while done < rows:
            table_ref[h, done : 2 * done] = pltpu.roll(table_ref[h, :done], done, 1)
            done *= 2


def unskew_kernel(table_ref, line_ref):
    heads, rows, cols = table_ref.shape
    row = lax.broadcasted_iota(jnp.int32, (8, cols), 0)
    for h in range(heads):
        value, left = table_ref[h], rows // 2
        while left >= 8:
            value = value[:left] + pltpu.roll(value[left:], cols - left, 1)
            left //= 2
        for shift in (1, 2, 4):
            value = jnp.where((row & shift) != 0, pltpu.roll(value, cols - shift, 1), value)
        line_ref[h] = jnp.sum(value, axis=0, keepdims=True)


def skew(line):
    heads, cols = line.shape
    return pl.pallas_call(
        skew_kernel,
        out_shape=jax.ShapeDtypeStruct((heads, TILE, cols), F32),
        compiler_params=pltpu.CompilerParams(vmem_limit_bytes=VMEM_LIMIT),
        name="skew",
    )(line[:, None, :])


def unskew(table):
    heads, _, cols = table.shape
    return pl.pallas_call(
        unskew_kernel,
        out_shape=jax.ShapeDtypeStruct((heads, 1, cols), F32),
        compiler_params=pltpu.CompilerParams(vmem_limit_bytes=VMEM_LIMIT),
        name="unskew",
    )(table)[:, 0]


def lanes_of(shape, half, part):
    lane = lax.broadcasted_iota(jnp.int32, shape, 1)
    return (lane >= half) if part else (lane < half)


def attend_fwd_kernel(seq_ref, q_ref, k_ref, v_ref, table_ref, out_ref, probs_ref, acc_ref):
    del seq_ref
    length, lanes = q_ref.shape
    half = lanes // 2
    chunk = 2 * TILE
    key = k_ref[...]
    value_t = v_ref[...].T
    for part in range(2):
        query = jnp.where(lanes_of((length, lanes), half, part), q_ref[...] * SCALE, 0).astype(BF)
        for c in range(length // chunk):
            cols = slice(c * chunk, (c + 1) * chunk)
            scores = contract(key, query[cols], 1, 1)
            pieces = []
            for kb in range(length // TILE):
                at = length - TILE * kb + chunk * c
                pieces.append(
                    scores[kb * TILE : (kb + 1) * TILE] + table_ref[part, :, at : at + chunk]
                )
            scores = jnp.concatenate(pieces, axis=0)
            top = jnp.max(scores, axis=0, keepdims=True)
            shifted = jnp.exp(scores - top)
            total = jnp.sum(shifted, axis=0, keepdims=True)
            probs = (shifted * (1.0 / total)).astype(BF)
            probs_ref[part, :, cols] = probs
            acc_ref[part * half : (part + 1) * half, cols] = jnp.dot(
                value_t[part * half : (part + 1) * half], probs, preferred_element_type=F32
            )
    out_ref[...] = acc_ref[...].T.astype(BF)


def attend_fwd(seq, qkv, table, length):
    heads, _, width = table.shape
    columns = qkv.shape[1] // 3
    pairs = heads // 2
    lanes = columns // pairs
    spec = [
        pl.BlockSpec((length, lanes), lambda p, s, j=j: (s[0], j * pairs + p)) for j in range(3)
    ]
    return pl.pallas_call(
        attend_fwd_kernel,
        out_shape=(
            jax.ShapeDtypeStruct((length, columns), BF),
            jax.ShapeDtypeStruct((heads, length, length), BF),
        ),
        grid_spec=pltpu.PrefetchScalarGridSpec(
            num_scalar_prefetch=1,
            grid=(pairs,),
            in_specs=spec + [pl.BlockSpec((2, TILE, width), lambda p, s: (p, 0, 0))],
            out_specs=[
                pl.BlockSpec((length, lanes), lambda p, s: (0, p)),
                pl.BlockSpec((2, length, length), lambda p, s: (p, 0, 0)),
            ],
            scratch_shapes=[pltpu.VMEM((lanes, length), F32)],
        ),
        compiler_params=pltpu.CompilerParams(vmem_limit_bytes=VMEM_LIMIT),
        cost_estimate=pl.CostEstimate(
            flops=heads * 8 * length * length * lanes,
            bytes_accessed=heads * length * length * 2 + 8 * length * columns,
            transcendentals=heads * length * length,
        ),
        name="attend_fwd",
    )(seq, qkv, qkv, qkv, table)


def attend_bwd_kernel(
    seq_ref, q_ref, k_ref, v_ref, grad_ref, probs_ref, sums_in_ref, out_ref, sums_ref, acc_ref
):
    del seq_ref
    length, lanes = q_ref.shape
    half = lanes // 2
    chunk = 2 * TILE
    pair = pl.program_id(0)
    columns = out_ref.shape[1] // 3
    key_t = k_ref[...].T
    value = v_ref[...]
    sums_ref[...] = sums_in_ref[...]
    grad_keys, grad_values = [], []
    for part in range(2):
        mask = lanes_of((length, lanes), half, part)
        grad = jnp.where(mask, grad_ref[...], 0).astype(BF)
        grad_key = jnp.zeros((length, lanes), F32)
        grad_value = jnp.zeros((length, lanes), F32)
        for c in range(length // chunk):
            cols = slice(c * chunk, (c + 1) * chunk)
            grad_probs = contract(value, grad[cols], 1, 1)
            probs_low = probs_ref[part, :, cols]
            probs = probs_low.astype(F32)
            delta = jnp.sum(probs * grad_probs, axis=0, keepdims=True)
            grad_scores = (probs * (grad_probs - delta)).astype(BF)
            grad_value += jnp.dot(probs_low, grad_ref[cols, :], preferred_element_type=F32)
            grad_key += jnp.dot(grad_scores, q_ref[cols, :], preferred_element_type=F32)
            acc_ref[part * half : (part + 1) * half, cols] = jnp.dot(
                key_t[part * half : (part + 1) * half], grad_scores, preferred_element_type=F32
            )
            for kb in range(length // TILE):
                at = length - TILE * kb + chunk * c
                sums_ref[part, :, at : at + chunk] += grad_scores[
                    kb * TILE : (kb + 1) * TILE
                ].astype(F32)
        grad_keys.append(grad_key)
        grad_values.append(grad_value)
    first = lanes_of((length, lanes), half, 0)
    at = pl.multiple_of(pair * lanes, lanes)
    out_ref[:, pl.ds(at, lanes)] = (acc_ref[...].T * SCALE).astype(BF)
    at = pl.multiple_of(columns + pair * lanes, lanes)
    out_ref[:, pl.ds(at, lanes)] = (jnp.where(first, *grad_keys) * SCALE).astype(BF)
    at = pl.multiple_of(2 * columns + pair * lanes, lanes)
    out_ref[:, pl.ds(at, lanes)] = jnp.where(first, *grad_values).astype(BF)


def attend_bwd(seq, qkv, grad, probs, sums, length):
    heads, _, width = sums.shape
    columns = qkv.shape[1] // 3
    pairs = heads // 2
    lanes = columns // pairs
    spec = [
        pl.BlockSpec((length, lanes), lambda p, s, j=j: (s[0], j * pairs + p)) for j in range(3)
    ]
    sums_spec = pl.BlockSpec((2, TILE, width), lambda p, s: (p, 0, 0))
    return pl.pallas_call(
        attend_bwd_kernel,
        out_shape=(
            jax.ShapeDtypeStruct((length, 3 * columns), BF),
            jax.ShapeDtypeStruct(sums.shape, F32),
        ),
        grid_spec=pltpu.PrefetchScalarGridSpec(
            num_scalar_prefetch=1,
            grid=(pairs,),
            in_specs=spec
            + [
                pl.BlockSpec((length, lanes), lambda p, s: (0, p)),
                pl.BlockSpec((2, length, length), lambda p, s: (p, 0, 0)),
                sums_spec,
            ],
            out_specs=[pl.BlockSpec((length, 3 * columns), lambda p, s: (0, 0)), sums_spec],
            scratch_shapes=[pltpu.VMEM((lanes, length), F32)],
        ),
        compiler_params=pltpu.CompilerParams(vmem_limit_bytes=VMEM_LIMIT),
        cost_estimate=pl.CostEstimate(
            flops=heads * 16 * length * length * lanes,
            bytes_accessed=heads * length * length * 2 + 16 * length * columns,
            transcendentals=0,
        ),
        name="attend_bwd",
    )(seq, qkv, qkv, qkv, grad, probs, sums)


def flipped(index, bits):
    out, step = index, 1
    while step <= bits:
        if bits & step:
            out = out + step * (1 - 2 * lax.rem(index // step, 2))
        step *= 2
    return out


def plane(d, position):
    return flipped(d, OFFSETS[position])


def greet(peers):
    barrier = pltpu.get_barrier_semaphore()
    for peer in peers:
        pl.semaphore_signal(barrier, inc=1, device_id=peer, device_id_type=pl.DeviceIdType.MESH)
    pl.semaphore_wait(barrier, len(peers))


def remote(source, target, send_sem, recv_sem, peer):
    return pltpu.make_async_remote_copy(
        src_ref=source,
        dst_ref=target,
        send_sem=send_sem,
        recv_sem=recv_sem,
        device_id=peer,
        device_id_type=pl.DeviceIdType.MESH,
    )


def attend_all_kernel(
    input_hbm,
    gain_ref,
    query_hbm,
    key_hbm,
    value_hbm,
    line_ref,
    cot_hbm,
    routing_ref,
    w_out_hbm,
    gain2_ref,
    attended_out,
    probs_out,
    came_out,
    normed_out,
    qkv_out,
    w_cat_out,
    cot_far_out,
    routing_far_out,
    mixed_ref,
    normed2_ref,
    input_ref,
    weight_ref,
    cot_ref,
    w_out_ref,
    table_ref,
    sends,
    acc_ref,
    block_ref,
    hold_ref,
    normed_ref,
    qkv_ref,
    attended_ref,
    w_cat,
    w_land,
    row_send,
    row_recv,
    hop_send,
    hop_recv,
    w_send,
    w_recv,
    plane_send,
    plane_recv,
    core_send,
    core_recv,
    far_send,
    far_recv,
    hold_sem,
    own_sem,
    load_sem,
):
    z, d = lax.axis_index("head"), lax.axis_index("dp")
    heads, _, _ = table_ref.shape
    replicas, length, columns = block_ref.shape
    groups, capacity, _ = sends.shape
    width = input_ref.shape[1]
    part_rows = w_land.shape[1]
    pairs = heads // 2
    lanes = columns // pairs
    half = lanes // 2
    chunk = 2 * TILE
    hops = [3, 2, 1]
    cot_load = pltpu.make_async_copy(cot_hbm, cot_ref, load_sem.at[0])
    w_out_load = pltpu.make_async_copy(w_out_hbm, w_out_ref, load_sem.at[1])
    weight_loads = [
        pltpu.make_async_copy(
            source, weight_ref.at[:, pl.ds(i * columns, columns)], load_sem.at[2 + i]
        )
        for i, source in enumerate((query_hbm, key_hbm, value_hbm))
    ]
    input_loads = {}
    for r in [3, 2, 1, 0]:
        span = pl.ds(pl.multiple_of(flipped(z, r) * length, length), length)
        input_loads[r] = pltpu.make_async_copy(
            input_hbm.at[span], input_ref.at[span], load_sem.at[5 + r]
        )
    for copy in [cot_load, input_loads[3]] + weight_loads:
        copy.start()
    for copy in [input_loads[2], input_loads[1], input_loads[0], w_out_load]:
        copy.start()
    greet([{"dp": plane(d, o)} for o in PEERS] + [{"head": flipped(z, r)} for r in hops])
    copies = []

    def launch(*what):
        copy = remote(*what)
        copy.start()
        copies.append(copy)
        return copy

    piece = w_out_hbm.at[pl.ds(pl.multiple_of(d * part_rows, part_rows), part_rows), :]
    w_hops = {}
    for r in hops:
        w_hops[r] = remote(piece, w_land.at[r], w_send.at[r], w_recv.at[r], {"head": flipped(z, r)})
        w_hops[r].start()
    cot_load.wait()
    half_plane = groups // 2

    def dispatch(start):
        span = slice(start, start + half_plane)
        first, second = selector(routing_ref, start * capacity, half_plane * capacity)
        sends[span, :, :width] = (
            jnp.dot((first + second).astype(BF), cot_ref[...], preferred_element_type=F32)
            .astype(BF)
            .reshape(half_plane, capacity, width)
        )
        sends[span, :, width:] = slot_signs(routing_ref, first, second).reshape(
            half_plane, capacity, TILE
        )

    def send_rows(start):
        for o in range(start, start + half_plane):
            if o:
                launch(
                    sends.at[o], came_out.at[o], row_send.at[o], row_recv.at[o], {"dp": plane(d, o)}
                )

    chips = [o for o, bits in enumerate(OFFSETS) if o and bits % 2 == 0]
    plane_copies = {}

    def w_rows(s, o):
        at = s * columns + plane(d, o) * part_rows
        return pl.ds(pl.multiple_of(at, part_rows), part_rows)

    dispatch(half_plane)
    for s in hops:
        w_hops[s].wait()
        at = w_rows(s, 0)
        w_cat[at, :] = w_land[s]
        for o in chips:
            plane_copies[s, o] = remote(
                w_land.at[s],
                w_cat.at[at, :],
                plane_send.at[s, o],
                plane_recv.at[s, o],
                {"dp": plane(d, o)},
            )
            plane_copies[s, o].start()
    send_rows(half_plane)
    dispatch(0)
    send_rows(0)
    own = pltpu.make_async_copy(sends.at[0], came_out.at[0], own_sem.at[0])
    own.start()
    far = {"head": flipped(z, 2)}
    launch(routing_ref, routing_far_out, far_send.at[0], far_recv.at[0], far)
    early = pl.ds(0, cot_far_out.shape[0])
    launch(cot_hbm.at[early], cot_far_out, far_send.at[1], far_recv.at[1], far)
    skew_kernel(line_ref, table_ref)
    w_out_load.wait()
    w_cat[:columns, :] = w_out_ref[...]

    moves = []
    for turn, r in enumerate(reversed(range(replicas))):
        start = flipped(z, r) * length
        slot = turn % 2
        if turn >= 2:
            for move in moves[turn - 2]:
                move.wait()

        input_loads[r].wait()

        def norm_step(i, carry, start=start, slot=slot):
            rows = pl.multiple_of(start + i * TILE, TILE)
            value = input_ref[pl.ds(rows, TILE), :].astype(F32)
            value = rms_norm(value, gain_ref[...])
            normed_ref[slot, pl.ds(pl.multiple_of(i * TILE, TILE), TILE), :] = value.astype(BF)
            return carry

        lax.fori_loop(0, length // TILE, norm_step, 0)
        if turn == 0:
            for copy in weight_loads:
                copy.wait()
        qkv_ref[slot] = jnp.dot(
            normed_ref[slot], weight_ref[...], preferred_element_type=F32
        ).astype(BF)

        def pair_step(pair, carry, slot=slot, r=r):
            def part_of(j):
                at = pl.multiple_of(j * columns + pair * lanes, lanes)
                return qkv_ref[slot, :, pl.ds(at, lanes)]

            key = part_of(1)
            value_t = part_of(2).T
            scaled = part_of(0) * SCALE
            for part in range(2):
                query = jnp.where(lanes_of((length, lanes), half, part), scaled, 0).astype(BF)
                for c in range(length // chunk):
                    cols = slice(c * chunk, (c + 1) * chunk)
                    scores = contract(key, query[cols], 1, 1)
                    pieces = []
                    for kb in range(length // TILE):
                        at = length - TILE * kb + chunk * c
                        pieces.append(
                            scores[kb * TILE : (kb + 1) * TILE]
                            + table_ref[pair * 2 + part, :, at : at + chunk]
                        )
                    scores = jnp.concatenate(pieces, axis=0)
                    top = jnp.max(scores, axis=0, keepdims=True)
                    shifted = jnp.exp(scores - top)
                    total = jnp.sum(shifted, axis=0, keepdims=True)
                    probs = (shifted * (1.0 / total)).astype(BF)
                    hold_ref[slot, pair * 2 + part, :, cols] = probs
                    acc_ref[part * half : (part + 1) * half, cols] = jnp.dot(
                        value_t[part * half : (part + 1) * half],
                        probs,
                        preferred_element_type=F32,
                    )
            at = pl.multiple_of(pair * lanes, lanes)
            block_ref[r, :, pl.ds(at, lanes)] = acc_ref[...].T.astype(BF)
            return carry

        lax.fori_loop(0, pairs, pair_step, 0)
        moves.append(
            [
                pltpu.make_async_copy(ref.at[slot], out.at[r], hold_sem.at[i, slot])
                for i, (ref, out) in enumerate(
                    ((hold_ref, probs_out), (normed_ref, normed_out), (qkv_ref, qkv_out))
                )
            ]
        )
        for move in moves[-1]:
            move.start()
        if r:
            launch(
                block_ref.at[r],
                attended_ref.at[:, pl.ds(r * columns, columns)],
                hop_send.at[r],
                hop_recv.at[r],
                {"head": flipped(z, r)},
            )
        else:
            attended_ref[:, :columns] = block_ref[0]
        if turn == 1:
            for s in hops:
                for o in [0] + chips:
                    if o:
                        plane_copies[s, o].wait_recv()
                    piece = w_cat.at[w_rows(s, o), :]
                    launch(piece, piece, core_send.at[s, o], core_recv.at[s, o], {"dp": plane(d, 1)})
    for copy in plane_copies.values():
        copy.wait_send()
    for copy in copies:
        copy.wait()
    outs = [
        pltpu.make_async_copy(attended_ref, attended_out, own_sem.at[1]),
        pltpu.make_async_copy(w_cat, w_cat_out, own_sem.at[2]),
    ]
    for copy in outs:
        copy.start()

    mixed_ref[...] = jnp.dot(attended_ref[...], w_cat[...], preferred_element_type=F32)

    def mixed_step(i, carry):
        at = pl.multiple_of(i * TILE, TILE)
        span = pl.ds(at, TILE)
        rows = pl.multiple_of(z * length + at, TILE)
        value = mixed_ref[span, :] + input_ref[pl.ds(rows, TILE), :].astype(F32)
        mixed_ref[span, :] = value
        normed2_ref[span, :] = rms_norm(value, gain2_ref[...]).astype(BF)
        return carry

    lax.fori_loop(0, length // TILE, mixed_step, 0)
    for move in moves[-2] + moves[-1] + outs + [own]:
        move.wait()


def attend_all(inputs, gain, weights, line, cot, routing, w_out, gain2, groups, capacity):
    heads, _, table_width = line.shape
    width = inputs.shape[1]
    length = cot.shape[0]
    replicas = inputs.shape[0] // length
    columns = weights[0].shape[1]
    lanes = 2 * columns // heads
    part_rows = columns // groups
    vmem = pl.BlockSpec(memory_space=pltpu.VMEM)
    hbm = pl.BlockSpec(memory_space=pl.ANY)
    came_shape = (groups, capacity, width + TILE)
    plane_sem = pltpu.SemaphoreType.DMA((groups,))
    hop_sem = pltpu.SemaphoreType.DMA((replicas,))
    both_sem = pltpu.SemaphoreType.DMA((replicas, groups))
    two_sem = pltpu.SemaphoreType.DMA((2,))
    return pl.pallas_call(
        attend_all_kernel,
        out_shape=(
            jax.ShapeDtypeStruct((length, replicas * columns), BF),
            jax.ShapeDtypeStruct((replicas, heads, length, length), BF),
            jax.ShapeDtypeStruct(came_shape, BF),
            jax.ShapeDtypeStruct((replicas, length, width), BF),
            jax.ShapeDtypeStruct((replicas, length, 3 * columns), BF),
            jax.ShapeDtypeStruct((replicas * columns, width), BF),
            jax.ShapeDtypeStruct((length // 2, width), BF),
            jax.ShapeDtypeStruct(routing.shape, routing.dtype),
            jax.ShapeDtypeStruct((length, width), F32),
            jax.ShapeDtypeStruct((length, width), BF),
        ),
        in_specs=[hbm, vmem, hbm, hbm, hbm, vmem, hbm, vmem, hbm, vmem],
        out_specs=[hbm] * 8 + [vmem] * 2,
        scratch_shapes=[
            pltpu.VMEM(inputs.shape, BF),
            pltpu.VMEM((width, 3 * columns), BF),
            pltpu.VMEM(cot.shape, BF),
            pltpu.VMEM(w_out.shape, BF),
            pltpu.VMEM((heads, TILE, table_width), F32),
            pltpu.VMEM(came_shape, BF),
            pltpu.VMEM((lanes, length), F32),
            pltpu.VMEM((replicas, length, columns), BF),
            pltpu.VMEM((2, heads, length, length), BF),
            pltpu.VMEM((2, length, width), BF),
            pltpu.VMEM((2, length, 3 * columns), BF),
            pltpu.VMEM((length, replicas * columns), BF),
            pltpu.VMEM((replicas * columns, width), BF),
            pltpu.VMEM((replicas, part_rows, width), BF),
            plane_sem,
            plane_sem,
            hop_sem,
            hop_sem,
            hop_sem,
            hop_sem,
            both_sem,
            both_sem,
            both_sem,
            both_sem,
            two_sem,
            two_sem,
            pltpu.SemaphoreType.DMA((3, 2)),
            pltpu.SemaphoreType.DMA((3,)),
            pltpu.SemaphoreType.DMA((9,)),
        ],
        compiler_params=pltpu.CompilerParams(
            vmem_limit_bytes=VMEM_MOST, collective_id=1, has_side_effects=True
        ),
        cost_estimate=pl.CostEstimate(
            flops=replicas * heads * 8 * length * length * lanes,
            bytes_accessed=replicas * heads * length * length * 4,
            transcendentals=replicas * heads * length * length,
        ),
        name="attend_all",
    )(inputs, gain, *weights, line, cot, routing, w_out, gain2)


def selector(routing, start, count):
    slot = lax.broadcasted_iota(jnp.int32, (count, routing.shape[1]), 0) + start
    return [jnp.where(slot == routing[k : k + 1], 1.0, 0.0) for k in range(2)]


def slot_signs(routing, first, second):
    lane = lax.broadcasted_iota(jnp.int32, (TILE, routing.shape[1]), 0)
    signs = jnp.where(lane == routing[3:4], 1.0, 0.0) - jnp.where(lane == routing[2:3], 1.0, 0.0)
    return contract((first - second).astype(BF), signs.astype(BF), 1, 1).astype(BF)


def token_selector(routing, slots):
    slot = lax.broadcasted_iota(jnp.int32, (routing.shape[0], slots), 1)
    return [jnp.where(slot == routing[:, k : k + 1], 1.0, 0.0) for k in range(2)]


def expert_tile(rows, scaled, gate_w, up_w, down_w):
    gate = jnp.dot(rows, gate_w, preferred_element_type=F32)
    up_part = jnp.dot(rows, up_w, preferred_element_type=F32)
    grad_hidden = contract(scaled, down_w, 1, 1)
    square = gate * gate
    bend = jnp.tanh(gate * (GELU_A + GELU_A * GELU_B * square))
    half = 0.5 + 0.5 * bend
    active = gate * half
    slope = half + 0.5 * gate * (1.0 - bend * bend) * (GELU_A + 3.0 * GELU_A * GELU_B * square)
    hidden = (active * up_part).astype(BF)
    grad_gate = (grad_hidden * up_part * slope).astype(BF)
    grad_up = (grad_hidden * active).astype(BF)
    return hidden, grad_gate, grad_up


def scaled_rows(rows, extended, router, width):
    logits = jnp.dot(rows, router, preferred_element_type=F32)
    sign = extended[:, width:].astype(F32)
    gap = jnp.sum(logits * sign, axis=1, keepdims=True)
    return (extended[:, :width].astype(F32) * (1.0 / (1.0 + jnp.exp(gap)))).astype(BF)


def expert_kernel(
    width,
    tile,
    normed_ref,
    routing_ref,
    cot_ref,
    router_ref,
    gate_hbm,
    up_hbm,
    down_hbm,
    cot_hbm,
    rows_out,
    hidden_out,
    grad_gate_out,
    grad_up_out,
    scaled_out,
    back_out,
    grad_back_out,
    slope_out,
    far_out,
    cot_far_out,
    gate_w,
    up_w,
    down_w,
    rows,
    sends,
    back,
    grad_back,
    slopes,
    hidden,
    grad_gate,
    grad_up,
    scaled,
    weight_sem,
    row_send,
    row_recv,
    slope_send,
    slope_recv,
    grad_send,
    grad_recv,
    unit_sem,
    keep_sem,
    far_sem,
):
    z, d = lax.axis_index("head"), lax.axis_index("dp")
    far = {"head": flipped(z, 2)}
    groups, capacity, _ = rows.shape
    units = gate_w.shape[1]
    tiles = units // tile
    count = 2 * capacity

    def weights_of(t):
        at = t * tile if isinstance(t, int) else pl.multiple_of(t * tile, tile)
        return [
            pltpu.make_async_copy(
                gate_hbm.at[:, pl.ds(at, tile)], gate_w.at[:, pl.ds(at, tile)], weight_sem.at[0, t]
            ),
            pltpu.make_async_copy(
                up_hbm.at[:, pl.ds(at, tile)], up_w.at[:, pl.ds(at, tile)], weight_sem.at[1, t]
            ),
            pltpu.make_async_copy(
                down_hbm.at[pl.ds(at, tile), :], down_w.at[pl.ds(at, tile), :], weight_sem.at[2, t]
            ),
        ]

    def start_weights(t, carry):
        for copy in weights_of(t):
            copy.start()
        return carry

    lax.fori_loop(0, tiles, start_weights, 0)
    greet([{"dp": plane(d, o)} for o in PEERS] + [far])
    pending = []
    arrivals = {}

    for start, number in ((2, 2), (4, groups - 4), (0, 2)):
        first, second = selector(routing_ref, start * capacity, number * capacity)
        sends[start : start + number] = (
            jnp.dot((first + second).astype(BF), normed_ref[...], preferred_element_type=F32)
            .astype(BF)
            .reshape(number, capacity, width)
        )
        for o in range(start, start + number):
            if o:
                arrivals[o] = remote(
                    sends.at[o], rows.at[o], row_send.at[o], row_recv.at[o], {"dp": plane(d, o)}
                )
                arrivals[o].start()
    over = [
        remote(normed_ref, far_out, far_sem.at[0, 0], far_sem.at[0, 1], far),
        remote(
            cot_hbm.at[pl.ds(cot_far_out.shape[0], cot_far_out.shape[0])],
            cot_far_out,
            far_sem.at[1, 0],
            far_sem.at[1, 1],
            far,
        ),
    ]
    for copy in over:
        copy.start()
    rows[0] = sends[0]

    unit_copies = {}
    order = list(range(groups // 2))
    for turn, j in enumerate(order):
        pair = (2 * j, 2 * j + 1)
        slot = turn % 2
        for o in pair:
            if o:
                arrivals[o].wait_recv()
        if turn >= 2:
            for copy in unit_copies[order[turn - 2]]:
                copy.wait()
        here = rows[2 * j : 2 * j + 2].reshape(count, width)
        extended = cot_ref[2 * j : 2 * j + 2].reshape(count, cot_ref.shape[2])
        scaled[2 * j : 2 * j + 2] = scaled_rows(here, extended, router_ref[...], width).reshape(
            2, capacity, width
        )

        def wide_tile(at, size, j=j, slot=slot):
            values = expert_tile(
                rows[2 * j : 2 * j + 2].reshape(count, width),
                scaled[2 * j : 2 * j + 2].reshape(count, width),
                gate_w[:, pl.ds(at, size)],
                up_w[:, pl.ds(at, size)],
                down_w[pl.ds(at, size), :],
            )
            for ref, value in zip((hidden, grad_gate, grad_up), values):
                ref[slot, :, pl.ds(at, size)] = value

        def tile_step(t, carry, j=j):
            if j == 0:
                for i in range(2):
                    for copy in weights_of(2 * t + i):
                        copy.wait()
            wide_tile(pl.multiple_of(2 * t * tile, tile), 2 * tile)
            return carry

        lax.fori_loop(0, tiles // 2, tile_step, 0)
        if tiles % 2:
            if j == 0:
                for copy in weights_of(tiles - 1):
                    copy.wait()
            wide_tile((tiles - 1) * tile, tile)
        span = pl.ds(j * count, count)
        unit_copies[j] = [
            pltpu.make_async_copy(ref.at[slot], out.at[span], unit_sem.at[slot, i])
            for i, (ref, out) in enumerate(
                ((hidden, hidden_out), (grad_gate, grad_gate_out), (grad_up, grad_up_out))
            )
        ]
        for copy in unit_copies[j]:
            copy.start()

        def back_step(t, carry, j=j, slot=slot):
            cols = pl.ds(pl.multiple_of(t * 2 * tile, 2 * tile), 2 * tile)
            value = jnp.dot(hidden[slot], down_w[:, cols], preferred_element_type=F32)
            back[2 * j : 2 * j + 2, :, cols] = value.astype(BF).reshape(2, capacity, 2 * tile)
            return carry

        def grad_step(t, carry, j=j, slot=slot):
            cols = pl.ds(pl.multiple_of(t * 2 * tile, 2 * tile), 2 * tile)
            value = contract(grad_gate[slot], gate_w[cols, :], 1, 1) + contract(
                grad_up[slot], up_w[cols, :], 1, 1
            )
            grad_back[2 * j : 2 * j + 2, :, cols] = value.astype(BF).reshape(2, capacity, 2 * tile)
            return carry

        def give(buffer, out, send_sem, recv_sem, pair=pair):
            for o in pair:
                if o:
                    copy = remote(
                        buffer.at[o],
                        out.at[o],
                        send_sem.at[o],
                        recv_sem.at[o],
                        {"dp": plane(d, o)},
                    )
                else:
                    copy = pltpu.make_async_copy(buffer.at[0], out.at[0], send_sem.at[0])
                copy.start()
                pending.append(copy)

        lax.fori_loop(0, width // (2 * tile), grad_step, 0)
        give(grad_back, grad_back_out, grad_send, grad_recv)
        lax.fori_loop(0, width // (2 * tile), back_step, 0)
        product = jnp.sum(
            cot_ref[2 * j : 2 * j + 2, :, :width].reshape(count, width).astype(F32)
            * back[2 * j : 2 * j + 2].reshape(count, width).astype(F32),
            axis=1,
            keepdims=True,
        )
        lane = lax.broadcasted_iota(jnp.int32, (count, TILE), 1)
        spread = jnp.zeros((count, TILE), F32)
        for k, term in enumerate(split_parts(product)):
            spread = jnp.where(lane == k, term.astype(F32), spread)
        slopes[2 * j : 2 * j + 2] = spread.astype(BF).reshape(2, capacity, TILE)
        give(slopes, slope_out, slope_send, slope_recv)

    keeps = [
        pltpu.make_async_copy(rows, rows_out, keep_sem.at[0]),
        pltpu.make_async_copy(scaled, scaled_out, keep_sem.at[1]),
        pltpu.make_async_copy(back, back_out, keep_sem.at[2]),
    ]
    for copy in keeps:
        copy.start()
    for j in order[-2:]:
        for copy in unit_copies[j]:
            copy.wait()
    for o in PEERS:
        arrivals[o].wait_send()
    for copy in pending + keeps + over:
        copy.wait()


def expert_stage(
    normed2, routing, cot, router, gate_w, up_w, down_w, cot_own, groups, capacity, tile
):
    width, units = gate_w.shape
    slots = groups * capacity
    vmem = pl.BlockSpec(memory_space=pltpu.VMEM)
    hbm = pl.BlockSpec(memory_space=pl.ANY)
    row_shape = jax.ShapeDtypeStruct((groups, capacity, width), BF)
    unit_shape = jax.ShapeDtypeStruct((slots, units), BF)
    row_buffer = pltpu.VMEM((groups, capacity, width), BF)
    unit_buffer = pltpu.VMEM((2, 2 * capacity, units), BF)
    row_sem = pltpu.SemaphoreType.DMA((groups,))
    return pl.pallas_call(
        functools.partial(expert_kernel, width, tile),
        out_shape=(row_shape,)
        + (unit_shape,) * 3
        + (row_shape,) * 3
        + (
            jax.ShapeDtypeStruct((groups, capacity, TILE), BF),
            jax.ShapeDtypeStruct(normed2.shape, BF),
            jax.ShapeDtypeStruct((normed2.shape[0] // 2, width), BF),
        ),
        in_specs=[vmem] * 4 + [hbm] * 4,
        out_specs=[hbm] * 10,
        scratch_shapes=[
            pltpu.VMEM((width, units), BF),
            pltpu.VMEM((width, units), BF),
            pltpu.VMEM((units, width), BF),
            row_buffer,
            row_buffer,
            row_buffer,
            row_buffer,
            pltpu.VMEM((groups, capacity, TILE), BF),
            unit_buffer,
            unit_buffer,
            unit_buffer,
            row_buffer,
            pltpu.SemaphoreType.DMA((3, units // tile)),
            row_sem,
            row_sem,
            row_sem,
            row_sem,
            row_sem,
            row_sem,
            pltpu.SemaphoreType.DMA((2, 3)),
            pltpu.SemaphoreType.DMA((3,)),
            pltpu.SemaphoreType.DMA((2, 2)),
        ],
        compiler_params=pltpu.CompilerParams(
            vmem_limit_bytes=VMEM_MOST, collective_id=2, has_side_effects=True
        ),
        cost_estimate=pl.CostEstimate(
            flops=12 * slots * width * units,
            bytes_accessed=6 * width * units + 6 * slots * units,
            transcendentals=slots * units,
        ),
        name="expert_stage",
    )(normed2, routing, cot, router, gate_w, up_w, down_w, cot_own)


def split_parts(value):
    first = value.astype(BF)
    rest = value - first.astype(F32)
    second = rest.astype(BF)
    return first, second, (rest - second.astype(F32)).astype(BF)


def combine_kernel(
    grad_back_ref,
    slot_slope_ref,
    routing_ref,
    mixed_ref,
    normed2_ref,
    cot_ref,
    router_ref,
    gain_ref,
    w_cat_ref,
    gates_ref,
    grad_mixed_ref,
    grad_branch_ref,
    grad_heads_ref,
    grad_router_ref,
    grad_norm2_ref,
    picked,
    slopes,
    gaps,
    pick,
):
    length, width = mixed_ref.shape

    slots = grad_back_ref.shape[0]
    first, second = token_selector(routing_ref, slots)
    gaps[...] = jnp.dot(
        (second - first).astype(BF), slot_slope_ref[...], preferred_element_type=F32
    )
    pick[...] = (first + second).astype(BF)

    picked[...] = jnp.dot(pick[...], grad_back_ref[...], preferred_element_type=F32)
    lane = lax.broadcasted_iota(jnp.int32, (TILE, TILE), 1)

    def row_step(i, total):
        span = pl.ds(pl.multiple_of(i * TILE, TILE), TILE)
        ids = routing_ref[span, :]
        sign = jnp.where(lane == ids[:, 3:4], 1.0, 0.0) - jnp.where(lane == ids[:, 2:3], 1.0, 0.0)
        logits = jnp.dot(normed2_ref[span, :], router_ref[...], preferred_element_type=F32)
        gap = jnp.sum(logits * sign, axis=1, keepdims=True)
        gate0, gate1 = 1.0 / (1.0 + jnp.exp(gap)), 1.0 / (1.0 + jnp.exp(-gap))
        cot = cot_ref[span, :].astype(F32)
        mixed = mixed_ref[span, :]
        gates_ref[span, :] = jnp.where(lane == 0, gate0, gate1)
        grad_gap = jnp.sum(gaps[span, :], axis=1, keepdims=True)
        slope = gate0 * gate1 * grad_gap * sign
        slopes[span, :] = slope
        grad_normed2 = picked[span, :] + sum(
            contract(part, router_ref[...], 1, 1) for part in split_parts(slope)
        )
        scale = lax.rsqrt(jnp.mean(mixed * mixed, axis=1, keepdims=True) + EPS)
        inner = grad_normed2 * gain_ref[...]
        mean = jnp.mean(inner * mixed, axis=1, keepdims=True)
        grad_mixed = cot + scale * inner - mixed * (scale * scale * scale * mean)
        grad_mixed_ref[span, :] = grad_mixed
        grad_branch_ref[span, :] = grad_mixed.astype(BF)
        return total + jnp.sum(grad_normed2 * mixed * scale, axis=0, keepdims=True)

    grad_norm2_ref[...] = lax.fori_loop(
        0, length // TILE, row_step, jnp.zeros((1, width), F32)
    )

    grad_heads_ref[...] = contract(grad_branch_ref[...], w_cat_ref[...], 1, 1).astype(BF)
    experts = grad_router_ref.shape[0]
    grad_router_ref[...] = sum(
        contract(part, normed2_ref[...], 0, 0) for part in split_parts(slopes[...])
    )[:experts]


def combine(grad_back, slot_slope, routing, mixed, normed2, cot, router, gain, w_cat, experts):
    length, width = mixed.shape
    vmem = pl.BlockSpec(memory_space=pltpu.VMEM)
    return pl.pallas_call(
        combine_kernel,
        out_shape=(
            jax.ShapeDtypeStruct((length, TILE), F32),
            jax.ShapeDtypeStruct((length, width), F32),
            jax.ShapeDtypeStruct((length, width), BF),
            jax.ShapeDtypeStruct((length, w_cat.shape[0]), BF),
            jax.ShapeDtypeStruct((experts, width), F32),
            jax.ShapeDtypeStruct((1, width), F32),
        ),
        in_specs=[vmem] * 9,
        out_specs=[vmem] * 6,
        scratch_shapes=[
            pltpu.VMEM((length, width), F32),
            pltpu.VMEM((length, TILE), F32),
            pltpu.VMEM((length, TILE), F32),
            pltpu.VMEM((length, grad_back.shape[0]), BF),
        ],
        compiler_params=pltpu.CompilerParams(vmem_limit_bytes=VMEM_MOST),
        cost_estimate=pl.CostEstimate(
            flops=3 * length * grad_back.shape[0] * width,
            bytes_accessed=4 * grad_back.shape[0] * width,
            transcendentals=0,
        ),
        name="combine",
    )(grad_back, slot_slope, routing, mixed, normed2, cot, router, gain, w_cat)


def attend_back_kernel(
    normed2_far,
    cot_first,
    cot_last,
    routing_ref,
    router_ref,
    grad_ref,
    qkv_hbm,
    probs_hbm,
    normed_hbm,
    query_hbm,
    key_hbm,
    value_hbm,
    attended_ref,
    grad_branch_ref,
    far_rows_ref,
    far_scaled_ref,
    carry_ref,
    part_sum_ref,
    qkv_w_ref,
    out_w_ref,
    lines_ref,
    sums_ref,
    acc_ref,
    sends,
    cot_far,
    grads,
    qkv_ref,
    probs_ref,
    normed_ref,
    grad_qkv_ref,
    weight_ref,
    weight_sum,
    parts,
    landed,
    far_send,
    far_recv,
    hop_send,
    hop_recv,
    part_send,
    part_recv,
    load_sem,
    weight_sem,
    own_sem,
):
    z, d = lax.axis_index("head"), lax.axis_index("dp")
    replicas, length, columns = grads.shape
    _, groups, capacity, _ = sends.shape
    width = normed2_far.shape[1]
    heads = sums_ref.shape[0]
    pairs = heads // 2
    lanes = columns // pairs
    half = lanes // 2
    chunk = 2 * TILE
    hops = [3, 2, 1]
    order = [1, 3, 0, 2]

    def loads(turn):
        r, slot = order[turn], turn % 2
        return [
            pltpu.make_async_copy(source.at[r], target.at[slot], load_sem.at[i, slot])
            for i, (source, target) in enumerate(
                ((qkv_hbm, qkv_ref), (probs_hbm, probs_ref), (normed_hbm, normed_ref))
            )
        ]

    weight_loads = [
        pltpu.make_async_copy(
            source, weight_ref.at[:, pl.ds(i * columns, columns)], weight_sem.at[i]
        )
        for i, source in enumerate((query_hbm, key_hbm, value_hbm))
    ]
    for copy in loads(0) + weight_loads:
        copy.start()
    greet([{"dp": plane(d, o)} for o in PEERS] + [{"head": flipped(z, r)} for r in hops])
    copies = []
    arrivals = {}
    for r in [1, 3, 2]:
        arrivals[r] = remote(
            grad_ref.at[:, pl.ds(r * columns, columns)],
            grads.at[r],
            hop_send.at[r],
            hop_recv.at[r],
            {"head": flipped(z, r)},
        )
        arrivals[r].start()
    half_plane = groups // 2
    at = 0
    for piece in (cot_first, cot_last):
        cot_far[at : at + piece.shape[0]] = piece[...]
        at += piece.shape[0]
    logits = contract(router_ref[...], normed2_far[...], 0, 1)
    expert = lax.broadcasted_iota(jnp.int32, logits.shape, 0)
    routing = routing_ref[...]
    sign = jnp.where(expert == routing[3:4], 1.0, 0.0) - jnp.where(expert == routing[2:3], 1.0, 0.0)
    gap = jnp.sum(logits * sign, axis=0, keepdims=True)
    gate0, gate1 = 1.0 / (1.0 + jnp.exp(gap)), 1.0 / (1.0 + jnp.exp(-gap))

    def dispatch(start):
        span = slice(start, start + half_plane)
        first, second = selector(routing_ref, start * capacity, half_plane * capacity)
        gate = jnp.sum(first * gate0 + second * gate1, axis=1, keepdims=True)
        both = (first + second).astype(BF)
        shape = (half_plane, capacity, width)
        sends[0, span] = (
            jnp.dot(both, normed2_far[...], preferred_element_type=F32).astype(BF).reshape(shape)
        )
        sends[1, span] = (
            (jnp.dot(both, cot_far[...], preferred_element_type=F32) * gate)
            .astype(BF)
            .reshape(shape)
        )
        for o in range(start, start + half_plane):
            for i, out in enumerate((far_rows_ref, far_scaled_ref)):
                if o:
                    copy = remote(
                        sends.at[i, o],
                        out.at[o],
                        far_send.at[i, o],
                        far_recv.at[i, o],
                        {"dp": plane(d, o)},
                    )
                else:
                    copy = pltpu.make_async_copy(sends.at[i, 0], out.at[0], own_sem.at[i])
                copy.start()
                copies.append(copy)

    dispatch(half_plane)
    sums_ref[...] = jnp.zeros_like(sums_ref)
    grads[0] = grad_ref[:, :columns]

    near = {"head": flipped(z, 1)}

    def part_copy(i, source, target, peer):
        return remote(parts.at[source], landed.at[target], part_send.at[i], part_recv.at[i], peer)

    inner = part_copy(0, 3, 0, near)
    direct = part_copy(1, 1, 1, near)

    for copy in weight_loads:
        copy.wait()
    for turn, r in enumerate(order):
        slot = turn % 2
        if turn + 1 < replicas:
            for copy in loads(turn + 1):
                copy.start()
        for copy in loads(turn):
            copy.wait()
        if r:
            arrivals[r].wait_recv()

        def pair_step(pair, carry, slot=slot, r=r):
            def part_of(j):
                at = pl.multiple_of(j * columns + pair * lanes, lanes)
                return qkv_ref[slot, :, pl.ds(at, lanes)]

            at = pl.multiple_of(pair * lanes, lanes)
            query, value = part_of(0), part_of(2)
            key_t = part_of(1).T
            grad_all = grads[r, :, pl.ds(at, lanes)]
            grad_keys, grad_values = [], []
            for part in range(2):
                mask = lanes_of((length, lanes), half, part)
                grad = jnp.where(mask, grad_all, 0).astype(BF)
                grad_key = jnp.zeros((length, lanes), F32)
                grad_value = jnp.zeros((length, lanes), F32)
                for c in range(length // chunk):
                    cols = slice(c * chunk, (c + 1) * chunk)
                    grad_probs = contract(value, grad[cols], 1, 1)
                    probs_low = probs_ref[slot, pair * 2 + part, :, cols]
                    probs = probs_low.astype(F32)
                    delta = jnp.sum(probs * grad_probs, axis=0, keepdims=True)
                    grad_scores = (probs * (grad_probs - delta)).astype(BF)
                    grad_value += jnp.dot(probs_low, grad_all[cols], preferred_element_type=F32)
                    grad_key += jnp.dot(grad_scores, query[cols], preferred_element_type=F32)
                    acc_ref[part * half : (part + 1) * half, cols] = jnp.dot(
                        key_t[part * half : (part + 1) * half],
                        grad_scores,
                        preferred_element_type=F32,
                    )
                    for kb in range(length // TILE):
                        to = length - TILE * kb + chunk * c
                        sums_ref[pair * 2 + part, :, to : to + chunk] += grad_scores[
                            kb * TILE : (kb + 1) * TILE
                        ].astype(F32)
                grad_keys.append(grad_key)
                grad_values.append(grad_value)
            first = lanes_of((length, lanes), half, 0)
            results = (
                acc_ref[...].T * SCALE,
                jnp.where(first, *grad_keys) * SCALE,
                jnp.where(first, *grad_values),
            )
            for j, result in enumerate(results):
                to = pl.multiple_of(j * columns + pair * lanes, lanes)
                grad_qkv_ref[slot, :, pl.ds(to, lanes)] = result.astype(BF)
            return carry

        lax.fori_loop(0, pairs, pair_step, 0)

        parts[r] = contract(grad_qkv_ref[slot], weight_ref[...], 1, 1).astype(BF)
        if r == 3:
            inner.start()
            dispatch(0)
        if r == 1:
            direct.start()

        def weight_step(i, carry, slot=slot, turn=turn):
            cols = pl.ds(pl.multiple_of(i * 2 * chunk, 2 * chunk), 2 * chunk)
            value = contract(normed_ref[slot, :, cols], grad_qkv_ref[slot], 0, 0)
            if turn:
                value = value + weight_sum[cols, :]
            if turn + 1 < replicas:
                weight_sum[cols, :] = value
            else:
                qkv_w_ref[cols, :] = value.astype(BF)
            return carry

        lax.fori_loop(0, width // (2 * chunk), weight_step, 0)

    out_w_ref[...] = contract(attended_ref[...], grad_branch_ref[...], 0, 0).astype(BF)
    unskew_kernel(sums_ref, lines_ref)

    for r in hops:
        arrivals[r].wait_send()
    for copy in copies:
        copy.wait()
    inner.wait()
    carry_ref[...] = (parts[2].astype(F32) + landed[0].astype(F32)).astype(BF)
    direct.wait()
    part_sum_ref[...] = parts[0].astype(F32) + landed[1].astype(F32)


def attend_back(
    normed2_far,
    cot_pieces,
    routing_far,
    router,
    grad_heads,
    qkv,
    probs,
    normed,
    weights,
    attended,
    grad_branch,
    groups,
    capacity,
):
    replicas, length, triple = qkv.shape
    heads = probs.shape[1]
    columns = triple // 3
    width = normed.shape[2]
    lanes = 2 * columns // heads
    far_shape = jax.ShapeDtypeStruct((groups, capacity, width), BF)
    vmem = pl.BlockSpec(memory_space=pltpu.VMEM)
    hbm = pl.BlockSpec(memory_space=pl.ANY)
    hop_sem = pltpu.SemaphoreType.DMA((replicas,))
    plane_sem = pltpu.SemaphoreType.DMA((2, groups))
    part_sem = pltpu.SemaphoreType.DMA((2,))
    return pl.pallas_call(
        attend_back_kernel,
        out_shape=(
            far_shape,
            far_shape,
            jax.ShapeDtypeStruct((length, width), BF),
            jax.ShapeDtypeStruct((length, width), F32),
            jax.ShapeDtypeStruct((width, triple), BF),
            jax.ShapeDtypeStruct((replicas * columns, width), BF),
            jax.ShapeDtypeStruct((heads, 1, 2 * length), F32),
        ),
        in_specs=[vmem] * 6 + [hbm] * 6 + [vmem] * 2,
        out_specs=[hbm] * 2 + [vmem] * 5,
        scratch_shapes=[
            pltpu.VMEM((heads, TILE, 2 * length), F32),
            pltpu.VMEM((lanes, length), F32),
            pltpu.VMEM((2, groups, capacity, width), BF),
            pltpu.VMEM((length, width), BF),
            pltpu.VMEM((replicas, length, columns), BF),
            pltpu.VMEM((2, length, triple), BF),
            pltpu.VMEM((2, heads, length, length), BF),
            pltpu.VMEM((2, length, width), BF),
            pltpu.VMEM((2, length, triple), BF),
            pltpu.VMEM((width, triple), BF),
            pltpu.VMEM((width, triple), F32),
            pltpu.VMEM((replicas, length, width), BF),
            pltpu.VMEM((2, length, width), BF),
            plane_sem,
            plane_sem,
            hop_sem,
            hop_sem,
            part_sem,
            part_sem,
            pltpu.SemaphoreType.DMA((3, 2)),
            pltpu.SemaphoreType.DMA((3,)),
            pltpu.SemaphoreType.DMA((2,)),
        ],
        compiler_params=pltpu.CompilerParams(
            vmem_limit_bytes=VMEM_MOST, collective_id=3, has_side_effects=True
        ),
        cost_estimate=pl.CostEstimate(
            flops=replicas * heads * 16 * length * length * lanes,
            bytes_accessed=replicas * heads * length * length * 4,
            transcendentals=0,
        ),
        name="attend_back",
    )(
        normed2_far,
        *cot_pieces,
        routing_far,
        router,
        grad_heads,
        qkv,
        probs,
        normed,
        *weights,
        attended,
        grad_branch,
    )


def last_kernel(
    tile,
    far_hbm,
    scaled_hbm,
    scaled_here_hbm,
    gates_ref,
    routing_ref,
    gain_ref,
    gate_hbm,
    up_hbm,
    down_hbm,
    grad_gate_hbm,
    grad_up_hbm,
    hidden_hbm,
    qkv_w_hbm,
    out_w_hbm,
    rows_hbm,
    carry_hbm,
    part_sum_hbm,
    input_hbm,
    back_hbm,
    norm2_ref,
    router_grad_ref,
    lines_ref,
    wide_out,
    wide_came,
    tall_out,
    tall_came,
    qkv_w_out,
    out_w_out,
    small_out,
    grad_input_out,
    output_out,
    back_out,
    far_ref,
    scaled,
    scaled_here,
    left,
    weights,
    downs,
    units,
    hidden,
    hidden_here,
    send_wide,
    keep_wide,
    send_tall,
    keep_tall,
    qkv_land,
    qkv_sum,
    out_land,
    out_sum,
    out_hop,
    out_last,
    small_own,
    small_land,
    small_sum,
    small_hop,
    small_last,
    work,
    own_input,
    carried,
    stream_sem,
    hidden_sem,
    wide_send,
    wide_recv,
    keep_sem,
    tall_send,
    tall_recv,
    tall_keep,
    first_send,
    first_recv,
    hop_send,
    hop_recv,
    third_send,
    third_recv,
    carry_sem,
    back_send,
    back_recv,
    own_sem,
):
    z, d = lax.axis_index("head"), lax.axis_index("dp")
    slots, width = scaled_here.shape
    groups = qkv_land.shape[0]
    capacity = slots // groups
    length = own_input.shape[0]
    chunk = 2 * TILE
    _, rows, total_units = send_wide.shape
    half_units = hidden_here.shape[1]
    tiles = total_units // tile
    low, high = lax.rem(z, 2), z // 2
    keep_at = pl.multiple_of(low * rows, rows)
    send_at = pl.multiple_of((1 - low) * rows, rows)
    near = {"head": flipped(z, 1)}
    count = 2 * capacity
    hops = [3, 2, 1]

    def streams(t):
        slot = lax.rem(t, 2)
        at = pl.multiple_of(t * tile, tile)
        cols = pl.ds(at, tile)
        return [
            pltpu.make_async_copy(gate_hbm.at[:, cols], weights.at[slot, 0], stream_sem.at[0, slot]),
            pltpu.make_async_copy(up_hbm.at[:, cols], weights.at[slot, 1], stream_sem.at[1, slot]),
            pltpu.make_async_copy(down_hbm.at[cols, :], downs.at[slot], stream_sem.at[2, slot]),
            pltpu.make_async_copy(
                grad_gate_hbm.at[:, cols], units.at[slot, 0], stream_sem.at[3, slot]
            ),
            pltpu.make_async_copy(
                grad_up_hbm.at[:, cols], units.at[slot, 1], stream_sem.at[4, slot]
            ),
        ]

    wide = 2 * rows
    for copy in streams(0):
        copy.start()
    far_loads = [
        pltpu.make_async_copy(source, target, own_sem.at[6 + i])
        for i, (source, target) in enumerate(
            ((far_hbm, far_ref), (scaled_hbm, scaled), (scaled_here_hbm, scaled_here))
        )
    ]
    for copy in far_loads:
        copy.start()
    loads = [
        pltpu.make_async_copy(
            rows_hbm.at[:, pl.ds(pl.multiple_of(high * wide, wide), wide)], left, own_sem.at[2]
        ),
        pltpu.make_async_copy(part_sum_hbm, work.at[0], own_sem.at[3]),
        pltpu.make_async_copy(
            input_hbm.at[pl.ds(pl.multiple_of(z * length, length), length)], own_input, own_sem.at[5]
        ),
    ]
    for copy in loads:
        copy.start()

    half_copy = pltpu.make_async_copy(
        hidden_hbm.at[:, pl.ds(pl.multiple_of(high * half_units, TILE), half_units)],
        hidden_here,
        hidden_sem,
    )
    half_copy.start()
    greet([{"dp": plane(d, o)} for o in PEERS] + [{"head": flipped(z, r)} for r in hops])

    carry = remote(
        carry_hbm, carried, carry_sem.at[0], carry_sem.at[1], {"head": flipped(z, 2)}
    )
    carry.start()
    for copy in far_loads[:2] + loads[:1]:
        copy.wait()
    columns = pl.ds(pl.multiple_of(high * wide, wide), wide)

    def wide_copy(i, t):
        at = pl.multiple_of(t * tile, tile)
        return remote(
            send_wide.at[i, :, pl.ds(at, tile)],
            wide_came.at[i, :, pl.ds(at, tile)],
            wide_send.at[i, t],
            wide_recv.at[i, t],
            near,
        )

    def keep_copy(i, t):
        at = pl.multiple_of(t * tile, tile)
        slot = lax.rem(t, 2)
        return pltpu.make_async_copy(
            keep_wide.at[i, slot], wide_out.at[i, :, pl.ds(at, tile)], keep_sem.at[i, slot]
        )

    def tile_step(t, carry):
        slot = lax.rem(t, 2)
        at = pl.multiple_of(t * tile, tile)

        @pl.when(t + 1 < tiles)
        def _():
            for copy in streams(t + 1):
                copy.start()

        for copy in streams(t):
            copy.wait()

        def chunk_step(j, inner):
            span = pl.ds(pl.multiple_of(j * count, count), count)
            values = expert_tile(
                far_ref[span], scaled[span], weights[slot, 0], weights[slot, 1], downs[slot]
            )
            hidden[span, pl.ds(at, tile)] = values[0]
            units[slot, 2, span, :] = values[1]
            units[slot, 3, span, :] = values[2]
            return inner

        lax.fori_loop(0, groups // 2, chunk_step, 0)
        @pl.when(t >= 2)
        def _():
            for i in range(2):
                keep_copy(i, t - 2).wait()

        for i in range(2):
            value = contract(left[...], units[slot, i], 0, 0) + contract(
                far_ref[:, columns], units[slot, 2 + i], 0, 0
            )
            upper = low == 1
            send_wide[i, :, pl.ds(at, tile)] = jnp.where(
                upper, value[:rows], value[rows:]
            ).astype(BF)
            keep_wide[i, slot] = jnp.where(upper, value[rows:], value[:rows])
            wide_copy(i, t).start()
            keep_copy(i, t).start()
        return carry

    tile_step(jnp.int32(0), 0)

    first = []
    for o in PEERS:
        peer = plane(d, o)
        for i, (source, target) in enumerate(
            (
                (qkv_w_hbm.at[peer], qkv_land.at[o]),
                (out_w_hbm.at[:, peer], out_land.at[o]),
            )
        ):
            copy = remote(source, target, first_send.at[i, o], first_recv.at[i, o], {"dp": peer})
            copy.start()
            first.append(copy)
    own = [
        pltpu.make_async_copy(qkv_w_hbm.at[d], qkv_land.at[0], own_sem.at[0]),
        pltpu.make_async_copy(out_w_hbm.at[:, d], out_land.at[0], own_sem.at[1]),
    ]
    for copy in own:
        copy.start()

    backs = []
    for o in PEERS:
        copy = remote(
            back_hbm.at[o], back_out.at[o], back_send.at[o], back_recv.at[o], {"dp": plane(d, o)}
        )
        copy.start()
        backs.append(copy)
    backs.append(pltpu.make_async_copy(back_hbm.at[0], back_out.at[0], back_send.at[0]))
    backs[-1].start()
    lax.fori_loop(1, tiles, tile_step, 0)

    carry.wait()
    for copy in loads[1:]:
        copy.wait()

    def norm_step(i, total):
        span = pl.ds(pl.multiple_of(i * TILE, TILE), TILE)
        grad_normed = work[0, span, :] + carried[span, :].astype(F32)
        value = own_input[span, :].astype(F32)
        scale = lax.rsqrt(jnp.mean(value * value, axis=1, keepdims=True) + EPS)
        inner = grad_normed * gain_ref[...]
        mean = jnp.mean(inner * value, axis=1, keepdims=True)
        work[1, span, :] = scale * inner - value * (scale * scale * scale * mean)
        return total + jnp.sum(grad_normed * value * scale, axis=0, keepdims=True)

    heads = lines_ref.shape[0]
    small_own[...] = jnp.zeros_like(small_own)
    small_own[0:1] = lax.fori_loop(0, length // TILE, norm_step, jnp.zeros((1, width), F32))
    small_own[1:2] = norm2_ref[...]
    for h in range(heads):
        small_own[2 + h : 3 + h] = lines_ref[h]
    small_own[8:] = router_grad_ref[...]
    ends = [pltpu.make_async_copy(work.at[1], grad_input_out, own_sem.at[4])]
    for copy in ends:
        copy.start()
    small = []

    def lanes(index):
        return pl.ds(pl.multiple_of(index * TILE, TILE), TILE)

    for o in PEERS:
        peer = plane(d, o)
        copy = remote(
            small_own.at[:, lanes(peer)],
            small_land.at[o],
            first_send.at[2, o],
            first_recv.at[2, o],
            {"dp": peer},
        )
        copy.start()
        small.append(copy)
    small_land[0] = small_own[:, lanes(d)]

    for copy in first:
        copy.wait()
    for copy in own:
        copy.wait()
    qkv_sum[...] = sum(qkv_land[o].astype(F32) for o in range(groups)).astype(BF)
    out_sum[...] = sum(out_land[o].astype(F32) for o in range(groups)).astype(BF)
    second = []
    for o in PEERS:
        copy = remote(
            qkv_sum, qkv_w_out.at[d], third_send.at[0, o], third_recv.at[0, o], {"dp": plane(d, o)}
        )
        copy.start()
        second.append(copy)
    mine = [pltpu.make_async_copy(qkv_sum, qkv_w_out.at[d], own_sem.at[0])]
    mine[0].start()
    over = []
    for r in hops:
        copy = remote(
            out_sum.at[r], out_hop.at[r], hop_send.at[0, r], hop_recv.at[0, r], {"head": flipped(z, r)}
        )
        copy.start()
        over.append(copy)

    half_copy.wait()
    far_loads[2].wait()
    share = half_units // 2
    halves = pl.ds(pl.multiple_of(high * half_units, TILE), half_units)

    def tall_copies(i):
        cols = pl.ds(pl.multiple_of(i * tile, tile), tile)
        return [
            remote(
                send_tall.at[:, cols], tall_came.at[:, cols], tall_send.at[i], tall_recv.at[i], near
            ),
            pltpu.make_async_copy(keep_tall.at[:, cols], tall_out.at[:, cols], tall_keep.at[i]),
        ]

    def tall_step(i, carry):
        cols = pl.ds(pl.multiple_of(i * tile, tile), tile)
        value = contract(hidden_here[...], scaled_here[:, cols], 0, 0) + contract(
            hidden[:, halves], scaled[:, cols], 0, 0
        )
        upper = low == 1
        send_tall[:, cols] = jnp.where(upper, value[:share], value[share:]).astype(BF)
        keep_tall[:, cols] = jnp.where(upper, value[share:], value[:share])
        for copy in tall_copies(i):
            copy.start()
        return carry

    lax.fori_loop(0, width // tile, tall_step, 0)
    for copy in small:
        copy.wait()
    small_sum[...] = sum(small_land[o] for o in range(groups))
    small_over = []
    for r in hops:
        copy = remote(
            small_sum, small_hop.at[r], hop_send.at[1, r], hop_recv.at[1, r], {"head": flipped(z, r)}
        )
        copy.start()
        small_over.append(copy)

    for copy in backs:
        copy.wait()
    rows_back = [
        pltpu.make_async_copy(
            back_out.at[o], hidden.at[o * capacity : (o + 1) * capacity, :width], back_recv.at[o]
        )
        for o in range(groups)
    ]
    for copy in rows_back:
        copy.start()
    for k, pick in enumerate(token_selector(routing_ref, slots)):
        hidden_here[k * length : (k + 1) * length, :slots] = pick.astype(BF)
    for copy in rows_back:
        copy.wait()

    def output_step(i, carry):
        cols = pl.ds(pl.multiple_of(i * chunk, chunk), chunk)
        work[0, :, cols] = sum(
            gates_ref[:, k : k + 1]
            * jnp.dot(
                hidden_here[k * length : (k + 1) * length, :slots],
                hidden[:, cols],
                preferred_element_type=F32,
            )
            for k in range(2)
        )
        return carry

    lax.fori_loop(0, width // chunk, output_step, 0)
    ends.append(pltpu.make_async_copy(work.at[0], output_out, own_sem.at[3]))
    ends[1].start()

    for copy in small_over:
        copy.wait()
    small_last[0] = small_sum[...]
    small_last[1] = small_sum[...] + sum(small_hop[r] for r in hops)
    small_out[:, :, lanes(d)] = small_last[...]
    for o in PEERS:
        copy = remote(
            small_last,
            small_out.at[:, :, lanes(d)],
            third_send.at[2, o],
            third_recv.at[2, o],
            {"dp": plane(d, o)},
        )
        copy.start()
        second.append(copy)
    for copy in over:
        copy.wait()
    out_last[...] = (
        out_sum[0].astype(F32) + sum(out_hop[r].astype(F32) for r in hops)
    ).astype(BF)
    for o in PEERS:
        copy = remote(
            out_last,
            out_w_out.at[d],
            third_send.at[1, o],
            third_recv.at[1, o],
            {"dp": plane(d, o)},
        )
        copy.start()
        second.append(copy)
    mine.append(pltpu.make_async_copy(out_last, out_w_out.at[d], own_sem.at[1]))
    mine[1].start()

    for i in range(2):
        for t in (tiles - 2, tiles - 1):
            keep_copy(i, t).wait()

    def wide_end(t, carry):
        for i in range(2):
            wide_copy(i, t).wait()
        return carry

    lax.fori_loop(0, tiles, wide_end, 0)
    for copy in second + mine + ends:
        copy.wait()

    def tall_end(i, carry):
        for copy in tall_copies(i):
            copy.wait()
        return carry

    lax.fori_loop(0, width // tile, tall_end, 0)


def last_stage(
    far, here, tokens, weights, grads_here, hidden_here, sums, finish, small, tile
):
    gate_w, up_w, down_w = weights
    width, units = gate_w.shape
    qkv_w, out_w = sums
    replicas, groups, part_rows, _ = out_w.shape
    slots = far[0].shape[0]
    length = tokens[0].shape[0]
    back = finish[-1]
    vmem = pl.BlockSpec(memory_space=pltpu.VMEM)
    hbm = pl.BlockSpec(memory_space=pl.ANY)
    rows, share = width // replicas, units // replicas
    small_shape = (8 + groups, width)
    plane_sem = pltpu.SemaphoreType.DMA((3, groups))
    hop_sem = pltpu.SemaphoreType.DMA((2, replicas))
    return pl.pallas_call(
        functools.partial(last_kernel, tile),
        out_shape=(
            jax.ShapeDtypeStruct((2, rows, units), F32),
            jax.ShapeDtypeStruct((2, rows, units), BF),
            jax.ShapeDtypeStruct((share, width), F32),
            jax.ShapeDtypeStruct((share, width), BF),
            jax.ShapeDtypeStruct(qkv_w.shape, BF),
            jax.ShapeDtypeStruct(out_w.shape[1:], BF),
            jax.ShapeDtypeStruct((2,) + small_shape, F32),
            jax.ShapeDtypeStruct((length, width), F32),
            jax.ShapeDtypeStruct((length, width), F32),
            jax.ShapeDtypeStruct(back.shape, BF),
        ),
        in_specs=[hbm] * 3 + [vmem] * 3 + [hbm] * 13 + [vmem] * 3,
        out_specs=[hbm] * 6 + [vmem] + [hbm] * 3,
        scratch_shapes=[
            pltpu.VMEM((slots, width), BF),
            pltpu.VMEM((slots, width), BF),
            pltpu.VMEM((slots, width), BF),
            pltpu.VMEM((slots, 2 * rows), BF),
            pltpu.VMEM((2, 2, width, tile), BF),
            pltpu.VMEM((2, tile, width), BF),
            pltpu.VMEM((2, 4, slots, tile), BF),
            pltpu.VMEM((slots, units), BF),
            pltpu.VMEM((slots, units // 2), BF),
            pltpu.VMEM((2, rows, units), BF),
            pltpu.VMEM((2, 2, rows, tile), F32),
            pltpu.VMEM((share, width), BF),
            pltpu.VMEM((share, width), F32),
            pltpu.VMEM(qkv_w.shape, BF),
            pltpu.VMEM(qkv_w.shape[1:], BF),
            pltpu.VMEM((groups, replicas, part_rows, width), BF),
            pltpu.VMEM((replicas, part_rows, width), BF),
            pltpu.VMEM((replicas, part_rows, width), BF),
            pltpu.VMEM((part_rows, width), BF),
            pltpu.VMEM(small_shape, F32),
            pltpu.VMEM((groups, small_shape[0], TILE), F32),
            pltpu.VMEM((small_shape[0], TILE), F32),
            pltpu.VMEM((replicas, small_shape[0], TILE), F32),
            pltpu.VMEM((2, small_shape[0], TILE), F32),
            pltpu.VMEM((2, length, width), F32),
            pltpu.VMEM((length, width), BF),
            pltpu.VMEM((length, width), BF),
            pltpu.SemaphoreType.DMA((5, 2)),
            pltpu.SemaphoreType.DMA,
            pltpu.SemaphoreType.DMA((2, units // tile)),
            pltpu.SemaphoreType.DMA((2, units // tile)),
            pltpu.SemaphoreType.DMA((2, 2)),
            pltpu.SemaphoreType.DMA((width // tile,)),
            pltpu.SemaphoreType.DMA((width // tile,)),
            pltpu.SemaphoreType.DMA((width // tile,)),
            plane_sem,
            plane_sem,
            hop_sem,
            hop_sem,
            plane_sem,
            plane_sem,
            pltpu.SemaphoreType.DMA((2,)),
            pltpu.SemaphoreType.DMA((groups,)),
            pltpu.SemaphoreType.DMA((groups,)),
            pltpu.SemaphoreType.DMA((9,)),
        ],
        compiler_params=pltpu.CompilerParams(
            vmem_limit_bytes=VMEM_MOST, collective_id=4, has_side_effects=True
        ),
        cost_estimate=pl.CostEstimate(
            flops=12 * slots * width * units,
            bytes_accessed=6 * width * units + 6 * slots * units,
            transcendentals=slots * units,
        ),
        name="last_stage",
    )(
        *far,
        here[1],
        *tokens,
        gate_w,
        up_w,
        down_w,
        *grads_here,
        hidden_here,
        qkv_w,
        out_w,
        here[0],
        *finish,
        *small,
    )


def finish_kernel(
    wide_kept,
    wide_came,
    tall_kept,
    tall_came,
    qkv_ref,
    out_ref,
    mixed_ref,
    expert_ref,
    grad_mixed_ref,
    grad_first_ref,
    summed_ref,
    line_ref,
    output_ref,
    grad_input_ref,
    query_out,
    key_out,
    value_out,
    out_out,
    gate_out,
    up_out,
    down_out,
    norm1_out,
    norm2_out,
    bias_out,
    router_out,
):
    output_ref[...] = mixed_ref[...] + expert_ref[...]
    grad_input_ref[...] = grad_mixed_ref[...] + grad_first_ref[...]
    gate_out[...] = wide_kept[0] + wide_came[0].astype(F32)
    up_out[...] = wide_kept[1] + wide_came[1].astype(F32)
    down_out[...] = tall_kept[...] + tall_came[...].astype(F32)
    columns = query_out.shape[1]
    for i, out in enumerate((query_out, key_out, value_out)):
        value = qkv_ref[:, :, i * columns : (i + 1) * columns].astype(F32)
        out[...] = value.reshape(out.shape)
    out_out[...] = out_ref[...].astype(F32).reshape(out_out.shape)

    @pl.when(pl.program_id(0) == 0)
    def _():
        norm1_out[...] = summed_ref[1, :1]
        norm2_out[...] = summed_ref[1, 1:2]
        heads = bias_out.shape[0]
        total = sum(contract(term, line_ref[...], 1, 1) for term in split_parts(summed_ref[0, :8]))
        bias_out[...] = total[2 : 2 + heads]
        router_out[...] = summed_ref[1, 8:]


def finish(wide, tall, qkv_w, out_w, tokens, summed, line, heads):
    steps = 8
    groups, part_rows, triple = qkv_w.shape
    _, out_rows, width = out_w.shape
    _, rows, units = wide[0].shape
    share = tall[0].shape[0]
    length = tokens[0].shape[0]
    columns = triple // 3
    experts = summed.shape[1] - 8

    def cut(shape, axis=0):
        parts = steps if shape[axis] == groups or shape[axis] % (16 * steps) == 0 else steps // 2
        turns = steps // parts
        block = tuple(n // parts if i == axis else n for i, n in enumerate(shape))
        return pl.BlockSpec(
            block, lambda t: tuple(t // turns if i == axis else 0 for i in range(len(shape)))
        )

    def whole(shape):
        return pl.BlockSpec(shape, lambda t: (0,) * len(shape))

    outs = [
        (length, width),
        (length, width),
        (groups * part_rows, columns),
        (groups * part_rows, columns),
        (groups * part_rows, columns),
        (groups * out_rows, width),
        (rows, units),
        (rows, units),
        (share, width),
    ]
    small = [(1, width), (1, width), (heads, line.shape[0]), (experts, width)]
    return pl.pallas_call(
        finish_kernel,
        out_shape=[jax.ShapeDtypeStruct(shape, F32) for shape in outs + small],
        grid=(steps,),
        in_specs=[cut(value.shape, 1) for value in wide]
        + [cut(value.shape) for value in tall]
        + [cut(qkv_w.shape), cut(out_w.shape)]
        + [cut(value.shape) for value in tokens]
        + [whole(summed.shape), whole(line.shape)],
        out_specs=[cut(shape) for shape in outs] + [whole(shape) for shape in small],
        compiler_params=pltpu.CompilerParams(vmem_limit_bytes=VMEM_MOST),
        cost_estimate=pl.CostEstimate(
            flops=4 * rows * units, bytes_accessed=48 * rows * units, transcendentals=0
        ),
        name="finish",
    )(*wide, *tall, qkv_w, out_w, *tokens, summed, line)


def expert_forward(rows, gate_w, up_w, grad_unscaled, slot_gates):
    gate_pre = jnp.dot(rows, gate_w, preferred_element_type=F32)
    up_pre = jnp.dot(rows, up_w, preferred_element_type=F32)
    hidden, pull = jax.vjp(geglu, gate_pre, up_pre)
    grad_gate_pre, grad_up_pre = pull(grad_unscaled * slot_gates)
    return hidden.astype(BF), grad_gate_pre.astype(BF), grad_up_pre.astype(BF)


def body_plain(
    block_input,
    cotangent,
    expert_ids,
    priority,
    rel_bucket,
    norm1_gain,
    w_query,
    w_key,
    w_value,
    w_out,
    pos_bias,
    norm2_gain,
    w_router,
    w_gate,
    w_up,
    w_down,
):
    group_rows, width = block_input.shape
    own_rows = cotangent.shape[0]
    buckets, heads_here = pos_bias.shape
    head_cols = w_query.shape[1]
    length = (rel_bucket.shape[0] + 1) // 2
    sequences = group_rows // length
    experts = w_router.shape[1]
    capacity = 5 * 2 * own_rows // (4 * experts)
    slot_count = experts * capacity
    replicas = lax.axis_size("head")
    groups = lax.axis_size("dp")
    me = lax.axis_index("head")
    far = replicas // 2
    far_perm = [(i, i ^ far) for i in range(replicas)]
    stepwise = own_rows == length and sequences == replicas

    def hop(value, r):
        return lax.ppermute(value, "head", [(i, i ^ r) for i in range(replicas)])

    def exchange(value):
        parts = value.reshape(experts, capacity, -1)
        return lax.all_to_all(parts, "dp", split_axis=0, concat_axis=0, tiled=True).reshape(
            slot_count, -1
        )

    dest = route_slots(expert_ids, priority[0], experts, capacity)
    dest_far = lax.ppermute(dest, "head", far_perm)
    slot_range = jnp.arange(slot_count, dtype=jnp.int32)[None, :]
    picks = [(dest[:, k : k + 1] == slot_range).astype(BF) for k in range(2)]
    both = picks[0] + picks[1]
    both_far = sum((dest_far[:, k : k + 1] == slot_range).astype(BF) for k in range(2))

    down_w, gate_w, up_w = w_down[0], w_gate[0], w_up[0]
    cot_here = exchange(contract(both, cotangent, 0, 0).astype(BF))
    cot_far_own = lax.ppermute(cotangent, "head", far_perm)
    cot_far = exchange(contract(both_far, cot_far_own, 0, 0).astype(BF))
    unscaled_here = contract(cot_here, down_w, 1, 1)
    unscaled_far = contract(cot_far, down_w, 1, 1)

    dp_at = lax.axis_index("dp")
    out_rows = head_cols // groups
    piece = lax.dynamic_slice_in_dim(w_out, dp_at * out_rows, out_rows, 0)
    w_out_all = lax.all_gather(piece, ("head", "dp"), axis=0, tiled=True)
    w_qkv = jnp.concatenate([w_query, w_key, w_value], axis=1)
    qkv_rows = width // groups
    piece = lax.dynamic_slice_in_dim(w_qkv, dp_at * qkv_rows, qkv_rows, 0)
    w_qkv_all = lax.all_gather(piece, ("head", "dp"), axis=0, tiled=True)
    if stepwise:
        order = [me ^ r for r in range(replicas)]
    else:
        order = list(range(replicas))
    w_out_all = w_out_all.reshape(replicas, head_cols, width)
    w_qkv_all = w_qkv_all.reshape(replicas, width, 3 * head_cols)
    w_out_cat = jnp.concatenate(
        [lax.dynamic_index_in_dim(w_out_all, o, 0, keepdims=False) for o in order], axis=0
    )

    inputs_all = block_input.astype(F32)
    normed = rms_norm(inputs_all, norm1_gain).astype(BF)
    qkv = jnp.dot(normed, w_qkv, preferred_element_type=F32).astype(BF)
    line = (rel_bucket[::-1][None, :] == jnp.arange(buckets, dtype=jnp.int32)[:, None]).astype(F32)
    line = jnp.pad(line, ((0, 0), (1, 0)))
    table = skew(contract(pos_bias, line, 0, 0, HIGH))
    kept = {}
    if stepwise:
        blocks = [None] * replicas
        for r in reversed(range(replicas)):
            attended_seq, probs = attend_fwd(order[r].reshape(1), qkv, table, length)
            kept[r] = probs
            blocks[r] = hop(attended_seq, r) if r else attended_seq
    else:
        seqs = []
        for s in range(sequences):
            attended_seq, kept[s] = attend_fwd(jnp.full((1,), s, jnp.int32), qkv, table, length)
            seqs.append(attended_seq)
        attended_all = jnp.concatenate(seqs, axis=0).reshape(replicas, own_rows, head_cols)
        attended_all = lax.all_to_all(attended_all, "head", split_axis=0, concat_axis=0, tiled=True)
        blocks = [attended_all[i] for i in range(replicas)]
    attended = jnp.concatenate(blocks, axis=1)

    branch = jnp.dot(attended, w_out_cat, preferred_element_type=F32)
    start_own = me * own_rows
    inputs_own = lax.dynamic_slice_in_dim(block_input, start_own, own_rows, 0).astype(F32)
    mixed = inputs_own + branch
    normed2_full, norm2_pull = jax.vjp(rms_norm, mixed, norm2_gain)
    normed2 = normed2_full.astype(BF)
    logits = jnp.dot(normed2, w_router, preferred_element_type=F32)
    expert_range = jnp.arange(experts, dtype=jnp.int32)
    chosen = (expert_ids[:, :, None] == expert_range[None, None, :]).astype(F32)
    gates = jax.nn.softmax(jnp.sum(chosen * logits[:, None, :], axis=2), axis=-1)

    def slot_gates_of(places, values):
        terms = sum(
            jnp.where(places[:, k : k + 1] == slot_range, values[:, k : k + 1], 0.0)
            for k in range(2)
        )
        return jnp.sum(terms, axis=0)

    rows_here = exchange(contract(both, normed2, 0, 0).astype(BF))
    gates_here = exchange(slot_gates_of(dest, gates))
    normed2_far = lax.ppermute(normed2, "head", far_perm)
    gates_far_own = lax.ppermute(gates, "head", far_perm)
    rows_far = exchange(contract(both_far, normed2_far, 0, 0).astype(BF))
    gates_far = exchange(slot_gates_of(dest_far, gates_far_own))

    hidden_here, ggp_here, gup_here = expert_forward(
        rows_here, gate_w, up_w, unscaled_here, gates_here
    )
    returned = jnp.dot(hidden_here, down_w, preferred_element_type=F32).astype(BF)
    came_back = exchange(returned)
    grad_routed = (contract(ggp_here, gate_w, 1, 1) + contract(gup_here, up_w, 1, 1)).astype(BF)
    grad_back = exchange(grad_routed)
    hidden_far, ggp_far, gup_far = expert_forward(rows_far, gate_w, up_w, unscaled_far, gates_far)
    scaled_here = (cot_here.astype(F32) * gates_here).astype(BF)
    scaled_far = (cot_far.astype(F32) * gates_far).astype(BF)

    low = me % far
    high = me // far

    def reduced(lefts, rights):
        rows = lefts[0].shape[1] // replicas

        def part(at):
            return sum(
                contract(lax.dynamic_slice_in_dim(left, at * rows, rows, 1), right, 0, 0)
                for left, right in zip(lefts, rights)
            )

        if far == 2:
            sent = hop(part(high * far + (1 - low)).astype(BF), 1)
            return (part(me) + sent.astype(F32))[None]
        whole = jnp.concatenate([part(high * far + i) for i in range(far)], axis=0).astype(BF)
        member = [[h * far + i for i in range(far)] for h in range(2)]
        return lax.psum_scatter(
            whole, "head", scatter_dimension=0, axis_index_groups=member, tiled=True
        ).astype(F32)[None]

    grad_down_w = reduced((hidden_here, hidden_far), (scaled_here, scaled_far))
    grad_gate_w = reduced((rows_here, rows_far), (ggp_here, ggp_far))
    grad_up_w = reduced((rows_here, rows_far), (gup_here, gup_far))

    chosen_rows = [jnp.dot(pick, came_back, preferred_element_type=F32) for pick in picks]
    output = mixed + sum(gates[:, k : k + 1] * chosen_rows[k] for k in range(2))
    grad_output = cotangent.astype(F32)
    grad_gates = jnp.stack([jnp.sum(grad_output * rows, axis=1) for rows in chosen_rows], axis=1)
    grad_normed2 = jnp.dot(both, grad_back, preferred_element_type=F32)
    grad_picked = gates * (grad_gates - jnp.sum(gates * grad_gates, axis=1, keepdims=True))
    grad_logits = jnp.sum(chosen * grad_picked[:, :, None], axis=1)
    grad_normed2 = grad_normed2 + contract(grad_logits, w_router.astype(F32), 1, 1, HIGH)
    grad_router = contract(normed2.astype(F32), grad_logits, 0, 0, HIGH)
    grad_mixed, grad_norm2 = norm2_pull(grad_normed2)
    grad_mixed = grad_mixed + grad_output
    grad_branch = grad_mixed.astype(BF)

    grad_wout = contract(attended, grad_branch, 0, 0).astype(BF)
    grad_wout = grad_wout.reshape(replicas, groups, out_rows, width)
    grad_wout = lax.psum_scatter(grad_wout, "dp", scatter_dimension=1, tiled=True)[:, 0]
    if stepwise:
        grad_wout = sum(
            (hop(grad_wout[r], r) if r else grad_wout[r]).astype(F32) for r in range(replicas)
        ).astype(BF)
    else:
        grad_wout = lax.psum_scatter(
            grad_wout.reshape(replicas * out_rows, width), "head", scatter_dimension=0, tiled=True
        )
    grad_out_proj = lax.all_gather(grad_wout, "dp", axis=0, tiled=True).astype(F32)

    grad_heads = contract(grad_branch, w_out_cat, 1, 1).astype(BF)
    sums = jnp.zeros((heads_here, TILE, 2 * length), F32)
    grad_blocks = [grad_heads[:, i * head_cols : (i + 1) * head_cols] for i in range(replicas)]
    grad_total = None
    weight_terms = []
    if stepwise:
        arrived = [hop(grad_blocks[r], r) if r else grad_blocks[0] for r in range(replicas)]
        for r in (0, 2, 3, 1):
            grad_qkv, sums = attend_bwd(order[r].reshape(1), qkv, arrived[r], kept[r], sums, length)
            normed_seq = lax.dynamic_slice_in_dim(normed, order[r] * length, length, 0)
            weight_terms.append(contract(normed_seq, grad_qkv, 0, 0))
            mine = hop(grad_qkv, r) if r else grad_qkv
            weight = lax.dynamic_index_in_dim(w_qkv_all, order[r], 0, keepdims=False)
            term = contract(mine, weight, 1, 1)
            grad_total = term if grad_total is None else grad_total + term
        grad_normed = grad_total
        grad_qkv_w = sum(weight_terms)
    else:
        stacked = jnp.stack(grad_blocks, axis=0)
        stacked = lax.all_to_all(stacked, "head", split_axis=0, concat_axis=0, tiled=True)
        stacked = stacked.reshape(group_rows, head_cols)
        seqs = []
        for s in range(sequences):
            grad_seq = stacked[s * length : (s + 1) * length]
            grad_qkv, sums = attend_bwd(
                jnp.full((1,), s, jnp.int32), qkv, grad_seq, kept[s], sums, length
            )
            seqs.append(grad_qkv)
        grad_qkv = jnp.concatenate(seqs, axis=0)
        grad_qkv_w = contract(normed, grad_qkv, 0, 0)
        grad_qkv = lax.all_to_all(
            grad_qkv.reshape(replicas, own_rows, 3 * head_cols),
            "head",
            split_axis=0,
            concat_axis=0,
            tiled=True,
        )
        grad_normed = sum(contract(grad_qkv[i], w_qkv_all[i], 1, 1) for i in range(replicas))

    _, norm1_pull = jax.vjp(rms_norm, inputs_own, norm1_gain)
    grad_first, grad_norm1 = norm1_pull(grad_normed)
    grad_input = grad_mixed + grad_first
    grad_bias = contract(unskew(sums), line, 1, 1, HIGH)
    grad_qkv_w, grad_bias = lax.psum((grad_qkv_w.astype(BF), grad_bias), "dp")
    grad_qkv_w = grad_qkv_w.astype(F32)
    grad_norm1, grad_norm2, grad_router = lax.psum(
        (grad_norm1, grad_norm2, grad_router), ("dp", "head")
    )
    return (
        output,
        grad_input,
        grad_norm1,
        grad_qkv_w[:, :head_cols],
        grad_qkv_w[:, head_cols : 2 * head_cols],
        grad_qkv_w[:, 2 * head_cols :],
        grad_out_proj,
        jnp.transpose(grad_bias),
        grad_norm2,
        grad_router,
        grad_gate_w,
        grad_up_w,
        grad_down_w,
    )


def body(*args):
    block_input, cotangent, rel_bucket, pos_bias, w_gate, w_router = (
        args[0],
        args[1],
        args[4],
        args[10],
        args[13],
        args[12],
    )
    own_rows = cotangent.shape[0]
    length = (rel_bucket.shape[0] + 1) // 2
    replicas, groups = lax.axis_size("head"), lax.axis_size("dp")
    experts = w_router.shape[1]
    capacity = 5 * 2 * own_rows // (4 * experts)
    stepwise = (
        own_rows == length
        and block_input.shape[0] == replicas * length
        and replicas == 4
        and groups == 8
        and experts == groups
        and capacity % 16 == 0
        and pos_bias.shape[1] in (2, 4, 6)
        and w_gate.shape[2] % 256 == 0
    )
    return body_steps(*args) if stepwise else body_plain(*args)


def body_steps(
    block_input,
    cotangent,
    expert_ids,
    priority,
    rel_bucket,
    norm1_gain,
    w_query,
    w_key,
    w_value,
    w_out,
    pos_bias,
    norm2_gain,
    w_router,
    w_gate,
    w_up,
    w_down,
):
    group_rows, width = block_input.shape
    own_rows = cotangent.shape[0]
    buckets, heads_here = pos_bias.shape
    head_cols = w_query.shape[1]
    length = (rel_bucket.shape[0] + 1) // 2
    experts = w_router.shape[1]
    capacity = 5 * 2 * own_rows // (4 * experts)
    slot_count = experts * capacity
    replicas, groups = lax.axis_size("head"), lax.axis_size("dp")
    me, dp_at = lax.axis_index("head"), lax.axis_index("dp")

    dest = route_slots(expert_ids, priority[0], experts, capacity)
    bits = (dest // capacity) ^ dp_at
    position = sum(p * (bits == offset).astype(jnp.int32) for p, offset in enumerate(OFFSETS))
    mixed_dest = jnp.where(
        dest < slot_count,
        position * capacity + dest % capacity,
        slot_count,
    )
    routing = jnp.concatenate([mixed_dest, expert_ids], axis=1)
    routing_rows = jnp.pad(routing.T, ((0, 4), (0, 0)))
    routing_cols = jnp.pad(routing, ((0, 0), (0, 4)))
    router_wide = jnp.pad(w_router, ((0, 0), (0, TILE - experts)))
    line = (rel_bucket[::-1][None, :] == jnp.arange(buckets, dtype=jnp.int32)[:, None]).astype(F32)
    line = jnp.pad(line, ((0, 0), (1, 0)))
    input_weights = (w_query, w_key, w_value)
    (
        attended,
        probs,
        cot_here,
        normed,
        qkv,
        w_cat,
        cot_far,
        routing_far,
        mixed,
        normed2,
    ) = attend_all(
        block_input,
        norm1_gain[None, :],
        input_weights,
        contract(pos_bias, line, 0, 0, HIGH)[:, None, :],
        cotangent,
        routing_rows,
        w_out,
        norm2_gain[None, :],
        groups,
        capacity,
    )

    gate_w, up_w, down_w = w_gate[0], w_up[0], w_down[0]
    tile = 256
    (
        rows_here,
        hidden_here,
        ggp_here,
        gup_here,
        scaled_here,
        back,
        grad_back,
        slot_slope,
        normed2_far,
        cot_far_rest,
    ) = expert_stage(
        normed2,
        routing_rows,
        cot_here,
        router_wide,
        gate_w,
        up_w,
        down_w,
        cotangent,
        groups,
        capacity,
        tile,
    )

    gates, grad_mixed, grad_branch, grad_heads, grad_router, grad_norm2 = combine(
        grad_back.reshape(slot_count, width),
        slot_slope.reshape(slot_count, TILE),
        routing_cols,
        mixed,
        normed2,
        cotangent,
        router_wide,
        norm2_gain[None, :],
        w_cat,
        experts,
    )

    far_rows, far_scaled, carry, part_sum, grad_qkv_w, grad_wout, lines = attend_back(
        normed2_far,
        (cot_far, cot_far_rest),
        routing_far,
        router_wide,
        grad_heads,
        qkv,
        probs,
        normed,
        input_weights,
        attended,
        grad_branch,
        groups,
        capacity,
    )

    (
        wide_kept,
        wide_came,
        tall_kept,
        tall_came,
        grad_qkv_w,
        grad_out_proj,
        summed,
        grad_first,
        expert_sum,
        _,
    ) = last_stage(
        (far_rows.reshape(slot_count, width), far_scaled.reshape(slot_count, width)),
        (rows_here.reshape(slot_count, width), scaled_here.reshape(slot_count, width)),
        (gates, routing_cols, norm1_gain[None, :]),
        (gate_w, up_w, down_w),
        (ggp_here, gup_here),
        hidden_here,
        (
            grad_qkv_w.reshape(groups, width // groups, 3 * head_cols),
            grad_wout.reshape(replicas, groups, head_cols // groups, width),
        ),
        (carry, part_sum, block_input, back),
        (grad_norm2, grad_router, lines),
        tile,
    )
    results = finish(
        (wide_kept, wide_came),
        (tall_kept, tall_came),
        grad_qkv_w,
        grad_out_proj,
        (mixed, expert_sum, grad_mixed, grad_first),
        summed,
        line.astype(BF),
        heads_here,
    )
    output, grad_input, grad_query_w, grad_key_w, grad_value_w, grad_out_proj = results[:6]
    grad_gate_w, grad_up_w, grad_down_w, grad_norm1, grad_norm2, grad_bias, grad_router = results[6:]
    return (
        output,
        grad_input,
        grad_norm1[0],
        grad_query_w,
        grad_key_w,
        grad_value_w,
        grad_out_proj,
        jnp.transpose(grad_bias),
        grad_norm2[0],
        jnp.transpose(grad_router),
        grad_gate_w[None],
        grad_up_w[None],
        grad_down_w[None],
    )


def solution(mesh):
    placed = (
        P("dp", None),
        P(("dp", "head"), None),
        P(("dp", "head"), None),
        P(("dp", "head"), None),
        P(),
        P(),
        P(None, "head"),
        P(None, "head"),
        P(None, "head"),
        P("head", None),
        P(None, "head"),
        P(),
        P(),
        P("dp", None, None),
        P("dp", None, None),
        P("dp", None, None),
    )
    return jax.shard_map(
        body,
        mesh=mesh,
        in_specs=placed,
        out_specs=(
            P(("dp", "head"), None),
            P(("dp", "head"), None),
            P(),
            P(None, "head"),
            P(None, "head"),
            P(None, "head"),
            P("head", None),
            P(None, "head"),
            P(),
            P(),
            P("dp", "head", None),
            P("dp", "head", None),
            P("dp", "head", None),
        ),
        check_vma=False,
    )
```

```python
import functools

import jax
import jax.numpy as jnp
from jax import lax
from jax.experimental import pallas as pl
from jax.experimental.pallas import tpu as pltpu
from jax.sharding import PartitionSpec as P

EPS = 1e-06
SCALE = 0.125
HIGH = lax.Precision.HIGHEST
TILE = 128
BF = jnp.bfloat16
F32 = jnp.float32
VMEM_LIMIT = 48 << 20
VMEM_MOST = 60 << 20
GELU_A = 0.7978845608028654
GELU_B = 0.044715
OFFSETS = [0, 1, 6, 7, 2, 4, 3, 5]
PEERS = [4, 5, 6, 7, 2, 3, 1]


def rms_norm(value, gain):
    return value * lax.rsqrt(jnp.mean(value * value, axis=-1, keepdims=True) + EPS) * gain


def geglu(gate, up_part):
    return jax.nn.gelu(gate) * up_part


def contract(left, right, left_dim, right_dim, precision=None):
    return lax.dot_general(
        left,
        right,
        (((left_dim,), (right_dim,)), ((), ())),
        precision=precision,
        preferred_element_type=jnp.float32,
    )


def route_slots(chosen, ranks, experts, capacity):
    count = chosen.shape[0]
    keys = jnp.concatenate([ranks, ranks + count])
    wanted = jnp.concatenate([chosen[:, 0], chosen[:, 1]])
    smaller = (wanted[:, None] == wanted[None, :]) & (keys[None, :] < keys[:, None])
    place = jnp.sum(smaller.astype(jnp.int32), axis=1)
    dest = jnp.where(place < capacity, wanted * capacity + place, experts * capacity)
    return jnp.stack([dest[:count], dest[count:]], axis=1)


def skew_kernel(line_ref, table_ref):
    heads, rows, cols = table_ref.shape
    row = lax.broadcasted_iota(jnp.int32, (8, cols), 0)
    for h in range(heads):
        value = jnp.broadcast_to(line_ref[h], (8, cols))
        for shift in (1, 2, 4):
            value = jnp.where((row & shift) != 0, pltpu.roll(value, shift, 1), value)
        table_ref[h, :8] = value
        done = 8
        while done < rows:
            table_ref[h, done : 2 * done] = pltpu.roll(table_ref[h, :done], done, 1)
            done *= 2


def unskew_kernel(table_ref, line_ref):
    heads, rows, cols = table_ref.shape
    row = lax.broadcasted_iota(jnp.int32, (8, cols), 0)
    for h in range(heads):
        value, left = table_ref[h], rows // 2
        while left >= 8:
            value = value[:left] + pltpu.roll(value[left:], cols - left, 1)
            left //= 2
        for shift in (1, 2, 4):
            value = jnp.where((row & shift) != 0, pltpu.roll(value, cols - shift, 1), value)
        line_ref[h] = jnp.sum(value, axis=0, keepdims=True)


def skew(line):
    heads, cols = line.shape
    return pl.pallas_call(
        skew_kernel,
        out_shape=jax.ShapeDtypeStruct((heads, TILE, cols), F32),
        compiler_params=pltpu.CompilerParams(vmem_limit_bytes=VMEM_LIMIT),
        name="skew",
    )(line[:, None, :])


def unskew(table):
    heads, _, cols = table.shape
    return pl.pallas_call(
        unskew_kernel,
        out_shape=jax.ShapeDtypeStruct((heads, 1, cols), F32),
        compiler_params=pltpu.CompilerParams(vmem_limit_bytes=VMEM_LIMIT),
        name="unskew",
    )(table)[:, 0]


def lanes_of(shape, half, part):
    lane = lax.broadcasted_iota(jnp.int32, shape, 1)
    return (lane >= half) if part else (lane < half)


def attend_fwd_kernel(seq_ref, q_ref, k_ref, v_ref, table_ref, out_ref, probs_ref, acc_ref):
    del seq_ref
    length, lanes = q_ref.shape
    half = lanes // 2
    chunk = 2 * TILE
    key = k_ref[...]
    value_t = v_ref[...].T
    for part in range(2):
        query = jnp.where(lanes_of((length, lanes), half, part), q_ref[...] * SCALE, 0).astype(BF)
        for c in range(length // chunk):
            cols = slice(c * chunk, (c + 1) * chunk)
            scores = contract(key, query[cols], 1, 1)
            pieces = []
            for kb in range(length // TILE):
                at = length - TILE * kb + chunk * c
                pieces.append(
                    scores[kb * TILE : (kb + 1) * TILE] + table_ref[part, :, at : at + chunk]
                )
            scores = jnp.concatenate(pieces, axis=0)
            top = jnp.max(scores, axis=0, keepdims=True)
            shifted = jnp.exp(scores - top)
            total = jnp.sum(shifted, axis=0, keepdims=True)
            probs = (shifted * (1.0 / total)).astype(BF)
            probs_ref[part, :, cols] = probs
            acc_ref[part * half : (part + 1) * half, cols] = jnp.dot(
                value_t[part * half : (part + 1) * half], probs, preferred_element_type=F32
            )
    out_ref[...] = acc_ref[...].T.astype(BF)


def attend_fwd(seq, qkv, table, length):
    heads, _, width = table.shape
    columns = qkv.shape[1] // 3
    pairs = heads // 2
    lanes = columns // pairs
    spec = [
        pl.BlockSpec((length, lanes), lambda p, s, j=j: (s[0], j * pairs + p)) for j in range(3)
    ]
    return pl.pallas_call(
        attend_fwd_kernel,
        out_shape=(
            jax.ShapeDtypeStruct((length, columns), BF),
            jax.ShapeDtypeStruct((heads, length, length), BF),
        ),
        grid_spec=pltpu.PrefetchScalarGridSpec(
            num_scalar_prefetch=1,
            grid=(pairs,),
            in_specs=spec + [pl.BlockSpec((2, TILE, width), lambda p, s: (p, 0, 0))],
            out_specs=[
                pl.BlockSpec((length, lanes), lambda p, s: (0, p)),
                pl.BlockSpec((2, length, length), lambda p, s: (p, 0, 0)),
            ],
            scratch_shapes=[pltpu.VMEM((lanes, length), F32)],
        ),
        compiler_params=pltpu.CompilerParams(vmem_limit_bytes=VMEM_LIMIT),
        cost_estimate=pl.CostEstimate(
            flops=heads * 8 * length * length * lanes,
            bytes_accessed=heads * length * length * 2 + 8 * length * columns,
            transcendentals=heads * length * length,
        ),
        name="attend_fwd",
    )(seq, qkv, qkv, qkv, table)


def attend_bwd_kernel(
    seq_ref, q_ref, k_ref, v_ref, grad_ref, probs_ref, sums_in_ref, out_ref, sums_ref, acc_ref
):
    del seq_ref
    length, lanes = q_ref.shape
    half = lanes // 2
    chunk = 2 * TILE
    pair = pl.program_id(0)
    columns = out_ref.shape[1] // 3
    key_t = k_ref[...].T
    value = v_ref[...]
    sums_ref[...] = sums_in_ref[...]
    grad_keys, grad_values = [], []
    for part in range(2):
        mask = lanes_of((length, lanes), half, part)
        grad = jnp.where(mask, grad_ref[...], 0).astype(BF)
        grad_key = jnp.zeros((length, lanes), F32)
        grad_value = jnp.zeros((length, lanes), F32)
        for c in range(length // chunk):
            cols = slice(c * chunk, (c + 1) * chunk)
            grad_probs = contract(value, grad[cols], 1, 1)
            probs_low = probs_ref[part, :, cols]
            probs = probs_low.astype(F32)
            delta = jnp.sum(probs * grad_probs, axis=0, keepdims=True)
            grad_scores = (probs * (grad_probs - delta)).astype(BF)
            grad_value += jnp.dot(probs_low, grad_ref[cols, :], preferred_element_type=F32)
            grad_key += jnp.dot(grad_scores, q_ref[cols, :], preferred_element_type=F32)
            acc_ref[part * half : (part + 1) * half, cols] = jnp.dot(
                key_t[part * half : (part + 1) * half], grad_scores, preferred_element_type=F32
            )
            for kb in range(length // TILE):
                at = length - TILE * kb + chunk * c
                sums_ref[part, :, at : at + chunk] += grad_scores[
                    kb * TILE : (kb + 1) * TILE
                ].astype(F32)
        grad_keys.append(grad_key)
        grad_values.append(grad_value)
    first = lanes_of((length, lanes), half, 0)
    at = pl.multiple_of(pair * lanes, lanes)
    out_ref[:, pl.ds(at, lanes)] = (acc_ref[...].T * SCALE).astype(BF)
    at = pl.multiple_of(columns + pair * lanes, lanes)
    out_ref[:, pl.ds(at, lanes)] = (jnp.where(first, *grad_keys) * SCALE).astype(BF)
    at = pl.multiple_of(2 * columns + pair * lanes, lanes)
    out_ref[:, pl.ds(at, lanes)] = jnp.where(first, *grad_values).astype(BF)


def attend_bwd(seq, qkv, grad, probs, sums, length):
    heads, _, width = sums.shape
    columns = qkv.shape[1] // 3
    pairs = heads // 2
    lanes = columns // pairs
    spec = [
        pl.BlockSpec((length, lanes), lambda p, s, j=j: (s[0], j * pairs + p)) for j in range(3)
    ]
    sums_spec = pl.BlockSpec((2, TILE, width), lambda p, s: (p, 0, 0))
    return pl.pallas_call(
        attend_bwd_kernel,
        out_shape=(
            jax.ShapeDtypeStruct((length, 3 * columns), BF),
            jax.ShapeDtypeStruct(sums.shape, F32),
        ),
        grid_spec=pltpu.PrefetchScalarGridSpec(
            num_scalar_prefetch=1,
            grid=(pairs,),
            in_specs=spec
            + [
                pl.BlockSpec((length, lanes), lambda p, s: (0, p)),
                pl.BlockSpec((2, length, length), lambda p, s: (p, 0, 0)),
                sums_spec,
            ],
            out_specs=[pl.BlockSpec((length, 3 * columns), lambda p, s: (0, 0)), sums_spec],
            scratch_shapes=[pltpu.VMEM((lanes, length), F32)],
        ),
        compiler_params=pltpu.CompilerParams(vmem_limit_bytes=VMEM_LIMIT),
        cost_estimate=pl.CostEstimate(
            flops=heads * 16 * length * length * lanes,
            bytes_accessed=heads * length * length * 2 + 16 * length * columns,
            transcendentals=0,
        ),
        name="attend_bwd",
    )(seq, qkv, qkv, qkv, grad, probs, sums)


def flipped(index, bits):
    out, step = index, 1
    while step <= bits:
        if bits & step:
            out = out + step * (1 - 2 * lax.rem(index // step, 2))
        step *= 2
    return out


def plane(d, position):
    return flipped(d, OFFSETS[position])


def greet(peers):
    barrier = pltpu.get_barrier_semaphore()
    for peer in peers:
        pl.semaphore_signal(barrier, inc=1, device_id=peer, device_id_type=pl.DeviceIdType.MESH)
    pl.semaphore_wait(barrier, len(peers))


def remote(source, target, send_sem, recv_sem, peer):
    return pltpu.make_async_remote_copy(
        src_ref=source,
        dst_ref=target,
        send_sem=send_sem,
        recv_sem=recv_sem,
        device_id=peer,
        device_id_type=pl.DeviceIdType.MESH,
    )


def attend_all_kernel(
    input_hbm,
    gain_ref,
    query_hbm,
    key_hbm,
    value_hbm,
    line_ref,
    cot_hbm,
    routing_ref,
    w_out_hbm,
    gain2_ref,
    attended_out,
    probs_out,
    came_out,
    normed_out,
    qkv_out,
    w_cat_out,
    cot_far_out,
    routing_far_out,
    mixed_ref,
    normed2_ref,
    input_ref,
    weight_ref,
    cot_ref,
    w_out_ref,
    table_ref,
    sends,
    acc_ref,
    block_ref,
    hold_ref,
    normed_ref,
    qkv_ref,
    attended_ref,
    w_cat,
    w_land,
    row_send,
    row_recv,
    hop_send,
    hop_recv,
    w_send,
    w_recv,
    plane_send,
    plane_recv,
    core_send,
    core_recv,
    far_send,
    far_recv,
    hold_sem,
    own_sem,
    load_sem,
):
    z, d = lax.axis_index("head"), lax.axis_index("dp")
    heads, _, _ = table_ref.shape
    replicas, length, columns = block_ref.shape
    groups, capacity, _ = sends.shape
    width = input_ref.shape[1]
    part_rows = w_land.shape[1]
    pairs = heads // 2
    lanes = columns // pairs
    half = lanes // 2
    chunk = 2 * TILE
    hops = [3, 2, 1]
    cot_load = pltpu.make_async_copy(cot_hbm, cot_ref, load_sem.at[0])
    w_out_load = pltpu.make_async_copy(w_out_hbm, w_out_ref, load_sem.at[1])
    weight_loads = [
        pltpu.make_async_copy(
            source, weight_ref.at[:, pl.ds(i * columns, columns)], load_sem.at[2 + i]
        )
        for i, source in enumerate((query_hbm, key_hbm, value_hbm))
    ]
    input_loads = {}
    for r in [3, 2, 1, 0]:
        span = pl.ds(pl.multiple_of(flipped(z, r) * length, length), length)
        input_loads[r] = pltpu.make_async_copy(
            input_hbm.at[span], input_ref.at[span], load_sem.at[5 + r]
        )
    for copy in [cot_load, input_loads[3]] + weight_loads:
        copy.start()
    for copy in [input_loads[2], input_loads[1], input_loads[0], w_out_load]:
        copy.start()
    greet([{"dp": plane(d, o)} for o in PEERS] + [{"head": flipped(z, r)} for r in hops])
    copies = []

    def launch(*what):
        copy = remote(*what)
        copy.start()
        copies.append(copy)
        return copy

    piece = w_out_hbm.at[pl.ds(pl.multiple_of(d * part_rows, part_rows), part_rows), :]
    w_hops = {}
    for r in hops:
        w_hops[r] = remote(piece, w_land.at[r], w_send.at[r], w_recv.at[r], {"head": flipped(z, r)})
        w_hops[r].start()
    cot_load.wait()
    half_plane = groups // 2

    def dispatch(start):
        span = slice(start, start + half_plane)
        first, second = selector(routing_ref, start * capacity, half_plane * capacity)
        sends[span, :, :width] = (
            jnp.dot((first + second).astype(BF), cot_ref[...], preferred_element_type=F32)
            .astype(BF)
            .reshape(half_plane, capacity, width)
        )
        sends[span, :, width:] = slot_signs(routing_ref, first, second).reshape(
            half_plane, capacity, TILE
        )

    def send_rows(start):
        for o in range(start, start + half_plane):
            if o:
                launch(
                    sends.at[o], came_out.at[o], row_send.at[o], row_recv.at[o], {"dp": plane(d, o)}
                )

    chips = [o for o, bits in enumerate(OFFSETS) if o and bits % 2 == 0]
    plane_copies = {}

    def w_rows(s, o):
        at = s * columns + plane(d, o) * part_rows
        return pl.ds(pl.multiple_of(at, part_rows), part_rows)

    dispatch(half_plane)
    for s in hops:
        w_hops[s].wait()
        at = w_rows(s, 0)
        w_cat[at, :] = w_land[s]
        for o in chips:
            plane_copies[s, o] = remote(
                w_land.at[s],
                w_cat.at[at, :],
                plane_send.at[s, o],
                plane_recv.at[s, o],
                {"dp": plane(d, o)},
            )
            plane_copies[s, o].start()
    send_rows(half_plane)
    dispatch(0)
    send_rows(0)
    own = pltpu.make_async_copy(sends.at[0], came_out.at[0], own_sem.at[0])
    own.start()
    far = {"head": flipped(z, 2)}
    launch(routing_ref, routing_far_out, far_send.at[0], far_recv.at[0], far)
    early = pl.ds(0, cot_far_out.shape[0])
    launch(cot_hbm.at[early], cot_far_out, far_send.at[1], far_recv.at[1], far)
    skew_kernel(line_ref, table_ref)
    w_out_load.wait()
    w_cat[:columns, :] = w_out_ref[...]

    moves = []
    for turn, r in enumerate(reversed(range(replicas))):
        start = flipped(z, r) * length
        slot = turn % 2
        if turn >= 2:
            for move in moves[turn - 2]:
                move.wait()

        input_loads[r].wait()

        def norm_step(i, carry, start=start, slot=slot):
            rows = pl.multiple_of(start + i * TILE, TILE)
            value = input_ref[pl.ds(rows, TILE), :].astype(F32)
            value = rms_norm(value, gain_ref[...])
            normed_ref[slot, pl.ds(pl.multiple_of(i * TILE, TILE), TILE), :] = value.astype(BF)
            return carry

        lax.fori_loop(0, length // TILE, norm_step, 0)
        if turn == 0:
            for copy in weight_loads:
                copy.wait()
        qkv_ref[slot] = jnp.dot(
            normed_ref[slot], weight_ref[...], preferred_element_type=F32
        ).astype(BF)

        def pair_step(pair, carry, slot=slot, r=r):
            def part_of(j):
                at = pl.multiple_of(j * columns + pair * lanes, lanes)
                return qkv_ref[slot, :, pl.ds(at, lanes)]

            key = part_of(1)
            value_t = part_of(2).T
            scaled = part_of(0) * SCALE
            for part in range(2):
                query = jnp.where(lanes_of((length, lanes), half, part), scaled, 0).astype(BF)
                for c in range(length // chunk):
                    cols = slice(c * chunk, (c + 1) * chunk)
                    scores = contract(key, query[cols], 1, 1)
                    pieces = []
                    for kb in range(length // TILE):
                        at = length - TILE * kb + chunk * c
                        pieces.append(
                            scores[kb * TILE : (kb + 1) * TILE]
                            + table_ref[pair * 2 + part, :, at : at + chunk]
                        )
                    scores = jnp.concatenate(pieces, axis=0)
                    top = jnp.max(scores, axis=0, keepdims=True)
                    shifted = jnp.exp(scores - top)
                    total = jnp.sum(shifted, axis=0, keepdims=True)
                    probs = (shifted * (1.0 / total)).astype(BF)
                    hold_ref[slot, pair * 2 + part, :, cols] = probs
                    acc_ref[part * half : (part + 1) * half, cols] = jnp.dot(
                        value_t[part * half : (part + 1) * half],
                        probs,
                        preferred_element_type=F32,
                    )
            at = pl.multiple_of(pair * lanes, lanes)
            block_ref[r, :, pl.ds(at, lanes)] = acc_ref[...].T.astype(BF)
            return carry

        lax.fori_loop(0, pairs, pair_step, 0)
        moves.append(
            [
                pltpu.make_async_copy(ref.at[slot], out.at[r], hold_sem.at[i, slot])
                for i, (ref, out) in enumerate(
                    ((hold_ref, probs_out), (normed_ref, normed_out), (qkv_ref, qkv_out))
                )
            ]
        )
        for move in moves[-1]:
            move.start()
        if r:
            launch(
                block_ref.at[r],
                attended_ref.at[:, pl.ds(r * columns, columns)],
                hop_send.at[r],
                hop_recv.at[r],
                {"head": flipped(z, r)},
            )
        else:
            attended_ref[:, :columns] = block_ref[0]
        if turn == 1:
            for s in hops:
                for o in [0] + chips:
                    if o:
                        plane_copies[s, o].wait_recv()
                    piece = w_cat.at[w_rows(s, o), :]
                    launch(piece, piece, core_send.at[s, o], core_recv.at[s, o], {"dp": plane(d, 1)})
    for copy in plane_copies.values():
        copy.wait_send()
    for copy in copies:
        copy.wait()
    outs = [
        pltpu.make_async_copy(attended_ref, attended_out, own_sem.at[1]),
        pltpu.make_async_copy(w_cat, w_cat_out, own_sem.at[2]),
    ]
    for copy in outs:
        copy.start()

    mixed_ref[...] = jnp.dot(attended_ref[...], w_cat[...], preferred_element_type=F32)

    def mixed_step(i, carry):
        at = pl.multiple_of(i * TILE, TILE)
        span = pl.ds(at, TILE)
        rows = pl.multiple_of(z * length + at, TILE)
        value = mixed_ref[span, :] + input_ref[pl.ds(rows, TILE), :].astype(F32)
        mixed_ref[span, :] = value
        normed2_ref[span, :] = rms_norm(value, gain2_ref[...]).astype(BF)
        return carry

    lax.fori_loop(0, length // TILE, mixed_step, 0)
    for move in moves[-2] + moves[-1] + outs + [own]:
        move.wait()


def attend_all(inputs, gain, weights, line, cot, routing, w_out, gain2, groups, capacity):
    heads, _, table_width = line.shape
    width = inputs.shape[1]
    length = cot.shape[0]
    replicas = inputs.shape[0] // length
    columns = weights[0].shape[1]
    lanes = 2 * columns // heads
    part_rows = columns // groups
    vmem = pl.BlockSpec(memory_space=pltpu.VMEM)
    hbm = pl.BlockSpec(memory_space=pl.ANY)
    came_shape = (groups, capacity, width + TILE)
    plane_sem = pltpu.SemaphoreType.DMA((groups,))
    hop_sem = pltpu.SemaphoreType.DMA((replicas,))
    both_sem = pltpu.SemaphoreType.DMA((replicas, groups))
    two_sem = pltpu.SemaphoreType.DMA((2,))
    return pl.pallas_call(
        attend_all_kernel,
        out_shape=(
            jax.ShapeDtypeStruct((length, replicas * columns), BF),
            jax.ShapeDtypeStruct((replicas, heads, length, length), BF),
            jax.ShapeDtypeStruct(came_shape, BF),
            jax.ShapeDtypeStruct((replicas, length, width), BF),
            jax.ShapeDtypeStruct((replicas, length, 3 * columns), BF),
            jax.ShapeDtypeStruct((replicas * columns, width), BF),
            jax.ShapeDtypeStruct((length // 2, width), BF),
            jax.ShapeDtypeStruct(routing.shape, routing.dtype),
            jax.ShapeDtypeStruct((length, width), F32),
            jax.ShapeDtypeStruct((length, width), BF),
        ),
        in_specs=[hbm, vmem, hbm, hbm, hbm, vmem, hbm, vmem, hbm, vmem],
        out_specs=[hbm] * 8 + [vmem] * 2,
        scratch_shapes=[
            pltpu.VMEM(inputs.shape, BF),
            pltpu.VMEM((width, 3 * columns), BF),
            pltpu.VMEM(cot.shape, BF),
            pltpu.VMEM(w_out.shape, BF),
            pltpu.VMEM((heads, TILE, table_width), F32),
            pltpu.VMEM(came_shape, BF),
            pltpu.VMEM((lanes, length), F32),
            pltpu.VMEM((replicas, length, columns), BF),
            pltpu.VMEM((2, heads, length, length), BF),
            pltpu.VMEM((2, length, width), BF),
            pltpu.VMEM((2, length, 3 * columns), BF),
            pltpu.VMEM((length, replicas * columns), BF),
            pltpu.VMEM((replicas * columns, width), BF),
            pltpu.VMEM((replicas, part_rows, width), BF),
            plane_sem,
            plane_sem,
            hop_sem,
            hop_sem,
            hop_sem,
            hop_sem,
            both_sem,
            both_sem,
            both_sem,
            both_sem,
            two_sem,
            two_sem,
            pltpu.SemaphoreType.DMA((3, 2)),
            pltpu.SemaphoreType.DMA((3,)),
            pltpu.SemaphoreType.DMA((9,)),
        ],
        compiler_params=pltpu.CompilerParams(
            vmem_limit_bytes=VMEM_MOST, collective_id=1, has_side_effects=True
        ),
        cost_estimate=pl.CostEstimate(
            flops=replicas * heads * 8 * length * length * lanes,
            bytes_accessed=replicas * heads * length * length * 4,
            transcendentals=replicas * heads * length * length,
        ),
        name="attend_all",
    )(inputs, gain, *weights, line, cot, routing, w_out, gain2)


def selector(routing, start, count):
    slot = lax.broadcasted_iota(jnp.int32, (count, routing.shape[1]), 0) + start
    return [jnp.where(slot == routing[k : k + 1], 1.0, 0.0) for k in range(2)]


def slot_signs(routing, first, second):
    lane = lax.broadcasted_iota(jnp.int32, (TILE, routing.shape[1]), 0)
    signs = jnp.where(lane == routing[3:4], 1.0, 0.0) - jnp.where(lane == routing[2:3], 1.0, 0.0)
    return contract((first - second).astype(BF), signs.astype(BF), 1, 1).astype(BF)


def token_selector(routing, slots):
    slot = lax.broadcasted_iota(jnp.int32, (routing.shape[0], slots), 1)
    return [jnp.where(slot == routing[:, k : k + 1], 1.0, 0.0) for k in range(2)]


def expert_tile(rows, scaled, gate_w, up_w, down_w):
    gate = jnp.dot(rows, gate_w, preferred_element_type=F32)
    up_part = jnp.dot(rows, up_w, preferred_element_type=F32)
    grad_hidden = contract(scaled, down_w, 1, 1)
    square = gate * gate
    bend = jnp.tanh(gate * (GELU_A + GELU_A * GELU_B * square))
    half = 0.5 + 0.5 * bend
    active = gate * half
    slope = half + 0.5 * gate * (1.0 - bend * bend) * (GELU_A + 3.0 * GELU_A * GELU_B * square)
    hidden = (active * up_part).astype(BF)
    grad_gate = (grad_hidden * up_part * slope).astype(BF)
    grad_up = (grad_hidden * active).astype(BF)
    return hidden, grad_gate, grad_up


def scaled_rows(rows, extended, router, width):
    logits = jnp.dot(rows, router, preferred_element_type=F32)
    sign = extended[:, width:].astype(F32)
    gap = jnp.sum(logits * sign, axis=1, keepdims=True)
    return (extended[:, :width].astype(F32) * (1.0 / (1.0 + jnp.exp(gap)))).astype(BF)


def expert_kernel(
    width,
    tile,
    normed_ref,
    routing_ref,
    cot_ref,
    router_ref,
    gate_hbm,
    up_hbm,
    down_hbm,
    cot_hbm,
    rows_out,
    hidden_out,
    grad_gate_out,
    grad_up_out,
    scaled_out,
    back_out,
    grad_back_out,
    slope_out,
    far_out,
    cot_far_out,
    gate_w,
    up_w,
    down_w,
    rows,
    sends,
    back,
    grad_back,
    slopes,
    hidden,
    grad_gate,
    grad_up,
    scaled,
    weight_sem,
    row_send,
    row_recv,
    slope_send,
    slope_recv,
    grad_send,
    grad_recv,
    unit_sem,
    keep_sem,
    far_sem,
):
    z, d = lax.axis_index("head"), lax.axis_index("dp")
    far = {"head": flipped(z, 2)}
    groups, capacity, _ = rows.shape
    units = gate_w.shape[1]
    tiles = units // tile
    count = 2 * capacity

    def weights_of(t):
        at = t * tile if isinstance(t, int) else pl.multiple_of(t * tile, tile)
        return [
            pltpu.make_async_copy(
                gate_hbm.at[:, pl.ds(at, tile)], gate_w.at[:, pl.ds(at, tile)], weight_sem.at[0, t]
            ),
            pltpu.make_async_copy(
                up_hbm.at[:, pl.ds(at, tile)], up_w.at[:, pl.ds(at, tile)], weight_sem.at[1, t]
            ),
            pltpu.make_async_copy(
                down_hbm.at[pl.ds(at, tile), :], down_w.at[pl.ds(at, tile), :], weight_sem.at[2, t]
            ),
        ]

    def start_weights(t, carry):
        for copy in weights_of(t):
            copy.start()
        return carry

    lax.fori_loop(0, tiles, start_weights, 0)
    greet([{"dp": plane(d, o)} for o in PEERS] + [far])
    pending = []
    arrivals = {}

    for start, number in ((2, 2), (4, groups - 4), (0, 2)):
        first, second = selector(routing_ref, start * capacity, number * capacity)
        sends[start : start + number] = (
            jnp.dot((first + second).astype(BF), normed_ref[...], preferred_element_type=F32)
            .astype(BF)
            .reshape(number, capacity, width)
        )
        for o in range(start, start + number):
            if o:
                arrivals[o] = remote(
                    sends.at[o], rows.at[o], row_send.at[o], row_recv.at[o], {"dp": plane(d, o)}
                )
                arrivals[o].start()
    over = [
        remote(normed_ref, far_out, far_sem.at[0, 0], far_sem.at[0, 1], far),
        remote(
            cot_hbm.at[pl.ds(cot_far_out.shape[0], cot_far_out.shape[0])],
            cot_far_out,
            far_sem.at[1, 0],
            far_sem.at[1, 1],
            far,
        ),
    ]
    for copy in over:
        copy.start()
    rows[0] = sends[0]

    unit_copies = {}
    order = list(range(groups // 2))
    for turn, j in enumerate(order):
        pair = (2 * j, 2 * j + 1)
        slot = turn % 2
        for o in pair:
            if o:
                arrivals[o].wait_recv()
        if turn >= 2:
            for copy in unit_copies[order[turn - 2]]:
                copy.wait()
        here = rows[2 * j : 2 * j + 2].reshape(count, width)
        extended = cot_ref[2 * j : 2 * j + 2].reshape(count, cot_ref.shape[2])
        scaled[2 * j : 2 * j + 2] = scaled_rows(here, extended, router_ref[...], width).reshape(
            2, capacity, width
        )

        def wide_tile(at, size, j=j, slot=slot):
            values = expert_tile(
                rows[2 * j : 2 * j + 2].reshape(count, width),
                scaled[2 * j : 2 * j + 2].reshape(count, width),
                gate_w[:, pl.ds(at, size)],
                up_w[:, pl.ds(at, size)],
                down_w[pl.ds(at, size), :],
            )
            for ref, value in zip((hidden, grad_gate, grad_up), values):
                ref[slot, :, pl.ds(at, size)] = value

        def tile_step(t, carry, j=j):
            if j == 0:
                for i in range(2):
                    for copy in weights_of(2 * t + i):
                        copy.wait()
            wide_tile(pl.multiple_of(2 * t * tile, tile), 2 * tile)
            return carry

        lax.fori_loop(0, tiles // 2, tile_step, 0)
        if tiles % 2:
            if j == 0:
                for copy in weights_of(tiles - 1):
                    copy.wait()
            wide_tile((tiles - 1) * tile, tile)
        span = pl.ds(j * count, count)
        unit_copies[j] = [
            pltpu.make_async_copy(ref.at[slot], out.at[span], unit_sem.at[slot, i])
            for i, (ref, out) in enumerate(
                ((hidden, hidden_out), (grad_gate, grad_gate_out), (grad_up, grad_up_out))
            )
        ]
        for copy in unit_copies[j]:
            copy.start()

        def back_step(t, carry, j=j, slot=slot):
            cols = pl.ds(pl.multiple_of(t * 2 * tile, 2 * tile), 2 * tile)
            value = jnp.dot(hidden[slot], down_w[:, cols], preferred_element_type=F32)
            back[2 * j : 2 * j + 2, :, cols] = value.astype(BF).reshape(2, capacity, 2 * tile)
            return carry

        def grad_step(t, carry, j=j, slot=slot):
            cols = pl.ds(pl.multiple_of(t * 2 * tile, 2 * tile), 2 * tile)
            value = contract(grad_gate[slot], gate_w[cols, :], 1, 1) + contract(
                grad_up[slot], up_w[cols, :], 1, 1
            )
            grad_back[2 * j : 2 * j + 2, :, cols] = value.astype(BF).reshape(2, capacity, 2 * tile)
            return carry

        def give(buffer, out, send_sem, recv_sem, pair=pair):
            for o in pair:
                if o:
                    copy = remote(
                        buffer.at[o],
                        out.at[o],
                        send_sem.at[o],
                        recv_sem.at[o],
                        {"dp": plane(d, o)},
                    )
                else:
                    copy = pltpu.make_async_copy(buffer.at[0], out.at[0], send_sem.at[0])
                copy.start()
                pending.append(copy)

        lax.fori_loop(0, width // (2 * tile), grad_step, 0)
        give(grad_back, grad_back_out, grad_send, grad_recv)
        lax.fori_loop(0, width // (2 * tile), back_step, 0)
        product = jnp.sum(
            cot_ref[2 * j : 2 * j + 2, :, :width].reshape(count, width).astype(F32)
            * back[2 * j : 2 * j + 2].reshape(count, width).astype(F32),
            axis=1,
            keepdims=True,
        )
        lane = lax.broadcasted_iota(jnp.int32, (count, TILE), 1)
        spread = jnp.zeros((count, TILE), F32)
        for k, term in enumerate(split_parts(product)):
            spread = jnp.where(lane == k, term.astype(F32), spread)
        slopes[2 * j : 2 * j + 2] = spread.astype(BF).reshape(2, capacity, TILE)
        give(slopes, slope_out, slope_send, slope_recv)

    keeps = [
        pltpu.make_async_copy(rows, rows_out, keep_sem.at[0]),
        pltpu.make_async_copy(scaled, scaled_out, keep_sem.at[1]),
        pltpu.make_async_copy(back, back_out, keep_sem.at[2]),
    ]
    for copy in keeps:
        copy.start()
    for j in order[-2:]:
        for copy in unit_copies[j]:
            copy.wait()
    for o in PEERS:
        arrivals[o].wait_send()
    for copy in pending + keeps + over:
        copy.wait()


def expert_stage(
    normed2, routing, cot, router, gate_w, up_w, down_w, cot_own, groups, capacity, tile
):
    width, units = gate_w.shape
    slots = groups * capacity
    vmem = pl.BlockSpec(memory_space=pltpu.VMEM)
    hbm = pl.BlockSpec(memory_space=pl.ANY)
    row_shape = jax.ShapeDtypeStruct((groups, capacity, width), BF)
    unit_shape = jax.ShapeDtypeStruct((slots, units), BF)
    row_buffer = pltpu.VMEM((groups, capacity, width), BF)
    unit_buffer = pltpu.VMEM((2, 2 * capacity, units), BF)
    row_sem = pltpu.SemaphoreType.DMA((groups,))
    return pl.pallas_call(
        functools.partial(expert_kernel, width, tile),
        out_shape=(row_shape,)
        + (unit_shape,) * 3
        + (row_shape,) * 3
        + (
            jax.ShapeDtypeStruct((groups, capacity, TILE), BF),
            jax.ShapeDtypeStruct(normed2.shape, BF),
            jax.ShapeDtypeStruct((normed2.shape[0] // 2, width), BF),
        ),
        in_specs=[vmem] * 4 + [hbm] * 4,
        out_specs=[hbm] * 10,
        scratch_shapes=[
            pltpu.VMEM((width, units), BF),
            pltpu.VMEM((width, units), BF),
            pltpu.VMEM((units, width), BF),
            row_buffer,
            row_buffer,
            row_buffer,
            row_buffer,
            pltpu.VMEM((groups, capacity, TILE), BF),
            unit_buffer,
            unit_buffer,
            unit_buffer,
            row_buffer,
            pltpu.SemaphoreType.DMA((3, units // tile)),
            row_sem,
            row_sem,
            row_sem,
            row_sem,
            row_sem,
            row_sem,
            pltpu.SemaphoreType.DMA((2, 3)),
            pltpu.SemaphoreType.DMA((3,)),
            pltpu.SemaphoreType.DMA((2, 2)),
        ],
        compiler_params=pltpu.CompilerParams(
            vmem_limit_bytes=VMEM_MOST, collective_id=2, has_side_effects=True
        ),
        cost_estimate=pl.CostEstimate(
            flops=12 * slots * width * units,
            bytes_accessed=6 * width * units + 6 * slots * units,
            transcendentals=slots * units,
        ),
        name="expert_stage",
    )(normed2, routing, cot, router, gate_w, up_w, down_w, cot_own)


def split_parts(value):
    first = value.astype(BF)
    rest = value - first.astype(F32)
    second = rest.astype(BF)
    return first, second, (rest - second.astype(F32)).astype(BF)


def combine_kernel(
    grad_back_ref,
    slot_slope_ref,
    routing_ref,
    mixed_ref,
    normed2_ref,
    cot_ref,
    router_ref,
    gain_ref,
    w_cat_ref,
    gates_ref,
    grad_mixed_ref,
    grad_branch_ref,
    grad_heads_ref,
    grad_router_ref,
    grad_norm2_ref,
    picked,
    slopes,
    gaps,
    pick,
):
    length, width = mixed_ref.shape

    slots = grad_back_ref.shape[0]
    first, second = token_selector(routing_ref, slots)
    gaps[...] = jnp.dot(
        (second - first).astype(BF), slot_slope_ref[...], preferred_element_type=F32
    )
    pick[...] = (first + second).astype(BF)

    picked[...] = jnp.dot(pick[...], grad_back_ref[...], preferred_element_type=F32)
    lane = lax.broadcasted_iota(jnp.int32, (TILE, TILE), 1)

    def row_step(i, total):
        span = pl.ds(pl.multiple_of(i * TILE, TILE), TILE)
        ids = routing_ref[span, :]
        sign = jnp.where(lane == ids[:, 3:4], 1.0, 0.0) - jnp.where(lane == ids[:, 2:3], 1.0, 0.0)
        logits = jnp.dot(normed2_ref[span, :], router_ref[...], preferred_element_type=F32)
        gap = jnp.sum(logits * sign, axis=1, keepdims=True)
        gate0, gate1 = 1.0 / (1.0 + jnp.exp(gap)), 1.0 / (1.0 + jnp.exp(-gap))
        cot = cot_ref[span, :].astype(F32)
        mixed = mixed_ref[span, :]
        gates_ref[span, :] = jnp.where(lane == 0, gate0, gate1)
        grad_gap = jnp.sum(gaps[span, :], axis=1, keepdims=True)
        slope = gate0 * gate1 * grad_gap * sign
        slopes[span, :] = slope
        grad_normed2 = picked[span, :] + sum(
            contract(part, router_ref[...], 1, 1) for part in split_parts(slope)
        )
        scale = lax.rsqrt(jnp.mean(mixed * mixed, axis=1, keepdims=True) + EPS)
        inner = grad_normed2 * gain_ref[...]
        mean = jnp.mean(inner * mixed, axis=1, keepdims=True)
        grad_mixed = cot + scale * inner - mixed * (scale * scale * scale * mean)
        grad_mixed_ref[span, :] = grad_mixed
        grad_branch_ref[span, :] = grad_mixed.astype(BF)
        return total + jnp.sum(grad_normed2 * mixed * scale, axis=0, keepdims=True)

    grad_norm2_ref[...] = lax.fori_loop(
        0, length // TILE, row_step, jnp.zeros((1, width), F32)
    )

    grad_heads_ref[...] = contract(grad_branch_ref[...], w_cat_ref[...], 1, 1).astype(BF)
    experts = grad_router_ref.shape[0]
    grad_router_ref[...] = sum(
        contract(part, normed2_ref[...], 0, 0) for part in split_parts(slopes[...])
    )[:experts]


def attend_back_kernel(
    normed2_far,
    cot_first,
    cot_last,
    routing_ref,
    router_ref,
    back_ref,
    slope_ref,
    columns_ref,
    mixed_ref,
    normed2_ref,
    cot_ref,
    gain_ref,
    w_cat_ref,
    qkv_hbm,
    probs_hbm,
    normed_hbm,
    query_hbm,
    key_hbm,
    value_hbm,
    attended_ref,
    far_rows_ref,
    far_scaled_ref,
    gates_ref,
    grad_mixed_ref,
    grad_router_ref,
    grad_norm2_ref,
    carry_ref,
    part_sum_ref,
    qkv_w_ref,
    out_w_ref,
    lines_ref,
    sums_ref,
    acc_ref,
    grad_branch_ref,
    grad_ref,
    slopes,
    gaps,
    pick,
    sends,
    cot_far,
    grads,
    qkv_ref,
    probs_ref,
    normed_ref,
    grad_qkv_ref,
    weight_ref,
    weight_sum,
    parts,
    landed,
    far_send,
    far_recv,
    hop_send,
    hop_recv,
    part_send,
    part_recv,
    load_sem,
    weight_sem,
    own_sem,
):
    z, d = lax.axis_index("head"), lax.axis_index("dp")
    replicas, length, columns = grads.shape
    _, groups, capacity, _ = sends.shape
    width = normed2_far.shape[1]
    heads = sums_ref.shape[0]
    pairs = heads // 2
    lanes = columns // pairs
    half = lanes // 2
    chunk = 2 * TILE
    hops = [3, 2, 1]
    order = [1, 3, 0, 2]

    def loads(turn):
        r, slot = order[turn], turn % 2
        return [
            pltpu.make_async_copy(source.at[r], target.at[slot], load_sem.at[i, slot])
            for i, (source, target) in enumerate(
                ((qkv_hbm, qkv_ref), (probs_hbm, probs_ref), (normed_hbm, normed_ref))
            )
        ]

    weight_loads = [
        pltpu.make_async_copy(
            source, weight_ref.at[:, pl.ds(i * columns, columns)], weight_sem.at[i]
        )
        for i, source in enumerate((query_hbm, key_hbm, value_hbm))
    ]
    for copy in loads(0) + weight_loads:
        copy.start()
    greet([{"dp": plane(d, o)} for o in PEERS] + [{"head": flipped(z, r)} for r in hops])
    copies = []
    combine_kernel(
        back_ref,
        slope_ref,
        columns_ref,
        mixed_ref,
        normed2_ref,
        cot_ref,
        router_ref,
        gain_ref,
        w_cat_ref,
        gates_ref,
        grad_mixed_ref,
        grad_branch_ref,
        grad_ref,
        grad_router_ref,
        grad_norm2_ref,
        part_sum_ref,
        slopes,
        gaps,
        pick,
    )
    arrivals = {}
    for r in [1, 3, 2]:
        arrivals[r] = remote(
            grad_ref.at[:, pl.ds(r * columns, columns)],
            grads.at[r],
            hop_send.at[r],
            hop_recv.at[r],
            {"head": flipped(z, r)},
        )
        arrivals[r].start()
    half_plane = groups // 2
    at = 0
    for piece in (cot_first, cot_last):
        cot_far[at : at + piece.shape[0]] = piece[...]
        at += piece.shape[0]
    logits = contract(router_ref[...], normed2_far[...], 0, 1)
    expert = lax.broadcasted_iota(jnp.int32, logits.shape, 0)
    routing = routing_ref[...]
    sign = jnp.where(expert == routing[3:4], 1.0, 0.0) - jnp.where(expert == routing[2:3], 1.0, 0.0)
    gap = jnp.sum(logits * sign, axis=0, keepdims=True)
    gate0, gate1 = 1.0 / (1.0 + jnp.exp(gap)), 1.0 / (1.0 + jnp.exp(-gap))

    def dispatch(start):
        span = slice(start, start + half_plane)
        first, second = selector(routing_ref, start * capacity, half_plane * capacity)
        gate = jnp.sum(first * gate0 + second * gate1, axis=1, keepdims=True)
        both = (first + second).astype(BF)
        shape = (half_plane, capacity, width)
        sends[0, span] = (
            jnp.dot(both, normed2_far[...], preferred_element_type=F32).astype(BF).reshape(shape)
        )
        sends[1, span] = (
            (jnp.dot(both, cot_far[...], preferred_element_type=F32) * gate)
            .astype(BF)
            .reshape(shape)
        )
        for o in range(start, start + half_plane):
            for i, out in enumerate((far_rows_ref, far_scaled_ref)):
                if o:
                    copy = remote(
                        sends.at[i, o],
                        out.at[o],
                        far_send.at[i, o],
                        far_recv.at[i, o],
                        {"dp": plane(d, o)},
                    )
                else:
                    copy = pltpu.make_async_copy(sends.at[i, 0], out.at[0], own_sem.at[i])
                copy.start()
                copies.append(copy)

    dispatch(half_plane)
    sums_ref[...] = jnp.zeros_like(sums_ref)
    grads[0] = grad_ref[:, :columns]

    near = {"head": flipped(z, 1)}

    def part_copy(i, source, target, peer):
        return remote(parts.at[source], landed.at[target], part_send.at[i], part_recv.at[i], peer)

    inner = part_copy(0, 3, 0, near)
    direct = part_copy(1, 1, 1, near)

    for copy in weight_loads:
        copy.wait()
    for turn, r in enumerate(order):
        slot = turn % 2
        if turn + 1 < replicas:
            for copy in loads(turn + 1):
                copy.start()
        for copy in loads(turn):
            copy.wait()
        if r:
            arrivals[r].wait_recv()

        def pair_step(pair, carry, slot=slot, r=r):
            def part_of(j):
                at = pl.multiple_of(j * columns + pair * lanes, lanes)
                return qkv_ref[slot, :, pl.ds(at, lanes)]

            at = pl.multiple_of(pair * lanes, lanes)
            query, value = part_of(0), part_of(2)
            key_t = part_of(1).T
            grad_all = grads[r, :, pl.ds(at, lanes)]
            grad_keys, grad_values = [], []
            for part in range(2):
                mask = lanes_of((length, lanes), half, part)
                grad = jnp.where(mask, grad_all, 0).astype(BF)
                grad_key = jnp.zeros((length, lanes), F32)
                grad_value = jnp.zeros((length, lanes), F32)
                for c in range(length // chunk):
                    cols = slice(c * chunk, (c + 1) * chunk)
                    grad_probs = contract(value, grad[cols], 1, 1)
                    probs_low = probs_ref[slot, pair * 2 + part, :, cols]
                    probs = probs_low.astype(F32)
                    delta = jnp.sum(probs * grad_probs, axis=0, keepdims=True)
                    grad_scores = (probs * (grad_probs - delta)).astype(BF)
                    grad_value += jnp.dot(probs_low, grad_all[cols], preferred_element_type=F32)
                    grad_key += jnp.dot(grad_scores, query[cols], preferred_element_type=F32)
                    acc_ref[part * half : (part + 1) * half, cols] = jnp.dot(
                        key_t[part * half : (part + 1) * half],
                        grad_scores,
                        preferred_element_type=F32,
                    )
                    for kb in range(length // TILE):
                        to = length - TILE * kb + chunk * c
                        sums_ref[pair * 2 + part, :, to : to + chunk] += grad_scores[
                            kb * TILE : (kb + 1) * TILE
                        ].astype(F32)
                grad_keys.append(grad_key)
                grad_values.append(grad_value)
            first = lanes_of((length, lanes), half, 0)
            results = (
                acc_ref[...].T * SCALE,
                jnp.where(first, *grad_keys) * SCALE,
                jnp.where(first, *grad_values),
            )
            for j, result in enumerate(results):
                to = pl.multiple_of(j * columns + pair * lanes, lanes)
                grad_qkv_ref[slot, :, pl.ds(to, lanes)] = result.astype(BF)
            return carry

        lax.fori_loop(0, pairs, pair_step, 0)

        parts[r] = contract(grad_qkv_ref[slot], weight_ref[...], 1, 1).astype(BF)
        if r == 3:
            inner.start()
            dispatch(0)
        if r == 1:
            direct.start()

        def weight_step(i, carry, slot=slot, turn=turn):
            cols = pl.ds(pl.multiple_of(i * 2 * chunk, 2 * chunk), 2 * chunk)
            value = contract(normed_ref[slot, :, cols], grad_qkv_ref[slot], 0, 0)
            if turn:
                value = value + weight_sum[cols, :]
            if turn + 1 < replicas:
                weight_sum[cols, :] = value
            else:
                qkv_w_ref[cols, :] = value.astype(BF)
            return carry

        lax.fori_loop(0, width // (2 * chunk), weight_step, 0)

    out_w_ref[...] = contract(attended_ref[...], grad_branch_ref[...], 0, 0).astype(BF)
    unskew_kernel(sums_ref, lines_ref)

    for r in hops:
        arrivals[r].wait_send()
    for copy in copies:
        copy.wait()
    inner.wait()
    carry_ref[...] = (parts[2].astype(F32) + landed[0].astype(F32)).astype(BF)
    direct.wait()
    part_sum_ref[...] = parts[0].astype(F32) + landed[1].astype(F32)


def attend_back(
    normed2_far,
    cot_pieces,
    routing_far,
    router,
    tokens,
    qkv,
    probs,
    normed,
    weights,
    attended,
    groups,
    capacity,
    experts,
):
    replicas, length, triple = qkv.shape
    heads = probs.shape[1]
    columns = triple // 3
    width = normed.shape[2]
    lanes = 2 * columns // heads
    far_shape = jax.ShapeDtypeStruct((groups, capacity, width), BF)
    vmem = pl.BlockSpec(memory_space=pltpu.VMEM)
    hbm = pl.BlockSpec(memory_space=pl.ANY)
    hop_sem = pltpu.SemaphoreType.DMA((replicas,))
    plane_sem = pltpu.SemaphoreType.DMA((2, groups))
    part_sem = pltpu.SemaphoreType.DMA((2,))
    return pl.pallas_call(
        attend_back_kernel,
        out_shape=(
            far_shape,
            far_shape,
            jax.ShapeDtypeStruct((length, TILE), F32),
            jax.ShapeDtypeStruct((length, width), F32),
            jax.ShapeDtypeStruct((experts, width), F32),
            jax.ShapeDtypeStruct((1, width), F32),
            jax.ShapeDtypeStruct((length, width), BF),
            jax.ShapeDtypeStruct((length, width), F32),
            jax.ShapeDtypeStruct((width, triple), BF),
            jax.ShapeDtypeStruct((replicas * columns, width), BF),
            jax.ShapeDtypeStruct((heads, 1, 2 * length), F32),
        ),
        in_specs=[vmem] * 13 + [hbm] * 6 + [vmem],
        out_specs=[hbm] * 2 + [vmem] * 9,
        scratch_shapes=[
            pltpu.VMEM((heads, TILE, 2 * length), F32),
            pltpu.VMEM((lanes, length), F32),
            pltpu.VMEM((length, width), BF),
            pltpu.VMEM((length, replicas * columns), BF),
            pltpu.VMEM((length, TILE), F32),
            pltpu.VMEM((length, TILE), F32),
            pltpu.VMEM((length, groups * capacity), BF),
            pltpu.VMEM((2, groups, capacity, width), BF),
            pltpu.VMEM((length, width), BF),
            pltpu.VMEM((replicas, length, columns), BF),
            pltpu.VMEM((2, length, triple), BF),
            pltpu.VMEM((2, heads, length, length), BF),
            pltpu.VMEM((2, length, width), BF),
            pltpu.VMEM((2, length, triple), BF),
            pltpu.VMEM((width, triple), BF),
            pltpu.VMEM((width, triple), F32),
            pltpu.VMEM((replicas, length, width), BF),
            pltpu.VMEM((2, length, width), BF),
            plane_sem,
            plane_sem,
            hop_sem,
            hop_sem,
            part_sem,
            part_sem,
            pltpu.SemaphoreType.DMA((3, 2)),
            pltpu.SemaphoreType.DMA((3,)),
            pltpu.SemaphoreType.DMA((2,)),
        ],
        compiler_params=pltpu.CompilerParams(
            vmem_limit_bytes=VMEM_MOST, collective_id=3, has_side_effects=True
        ),
        cost_estimate=pl.CostEstimate(
            flops=replicas * heads * 16 * length * length * lanes,
            bytes_accessed=replicas * heads * length * length * 4,
            transcendentals=0,
        ),
        name="attend_back",
    )(
        normed2_far,
        *cot_pieces,
        routing_far,
        router,
        *tokens,
        qkv,
        probs,
        normed,
        *weights,
        attended,
    )


def last_kernel(
    tile,
    far_hbm,
    scaled_hbm,
    scaled_here_hbm,
    gates_ref,
    routing_ref,
    gain_ref,
    gate_hbm,
    up_hbm,
    down_hbm,
    grad_gate_hbm,
    grad_up_hbm,
    hidden_hbm,
    qkv_w_hbm,
    out_w_hbm,
    rows_hbm,
    carry_hbm,
    part_sum_hbm,
    input_hbm,
    back_hbm,
    norm2_ref,
    router_grad_ref,
    lines_ref,
    wide_out,
    wide_came,
    tall_out,
    tall_came,
    qkv_w_out,
    out_w_out,
    small_out,
    grad_input_out,
    output_out,
    back_out,
    far_ref,
    scaled,
    scaled_here,
    left,
    weights,
    downs,
    units,
    hidden,
    hidden_here,
    send_wide,
    keep_wide,
    send_tall,
    keep_tall,
    qkv_land,
    qkv_sum,
    out_land,
    out_sum,
    out_hop,
    out_last,
    small_own,
    small_land,
    small_sum,
    small_hop,
    small_last,
    work,
    own_input,
    carried,
    stream_sem,
    hidden_sem,
    wide_send,
    wide_recv,
    keep_sem,
    tall_send,
    tall_recv,
    tall_keep,
    first_send,
    first_recv,
    hop_send,
    hop_recv,
    third_send,
    third_recv,
    carry_sem,
    back_send,
    back_recv,
    own_sem,
):
    z, d = lax.axis_index("head"), lax.axis_index("dp")
    slots, width = scaled_here.shape
    groups = qkv_land.shape[0]
    capacity = slots // groups
    length = own_input.shape[0]
    chunk = 2 * TILE
    _, rows, total_units = send_wide.shape
    half_units = hidden_here.shape[1]
    tiles = total_units // tile
    low, high = lax.rem(z, 2), z // 2
    keep_at = pl.multiple_of(low * rows, rows)
    send_at = pl.multiple_of((1 - low) * rows, rows)
    near = {"head": flipped(z, 1)}
    count = 2 * capacity
    hops = [3, 2, 1]

    def streams(t):
        slot = lax.rem(t, 2)
        at = pl.multiple_of(t * tile, tile)
        cols = pl.ds(at, tile)
        return [
            pltpu.make_async_copy(gate_hbm.at[:, cols], weights.at[slot, 0], stream_sem.at[0, slot]),
            pltpu.make_async_copy(up_hbm.at[:, cols], weights.at[slot, 1], stream_sem.at[1, slot]),
            pltpu.make_async_copy(down_hbm.at[cols, :], downs.at[slot], stream_sem.at[2, slot]),
            pltpu.make_async_copy(
                grad_gate_hbm.at[:, cols], units.at[slot, 0], stream_sem.at[3, slot]
            ),
            pltpu.make_async_copy(
                grad_up_hbm.at[:, cols], units.at[slot, 1], stream_sem.at[4, slot]
            ),
        ]

    wide = 2 * rows
    for copy in streams(0):
        copy.start()
    far_loads = [
        pltpu.make_async_copy(source, target, own_sem.at[6 + i])
        for i, (source, target) in enumerate(
            ((far_hbm, far_ref), (scaled_hbm, scaled), (scaled_here_hbm, scaled_here))
        )
    ]
    for copy in far_loads:
        copy.start()
    loads = [
        pltpu.make_async_copy(
            rows_hbm.at[:, pl.ds(pl.multiple_of(high * wide, wide), wide)], left, own_sem.at[2]
        ),
        pltpu.make_async_copy(part_sum_hbm, work.at[0], own_sem.at[3]),
        pltpu.make_async_copy(
            input_hbm.at[pl.ds(pl.multiple_of(z * length, length), length)], own_input, own_sem.at[5]
        ),
    ]
    for copy in loads:
        copy.start()

    half_copy = pltpu.make_async_copy(
        hidden_hbm.at[:, pl.ds(pl.multiple_of(high * half_units, TILE), half_units)],
        hidden_here,
        hidden_sem,
    )
    half_copy.start()
    greet([{"dp": plane(d, o)} for o in PEERS] + [{"head": flipped(z, r)} for r in hops])

    carry = remote(
        carry_hbm, carried, carry_sem.at[0], carry_sem.at[1], {"head": flipped(z, 2)}
    )
    carry.start()
    for copy in far_loads[:2] + loads[:1]:
        copy.wait()
    columns = pl.ds(pl.multiple_of(high * wide, wide), wide)

    def wide_copy(i, t):
        at = pl.multiple_of(t * tile, tile)
        return remote(
            send_wide.at[i, :, pl.ds(at, tile)],
            wide_came.at[i, :, pl.ds(at, tile)],
            wide_send.at[i, t],
            wide_recv.at[i, t],
            near,
        )

    def keep_copy(i, t):
        at = pl.multiple_of(t * tile, tile)
        slot = lax.rem(t, 2)
        return pltpu.make_async_copy(
            keep_wide.at[i, slot], wide_out.at[i, :, pl.ds(at, tile)], keep_sem.at[i, slot]
        )

    def tile_step(t, carry):
        slot = lax.rem(t, 2)
        at = pl.multiple_of(t * tile, tile)

        @pl.when(t + 1 < tiles)
        def _():
            for copy in streams(t + 1):
                copy.start()

        for copy in streams(t):
            copy.wait()

        def chunk_step(j, inner):
            span = pl.ds(pl.multiple_of(j * count, count), count)
            values = expert_tile(
                far_ref[span], scaled[span], weights[slot, 0], weights[slot, 1], downs[slot]
            )
            hidden[span, pl.ds(at, tile)] = values[0]
            units[slot, 2, span, :] = values[1]
            units[slot, 3, span, :] = values[2]
            return inner

        lax.fori_loop(0, groups // 2, chunk_step, 0)
        @pl.when(t >= 2)
        def _():
            for i in range(2):
                keep_copy(i, t - 2).wait()

        for i in range(2):
            value = contract(left[...], units[slot, i], 0, 0) + contract(
                far_ref[:, columns], units[slot, 2 + i], 0, 0
            )
            upper = low == 1
            send_wide[i, :, pl.ds(at, tile)] = jnp.where(
                upper, value[:rows], value[rows:]
            ).astype(BF)
            keep_wide[i, slot] = jnp.where(upper, value[rows:], value[:rows])
            wide_copy(i, t).start()
            keep_copy(i, t).start()
        return carry

    tile_step(jnp.int32(0), 0)

    first = []
    for o in PEERS:
        peer = plane(d, o)
        for i, (source, target) in enumerate(
            (
                (qkv_w_hbm.at[peer], qkv_land.at[o]),
                (out_w_hbm.at[:, peer], out_land.at[o]),
            )
        ):
            copy = remote(source, target, first_send.at[i, o], first_recv.at[i, o], {"dp": peer})
            copy.start()
            first.append(copy)
    own = [
        pltpu.make_async_copy(qkv_w_hbm.at[d], qkv_land.at[0], own_sem.at[0]),
        pltpu.make_async_copy(out_w_hbm.at[:, d], out_land.at[0], own_sem.at[1]),
    ]
    for copy in own:
        copy.start()

    backs = []
    for o in PEERS:
        copy = remote(
            back_hbm.at[o], back_out.at[o], back_send.at[o], back_recv.at[o], {"dp": plane(d, o)}
        )
        copy.start()
        backs.append(copy)
    backs.append(pltpu.make_async_copy(back_hbm.at[0], back_out.at[0], back_send.at[0]))
    backs[-1].start()
    lax.fori_loop(1, tiles, tile_step, 0)

    carry.wait()
    for copy in loads[1:]:
        copy.wait()

    def norm_step(i, total):
        span = pl.ds(pl.multiple_of(i * TILE, TILE), TILE)
        grad_normed = work[0, span, :] + carried[span, :].astype(F32)
        value = own_input[span, :].astype(F32)
        scale = lax.rsqrt(jnp.mean(value * value, axis=1, keepdims=True) + EPS)
        inner = grad_normed * gain_ref[...]
        mean = jnp.mean(inner * value, axis=1, keepdims=True)
        work[1, span, :] = scale * inner - value * (scale * scale * scale * mean)
        return total + jnp.sum(grad_normed * value * scale, axis=0, keepdims=True)

    heads = lines_ref.shape[0]
    small_own[...] = jnp.zeros_like(small_own)
    small_own[0:1] = lax.fori_loop(0, length // TILE, norm_step, jnp.zeros((1, width), F32))
    small_own[1:2] = norm2_ref[...]
    for h in range(heads):
        small_own[2 + h : 3 + h] = lines_ref[h]
    small_own[8:] = router_grad_ref[...]
    ends = [pltpu.make_async_copy(work.at[1], grad_input_out, own_sem.at[4])]
    for copy in ends:
        copy.start()
    small = []

    def lanes(index):
        return pl.ds(pl.multiple_of(index * TILE, TILE), TILE)

    for o in PEERS:
        peer = plane(d, o)
        copy = remote(
            small_own.at[:, lanes(peer)],
            small_land.at[o],
            first_send.at[2, o],
            first_recv.at[2, o],
            {"dp": peer},
        )
        copy.start()
        small.append(copy)
    small_land[0] = small_own[:, lanes(d)]

    for copy in first:
        copy.wait()
    for copy in own:
        copy.wait()
    qkv_sum[...] = sum(qkv_land[o].astype(F32) for o in range(groups)).astype(BF)
    out_sum[...] = sum(out_land[o].astype(F32) for o in range(groups)).astype(BF)
    second = []
    for o in PEERS:
        copy = remote(
            qkv_sum, qkv_w_out.at[d], third_send.at[0, o], third_recv.at[0, o], {"dp": plane(d, o)}
        )
        copy.start()
        second.append(copy)
    mine = [pltpu.make_async_copy(qkv_sum, qkv_w_out.at[d], own_sem.at[0])]
    mine[0].start()
    over = []
    for r in hops:
        copy = remote(
            out_sum.at[r], out_hop.at[r], hop_send.at[0, r], hop_recv.at[0, r], {"head": flipped(z, r)}
        )
        copy.start()
        over.append(copy)

    half_copy.wait()
    far_loads[2].wait()
    share = half_units // 2
    halves = pl.ds(pl.multiple_of(high * half_units, TILE), half_units)

    def tall_copies(i):
        cols = pl.ds(pl.multiple_of(i * tile, tile), tile)
        return [
            remote(
                send_tall.at[:, cols], tall_came.at[:, cols], tall_send.at[i], tall_recv.at[i], near
            ),
            pltpu.make_async_copy(keep_tall.at[:, cols], tall_out.at[:, cols], tall_keep.at[i]),
        ]

    def tall_step(i, carry):
        cols = pl.ds(pl.multiple_of(i * tile, tile), tile)
        value = contract(hidden_here[...], scaled_here[:, cols], 0, 0) + contract(
            hidden[:, halves], scaled[:, cols], 0, 0
        )
        upper = low == 1
        send_tall[:, cols] = jnp.where(upper, value[:share], value[share:]).astype(BF)
        keep_tall[:, cols] = jnp.where(upper, value[share:], value[:share])
        for copy in tall_copies(i):
            copy.start()
        return carry

    lax.fori_loop(0, width // tile, tall_step, 0)
    for copy in small:
        copy.wait()
    small_sum[...] = sum(small_land[o] for o in range(groups))
    small_over = []
    for r in hops:
        copy = remote(
            small_sum, small_hop.at[r], hop_send.at[1, r], hop_recv.at[1, r], {"head": flipped(z, r)}
        )
        copy.start()
        small_over.append(copy)

    for copy in backs:
        copy.wait()
    rows_back = [
        pltpu.make_async_copy(
            back_out.at[o], hidden.at[o * capacity : (o + 1) * capacity, :width], back_recv.at[o]
        )
        for o in range(groups)
    ]
    for copy in rows_back:
        copy.start()
    for k, pick in enumerate(token_selector(routing_ref, slots)):
        hidden_here[k * length : (k + 1) * length, :slots] = pick.astype(BF)
    for copy in rows_back:
        copy.wait()

    def output_step(i, carry):
        cols = pl.ds(pl.multiple_of(i * chunk, chunk), chunk)
        work[0, :, cols] = sum(
            gates_ref[:, k : k + 1]
            * jnp.dot(
                hidden_here[k * length : (k + 1) * length, :slots],
                hidden[:, cols],
                preferred_element_type=F32,
            )
            for k in range(2)
        )
        return carry

    lax.fori_loop(0, width // chunk, output_step, 0)
    ends.append(pltpu.make_async_copy(work.at[0], output_out, own_sem.at[3]))
    ends[1].start()

    for copy in small_over:
        copy.wait()
    small_last[0] = small_sum[...]
    small_last[1] = small_sum[...] + sum(small_hop[r] for r in hops)
    small_out[:, :, lanes(d)] = small_last[...]
    for o in PEERS:
        copy = remote(
            small_last,
            small_out.at[:, :, lanes(d)],
            third_send.at[2, o],
            third_recv.at[2, o],
            {"dp": plane(d, o)},
        )
        copy.start()
        second.append(copy)
    for copy in over:
        copy.wait()
    out_last[...] = (
        out_sum[0].astype(F32) + sum(out_hop[r].astype(F32) for r in hops)
    ).astype(BF)
    for o in PEERS:
        copy = remote(
            out_last,
            out_w_out.at[d],
            third_send.at[1, o],
            third_recv.at[1, o],
            {"dp": plane(d, o)},
        )
        copy.start()
        second.append(copy)
    mine.append(pltpu.make_async_copy(out_last, out_w_out.at[d], own_sem.at[1]))
    mine[1].start()

    for i in range(2):
        for t in (tiles - 2, tiles - 1):
            keep_copy(i, t).wait()

    def wide_end(t, carry):
        for i in range(2):
            wide_copy(i, t).wait()
        return carry

    lax.fori_loop(0, tiles, wide_end, 0)
    for copy in second + mine + ends:
        copy.wait()

    def tall_end(i, carry):
        for copy in tall_copies(i):
            copy.wait()
        return carry

    lax.fori_loop(0, width // tile, tall_end, 0)


def last_stage(
    far, here, tokens, weights, grads_here, hidden_here, sums, finish, small, tile
):
    gate_w, up_w, down_w = weights
    width, units = gate_w.shape
    qkv_w, out_w = sums
    replicas, groups, part_rows, _ = out_w.shape
    slots = far[0].shape[0]
    length = tokens[0].shape[0]
    back = finish[-1]
    vmem = pl.BlockSpec(memory_space=pltpu.VMEM)
    hbm = pl.BlockSpec(memory_space=pl.ANY)
    rows, share = width // replicas, units // replicas
    small_shape = (8 + groups, width)
    plane_sem = pltpu.SemaphoreType.DMA((3, groups))
    hop_sem = pltpu.SemaphoreType.DMA((2, replicas))
    return pl.pallas_call(
        functools.partial(last_kernel, tile),
        out_shape=(
            jax.ShapeDtypeStruct((2, rows, units), F32),
            jax.ShapeDtypeStruct((2, rows, units), BF),
            jax.ShapeDtypeStruct((share, width), F32),
            jax.ShapeDtypeStruct((share, width), BF),
            jax.ShapeDtypeStruct(qkv_w.shape, BF),
            jax.ShapeDtypeStruct(out_w.shape[1:], BF),
            jax.ShapeDtypeStruct((2,) + small_shape, F32),
            jax.ShapeDtypeStruct((length, width), F32),
            jax.ShapeDtypeStruct((length, width), F32),
            jax.ShapeDtypeStruct(back.shape, BF),
        ),
        in_specs=[hbm] * 3 + [vmem] * 3 + [hbm] * 13 + [vmem] * 3,
        out_specs=[hbm] * 6 + [vmem] + [hbm] * 3,
        scratch_shapes=[
            pltpu.VMEM((slots, width), BF),
            pltpu.VMEM((slots, width), BF),
            pltpu.VMEM((slots, width), BF),
            pltpu.VMEM((slots, 2 * rows), BF),
            pltpu.VMEM((2, 2, width, tile), BF),
            pltpu.VMEM((2, tile, width), BF),
            pltpu.VMEM((2, 4, slots, tile), BF),
            pltpu.VMEM((slots, units), BF),
            pltpu.VMEM((slots, units // 2), BF),
            pltpu.VMEM((2, rows, units), BF),
            pltpu.VMEM((2, 2, rows, tile), F32),
            pltpu.VMEM((share, width), BF),
            pltpu.VMEM((share, width), F32),
            pltpu.VMEM(qkv_w.shape, BF),
            pltpu.VMEM(qkv_w.shape[1:], BF),
            pltpu.VMEM((groups, replicas, part_rows, width), BF),
            pltpu.VMEM((replicas, part_rows, width), BF),
            pltpu.VMEM((replicas, part_rows, width), BF),
            pltpu.VMEM((part_rows, width), BF),
            pltpu.VMEM(small_shape, F32),
            pltpu.VMEM((groups, small_shape[0], TILE), F32),
            pltpu.VMEM((small_shape[0], TILE), F32),
            pltpu.VMEM((replicas, small_shape[0], TILE), F32),
            pltpu.VMEM((2, small_shape[0], TILE), F32),
            pltpu.VMEM((2, length, width), F32),
            pltpu.VMEM((length, width), BF),
            pltpu.VMEM((length, width), BF),
            pltpu.SemaphoreType.DMA((5, 2)),
            pltpu.SemaphoreType.DMA,
            pltpu.SemaphoreType.DMA((2, units // tile)),
            pltpu.SemaphoreType.DMA((2, units // tile)),
            pltpu.SemaphoreType.DMA((2, 2)),
            pltpu.SemaphoreType.DMA((width // tile,)),
            pltpu.SemaphoreType.DMA((width // tile,)),
            pltpu.SemaphoreType.DMA((width // tile,)),
            plane_sem,
            plane_sem,
            hop_sem,
            hop_sem,
            plane_sem,
            plane_sem,
            pltpu.SemaphoreType.DMA((2,)),
            pltpu.SemaphoreType.DMA((groups,)),
            pltpu.SemaphoreType.DMA((groups,)),
            pltpu.SemaphoreType.DMA((9,)),
        ],
        compiler_params=pltpu.CompilerParams(
            vmem_limit_bytes=VMEM_MOST, collective_id=4, has_side_effects=True
        ),
        cost_estimate=pl.CostEstimate(
            flops=12 * slots * width * units,
            bytes_accessed=6 * width * units + 6 * slots * units,
            transcendentals=slots * units,
        ),
        name="last_stage",
    )(
        *far,
        here[1],
        *tokens,
        gate_w,
        up_w,
        down_w,
        *grads_here,
        hidden_here,
        qkv_w,
        out_w,
        here[0],
        *finish,
        *small,
    )


def finish_kernel(
    wide_kept,
    wide_came,
    tall_kept,
    tall_came,
    qkv_ref,
    out_ref,
    mixed_ref,
    expert_ref,
    grad_mixed_ref,
    grad_first_ref,
    summed_ref,
    line_ref,
    output_ref,
    grad_input_ref,
    query_out,
    key_out,
    value_out,
    out_out,
    gate_out,
    up_out,
    down_out,
    norm1_out,
    norm2_out,
    bias_out,
    router_out,
):
    output_ref[...] = mixed_ref[...] + expert_ref[...]
    grad_input_ref[...] = grad_mixed_ref[...] + grad_first_ref[...]
    gate_out[...] = wide_kept[0] + wide_came[0].astype(F32)
    up_out[...] = wide_kept[1] + wide_came[1].astype(F32)
    down_out[...] = tall_kept[...] + tall_came[...].astype(F32)
    columns = query_out.shape[1]
    for i, out in enumerate((query_out, key_out, value_out)):
        value = qkv_ref[:, :, i * columns : (i + 1) * columns].astype(F32)
        out[...] = value.reshape(out.shape)
    out_out[...] = out_ref[...].astype(F32).reshape(out_out.shape)

    @pl.when(pl.program_id(0) == 0)
    def _():
        norm1_out[...] = summed_ref[1, :1]
        norm2_out[...] = summed_ref[1, 1:2]
        heads = bias_out.shape[0]
        total = sum(contract(term, line_ref[...], 1, 1) for term in split_parts(summed_ref[0, :8]))
        bias_out[...] = total[2 : 2 + heads]
        router_out[...] = summed_ref[1, 8:]


def finish(wide, tall, qkv_w, out_w, tokens, summed, line, heads):
    steps = 4
    groups, part_rows, triple = qkv_w.shape
    _, out_rows, width = out_w.shape
    _, rows, units = wide[0].shape
    share = tall[0].shape[0]
    length = tokens[0].shape[0]
    columns = triple // 3
    experts = summed.shape[1] - 8

    def cut(shape, axis=0):
        block = tuple(n // steps if i == axis else n for i, n in enumerate(shape))
        return pl.BlockSpec(block, lambda t: tuple(t if i == axis else 0 for i in range(len(shape))))

    def whole(shape):
        return pl.BlockSpec(shape, lambda t: (0,) * len(shape))

    outs = [
        (length, width),
        (length, width),
        (groups * part_rows, columns),
        (groups * part_rows, columns),
        (groups * part_rows, columns),
        (groups * out_rows, width),
        (rows, units),
        (rows, units),
        (share, width),
    ]
    small = [(1, width), (1, width), (heads, line.shape[0]), (experts, width)]
    return pl.pallas_call(
        finish_kernel,
        out_shape=[jax.ShapeDtypeStruct(shape, F32) for shape in outs + small],
        grid=(steps,),
        in_specs=[cut(value.shape, 1) for value in wide]
        + [cut(value.shape) for value in tall]
        + [cut(qkv_w.shape), cut(out_w.shape)]
        + [cut(value.shape) for value in tokens]
        + [whole(summed.shape), whole(line.shape)],
        out_specs=[cut(shape) for shape in outs] + [whole(shape) for shape in small],
        compiler_params=pltpu.CompilerParams(vmem_limit_bytes=VMEM_MOST),
        cost_estimate=pl.CostEstimate(
            flops=4 * rows * units, bytes_accessed=48 * rows * units, transcendentals=0
        ),
        name="finish",
    )(*wide, *tall, qkv_w, out_w, *tokens, summed, line)


def expert_forward(rows, gate_w, up_w, grad_unscaled, slot_gates):
    gate_pre = jnp.dot(rows, gate_w, preferred_element_type=F32)
    up_pre = jnp.dot(rows, up_w, preferred_element_type=F32)
    hidden, pull = jax.vjp(geglu, gate_pre, up_pre)
    grad_gate_pre, grad_up_pre = pull(grad_unscaled * slot_gates)
    return hidden.astype(BF), grad_gate_pre.astype(BF), grad_up_pre.astype(BF)


def body_plain(
    block_input,
    cotangent,
    expert_ids,
    priority,
    rel_bucket,
    norm1_gain,
    w_query,
    w_key,
    w_value,
    w_out,
    pos_bias,
    norm2_gain,
    w_router,
    w_gate,
    w_up,
    w_down,
):
    group_rows, width = block_input.shape
    own_rows = cotangent.shape[0]
    buckets, heads_here = pos_bias.shape
    head_cols = w_query.shape[1]
    length = (rel_bucket.shape[0] + 1) // 2
    sequences = group_rows // length
    experts = w_router.shape[1]
    capacity = 5 * 2 * own_rows // (4 * experts)
    slot_count = experts * capacity
    replicas = lax.axis_size("head")
    groups = lax.axis_size("dp")
    me = lax.axis_index("head")
    far = replicas // 2
    far_perm = [(i, i ^ far) for i in range(replicas)]
    stepwise = own_rows == length and sequences == replicas

    def hop(value, r):
        return lax.ppermute(value, "head", [(i, i ^ r) for i in range(replicas)])

    def exchange(value):
        parts = value.reshape(experts, capacity, -1)
        return lax.all_to_all(parts, "dp", split_axis=0, concat_axis=0, tiled=True).reshape(
            slot_count, -1
        )

    dest = route_slots(expert_ids, priority[0], experts, capacity)
    dest_far = lax.ppermute(dest, "head", far_perm)
    slot_range = jnp.arange(slot_count, dtype=jnp.int32)[None, :]
    picks = [(dest[:, k : k + 1] == slot_range).astype(BF) for k in range(2)]
    both = picks[0] + picks[1]
    both_far = sum((dest_far[:, k : k + 1] == slot_range).astype(BF) for k in range(2))

    down_w, gate_w, up_w = w_down[0], w_gate[0], w_up[0]
    cot_here = exchange(contract(both, cotangent, 0, 0).astype(BF))
    cot_far_own = lax.ppermute(cotangent, "head", far_perm)
    cot_far = exchange(contract(both_far, cot_far_own, 0, 0).astype(BF))
    unscaled_here = contract(cot_here, down_w, 1, 1)
    unscaled_far = contract(cot_far, down_w, 1, 1)

    dp_at = lax.axis_index("dp")
    out_rows = head_cols // groups
    piece = lax.dynamic_slice_in_dim(w_out, dp_at * out_rows, out_rows, 0)
    w_out_all = lax.all_gather(piece, ("head", "dp"), axis=0, tiled=True)
    w_qkv = jnp.concatenate([w_query, w_key, w_value], axis=1)
    qkv_rows = width // groups
    piece = lax.dynamic_slice_in_dim(w_qkv, dp_at * qkv_rows, qkv_rows, 0)
    w_qkv_all = lax.all_gather(piece, ("head", "dp"), axis=0, tiled=True)
    if stepwise:
        order = [me ^ r for r in range(replicas)]
    else:
        order = list(range(replicas))
    w_out_all = w_out_all.reshape(replicas, head_cols, width)
    w_qkv_all = w_qkv_all.reshape(replicas, width, 3 * head_cols)
    w_out_cat = jnp.concatenate(
        [lax.dynamic_index_in_dim(w_out_all, o, 0, keepdims=False) for o in order], axis=0
    )

    inputs_all = block_input.astype(F32)
    normed = rms_norm(inputs_all, norm1_gain).astype(BF)
    qkv = jnp.dot(normed, w_qkv, preferred_element_type=F32).astype(BF)
    line = (rel_bucket[::-1][None, :] == jnp.arange(buckets, dtype=jnp.int32)[:, None]).astype(F32)
    line = jnp.pad(line, ((0, 0), (1, 0)))
    table = skew(contract(pos_bias, line, 0, 0, HIGH))
    kept = {}
    if stepwise:
        blocks = [None] * replicas
        for r in reversed(range(replicas)):
            attended_seq, probs = attend_fwd(order[r].reshape(1), qkv, table, length)
            kept[r] = probs
            blocks[r] = hop(attended_seq, r) if r else attended_seq
    else:
        seqs = []
        for s in range(sequences):
            attended_seq, kept[s] = attend_fwd(jnp.full((1,), s, jnp.int32), qkv, table, length)
            seqs.append(attended_seq)
        attended_all = jnp.concatenate(seqs, axis=0).reshape(replicas, own_rows, head_cols)
        attended_all = lax.all_to_all(attended_all, "head", split_axis=0, concat_axis=0, tiled=True)
        blocks = [attended_all[i] for i in range(replicas)]
    attended = jnp.concatenate(blocks, axis=1)

    branch = jnp.dot(attended, w_out_cat, preferred_element_type=F32)
    start_own = me * own_rows
    inputs_own = lax.dynamic_slice_in_dim(block_input, start_own, own_rows, 0).astype(F32)
    mixed = inputs_own + branch
    normed2_full, norm2_pull = jax.vjp(rms_norm, mixed, norm2_gain)
    normed2 = normed2_full.astype(BF)
    logits = jnp.dot(normed2, w_router, preferred_element_type=F32)
    expert_range = jnp.arange(experts, dtype=jnp.int32)
    chosen = (expert_ids[:, :, None] == expert_range[None, None, :]).astype(F32)
    gates = jax.nn.softmax(jnp.sum(chosen * logits[:, None, :], axis=2), axis=-1)

    def slot_gates_of(places, values):
        terms = sum(
            jnp.where(places[:, k : k + 1] == slot_range, values[:, k : k + 1], 0.0)
            for k in range(2)
        )
        return jnp.sum(terms, axis=0)

    rows_here = exchange(contract(both, normed2, 0, 0).astype(BF))
    gates_here = exchange(slot_gates_of(dest, gates))
    normed2_far = lax.ppermute(normed2, "head", far_perm)
    gates_far_own = lax.ppermute(gates, "head", far_perm)
    rows_far = exchange(contract(both_far, normed2_far, 0, 0).astype(BF))
    gates_far = exchange(slot_gates_of(dest_far, gates_far_own))

    hidden_here, ggp_here, gup_here = expert_forward(
        rows_here, gate_w, up_w, unscaled_here, gates_here
    )
    returned = jnp.dot(hidden_here, down_w, preferred_element_type=F32).astype(BF)
    came_back = exchange(returned)
    grad_routed = (contract(ggp_here, gate_w, 1, 1) + contract(gup_here, up_w, 1, 1)).astype(BF)
    grad_back = exchange(grad_routed)
    hidden_far, ggp_far, gup_far = expert_forward(rows_far, gate_w, up_w, unscaled_far, gates_far)
    scaled_here = (cot_here.astype(F32) * gates_here).astype(BF)
    scaled_far = (cot_far.astype(F32) * gates_far).astype(BF)

    low = me % far
    high = me // far

    def reduced(lefts, rights):
        rows = lefts[0].shape[1] // replicas

        def part(at):
            return sum(
                contract(lax.dynamic_slice_in_dim(left, at * rows, rows, 1), right, 0, 0)
                for left, right in zip(lefts, rights)
            )

        if far == 2:
            sent = hop(part(high * far + (1 - low)).astype(BF), 1)
            return (part(me) + sent.astype(F32))[None]
        whole = jnp.concatenate([part(high * far + i) for i in range(far)], axis=0).astype(BF)
        member = [[h * far + i for i in range(far)] for h in range(2)]
        return lax.psum_scatter(
            whole, "head", scatter_dimension=0, axis_index_groups=member, tiled=True
        ).astype(F32)[None]

    grad_down_w = reduced((hidden_here, hidden_far), (scaled_here, scaled_far))
    grad_gate_w = reduced((rows_here, rows_far), (ggp_here, ggp_far))
    grad_up_w = reduced((rows_here, rows_far), (gup_here, gup_far))

    chosen_rows = [jnp.dot(pick, came_back, preferred_element_type=F32) for pick in picks]
    output = mixed + sum(gates[:, k : k + 1] * chosen_rows[k] for k in range(2))
    grad_output = cotangent.astype(F32)
    grad_gates = jnp.stack([jnp.sum(grad_output * rows, axis=1) for rows in chosen_rows], axis=1)
    grad_normed2 = jnp.dot(both, grad_back, preferred_element_type=F32)
    grad_picked = gates * (grad_gates - jnp.sum(gates * grad_gates, axis=1, keepdims=True))
    grad_logits = jnp.sum(chosen * grad_picked[:, :, None], axis=1)
    grad_normed2 = grad_normed2 + contract(grad_logits, w_router.astype(F32), 1, 1, HIGH)
    grad_router = contract(normed2.astype(F32), grad_logits, 0, 0, HIGH)
    grad_mixed, grad_norm2 = norm2_pull(grad_normed2)
    grad_mixed = grad_mixed + grad_output
    grad_branch = grad_mixed.astype(BF)

    grad_wout = contract(attended, grad_branch, 0, 0).astype(BF)
    grad_wout = grad_wout.reshape(replicas, groups, out_rows, width)
    grad_wout = lax.psum_scatter(grad_wout, "dp", scatter_dimension=1, tiled=True)[:, 0]
    if stepwise:
        grad_wout = sum(
            (hop(grad_wout[r], r) if r else grad_wout[r]).astype(F32) for r in range(replicas)
        ).astype(BF)
    else:
        grad_wout = lax.psum_scatter(
            grad_wout.reshape(replicas * out_rows, width), "head", scatter_dimension=0, tiled=True
        )
    grad_out_proj = lax.all_gather(grad_wout, "dp", axis=0, tiled=True).astype(F32)

    grad_heads = contract(grad_branch, w_out_cat, 1, 1).astype(BF)
    sums = jnp.zeros((heads_here, TILE, 2 * length), F32)
    grad_blocks = [grad_heads[:, i * head_cols : (i + 1) * head_cols] for i in range(replicas)]
    grad_total = None
    weight_terms = []
    if stepwise:
        arrived = [hop(grad_blocks[r], r) if r else grad_blocks[0] for r in range(replicas)]
        for r in (0, 2, 3, 1):
            grad_qkv, sums = attend_bwd(order[r].reshape(1), qkv, arrived[r], kept[r], sums, length)
            normed_seq = lax.dynamic_slice_in_dim(normed, order[r] * length, length, 0)
            weight_terms.append(contract(normed_seq, grad_qkv, 0, 0))
            mine = hop(grad_qkv, r) if r else grad_qkv
            weight = lax.dynamic_index_in_dim(w_qkv_all, order[r], 0, keepdims=False)
            term = contract(mine, weight, 1, 1)
            grad_total = term if grad_total is None else grad_total + term
        grad_normed = grad_total
        grad_qkv_w = sum(weight_terms)
    else:
        stacked = jnp.stack(grad_blocks, axis=0)
        stacked = lax.all_to_all(stacked, "head", split_axis=0, concat_axis=0, tiled=True)
        stacked = stacked.reshape(group_rows, head_cols)
        seqs = []
        for s in range(sequences):
            grad_seq = stacked[s * length : (s + 1) * length]
            grad_qkv, sums = attend_bwd(
                jnp.full((1,), s, jnp.int32), qkv, grad_seq, kept[s], sums, length
            )
            seqs.append(grad_qkv)
        grad_qkv = jnp.concatenate(seqs, axis=0)
        grad_qkv_w = contract(normed, grad_qkv, 0, 0)
        grad_qkv = lax.all_to_all(
            grad_qkv.reshape(replicas, own_rows, 3 * head_cols),
            "head",
            split_axis=0,
            concat_axis=0,
            tiled=True,
        )
        grad_normed = sum(contract(grad_qkv[i], w_qkv_all[i], 1, 1) for i in range(replicas))

    _, norm1_pull = jax.vjp(rms_norm, inputs_own, norm1_gain)
    grad_first, grad_norm1 = norm1_pull(grad_normed)
    grad_input = grad_mixed + grad_first
    grad_bias = contract(unskew(sums), line, 1, 1, HIGH)
    grad_qkv_w, grad_bias = lax.psum((grad_qkv_w.astype(BF), grad_bias), "dp")
    grad_qkv_w = grad_qkv_w.astype(F32)
    grad_norm1, grad_norm2, grad_router = lax.psum(
        (grad_norm1, grad_norm2, grad_router), ("dp", "head")
    )
    return (
        output,
        grad_input,
        grad_norm1,
        grad_qkv_w[:, :head_cols],
        grad_qkv_w[:, head_cols : 2 * head_cols],
        grad_qkv_w[:, 2 * head_cols :],
        grad_out_proj,
        jnp.transpose(grad_bias),
        grad_norm2,
        grad_router,
        grad_gate_w,
        grad_up_w,
        grad_down_w,
    )


def body(*args):
    block_input, cotangent, rel_bucket, pos_bias, w_gate, w_router = (
        args[0],
        args[1],
        args[4],
        args[10],
        args[13],
        args[12],
    )
    own_rows = cotangent.shape[0]
    length = (rel_bucket.shape[0] + 1) // 2
    replicas, groups = lax.axis_size("head"), lax.axis_size("dp")
    experts = w_router.shape[1]
    capacity = 5 * 2 * own_rows // (4 * experts)
    stepwise = (
        own_rows == length
        and block_input.shape[0] == replicas * length
        and replicas == 4
        and groups == 8
        and experts == groups
        and capacity % 16 == 0
        and pos_bias.shape[1] in (2, 4, 6)
        and w_gate.shape[2] % 256 == 0
    )
    return body_steps(*args) if stepwise else body_plain(*args)


def body_steps(
    block_input,
    cotangent,
    expert_ids,
    priority,
    rel_bucket,
    norm1_gain,
    w_query,
    w_key,
    w_value,
    w_out,
    pos_bias,
    norm2_gain,
    w_router,
    w_gate,
    w_up,
    w_down,
):
    group_rows, width = block_input.shape
    own_rows = cotangent.shape[0]
    buckets, heads_here = pos_bias.shape
    head_cols = w_query.shape[1]
    length = (rel_bucket.shape[0] + 1) // 2
    experts = w_router.shape[1]
    capacity = 5 * 2 * own_rows // (4 * experts)
    slot_count = experts * capacity
    replicas, groups = lax.axis_size("head"), lax.axis_size("dp")
    me, dp_at = lax.axis_index("head"), lax.axis_index("dp")

    dest = route_slots(expert_ids, priority[0], experts, capacity)
    bits = (dest // capacity) ^ dp_at
    position = sum(p * (bits == offset).astype(jnp.int32) for p, offset in enumerate(OFFSETS))
    mixed_dest = jnp.where(
        dest < slot_count,
        position * capacity + dest % capacity,
        slot_count,
    )
    routing = jnp.concatenate([mixed_dest, expert_ids], axis=1)
    routing_rows = jnp.pad(routing.T, ((0, 4), (0, 0)))
    routing_cols = jnp.pad(routing, ((0, 0), (0, 4)))
    router_wide = jnp.pad(w_router, ((0, 0), (0, TILE - experts)))
    line = (rel_bucket[::-1][None, :] == jnp.arange(buckets, dtype=jnp.int32)[:, None]).astype(F32)
    line = jnp.pad(line, ((0, 0), (1, 0)))
    input_weights = (w_query, w_key, w_value)
    (
        attended,
        probs,
        cot_here,
        normed,
        qkv,
        w_cat,
        cot_far,
        routing_far,
        mixed,
        normed2,
    ) = attend_all(
        block_input,
        norm1_gain[None, :],
        input_weights,
        contract(pos_bias, line, 0, 0, HIGH)[:, None, :],
        cotangent,
        routing_rows,
        w_out,
        norm2_gain[None, :],
        groups,
        capacity,
    )

    gate_w, up_w, down_w = w_gate[0], w_up[0], w_down[0]
    tile = 256
    (
        rows_here,
        hidden_here,
        ggp_here,
        gup_here,
        scaled_here,
        back,
        grad_back,
        slot_slope,
        normed2_far,
        cot_far_rest,
    ) = expert_stage(
        normed2,
        routing_rows,
        cot_here,
        router_wide,
        gate_w,
        up_w,
        down_w,
        cotangent,
        groups,
        capacity,
        tile,
    )

    (
        far_rows,
        far_scaled,
        gates,
        grad_mixed,
        grad_router,
        grad_norm2,
        carry,
        part_sum,
        grad_qkv_w,
        grad_wout,
        lines,
    ) = attend_back(
        normed2_far,
        (cot_far, cot_far_rest),
        routing_far,
        router_wide,
        (
            grad_back.reshape(slot_count, width),
            slot_slope.reshape(slot_count, TILE),
            routing_cols,
            mixed,
            normed2,
            cotangent,
            norm2_gain[None, :],
            w_cat,
        ),
        qkv,
        probs,
        normed,
        input_weights,
        attended,
        groups,
        capacity,
        experts,
    )

    (
        wide_kept,
        wide_came,
        tall_kept,
        tall_came,
        grad_qkv_w,
        grad_out_proj,
        summed,
        grad_first,
        expert_sum,
        _,
    ) = last_stage(
        (far_rows.reshape(slot_count, width), far_scaled.reshape(slot_count, width)),
        (rows_here.reshape(slot_count, width), scaled_here.reshape(slot_count, width)),
        (gates, routing_cols, norm1_gain[None, :]),
        (gate_w, up_w, down_w),
        (ggp_here, gup_here),
        hidden_here,
        (
            grad_qkv_w.reshape(groups, width // groups, 3 * head_cols),
            grad_wout.reshape(replicas, groups, head_cols // groups, width),
        ),
        (carry, part_sum, block_input, back),
        (grad_norm2, grad_router, lines),
        tile,
    )
    results = finish(
        (wide_kept, wide_came),
        (tall_kept, tall_came),
        grad_qkv_w,
        grad_out_proj,
        (mixed, expert_sum, grad_mixed, grad_first),
        summed,
        line.astype(BF),
        heads_here,
    )
    output, grad_input, grad_query_w, grad_key_w, grad_value_w, grad_out_proj = results[:6]
    grad_gate_w, grad_up_w, grad_down_w, grad_norm1, grad_norm2, grad_bias, grad_router = results[6:]
    return (
        output,
        grad_input,
        grad_norm1[0],
        grad_query_w,
        grad_key_w,
        grad_value_w,
        grad_out_proj,
        jnp.transpose(grad_bias),
        grad_norm2[0],
        jnp.transpose(grad_router),
        grad_gate_w[None],
        grad_up_w[None],
        grad_down_w[None],
    )


def solution(mesh):
    placed = (
        P("dp", None),
        P(("dp", "head"), None),
        P(("dp", "head"), None),
        P(("dp", "head"), None),
        P(),
        P(),
        P(None, "head"),
        P(None, "head"),
        P(None, "head"),
        P("head", None),
        P(None, "head"),
        P(),
        P(),
        P("dp", None, None),
        P("dp", None, None),
        P("dp", None, None),
    )
    return jax.shard_map(
        body,
        mesh=mesh,
        in_specs=placed,
        out_specs=(
            P(("dp", "head"), None),
            P(("dp", "head"), None),
            P(),
            P(None, "head"),
            P(None, "head"),
            P(None, "head"),
            P("head", None),
            P(None, "head"),
            P(),
            P(),
            P("dp", "head", None),
            P("dp", "head", None),
            P("dp", "head", None),
        ),
        check_vma=False,
    )
```

```python
import functools

import jax
import jax.numpy as jnp
from jax import lax
from jax.experimental import pallas as pl
from jax.experimental.pallas import tpu as pltpu
from jax.sharding import PartitionSpec as P

EPS = 1e-06
SCALE = 0.125
HIGH = lax.Precision.HIGHEST
TILE = 128
BF = jnp.bfloat16
F32 = jnp.float32
VMEM_LIMIT = 48 << 20
VMEM_MOST = 60 << 20
GELU_A = 0.7978845608028654
GELU_B = 0.044715
OFFSETS = [0, 1, 6, 7, 2, 4, 3, 5]
PEERS = [4, 5, 6, 7, 2, 3, 1]


def rms_norm(value, gain):
    return value * lax.rsqrt(jnp.mean(value * value, axis=-1, keepdims=True) + EPS) * gain


def geglu(gate, up_part):
    return jax.nn.gelu(gate) * up_part


def contract(left, right, left_dim, right_dim, precision=None):
    return lax.dot_general(
        left,
        right,
        (((left_dim,), (right_dim,)), ((), ())),
        precision=precision,
        preferred_element_type=jnp.float32,
    )


def route_slots(chosen, ranks, experts, capacity):
    count = chosen.shape[0]
    keys = jnp.concatenate([ranks, ranks + count])
    wanted = jnp.concatenate([chosen[:, 0], chosen[:, 1]])
    smaller = (wanted[:, None] == wanted[None, :]) & (keys[None, :] < keys[:, None])
    place = jnp.sum(smaller.astype(jnp.int32), axis=1)
    dest = jnp.where(place < capacity, wanted * capacity + place, experts * capacity)
    return jnp.stack([dest[:count], dest[count:]], axis=1)


def skew_kernel(line_ref, table_ref):
    heads, rows, cols = table_ref.shape
    row = lax.broadcasted_iota(jnp.int32, (8, cols), 0)
    for h in range(heads):
        value = jnp.broadcast_to(line_ref[h], (8, cols))
        for shift in (1, 2, 4):
            value = jnp.where((row & shift) != 0, pltpu.roll(value, shift, 1), value)
        table_ref[h, :8] = value
        done = 8
        while done < rows:
            table_ref[h, done : 2 * done] = pltpu.roll(table_ref[h, :done], done, 1)
            done *= 2


def unskew_kernel(table_ref, line_ref):
    heads, rows, cols = table_ref.shape
    row = lax.broadcasted_iota(jnp.int32, (8, cols), 0)
    for h in range(heads):
        value, left = table_ref[h], rows // 2
        while left >= 8:
            value = value[:left] + pltpu.roll(value[left:], cols - left, 1)
            left //= 2
        for shift in (1, 2, 4):
            value = jnp.where((row & shift) != 0, pltpu.roll(value, cols - shift, 1), value)
        line_ref[h] = jnp.sum(value, axis=0, keepdims=True)


def skew(line):
    heads, cols = line.shape
    return pl.pallas_call(
        skew_kernel,
        out_shape=jax.ShapeDtypeStruct((heads, TILE, cols), F32),
        compiler_params=pltpu.CompilerParams(vmem_limit_bytes=VMEM_LIMIT),
        name="skew",
    )(line[:, None, :])


def unskew(table):
    heads, _, cols = table.shape
    return pl.pallas_call(
        unskew_kernel,
        out_shape=jax.ShapeDtypeStruct((heads, 1, cols), F32),
        compiler_params=pltpu.CompilerParams(vmem_limit_bytes=VMEM_LIMIT),
        name="unskew",
    )(table)[:, 0]


def lanes_of(shape, half, part):
    lane = lax.broadcasted_iota(jnp.int32, shape, 1)
    return (lane >= half) if part else (lane < half)


def attend_fwd_kernel(seq_ref, q_ref, k_ref, v_ref, table_ref, out_ref, probs_ref, acc_ref):
    del seq_ref
    length, lanes = q_ref.shape
    half = lanes // 2
    chunk = 2 * TILE
    key = k_ref[...]
    value_t = v_ref[...].T
    for part in range(2):
        query = jnp.where(lanes_of((length, lanes), half, part), q_ref[...] * SCALE, 0).astype(BF)
        for c in range(length // chunk):
            cols = slice(c * chunk, (c + 1) * chunk)
            scores = contract(key, query[cols], 1, 1)
            pieces = []
            for kb in range(length // TILE):
                at = length - TILE * kb + chunk * c
                pieces.append(
                    scores[kb * TILE : (kb + 1) * TILE] + table_ref[part, :, at : at + chunk]
                )
            scores = jnp.concatenate(pieces, axis=0)
            top = jnp.max(scores, axis=0, keepdims=True)
            shifted = jnp.exp(scores - top)
            total = jnp.sum(shifted, axis=0, keepdims=True)
            probs = (shifted * (1.0 / total)).astype(BF)
            probs_ref[part, :, cols] = probs
            acc_ref[part * half : (part + 1) * half, cols] = jnp.dot(
                value_t[part * half : (part + 1) * half], probs, preferred_element_type=F32
            )
    out_ref[...] = acc_ref[...].T.astype(BF)


def attend_fwd(seq, qkv, table, length):
    heads, _, width = table.shape
    columns = qkv.shape[1] // 3
    pairs = heads // 2
    lanes = columns // pairs
    spec = [
        pl.BlockSpec((length, lanes), lambda p, s, j=j: (s[0], j * pairs + p)) for j in range(3)
    ]
    return pl.pallas_call(
        attend_fwd_kernel,
        out_shape=(
            jax.ShapeDtypeStruct((length, columns), BF),
            jax.ShapeDtypeStruct((heads, length, length), BF),
        ),
        grid_spec=pltpu.PrefetchScalarGridSpec(
            num_scalar_prefetch=1,
            grid=(pairs,),
            in_specs=spec + [pl.BlockSpec((2, TILE, width), lambda p, s: (p, 0, 0))],
            out_specs=[
                pl.BlockSpec((length, lanes), lambda p, s: (0, p)),
                pl.BlockSpec((2, length, length), lambda p, s: (p, 0, 0)),
            ],
            scratch_shapes=[pltpu.VMEM((lanes, length), F32)],
        ),
        compiler_params=pltpu.CompilerParams(vmem_limit_bytes=VMEM_LIMIT),
        cost_estimate=pl.CostEstimate(
            flops=heads * 8 * length * length * lanes,
            bytes_accessed=heads * length * length * 2 + 8 * length * columns,
            transcendentals=heads * length * length,
        ),
        name="attend_fwd",
    )(seq, qkv, qkv, qkv, table)


def attend_bwd_kernel(
    seq_ref, q_ref, k_ref, v_ref, grad_ref, probs_ref, sums_in_ref, out_ref, sums_ref, acc_ref
):
    del seq_ref
    length, lanes = q_ref.shape
    half = lanes // 2
    chunk = 2 * TILE
    pair = pl.program_id(0)
    columns = out_ref.shape[1] // 3
    key_t = k_ref[...].T
    value = v_ref[...]
    sums_ref[...] = sums_in_ref[...]
    grad_keys, grad_values = [], []
    for part in range(2):
        mask = lanes_of((length, lanes), half, part)
        grad = jnp.where(mask, grad_ref[...], 0).astype(BF)
        grad_key = jnp.zeros((length, lanes), F32)
        grad_value = jnp.zeros((length, lanes), F32)
        for c in range(length // chunk):
            cols = slice(c * chunk, (c + 1) * chunk)
            grad_probs = contract(value, grad[cols], 1, 1)
            probs_low = probs_ref[part, :, cols]
            probs = probs_low.astype(F32)
            delta = jnp.sum(probs * grad_probs, axis=0, keepdims=True)
            grad_scores = (probs * (grad_probs - delta)).astype(BF)
            grad_value += jnp.dot(probs_low, grad_ref[cols, :], preferred_element_type=F32)
            grad_key += jnp.dot(grad_scores, q_ref[cols, :], preferred_element_type=F32)
            acc_ref[part * half : (part + 1) * half, cols] = jnp.dot(
                key_t[part * half : (part + 1) * half], grad_scores, preferred_element_type=F32
            )
            for kb in range(length // TILE):
                at = length - TILE * kb + chunk * c
                sums_ref[part, :, at : at + chunk] += grad_scores[
                    kb * TILE : (kb + 1) * TILE
                ].astype(F32)
        grad_keys.append(grad_key)
        grad_values.append(grad_value)
    first = lanes_of((length, lanes), half, 0)
    at = pl.multiple_of(pair * lanes, lanes)
    out_ref[:, pl.ds(at, lanes)] = (acc_ref[...].T * SCALE).astype(BF)
    at = pl.multiple_of(columns + pair * lanes, lanes)
    out_ref[:, pl.ds(at, lanes)] = (jnp.where(first, *grad_keys) * SCALE).astype(BF)
    at = pl.multiple_of(2 * columns + pair * lanes, lanes)
    out_ref[:, pl.ds(at, lanes)] = jnp.where(first, *grad_values).astype(BF)


def attend_bwd(seq, qkv, grad, probs, sums, length):
    heads, _, width = sums.shape
    columns = qkv.shape[1] // 3
    pairs = heads // 2
    lanes = columns // pairs
    spec = [
        pl.BlockSpec((length, lanes), lambda p, s, j=j: (s[0], j * pairs + p)) for j in range(3)
    ]
    sums_spec = pl.BlockSpec((2, TILE, width), lambda p, s: (p, 0, 0))
    return pl.pallas_call(
        attend_bwd_kernel,
        out_shape=(
            jax.ShapeDtypeStruct((length, 3 * columns), BF),
            jax.ShapeDtypeStruct(sums.shape, F32),
        ),
        grid_spec=pltpu.PrefetchScalarGridSpec(
            num_scalar_prefetch=1,
            grid=(pairs,),
            in_specs=spec
            + [
                pl.BlockSpec((length, lanes), lambda p, s: (0, p)),
                pl.BlockSpec((2, length, length), lambda p, s: (p, 0, 0)),
                sums_spec,
            ],
            out_specs=[pl.BlockSpec((length, 3 * columns), lambda p, s: (0, 0)), sums_spec],
            scratch_shapes=[pltpu.VMEM((lanes, length), F32)],
        ),
        compiler_params=pltpu.CompilerParams(vmem_limit_bytes=VMEM_LIMIT),
        cost_estimate=pl.CostEstimate(
            flops=heads * 16 * length * length * lanes,
            bytes_accessed=heads * length * length * 2 + 16 * length * columns,
            transcendentals=0,
        ),
        name="attend_bwd",
    )(seq, qkv, qkv, qkv, grad, probs, sums)


def flipped(index, bits):
    out, step = index, 1
    while step <= bits:
        if bits & step:
            out = out + step * (1 - 2 * lax.rem(index // step, 2))
        step *= 2
    return out


def plane(d, position):
    return flipped(d, OFFSETS[position])


def greet(peers):
    barrier = pltpu.get_barrier_semaphore()
    for peer in peers:
        pl.semaphore_signal(barrier, inc=1, device_id=peer, device_id_type=pl.DeviceIdType.MESH)
    pl.semaphore_wait(barrier, len(peers))


def remote(source, target, send_sem, recv_sem, peer):
    return pltpu.make_async_remote_copy(
        src_ref=source,
        dst_ref=target,
        send_sem=send_sem,
        recv_sem=recv_sem,
        device_id=peer,
        device_id_type=pl.DeviceIdType.MESH,
    )


def attend_all_kernel(
    input_hbm,
    gain_ref,
    query_hbm,
    key_hbm,
    value_hbm,
    line_ref,
    cot_hbm,
    routing_ref,
    w_out_hbm,
    gain2_ref,
    attended_out,
    probs_out,
    came_out,
    normed_out,
    qkv_out,
    w_cat_out,
    cot_far_out,
    routing_far_out,
    mixed_ref,
    normed2_ref,
    input_ref,
    weight_ref,
    cot_ref,
    w_out_ref,
    table_ref,
    sends,
    acc_ref,
    block_ref,
    hold_ref,
    normed_ref,
    qkv_ref,
    attended_ref,
    w_cat,
    w_land,
    row_send,
    row_recv,
    hop_send,
    hop_recv,
    w_send,
    w_recv,
    plane_send,
    plane_recv,
    core_send,
    core_recv,
    far_send,
    far_recv,
    hold_sem,
    own_sem,
    load_sem,
):
    z, d = lax.axis_index("head"), lax.axis_index("dp")
    heads, _, _ = table_ref.shape
    replicas, length, columns = block_ref.shape
    groups, capacity, _ = sends.shape
    width = input_ref.shape[1]
    part_rows = w_land.shape[1]
    pairs = heads // 2
    lanes = columns // pairs
    half = lanes // 2
    chunk = 2 * TILE
    hops = [3, 2, 1]
    cot_load = pltpu.make_async_copy(cot_hbm, cot_ref, load_sem.at[0])
    w_out_load = pltpu.make_async_copy(w_out_hbm, w_out_ref, load_sem.at[1])
    weight_loads = [
        pltpu.make_async_copy(
            source, weight_ref.at[:, pl.ds(i * columns, columns)], load_sem.at[2 + i]
        )
        for i, source in enumerate((query_hbm, key_hbm, value_hbm))
    ]
    input_loads = {}
    for r in [3, 2, 1, 0]:
        span = pl.ds(pl.multiple_of(flipped(z, r) * length, length), length)
        input_loads[r] = pltpu.make_async_copy(
            input_hbm.at[span], input_ref.at[span], load_sem.at[5 + r]
        )
    for copy in [cot_load, input_loads[3]] + weight_loads:
        copy.start()
    for copy in [input_loads[2], input_loads[1], input_loads[0], w_out_load]:
        copy.start()
    greet([{"dp": plane(d, o)} for o in PEERS] + [{"head": flipped(z, r)} for r in hops])
    copies = []

    def launch(*what):
        copy = remote(*what)
        copy.start()
        copies.append(copy)
        return copy

    piece = w_out_hbm.at[pl.ds(pl.multiple_of(d * part_rows, part_rows), part_rows), :]
    w_hops = {}
    for r in hops:
        w_hops[r] = remote(piece, w_land.at[r], w_send.at[r], w_recv.at[r], {"head": flipped(z, r)})
        w_hops[r].start()
    cot_load.wait()
    half_plane = groups // 2

    def dispatch(start):
        span = slice(start, start + half_plane)
        first, second = selector(routing_ref, start * capacity, half_plane * capacity)
        sends[span, :, :width] = (
            jnp.dot((first + second).astype(BF), cot_ref[...], preferred_element_type=F32)
            .astype(BF)
            .reshape(half_plane, capacity, width)
        )
        sends[span, :, width:] = slot_signs(routing_ref, first, second).reshape(
            half_plane, capacity, TILE
        )

    def send_rows(start):
        for o in range(start, start + half_plane):
            if o:
                launch(
                    sends.at[o], came_out.at[o], row_send.at[o], row_recv.at[o], {"dp": plane(d, o)}
                )

    chips = [o for o, bits in enumerate(OFFSETS) if o and bits % 2 == 0]
    plane_copies = {}

    def w_rows(s, o):
        at = s * columns + plane(d, o) * part_rows
        return pl.ds(pl.multiple_of(at, part_rows), part_rows)

    dispatch(half_plane)
    for s in hops:
        w_hops[s].wait()
        at = w_rows(s, 0)
        w_cat[at, :] = w_land[s]
        for o in chips:
            plane_copies[s, o] = remote(
                w_land.at[s],
                w_cat.at[at, :],
                plane_send.at[s, o],
                plane_recv.at[s, o],
                {"dp": plane(d, o)},
            )
            plane_copies[s, o].start()
    send_rows(half_plane)
    dispatch(0)
    send_rows(0)
    own = pltpu.make_async_copy(sends.at[0], came_out.at[0], own_sem.at[0])
    own.start()
    far = {"head": flipped(z, 2)}
    launch(routing_ref, routing_far_out, far_send.at[0], far_recv.at[0], far)
    early = pl.ds(0, cot_far_out.shape[0])
    launch(cot_hbm.at[early], cot_far_out, far_send.at[1], far_recv.at[1], far)
    skew_kernel(line_ref, table_ref)
    w_out_load.wait()
    w_cat[:columns, :] = w_out_ref[...]

    moves = []
    for turn, r in enumerate(reversed(range(replicas))):
        start = flipped(z, r) * length
        slot = turn % 2
        if turn >= 2:
            for move in moves[turn - 2]:
                move.wait()

        input_loads[r].wait()

        def norm_step(i, carry, start=start, slot=slot):
            rows = pl.multiple_of(start + i * TILE, TILE)
            value = input_ref[pl.ds(rows, TILE), :].astype(F32)
            value = rms_norm(value, gain_ref[...])
            normed_ref[slot, pl.ds(pl.multiple_of(i * TILE, TILE), TILE), :] = value.astype(BF)
            return carry

        lax.fori_loop(0, length // TILE, norm_step, 0)
        if turn == 0:
            for copy in weight_loads:
                copy.wait()
        qkv_ref[slot] = jnp.dot(
            normed_ref[slot], weight_ref[...], preferred_element_type=F32
        ).astype(BF)

        def pair_step(pair, carry, slot=slot, r=r):
            def part_of(j):
                at = pl.multiple_of(j * columns + pair * lanes, lanes)
                return qkv_ref[slot, :, pl.ds(at, lanes)]

            key = part_of(1)
            value_t = part_of(2).T
            scaled = part_of(0) * SCALE
            for part in range(2):
                query = jnp.where(lanes_of((length, lanes), half, part), scaled, 0).astype(BF)
                for c in range(length // chunk):
                    cols = slice(c * chunk, (c + 1) * chunk)
                    scores = contract(key, query[cols], 1, 1)
                    pieces = []
                    for kb in range(length // TILE):
                        at = length - TILE * kb + chunk * c
                        pieces.append(
                            scores[kb * TILE : (kb + 1) * TILE]
                            + table_ref[pair * 2 + part, :, at : at + chunk]
                        )
                    scores = jnp.concatenate(pieces, axis=0)
                    top = jnp.max(scores, axis=0, keepdims=True)
                    shifted = jnp.exp(scores - top)
                    total = jnp.sum(shifted, axis=0, keepdims=True)
                    probs = (shifted * (1.0 / total)).astype(BF)
                    hold_ref[slot, pair * 2 + part, :, cols] = probs
                    acc_ref[part * half : (part + 1) * half, cols] = jnp.dot(
                        value_t[part * half : (part + 1) * half],
                        probs,
                        preferred_element_type=F32,
                    )
            at = pl.multiple_of(pair * lanes, lanes)
            block_ref[r, :, pl.ds(at, lanes)] = acc_ref[...].T.astype(BF)
            return carry

        lax.fori_loop(0, pairs, pair_step, 0)
        moves.append(
            [
                pltpu.make_async_copy(ref.at[slot], out.at[r], hold_sem.at[i, slot])
                for i, (ref, out) in enumerate(
                    ((hold_ref, probs_out), (normed_ref, normed_out), (qkv_ref, qkv_out))
                )
            ]
        )
        for move in moves[-1]:
            move.start()
        if r:
            launch(
                block_ref.at[r],
                attended_ref.at[:, pl.ds(r * columns, columns)],
                hop_send.at[r],
                hop_recv.at[r],
                {"head": flipped(z, r)},
            )
        else:
            attended_ref[:, :columns] = block_ref[0]
        if turn == 1:
            for s in hops:
                for o in [0] + chips:
                    if o:
                        plane_copies[s, o].wait_recv()
                    piece = w_cat.at[w_rows(s, o), :]
                    launch(piece, piece, core_send.at[s, o], core_recv.at[s, o], {"dp": plane(d, 1)})
    for copy in plane_copies.values():
        copy.wait_send()
    for copy in copies:
        copy.wait()
    outs = [
        pltpu.make_async_copy(attended_ref, attended_out, own_sem.at[1]),
        pltpu.make_async_copy(w_cat, w_cat_out, own_sem.at[2]),
    ]
    for copy in outs:
        copy.start()

    mixed_ref[...] = jnp.dot(attended_ref[...], w_cat[...], preferred_element_type=F32)

    def mixed_step(i, carry):
        at = pl.multiple_of(i * TILE, TILE)
        span = pl.ds(at, TILE)
        rows = pl.multiple_of(z * length + at, TILE)
        value = mixed_ref[span, :] + input_ref[pl.ds(rows, TILE), :].astype(F32)
        mixed_ref[span, :] = value
        normed2_ref[span, :] = rms_norm(value, gain2_ref[...]).astype(BF)
        return carry

    lax.fori_loop(0, length // TILE, mixed_step, 0)
    for move in moves[-2] + moves[-1] + outs + [own]:
        move.wait()


def attend_all(inputs, gain, weights, line, cot, routing, w_out, gain2, groups, capacity):
    heads, _, table_width = line.shape
    width = inputs.shape[1]
    length = cot.shape[0]
    replicas = inputs.shape[0] // length
    columns = weights[0].shape[1]
    lanes = 2 * columns // heads
    part_rows = columns // groups
    vmem = pl.BlockSpec(memory_space=pltpu.VMEM)
    hbm = pl.BlockSpec(memory_space=pl.ANY)
    came_shape = (groups, capacity, width + TILE)
    plane_sem = pltpu.SemaphoreType.DMA((groups,))
    hop_sem = pltpu.SemaphoreType.DMA((replicas,))
    both_sem = pltpu.SemaphoreType.DMA((replicas, groups))
    two_sem = pltpu.SemaphoreType.DMA((2,))
    return pl.pallas_call(
        attend_all_kernel,
        out_shape=(
            jax.ShapeDtypeStruct((length, replicas * columns), BF),
            jax.ShapeDtypeStruct((replicas, heads, length, length), BF),
            jax.ShapeDtypeStruct(came_shape, BF),
            jax.ShapeDtypeStruct((replicas, length, width), BF),
            jax.ShapeDtypeStruct((replicas, length, 3 * columns), BF),
            jax.ShapeDtypeStruct((replicas * columns, width), BF),
            jax.ShapeDtypeStruct((length // 2, width), BF),
            jax.ShapeDtypeStruct(routing.shape, routing.dtype),
            jax.ShapeDtypeStruct((length, width), F32),
            jax.ShapeDtypeStruct((length, width), BF),
        ),
        in_specs=[hbm, vmem, hbm, hbm, hbm, vmem, hbm, vmem, hbm, vmem],
        out_specs=[hbm] * 8 + [vmem] * 2,
        scratch_shapes=[
            pltpu.VMEM(inputs.shape, BF),
            pltpu.VMEM((width, 3 * columns), BF),
            pltpu.VMEM(cot.shape, BF),
            pltpu.VMEM(w_out.shape, BF),
            pltpu.VMEM((heads, TILE, table_width), F32),
            pltpu.VMEM(came_shape, BF),
            pltpu.VMEM((lanes, length), F32),
            pltpu.VMEM((replicas, length, columns), BF),
            pltpu.VMEM((2, heads, length, length), BF),
            pltpu.VMEM((2, length, width), BF),
            pltpu.VMEM((2, length, 3 * columns), BF),
            pltpu.VMEM((length, replicas * columns), BF),
            pltpu.VMEM((replicas * columns, width), BF),
            pltpu.VMEM((replicas, part_rows, width), BF),
            plane_sem,
            plane_sem,
            hop_sem,
            hop_sem,
            hop_sem,
            hop_sem,
            both_sem,
            both_sem,
            both_sem,
            both_sem,
            two_sem,
            two_sem,
            pltpu.SemaphoreType.DMA((3, 2)),
            pltpu.SemaphoreType.DMA((3,)),
            pltpu.SemaphoreType.DMA((9,)),
        ],
        compiler_params=pltpu.CompilerParams(
            vmem_limit_bytes=VMEM_MOST, collective_id=1, has_side_effects=True
        ),
        cost_estimate=pl.CostEstimate(
            flops=replicas * heads * 8 * length * length * lanes,
            bytes_accessed=replicas * heads * length * length * 4,
            transcendentals=replicas * heads * length * length,
        ),
        name="attend_all",
    )(inputs, gain, *weights, line, cot, routing, w_out, gain2)


def selector(routing, start, count):
    slot = lax.broadcasted_iota(jnp.int32, (count, routing.shape[1]), 0) + start
    return [jnp.where(slot == routing[k : k + 1], 1.0, 0.0) for k in range(2)]


def slot_signs(routing, first, second):
    lane = lax.broadcasted_iota(jnp.int32, (TILE, routing.shape[1]), 0)
    signs = jnp.where(lane == routing[3:4], 1.0, 0.0) - jnp.where(lane == routing[2:3], 1.0, 0.0)
    return contract((first - second).astype(BF), signs.astype(BF), 1, 1).astype(BF)


def token_selector(routing, slots):
    slot = lax.broadcasted_iota(jnp.int32, (routing.shape[0], slots), 1)
    return [jnp.where(slot == routing[:, k : k + 1], 1.0, 0.0) for k in range(2)]


def expert_tile(rows, scaled, gate_w, up_w, down_w):
    gate = jnp.dot(rows, gate_w, preferred_element_type=F32)
    up_part = jnp.dot(rows, up_w, preferred_element_type=F32)
    grad_hidden = contract(scaled, down_w, 1, 1)
    square = gate * gate
    bend = jnp.tanh(gate * (GELU_A + GELU_A * GELU_B * square))
    half = 0.5 + 0.5 * bend
    active = gate * half
    slope = half + 0.5 * gate * (1.0 - bend * bend) * (GELU_A + 3.0 * GELU_A * GELU_B * square)
    hidden = (active * up_part).astype(BF)
    grad_gate = (grad_hidden * up_part * slope).astype(BF)
    grad_up = (grad_hidden * active).astype(BF)
    return hidden, grad_gate, grad_up


def scaled_rows(rows, extended, router, width):
    logits = jnp.dot(rows, router, preferred_element_type=F32)
    sign = extended[:, width:].astype(F32)
    gap = jnp.sum(logits * sign, axis=1, keepdims=True)
    return (extended[:, :width].astype(F32) * (1.0 / (1.0 + jnp.exp(gap)))).astype(BF)


def expert_kernel(
    width,
    tile,
    normed_ref,
    routing_ref,
    cot_ref,
    router_ref,
    gate_hbm,
    up_hbm,
    down_hbm,
    cot_hbm,
    rows_out,
    hidden_out,
    grad_gate_out,
    grad_up_out,
    scaled_out,
    back_out,
    grad_back_out,
    slope_out,
    far_out,
    cot_far_out,
    gate_w,
    up_w,
    down_w,
    rows,
    sends,
    back,
    grad_back,
    slopes,
    hidden,
    grad_gate,
    grad_up,
    scaled,
    weight_sem,
    row_send,
    row_recv,
    slope_send,
    slope_recv,
    grad_send,
    grad_recv,
    unit_sem,
    keep_sem,
    far_sem,
):
    z, d = lax.axis_index("head"), lax.axis_index("dp")
    far = {"head": flipped(z, 2)}
    groups, capacity, _ = rows.shape
    units = gate_w.shape[1]
    tiles = units // tile
    count = 2 * capacity

    def weights_of(t):
        at = t * tile if isinstance(t, int) else pl.multiple_of(t * tile, tile)
        return [
            pltpu.make_async_copy(
                gate_hbm.at[:, pl.ds(at, tile)], gate_w.at[:, pl.ds(at, tile)], weight_sem.at[0, t]
            ),
            pltpu.make_async_copy(
                up_hbm.at[:, pl.ds(at, tile)], up_w.at[:, pl.ds(at, tile)], weight_sem.at[1, t]
            ),
            pltpu.make_async_copy(
                down_hbm.at[pl.ds(at, tile), :], down_w.at[pl.ds(at, tile), :], weight_sem.at[2, t]
            ),
        ]

    def start_weights(t, carry):
        for copy in weights_of(t):
            copy.start()
        return carry

    lax.fori_loop(0, tiles, start_weights, 0)
    greet([{"dp": plane(d, o)} for o in PEERS] + [far])
    pending = []
    arrivals = {}

    for start, number in ((2, 2), (4, groups - 4), (0, 2)):
        first, second = selector(routing_ref, start * capacity, number * capacity)
        sends[start : start + number] = (
            jnp.dot((first + second).astype(BF), normed_ref[...], preferred_element_type=F32)
            .astype(BF)
            .reshape(number, capacity, width)
        )
        for o in range(start, start + number):
            if o:
                arrivals[o] = remote(
                    sends.at[o], rows.at[o], row_send.at[o], row_recv.at[o], {"dp": plane(d, o)}
                )
                arrivals[o].start()
    over = [
        remote(normed_ref, far_out, far_sem.at[0, 0], far_sem.at[0, 1], far),
        remote(
            cot_hbm.at[pl.ds(cot_far_out.shape[0], cot_far_out.shape[0])],
            cot_far_out,
            far_sem.at[1, 0],
            far_sem.at[1, 1],
            far,
        ),
    ]
    for copy in over:
        copy.start()
    rows[0] = sends[0]

    unit_copies = {}
    order = list(range(groups // 2))
    for turn, j in enumerate(order):
        pair = (2 * j, 2 * j + 1)
        slot = turn % 2
        for o in pair:
            if o:
                arrivals[o].wait_recv()
        if turn >= 2:
            for copy in unit_copies[order[turn - 2]]:
                copy.wait()
        here = rows[2 * j : 2 * j + 2].reshape(count, width)
        extended = cot_ref[2 * j : 2 * j + 2].reshape(count, cot_ref.shape[2])
        scaled[2 * j : 2 * j + 2] = scaled_rows(here, extended, router_ref[...], width).reshape(
            2, capacity, width
        )

        def wide_tile(at, size, j=j, slot=slot):
            values = expert_tile(
                rows[2 * j : 2 * j + 2].reshape(count, width),
                scaled[2 * j : 2 * j + 2].reshape(count, width),
                gate_w[:, pl.ds(at, size)],
                up_w[:, pl.ds(at, size)],
                down_w[pl.ds(at, size), :],
            )
            for ref, value in zip((hidden, grad_gate, grad_up), values):
                ref[slot, :, pl.ds(at, size)] = value

        def tile_step(t, carry, j=j):
            if j == 0:
                for i in range(2):
                    for copy in weights_of(2 * t + i):
                        copy.wait()
            wide_tile(pl.multiple_of(2 * t * tile, tile), 2 * tile)
            return carry

        lax.fori_loop(0, tiles // 2, tile_step, 0)
        if tiles % 2:
            if j == 0:
                for copy in weights_of(tiles - 1):
                    copy.wait()
            wide_tile((tiles - 1) * tile, tile)
        span = pl.ds(j * count, count)
        unit_copies[j] = [
            pltpu.make_async_copy(ref.at[slot], out.at[span], unit_sem.at[slot, i])
            for i, (ref, out) in enumerate(
                ((hidden, hidden_out), (grad_gate, grad_gate_out), (grad_up, grad_up_out))
            )
        ]
        for copy in unit_copies[j]:
            copy.start()

        def back_step(t, carry, j=j, slot=slot):
            cols = pl.ds(pl.multiple_of(t * 2 * tile, 2 * tile), 2 * tile)
            value = jnp.dot(hidden[slot], down_w[:, cols], preferred_element_type=F32)
            back[2 * j : 2 * j + 2, :, cols] = value.astype(BF).reshape(2, capacity, 2 * tile)
            return carry

        def grad_step(t, carry, j=j, slot=slot):
            cols = pl.ds(pl.multiple_of(t * 2 * tile, 2 * tile), 2 * tile)
            value = contract(grad_gate[slot], gate_w[cols, :], 1, 1) + contract(
                grad_up[slot], up_w[cols, :], 1, 1
            )
            grad_back[2 * j : 2 * j + 2, :, cols] = value.astype(BF).reshape(2, capacity, 2 * tile)
            return carry

        def give(buffer, out, send_sem, recv_sem, pair=pair):
            for o in pair:
                if o:
                    copy = remote(
                        buffer.at[o],
                        out.at[o],
                        send_sem.at[o],
                        recv_sem.at[o],
                        {"dp": plane(d, o)},
                    )
                else:
                    copy = pltpu.make_async_copy(buffer.at[0], out.at[0], send_sem.at[0])
                copy.start()
                pending.append(copy)

        lax.fori_loop(0, width // (2 * tile), grad_step, 0)
        give(grad_back, grad_back_out, grad_send, grad_recv)
        lax.fori_loop(0, width // (2 * tile), back_step, 0)
        product = jnp.sum(
            cot_ref[2 * j : 2 * j + 2, :, :width].reshape(count, width).astype(F32)
            * back[2 * j : 2 * j + 2].reshape(count, width).astype(F32),
            axis=1,
            keepdims=True,
        )
        lane = lax.broadcasted_iota(jnp.int32, (count, TILE), 1)
        spread = jnp.zeros((count, TILE), F32)
        for k, term in enumerate(split_parts(product)):
            spread = jnp.where(lane == k, term.astype(F32), spread)
        slopes[2 * j : 2 * j + 2] = spread.astype(BF).reshape(2, capacity, TILE)
        give(slopes, slope_out, slope_send, slope_recv)

    keeps = [
        pltpu.make_async_copy(rows, rows_out, keep_sem.at[0]),
        pltpu.make_async_copy(scaled, scaled_out, keep_sem.at[1]),
        pltpu.make_async_copy(back, back_out, keep_sem.at[2]),
    ]
    for copy in keeps:
        copy.start()
    for j in order[-2:]:
        for copy in unit_copies[j]:
            copy.wait()
    for o in PEERS:
        arrivals[o].wait_send()
    for copy in pending + keeps + over:
        copy.wait()


def expert_stage(
    normed2, routing, cot, router, gate_w, up_w, down_w, cot_own, groups, capacity, tile
):
    width, units = gate_w.shape
    slots = groups * capacity
    vmem = pl.BlockSpec(memory_space=pltpu.VMEM)
    hbm = pl.BlockSpec(memory_space=pl.ANY)
    row_shape = jax.ShapeDtypeStruct((groups, capacity, width), BF)
    unit_shape = jax.ShapeDtypeStruct((slots, units), BF)
    row_buffer = pltpu.VMEM((groups, capacity, width), BF)
    unit_buffer = pltpu.VMEM((2, 2 * capacity, units), BF)
    row_sem = pltpu.SemaphoreType.DMA((groups,))
    return pl.pallas_call(
        functools.partial(expert_kernel, width, tile),
        out_shape=(row_shape,)
        + (unit_shape,) * 3
        + (row_shape,) * 3
        + (
            jax.ShapeDtypeStruct((groups, capacity, TILE), BF),
            jax.ShapeDtypeStruct(normed2.shape, BF),
            jax.ShapeDtypeStruct((normed2.shape[0] // 2, width), BF),
        ),
        in_specs=[vmem] * 4 + [hbm] * 4,
        out_specs=[hbm] * 10,
        scratch_shapes=[
            pltpu.VMEM((width, units), BF),
            pltpu.VMEM((width, units), BF),
            pltpu.VMEM((units, width), BF),
            row_buffer,
            row_buffer,
            row_buffer,
            row_buffer,
            pltpu.VMEM((groups, capacity, TILE), BF),
            unit_buffer,
            unit_buffer,
            unit_buffer,
            row_buffer,
            pltpu.SemaphoreType.DMA((3, units // tile)),
            row_sem,
            row_sem,
            row_sem,
            row_sem,
            row_sem,
            row_sem,
            pltpu.SemaphoreType.DMA((2, 3)),
            pltpu.SemaphoreType.DMA((3,)),
            pltpu.SemaphoreType.DMA((2, 2)),
        ],
        compiler_params=pltpu.CompilerParams(
            vmem_limit_bytes=VMEM_MOST, collective_id=2, has_side_effects=True
        ),
        cost_estimate=pl.CostEstimate(
            flops=12 * slots * width * units,
            bytes_accessed=6 * width * units + 6 * slots * units,
            transcendentals=slots * units,
        ),
        name="expert_stage",
    )(normed2, routing, cot, router, gate_w, up_w, down_w, cot_own)


def split_parts(value):
    first = value.astype(BF)
    rest = value - first.astype(F32)
    second = rest.astype(BF)
    return first, second, (rest - second.astype(F32)).astype(BF)


def combine_kernel(
    grad_back_ref,
    slot_slope_ref,
    routing_ref,
    mixed_ref,
    normed2_ref,
    cot_ref,
    router_ref,
    gain_ref,
    w_cat_ref,
    gates_ref,
    grad_mixed_ref,
    grad_branch_ref,
    grad_heads_ref,
    grad_router_ref,
    grad_norm2_ref,
    picked,
    slopes,
    gaps,
    pick,
):
    length, width = mixed_ref.shape

    slots = grad_back_ref.shape[0]
    first, second = token_selector(routing_ref, slots)
    gaps[...] = jnp.dot(
        (second - first).astype(BF), slot_slope_ref[...], preferred_element_type=F32
    )
    pick[...] = (first + second).astype(BF)

    picked[...] = jnp.dot(pick[...], grad_back_ref[...], preferred_element_type=F32)
    lane = lax.broadcasted_iota(jnp.int32, (TILE, TILE), 1)

    def row_step(i, total):
        span = pl.ds(pl.multiple_of(i * TILE, TILE), TILE)
        ids = routing_ref[span, :]
        sign = jnp.where(lane == ids[:, 3:4], 1.0, 0.0) - jnp.where(lane == ids[:, 2:3], 1.0, 0.0)
        logits = jnp.dot(normed2_ref[span, :], router_ref[...], preferred_element_type=F32)
        gap = jnp.sum(logits * sign, axis=1, keepdims=True)
        gate0, gate1 = 1.0 / (1.0 + jnp.exp(gap)), 1.0 / (1.0 + jnp.exp(-gap))
        cot = cot_ref[span, :].astype(F32)
        mixed = mixed_ref[span, :]
        gates_ref[span, :] = jnp.where(lane == 0, gate0, gate1)
        grad_gap = jnp.sum(gaps[span, :], axis=1, keepdims=True)
        slope = gate0 * gate1 * grad_gap * sign
        slopes[span, :] = slope
        grad_normed2 = picked[span, :] + sum(
            contract(part, router_ref[...], 1, 1) for part in split_parts(slope)
        )
        scale = lax.rsqrt(jnp.mean(mixed * mixed, axis=1, keepdims=True) + EPS)
        inner = grad_normed2 * gain_ref[...]
        mean = jnp.mean(inner * mixed, axis=1, keepdims=True)
        grad_mixed = cot + scale * inner - mixed * (scale * scale * scale * mean)
        grad_mixed_ref[span, :] = grad_mixed
        grad_branch_ref[span, :] = grad_mixed.astype(BF)
        return total + jnp.sum(grad_normed2 * mixed * scale, axis=0, keepdims=True)

    grad_norm2_ref[...] = lax.fori_loop(
        0, length // TILE, row_step, jnp.zeros((1, width), F32)
    )

    grad_heads_ref[...] = contract(grad_branch_ref[...], w_cat_ref[...], 1, 1).astype(BF)
    experts = grad_router_ref.shape[0]
    grad_router_ref[...] = sum(
        contract(part, normed2_ref[...], 0, 0) for part in split_parts(slopes[...])
    )[:experts]


def attend_back_kernel(
    normed2_far,
    cot_first,
    cot_last,
    routing_ref,
    router_ref,
    back_ref,
    slope_ref,
    columns_ref,
    mixed_ref,
    normed2_ref,
    cot_ref,
    gain_ref,
    w_cat_ref,
    qkv_hbm,
    probs_hbm,
    normed_hbm,
    query_hbm,
    key_hbm,
    value_hbm,
    attended_ref,
    far_rows_ref,
    far_scaled_ref,
    gates_ref,
    grad_mixed_ref,
    grad_router_ref,
    grad_norm2_ref,
    carry_ref,
    part_sum_ref,
    qkv_w_ref,
    out_w_ref,
    lines_ref,
    sums_ref,
    acc_ref,
    grad_branch_ref,
    grad_ref,
    slopes,
    gaps,
    pick,
    sends,
    cot_far,
    grads,
    qkv_ref,
    probs_ref,
    normed_ref,
    grad_qkv_ref,
    weight_ref,
    weight_sum,
    parts,
    landed,
    far_send,
    far_recv,
    hop_send,
    hop_recv,
    part_send,
    part_recv,
    load_sem,
    weight_sem,
    own_sem,
):
    z, d = lax.axis_index("head"), lax.axis_index("dp")
    replicas, length, columns = grads.shape
    _, groups, capacity, _ = sends.shape
    width = normed2_far.shape[1]
    heads = sums_ref.shape[0]
    pairs = heads // 2
    lanes = columns // pairs
    half = lanes // 2
    chunk = 2 * TILE
    hops = [3, 2, 1]
    order = [1, 3, 0, 2]

    def loads(turn):
        r, slot = order[turn], turn % 2
        return [
            pltpu.make_async_copy(source.at[r], target.at[slot], load_sem.at[i, slot])
            for i, (source, target) in enumerate(
                ((qkv_hbm, qkv_ref), (probs_hbm, probs_ref), (normed_hbm, normed_ref))
            )
        ]

    weight_loads = [
        pltpu.make_async_copy(
            source, weight_ref.at[:, pl.ds(i * columns, columns)], weight_sem.at[i]
        )
        for i, source in enumerate((query_hbm, key_hbm, value_hbm))
    ]
    for copy in loads(0) + weight_loads:
        copy.start()
    greet([{"dp": plane(d, o)} for o in PEERS] + [{"head": flipped(z, r)} for r in hops])
    copies = []
    combine_kernel(
        back_ref,
        slope_ref,
        columns_ref,
        mixed_ref,
        normed2_ref,
        cot_ref,
        router_ref,
        gain_ref,
        w_cat_ref,
        gates_ref,
        grad_mixed_ref,
        grad_branch_ref,
        grad_ref,
        grad_router_ref,
        grad_norm2_ref,
        part_sum_ref,
        slopes,
        gaps,
        pick,
    )
    arrivals = {}
    for r in [1, 3, 2]:
        arrivals[r] = remote(
            grad_ref.at[:, pl.ds(r * columns, columns)],
            grads.at[r],
            hop_send.at[r],
            hop_recv.at[r],
            {"head": flipped(z, r)},
        )
        arrivals[r].start()
    half_plane = groups // 2
    at = 0
    for piece in (cot_first, cot_last):
        cot_far[at : at + piece.shape[0]] = piece[...]
        at += piece.shape[0]
    logits = contract(router_ref[...], normed2_far[...], 0, 1)
    expert = lax.broadcasted_iota(jnp.int32, logits.shape, 0)
    routing = routing_ref[...]
    sign = jnp.where(expert == routing[3:4], 1.0, 0.0) - jnp.where(expert == routing[2:3], 1.0, 0.0)
    gap = jnp.sum(logits * sign, axis=0, keepdims=True)
    gate0, gate1 = 1.0 / (1.0 + jnp.exp(gap)), 1.0 / (1.0 + jnp.exp(-gap))

    def dispatch(start):
        span = slice(start, start + half_plane)
        first, second = selector(routing_ref, start * capacity, half_plane * capacity)
        gate = jnp.sum(first * gate0 + second * gate1, axis=1, keepdims=True)
        both = (first + second).astype(BF)
        shape = (half_plane, capacity, width)
        sends[0, span] = (
            jnp.dot(both, normed2_far[...], preferred_element_type=F32).astype(BF).reshape(shape)
        )
        sends[1, span] = (
            (jnp.dot(both, cot_far[...], preferred_element_type=F32) * gate)
            .astype(BF)
            .reshape(shape)
        )
        for o in range(start, start + half_plane):
            for i, out in enumerate((far_rows_ref, far_scaled_ref)):
                if o:
                    copy = remote(
                        sends.at[i, o],
                        out.at[o],
                        far_send.at[i, o],
                        far_recv.at[i, o],
                        {"dp": plane(d, o)},
                    )
                else:
                    copy = pltpu.make_async_copy(sends.at[i, 0], out.at[0], own_sem.at[i])
                copy.start()
                copies.append(copy)

    dispatch(half_plane)
    sums_ref[...] = jnp.zeros_like(sums_ref)
    grads[0] = grad_ref[:, :columns]

    near = {"head": flipped(z, 1)}

    def part_copy(i, source, target, peer):
        return remote(parts.at[source], landed.at[target], part_send.at[i], part_recv.at[i], peer)

    inner = part_copy(0, 3, 0, near)
    direct = part_copy(1, 1, 1, near)

    for copy in weight_loads:
        copy.wait()
    for turn, r in enumerate(order):
        slot = turn % 2
        if turn + 1 < replicas:
            for copy in loads(turn + 1):
                copy.start()
        for copy in loads(turn):
            copy.wait()
        if r:
            arrivals[r].wait_recv()

        def pair_step(pair, carry, slot=slot, r=r):
            def part_of(j):
                at = pl.multiple_of(j * columns + pair * lanes, lanes)
                return qkv_ref[slot, :, pl.ds(at, lanes)]

            at = pl.multiple_of(pair * lanes, lanes)
            query, value = part_of(0), part_of(2)
            key_t = part_of(1).T
            grad_all = grads[r, :, pl.ds(at, lanes)]
            grad_keys, grad_values = [], []
            for part in range(2):
                mask = lanes_of((length, lanes), half, part)
                grad = jnp.where(mask, grad_all, 0).astype(BF)
                grad_key = jnp.zeros((length, lanes), F32)
                grad_value = jnp.zeros((length, lanes), F32)
                for c in range(length // chunk):
                    cols = slice(c * chunk, (c + 1) * chunk)
                    grad_probs = contract(value, grad[cols], 1, 1)
                    probs_low = probs_ref[slot, pair * 2 + part, :, cols]
                    probs = probs_low.astype(F32)
                    delta = jnp.sum(probs * grad_probs, axis=0, keepdims=True)
                    grad_scores = (probs * (grad_probs - delta)).astype(BF)
                    grad_value += jnp.dot(probs_low, grad_all[cols], preferred_element_type=F32)
                    grad_key += jnp.dot(grad_scores, query[cols], preferred_element_type=F32)
                    acc_ref[part * half : (part + 1) * half, cols] = jnp.dot(
                        key_t[part * half : (part + 1) * half],
                        grad_scores,
                        preferred_element_type=F32,
                    )
                    for kb in range(length // TILE):
                        to = length - TILE * kb + chunk * c
                        sums_ref[pair * 2 + part, :, to : to + chunk] += grad_scores[
                            kb * TILE : (kb + 1) * TILE
                        ].astype(F32)
                grad_keys.append(grad_key)
                grad_values.append(grad_value)
            first = lanes_of((length, lanes), half, 0)
            results = (
                acc_ref[...].T * SCALE,
                jnp.where(first, *grad_keys) * SCALE,
                jnp.where(first, *grad_values),
            )
            for j, result in enumerate(results):
                to = pl.multiple_of(j * columns + pair * lanes, lanes)
                grad_qkv_ref[slot, :, pl.ds(to, lanes)] = result.astype(BF)
            return carry

        lax.fori_loop(0, pairs, pair_step, 0)

        parts[r] = contract(grad_qkv_ref[slot], weight_ref[...], 1, 1).astype(BF)
        if r == 3:
            inner.start()
            dispatch(0)
        if r == 1:
            direct.start()

        def weight_step(i, carry, slot=slot, turn=turn):
            cols = pl.ds(pl.multiple_of(i * 2 * chunk, 2 * chunk), 2 * chunk)
            value = contract(normed_ref[slot, :, cols], grad_qkv_ref[slot], 0, 0)
            if turn:
                value = value + weight_sum[cols, :]
            if turn + 1 < replicas:
                weight_sum[cols, :] = value
            else:
                qkv_w_ref[cols, :] = value.astype(BF)
            return carry

        lax.fori_loop(0, width // (2 * chunk), weight_step, 0)

    out_w_ref[...] = contract(attended_ref[...], grad_branch_ref[...], 0, 0).astype(BF)
    unskew_kernel(sums_ref, lines_ref)

    for r in hops:
        arrivals[r].wait_send()
    for copy in copies:
        copy.wait()
    inner.wait()
    carry_ref[...] = (parts[2].astype(F32) + landed[0].astype(F32)).astype(BF)
    direct.wait()
    part_sum_ref[...] = parts[0].astype(F32) + landed[1].astype(F32)


def attend_back(
    normed2_far,
    cot_pieces,
    routing_far,
    router,
    tokens,
    qkv,
    probs,
    normed,
    weights,
    attended,
    groups,
    capacity,
    experts,
):
    replicas, length, triple = qkv.shape
    heads = probs.shape[1]
    columns = triple // 3
    width = normed.shape[2]
    lanes = 2 * columns // heads
    far_shape = jax.ShapeDtypeStruct((groups, capacity, width), BF)
    vmem = pl.BlockSpec(memory_space=pltpu.VMEM)
    hbm = pl.BlockSpec(memory_space=pl.ANY)
    hop_sem = pltpu.SemaphoreType.DMA((replicas,))
    plane_sem = pltpu.SemaphoreType.DMA((2, groups))
    part_sem = pltpu.SemaphoreType.DMA((2,))
    return pl.pallas_call(
        attend_back_kernel,
        out_shape=(
            far_shape,
            far_shape,
            jax.ShapeDtypeStruct((length, TILE), F32),
            jax.ShapeDtypeStruct((length, width), F32),
            jax.ShapeDtypeStruct((experts, width), F32),
            jax.ShapeDtypeStruct((1, width), F32),
            jax.ShapeDtypeStruct((length, width), BF),
            jax.ShapeDtypeStruct((length, width), F32),
            jax.ShapeDtypeStruct((width, triple), BF),
            jax.ShapeDtypeStruct((replicas * columns, width), BF),
            jax.ShapeDtypeStruct((heads, 1, 2 * length), F32),
        ),
        in_specs=[vmem] * 13 + [hbm] * 6 + [vmem],
        out_specs=[hbm] * 2 + [vmem] * 9,
        scratch_shapes=[
            pltpu.VMEM((heads, TILE, 2 * length), F32),
            pltpu.VMEM((lanes, length), F32),
            pltpu.VMEM((length, width), BF),
            pltpu.VMEM((length, replicas * columns), BF),
            pltpu.VMEM((length, TILE), F32),
            pltpu.VMEM((length, TILE), F32),
            pltpu.VMEM((length, groups * capacity), BF),
            pltpu.VMEM((2, groups, capacity, width), BF),
            pltpu.VMEM((length, width), BF),
            pltpu.VMEM((replicas, length, columns), BF),
            pltpu.VMEM((2, length, triple), BF),
            pltpu.VMEM((2, heads, length, length), BF),
            pltpu.VMEM((2, length, width), BF),
            pltpu.VMEM((2, length, triple), BF),
            pltpu.VMEM((width, triple), BF),
            pltpu.VMEM((width, triple), F32),
            pltpu.VMEM((replicas, length, width), BF),
            pltpu.VMEM((2, length, width), BF),
            plane_sem,
            plane_sem,
            hop_sem,
            hop_sem,
            part_sem,
            part_sem,
            pltpu.SemaphoreType.DMA((3, 2)),
            pltpu.SemaphoreType.DMA((3,)),
            pltpu.SemaphoreType.DMA((2,)),
        ],
        compiler_params=pltpu.CompilerParams(
            vmem_limit_bytes=VMEM_MOST, collective_id=3, has_side_effects=True
        ),
        cost_estimate=pl.CostEstimate(
            flops=replicas * heads * 16 * length * length * lanes,
            bytes_accessed=replicas * heads * length * length * 4,
            transcendentals=0,
        ),
        name="attend_back",
    )(
        normed2_far,
        *cot_pieces,
        routing_far,
        router,
        *tokens,
        qkv,
        probs,
        normed,
        *weights,
        attended,
    )


def last_kernel(
    tile,
    far_hbm,
    scaled_hbm,
    scaled_here_hbm,
    gates_ref,
    routing_ref,
    gain_ref,
    gate_hbm,
    up_hbm,
    down_hbm,
    grad_gate_hbm,
    grad_up_hbm,
    hidden_hbm,
    qkv_w_hbm,
    out_w_hbm,
    rows_hbm,
    carry_hbm,
    part_sum_hbm,
    input_hbm,
    back_hbm,
    norm2_ref,
    router_grad_ref,
    lines_ref,
    wide_out,
    wide_came,
    tall_out,
    tall_came,
    qkv_w_out,
    out_w_out,
    small_out,
    grad_input_out,
    output_out,
    back_out,
    far_ref,
    scaled,
    scaled_here,
    left,
    weights,
    downs,
    units,
    hidden,
    hidden_here,
    send_wide,
    keep_wide,
    send_tall,
    keep_tall,
    qkv_land,
    qkv_sum,
    out_land,
    out_sum,
    out_hop,
    out_last,
    small_own,
    small_land,
    small_sum,
    small_hop,
    small_last,
    work,
    own_input,
    carried,
    stream_sem,
    hidden_sem,
    wide_send,
    wide_recv,
    keep_sem,
    tall_send,
    tall_recv,
    tall_keep,
    first_send,
    first_recv,
    hop_send,
    hop_recv,
    third_send,
    third_recv,
    carry_sem,
    back_send,
    back_recv,
    own_sem,
):
    z, d = lax.axis_index("head"), lax.axis_index("dp")
    slots, width = scaled_here.shape
    groups = qkv_land.shape[0]
    capacity = slots // groups
    length = own_input.shape[0]
    chunk = 2 * TILE
    _, rows, total_units = send_wide.shape
    half_units = hidden_here.shape[1]
    tiles = total_units // tile
    low, high = lax.rem(z, 2), z // 2
    keep_at = pl.multiple_of(low * rows, rows)
    send_at = pl.multiple_of((1 - low) * rows, rows)
    near = {"head": flipped(z, 1)}
    count = 2 * capacity
    hops = [3, 2, 1]

    def streams(t):
        slot = lax.rem(t, 2)
        at = pl.multiple_of(t * tile, tile)
        cols = pl.ds(at, tile)
        return [
            pltpu.make_async_copy(gate_hbm.at[:, cols], weights.at[slot, 0], stream_sem.at[0, slot]),
            pltpu.make_async_copy(up_hbm.at[:, cols], weights.at[slot, 1], stream_sem.at[1, slot]),
            pltpu.make_async_copy(down_hbm.at[cols, :], downs.at[slot], stream_sem.at[2, slot]),
            pltpu.make_async_copy(
                grad_gate_hbm.at[:, cols], units.at[slot, 0], stream_sem.at[3, slot]
            ),
            pltpu.make_async_copy(
                grad_up_hbm.at[:, cols], units.at[slot, 1], stream_sem.at[4, slot]
            ),
        ]

    wide = 2 * rows
    for copy in streams(0):
        copy.start()
    far_loads = [
        pltpu.make_async_copy(source, target, own_sem.at[6 + i])
        for i, (source, target) in enumerate(
            ((far_hbm, far_ref), (scaled_hbm, scaled), (scaled_here_hbm, scaled_here))
        )
    ]
    for copy in far_loads:
        copy.start()
    loads = [
        pltpu.make_async_copy(
            rows_hbm.at[:, pl.ds(pl.multiple_of(high * wide, wide), wide)], left, own_sem.at[2]
        ),
        pltpu.make_async_copy(part_sum_hbm, work.at[0], own_sem.at[3]),
        pltpu.make_async_copy(
            input_hbm.at[pl.ds(pl.multiple_of(z * length, length), length)], own_input, own_sem.at[5]
        ),
    ]
    for copy in loads:
        copy.start()

    half_copy = pltpu.make_async_copy(
        hidden_hbm.at[:, pl.ds(pl.multiple_of(high * half_units, TILE), half_units)],
        hidden_here,
        hidden_sem,
    )
    half_copy.start()
    greet([{"dp": plane(d, o)} for o in PEERS] + [{"head": flipped(z, r)} for r in hops])

    carry = remote(
        carry_hbm, carried, carry_sem.at[0], carry_sem.at[1], {"head": flipped(z, 2)}
    )
    carry.start()
    for copy in far_loads[:2] + loads[:1]:
        copy.wait()
    columns = pl.ds(pl.multiple_of(high * wide, wide), wide)

    def wide_copy(i, t):
        at = pl.multiple_of(t * tile, tile)
        return remote(
            send_wide.at[i, :, pl.ds(at, tile)],
            wide_came.at[i, :, pl.ds(at, tile)],
            wide_send.at[i, t],
            wide_recv.at[i, t],
            near,
        )

    def keep_copy(i, t):
        at = pl.multiple_of(t * tile, tile)
        slot = lax.rem(t, 2)
        return pltpu.make_async_copy(
            keep_wide.at[i, slot], wide_out.at[i, :, pl.ds(at, tile)], keep_sem.at[i, slot]
        )

    def tile_step(t, carry):
        slot = lax.rem(t, 2)
        at = pl.multiple_of(t * tile, tile)

        @pl.when(t + 1 < tiles)
        def _():
            for copy in streams(t + 1):
                copy.start()

        for copy in streams(t):
            copy.wait()

        def chunk_step(j, inner):
            span = pl.ds(pl.multiple_of(j * count, count), count)
            values = expert_tile(
                far_ref[span], scaled[span], weights[slot, 0], weights[slot, 1], downs[slot]
            )
            hidden[span, pl.ds(at, tile)] = values[0]
            units[slot, 2, span, :] = values[1]
            units[slot, 3, span, :] = values[2]
            return inner

        lax.fori_loop(0, groups // 2, chunk_step, 0)
        @pl.when(t >= 2)
        def _():
            for i in range(2):
                keep_copy(i, t - 2).wait()

        for i in range(2):
            value = contract(left[...], units[slot, i], 0, 0) + contract(
                far_ref[:, columns], units[slot, 2 + i], 0, 0
            )
            upper = low == 1
            send_wide[i, :, pl.ds(at, tile)] = jnp.where(
                upper, value[:rows], value[rows:]
            ).astype(BF)
            keep_wide[i, slot] = jnp.where(upper, value[rows:], value[:rows])
            wide_copy(i, t).start()
            keep_copy(i, t).start()
        return carry

    tile_step(jnp.int32(0), 0)

    first = []
    for o in PEERS:
        peer = plane(d, o)
        for i, (source, target) in enumerate(
            (
                (qkv_w_hbm.at[peer], qkv_land.at[o]),
                (out_w_hbm.at[:, peer], out_land.at[o]),
            )
        ):
            copy = remote(source, target, first_send.at[i, o], first_recv.at[i, o], {"dp": peer})
            copy.start()
            first.append(copy)
    own = [
        pltpu.make_async_copy(qkv_w_hbm.at[d], qkv_land.at[0], own_sem.at[0]),
        pltpu.make_async_copy(out_w_hbm.at[:, d], out_land.at[0], own_sem.at[1]),
    ]
    for copy in own:
        copy.start()

    backs = []
    for o in PEERS:
        copy = remote(
            back_hbm.at[o], back_out.at[o], back_send.at[o], back_recv.at[o], {"dp": plane(d, o)}
        )
        copy.start()
        backs.append(copy)
    backs.append(pltpu.make_async_copy(back_hbm.at[0], back_out.at[0], back_send.at[0]))
    backs[-1].start()
    lax.fori_loop(1, tiles, tile_step, 0)

    carry.wait()
    for copy in loads[1:]:
        copy.wait()

    def norm_step(i, total):
        span = pl.ds(pl.multiple_of(i * TILE, TILE), TILE)
        grad_normed = work[0, span, :] + carried[span, :].astype(F32)
        value = own_input[span, :].astype(F32)
        scale = lax.rsqrt(jnp.mean(value * value, axis=1, keepdims=True) + EPS)
        inner = grad_normed * gain_ref[...]
        mean = jnp.mean(inner * value, axis=1, keepdims=True)
        work[1, span, :] = scale * inner - value * (scale * scale * scale * mean)
        return total + jnp.sum(grad_normed * value * scale, axis=0, keepdims=True)

    heads = lines_ref.shape[0]
    small_own[...] = jnp.zeros_like(small_own)
    small_own[0:1] = lax.fori_loop(0, length // TILE, norm_step, jnp.zeros((1, width), F32))
    small_own[1:2] = norm2_ref[...]
    for h in range(heads):
        small_own[2 + h : 3 + h] = lines_ref[h]
    small_own[8:] = router_grad_ref[...]
    ends = [pltpu.make_async_copy(work.at[1], grad_input_out, own_sem.at[4])]
    for copy in ends:
        copy.start()
    small = []

    def lanes(index):
        return pl.ds(pl.multiple_of(index * TILE, TILE), TILE)

    for o in PEERS:
        peer = plane(d, o)
        copy = remote(
            small_own.at[:, lanes(peer)],
            small_land.at[o],
            first_send.at[2, o],
            first_recv.at[2, o],
            {"dp": peer},
        )
        copy.start()
        small.append(copy)
    small_land[0] = small_own[:, lanes(d)]

    for copy in first:
        copy.wait()
    for copy in own:
        copy.wait()
    qkv_sum[...] = sum(qkv_land[o].astype(F32) for o in range(groups)).astype(BF)
    out_sum[...] = sum(out_land[o].astype(F32) for o in range(groups)).astype(BF)
    second = []
    for o in PEERS:
        copy = remote(
            qkv_sum, qkv_w_out.at[d], third_send.at[0, o], third_recv.at[0, o], {"dp": plane(d, o)}
        )
        copy.start()
        second.append(copy)
    mine = [pltpu.make_async_copy(qkv_sum, qkv_w_out.at[d], own_sem.at[0])]
    mine[0].start()
    over = []
    for r in hops:
        copy = remote(
            out_sum.at[r], out_hop.at[r], hop_send.at[0, r], hop_recv.at[0, r], {"head": flipped(z, r)}
        )
        copy.start()
        over.append(copy)

    half_copy.wait()
    far_loads[2].wait()
    share = half_units // 2
    halves = pl.ds(pl.multiple_of(high * half_units, TILE), half_units)

    def tall_copies(i):
        cols = pl.ds(pl.multiple_of(i * tile, tile), tile)
        return [
            remote(
                send_tall.at[:, cols], tall_came.at[:, cols], tall_send.at[i], tall_recv.at[i], near
            ),
            pltpu.make_async_copy(keep_tall.at[:, cols], tall_out.at[:, cols], tall_keep.at[i]),
        ]

    def tall_step(i, carry):
        cols = pl.ds(pl.multiple_of(i * tile, tile), tile)
        value = contract(hidden_here[...], scaled_here[:, cols], 0, 0) + contract(
            hidden[:, halves], scaled[:, cols], 0, 0
        )
        upper = low == 1
        send_tall[:, cols] = jnp.where(upper, value[:share], value[share:]).astype(BF)
        keep_tall[:, cols] = jnp.where(upper, value[share:], value[:share])
        for copy in tall_copies(i):
            copy.start()
        return carry

    lax.fori_loop(0, width // tile, tall_step, 0)
    for copy in small:
        copy.wait()
    small_sum[...] = sum(small_land[o] for o in range(groups))
    small_over = []
    for r in hops:
        copy = remote(
            small_sum, small_hop.at[r], hop_send.at[1, r], hop_recv.at[1, r], {"head": flipped(z, r)}
        )
        copy.start()
        small_over.append(copy)

    for copy in backs:
        copy.wait()
    rows_back = [
        pltpu.make_async_copy(
            back_out.at[o], hidden.at[o * capacity : (o + 1) * capacity, :width], back_recv.at[o]
        )
        for o in range(groups)
    ]
    for copy in rows_back:
        copy.start()
    for k, pick in enumerate(token_selector(routing_ref, slots)):
        hidden_here[k * length : (k + 1) * length, :slots] = pick.astype(BF)
    for copy in rows_back:
        copy.wait()

    def output_step(i, carry):
        cols = pl.ds(pl.multiple_of(i * chunk, chunk), chunk)
        work[0, :, cols] = sum(
            gates_ref[:, k : k + 1]
            * jnp.dot(
                hidden_here[k * length : (k + 1) * length, :slots],
                hidden[:, cols],
                preferred_element_type=F32,
            )
            for k in range(2)
        )
        return carry

    lax.fori_loop(0, width // chunk, output_step, 0)
    ends.append(pltpu.make_async_copy(work.at[0], output_out, own_sem.at[3]))
    ends[1].start()

    for copy in small_over:
        copy.wait()
    small_last[0] = small_sum[...]
    small_last[1] = small_sum[...] + sum(small_hop[r] for r in hops)
    small_out[:, :, lanes(d)] = small_last[...]
    for o in PEERS:
        copy = remote(
            small_last,
            small_out.at[:, :, lanes(d)],
            third_send.at[2, o],
            third_recv.at[2, o],
            {"dp": plane(d, o)},
        )
        copy.start()
        second.append(copy)
    for copy in over:
        copy.wait()
    out_last[...] = (
        out_sum[0].astype(F32) + sum(out_hop[r].astype(F32) for r in hops)
    ).astype(BF)
    for o in PEERS:
        copy = remote(
            out_last,
            out_w_out.at[d],
            third_send.at[1, o],
            third_recv.at[1, o],
            {"dp": plane(d, o)},
        )
        copy.start()
        second.append(copy)
    mine.append(pltpu.make_async_copy(out_last, out_w_out.at[d], own_sem.at[1]))
    mine[1].start()

    for i in range(2):
        for t in (tiles - 2, tiles - 1):
            keep_copy(i, t).wait()

    def wide_end(t, carry):
        for i in range(2):
            wide_copy(i, t).wait()
        return carry

    lax.fori_loop(0, tiles, wide_end, 0)
    for copy in second + mine + ends:
        copy.wait()

    def tall_end(i, carry):
        for copy in tall_copies(i):
            copy.wait()
        return carry

    lax.fori_loop(0, width // tile, tall_end, 0)


def last_stage(
    far, here, tokens, weights, grads_here, hidden_here, sums, finish, small, tile
):
    gate_w, up_w, down_w = weights
    width, units = gate_w.shape
    qkv_w, out_w = sums
    replicas, groups, part_rows, _ = out_w.shape
    slots = far[0].shape[0]
    length = tokens[0].shape[0]
    back = finish[-1]
    vmem = pl.BlockSpec(memory_space=pltpu.VMEM)
    hbm = pl.BlockSpec(memory_space=pl.ANY)
    rows, share = width // replicas, units // replicas
    small_shape = (8 + groups, width)
    plane_sem = pltpu.SemaphoreType.DMA((3, groups))
    hop_sem = pltpu.SemaphoreType.DMA((2, replicas))
    return pl.pallas_call(
        functools.partial(last_kernel, tile),
        out_shape=(
            jax.ShapeDtypeStruct((2, rows, units), F32),
            jax.ShapeDtypeStruct((2, rows, units), BF),
            jax.ShapeDtypeStruct((share, width), F32),
            jax.ShapeDtypeStruct((share, width), BF),
            jax.ShapeDtypeStruct(qkv_w.shape, BF),
            jax.ShapeDtypeStruct(out_w.shape[1:], BF),
            jax.ShapeDtypeStruct((2,) + small_shape, F32),
            jax.ShapeDtypeStruct((length, width), F32),
            jax.ShapeDtypeStruct((length, width), F32),
            jax.ShapeDtypeStruct(back.shape, BF),
        ),
        in_specs=[hbm] * 3 + [vmem] * 3 + [hbm] * 13 + [vmem] * 3,
        out_specs=[hbm] * 6 + [vmem] + [hbm] * 3,
        scratch_shapes=[
            pltpu.VMEM((slots, width), BF),
            pltpu.VMEM((slots, width), BF),
            pltpu.VMEM((slots, width), BF),
            pltpu.VMEM((slots, 2 * rows), BF),
            pltpu.VMEM((2, 2, width, tile), BF),
            pltpu.VMEM((2, tile, width), BF),
            pltpu.VMEM((2, 4, slots, tile), BF),
            pltpu.VMEM((slots, units), BF),
            pltpu.VMEM((slots, units // 2), BF),
            pltpu.VMEM((2, rows, units), BF),
            pltpu.VMEM((2, 2, rows, tile), F32),
            pltpu.VMEM((share, width), BF),
            pltpu.VMEM((share, width), F32),
            pltpu.VMEM(qkv_w.shape, BF),
            pltpu.VMEM(qkv_w.shape[1:], BF),
            pltpu.VMEM((groups, replicas, part_rows, width), BF),
            pltpu.VMEM((replicas, part_rows, width), BF),
            pltpu.VMEM((replicas, part_rows, width), BF),
            pltpu.VMEM((part_rows, width), BF),
            pltpu.VMEM(small_shape, F32),
            pltpu.VMEM((groups, small_shape[0], TILE), F32),
            pltpu.VMEM((small_shape[0], TILE), F32),
            pltpu.VMEM((replicas, small_shape[0], TILE), F32),
            pltpu.VMEM((2, small_shape[0], TILE), F32),
            pltpu.VMEM((2, length, width), F32),
            pltpu.VMEM((length, width), BF),
            pltpu.VMEM((length, width), BF),
            pltpu.SemaphoreType.DMA((5, 2)),
            pltpu.SemaphoreType.DMA,
            pltpu.SemaphoreType.DMA((2, units // tile)),
            pltpu.SemaphoreType.DMA((2, units // tile)),
            pltpu.SemaphoreType.DMA((2, 2)),
            pltpu.SemaphoreType.DMA((width // tile,)),
            pltpu.SemaphoreType.DMA((width // tile,)),
            pltpu.SemaphoreType.DMA((width // tile,)),
            plane_sem,
            plane_sem,
            hop_sem,
            hop_sem,
            plane_sem,
            plane_sem,
            pltpu.SemaphoreType.DMA((2,)),
            pltpu.SemaphoreType.DMA((groups,)),
            pltpu.SemaphoreType.DMA((groups,)),
            pltpu.SemaphoreType.DMA((9,)),
        ],
        compiler_params=pltpu.CompilerParams(
            vmem_limit_bytes=VMEM_MOST, collective_id=4, has_side_effects=True
        ),
        cost_estimate=pl.CostEstimate(
            flops=12 * slots * width * units,
            bytes_accessed=6 * width * units + 6 * slots * units,
            transcendentals=slots * units,
        ),
        name="last_stage",
    )(
        *far,
        here[1],
        *tokens,
        gate_w,
        up_w,
        down_w,
        *grads_here,
        hidden_here,
        qkv_w,
        out_w,
        here[0],
        *finish,
        *small,
    )


def finish_kernel(
    wide_kept,
    wide_came,
    tall_kept,
    tall_came,
    qkv_ref,
    out_ref,
    mixed_ref,
    expert_ref,
    grad_mixed_ref,
    grad_first_ref,
    summed_ref,
    line_ref,
    output_ref,
    grad_input_ref,
    query_out,
    key_out,
    value_out,
    out_out,
    gate_out,
    up_out,
    down_out,
    norm1_out,
    norm2_out,
    bias_out,
    router_out,
):
    output_ref[...] = mixed_ref[...] + expert_ref[...]
    grad_input_ref[...] = grad_mixed_ref[...] + grad_first_ref[...]
    gate_out[...] = wide_kept[0] + wide_came[0].astype(F32)
    up_out[...] = wide_kept[1] + wide_came[1].astype(F32)
    down_out[...] = tall_kept[...] + tall_came[...].astype(F32)
    columns = query_out.shape[1]
    for i, out in enumerate((query_out, key_out, value_out)):
        value = qkv_ref[:, :, i * columns : (i + 1) * columns].astype(F32)
        out[...] = value.reshape(out.shape)
    out_out[...] = out_ref[...].astype(F32).reshape(out_out.shape)

    @pl.when(pl.program_id(0) == 0)
    def _():
        norm1_out[...] = summed_ref[1, :1]
        norm2_out[...] = summed_ref[1, 1:2]
        heads = bias_out.shape[0]
        buckets = line_ref[...].astype(BF)
        total = sum(contract(term, buckets, 1, 1) for term in split_parts(summed_ref[0, :8]))
        bias_out[...] = total[2 : 2 + heads]
        router_out[...] = summed_ref[1, 8:]


def finish(wide, tall, qkv_w, out_w, tokens, summed, line, heads):
    steps = 4
    groups, part_rows, triple = qkv_w.shape
    _, out_rows, width = out_w.shape
    _, rows, units = wide[0].shape
    share = tall[0].shape[0]
    length = tokens[0].shape[0]
    columns = triple // 3
    experts = summed.shape[1] - 8

    def cut(shape, axis=0):
        block = tuple(n // steps if i == axis else n for i, n in enumerate(shape))
        return pl.BlockSpec(block, lambda t: tuple(t if i == axis else 0 for i in range(len(shape))))

    def whole(shape):
        return pl.BlockSpec(shape, lambda t: (0,) * len(shape))

    outs = [
        (length, width),
        (length, width),
        (groups * part_rows, columns),
        (groups * part_rows, columns),
        (groups * part_rows, columns),
        (groups * out_rows, width),
        (rows, units),
        (rows, units),
        (share, width),
    ]
    small = [(1, width), (1, width), (heads, line.shape[0]), (experts, width)]
    return pl.pallas_call(
        finish_kernel,
        out_shape=[jax.ShapeDtypeStruct(shape, F32) for shape in outs + small],
        grid=(steps,),
        in_specs=[cut(value.shape, 1) for value in wide]
        + [cut(value.shape) for value in tall]
        + [cut(qkv_w.shape), cut(out_w.shape)]
        + [cut(value.shape) for value in tokens]
        + [whole(summed.shape), whole(line.shape)],
        out_specs=[cut(shape) for shape in outs] + [whole(shape) for shape in small],
        compiler_params=pltpu.CompilerParams(vmem_limit_bytes=VMEM_MOST),
        cost_estimate=pl.CostEstimate(
            flops=4 * rows * units, bytes_accessed=48 * rows * units, transcendentals=0
        ),
        name="finish",
    )(*wide, *tall, qkv_w, out_w, *tokens, summed, line)


def expert_forward(rows, gate_w, up_w, grad_unscaled, slot_gates):
    gate_pre = jnp.dot(rows, gate_w, preferred_element_type=F32)
    up_pre = jnp.dot(rows, up_w, preferred_element_type=F32)
    hidden, pull = jax.vjp(geglu, gate_pre, up_pre)
    grad_gate_pre, grad_up_pre = pull(grad_unscaled * slot_gates)
    return hidden.astype(BF), grad_gate_pre.astype(BF), grad_up_pre.astype(BF)


def body_plain(
    block_input,
    cotangent,
    expert_ids,
    priority,
    rel_bucket,
    norm1_gain,
    w_query,
    w_key,
    w_value,
    w_out,
    pos_bias,
    norm2_gain,
    w_router,
    w_gate,
    w_up,
    w_down,
):
    group_rows, width = block_input.shape
    own_rows = cotangent.shape[0]
    buckets, heads_here = pos_bias.shape
    head_cols = w_query.shape[1]
    length = (rel_bucket.shape[0] + 1) // 2
    sequences = group_rows // length
    experts = w_router.shape[1]
    capacity = 5 * 2 * own_rows // (4 * experts)
    slot_count = experts * capacity
    replicas = lax.axis_size("head")
    groups = lax.axis_size("dp")
    me = lax.axis_index("head")
    far = replicas // 2
    far_perm = [(i, i ^ far) for i in range(replicas)]
    stepwise = own_rows == length and sequences == replicas

    def hop(value, r):
        return lax.ppermute(value, "head", [(i, i ^ r) for i in range(replicas)])

    def exchange(value):
        parts = value.reshape(experts, capacity, -1)
        return lax.all_to_all(parts, "dp", split_axis=0, concat_axis=0, tiled=True).reshape(
            slot_count, -1
        )

    dest = route_slots(expert_ids, priority[0], experts, capacity)
    dest_far = lax.ppermute(dest, "head", far_perm)
    slot_range = jnp.arange(slot_count, dtype=jnp.int32)[None, :]
    picks = [(dest[:, k : k + 1] == slot_range).astype(BF) for k in range(2)]
    both = picks[0] + picks[1]
    both_far = sum((dest_far[:, k : k + 1] == slot_range).astype(BF) for k in range(2))

    down_w, gate_w, up_w = w_down[0], w_gate[0], w_up[0]
    cot_here = exchange(contract(both, cotangent, 0, 0).astype(BF))
    cot_far_own = lax.ppermute(cotangent, "head", far_perm)
    cot_far = exchange(contract(both_far, cot_far_own, 0, 0).astype(BF))
    unscaled_here = contract(cot_here, down_w, 1, 1)
    unscaled_far = contract(cot_far, down_w, 1, 1)

    dp_at = lax.axis_index("dp")
    out_rows = head_cols // groups
    piece = lax.dynamic_slice_in_dim(w_out, dp_at * out_rows, out_rows, 0)
    w_out_all = lax.all_gather(piece, ("head", "dp"), axis=0, tiled=True)
    w_qkv = jnp.concatenate([w_query, w_key, w_value], axis=1)
    qkv_rows = width // groups
    piece = lax.dynamic_slice_in_dim(w_qkv, dp_at * qkv_rows, qkv_rows, 0)
    w_qkv_all = lax.all_gather(piece, ("head", "dp"), axis=0, tiled=True)
    if stepwise:
        order = [me ^ r for r in range(replicas)]
    else:
        order = list(range(replicas))
    w_out_all = w_out_all.reshape(replicas, head_cols, width)
    w_qkv_all = w_qkv_all.reshape(replicas, width, 3 * head_cols)
    w_out_cat = jnp.concatenate(
        [lax.dynamic_index_in_dim(w_out_all, o, 0, keepdims=False) for o in order], axis=0
    )

    inputs_all = block_input.astype(F32)
    normed = rms_norm(inputs_all, norm1_gain).astype(BF)
    qkv = jnp.dot(normed, w_qkv, preferred_element_type=F32).astype(BF)
    line = (rel_bucket[::-1][None, :] == jnp.arange(buckets, dtype=jnp.int32)[:, None]).astype(F32)
    line = jnp.pad(line, ((0, 0), (1, 0)))
    table = skew(contract(pos_bias, line, 0, 0, HIGH))
    kept = {}
    if stepwise:
        blocks = [None] * replicas
        for r in reversed(range(replicas)):
            attended_seq, probs = attend_fwd(order[r].reshape(1), qkv, table, length)
            kept[r] = probs
            blocks[r] = hop(attended_seq, r) if r else attended_seq
    else:
        seqs = []
        for s in range(sequences):
            attended_seq, kept[s] = attend_fwd(jnp.full((1,), s, jnp.int32), qkv, table, length)
            seqs.append(attended_seq)
        attended_all = jnp.concatenate(seqs, axis=0).reshape(replicas, own_rows, head_cols)
        attended_all = lax.all_to_all(attended_all, "head", split_axis=0, concat_axis=0, tiled=True)
        blocks = [attended_all[i] for i in range(replicas)]
    attended = jnp.concatenate(blocks, axis=1)

    branch = jnp.dot(attended, w_out_cat, preferred_element_type=F32)
    start_own = me * own_rows
    inputs_own = lax.dynamic_slice_in_dim(block_input, start_own, own_rows, 0).astype(F32)
    mixed = inputs_own + branch
    normed2_full, norm2_pull = jax.vjp(rms_norm, mixed, norm2_gain)
    normed2 = normed2_full.astype(BF)
    logits = jnp.dot(normed2, w_router, preferred_element_type=F32)
    expert_range = jnp.arange(experts, dtype=jnp.int32)
    chosen = (expert_ids[:, :, None] == expert_range[None, None, :]).astype(F32)
    gates = jax.nn.softmax(jnp.sum(chosen * logits[:, None, :], axis=2), axis=-1)

    def slot_gates_of(places, values):
        terms = sum(
            jnp.where(places[:, k : k + 1] == slot_range, values[:, k : k + 1], 0.0)
            for k in range(2)
        )
        return jnp.sum(terms, axis=0)

    rows_here = exchange(contract(both, normed2, 0, 0).astype(BF))
    gates_here = exchange(slot_gates_of(dest, gates))
    normed2_far = lax.ppermute(normed2, "head", far_perm)
    gates_far_own = lax.ppermute(gates, "head", far_perm)
    rows_far = exchange(contract(both_far, normed2_far, 0, 0).astype(BF))
    gates_far = exchange(slot_gates_of(dest_far, gates_far_own))

    hidden_here, ggp_here, gup_here = expert_forward(
        rows_here, gate_w, up_w, unscaled_here, gates_here
    )
    returned = jnp.dot(hidden_here, down_w, preferred_element_type=F32).astype(BF)
    came_back = exchange(returned)
    grad_routed = (contract(ggp_here, gate_w, 1, 1) + contract(gup_here, up_w, 1, 1)).astype(BF)
    grad_back = exchange(grad_routed)
    hidden_far, ggp_far, gup_far = expert_forward(rows_far, gate_w, up_w, unscaled_far, gates_far)
    scaled_here = (cot_here.astype(F32) * gates_here).astype(BF)
    scaled_far = (cot_far.astype(F32) * gates_far).astype(BF)

    low = me % far
    high = me // far

    def reduced(lefts, rights):
        rows = lefts[0].shape[1] // replicas

        def part(at):
            return sum(
                contract(lax.dynamic_slice_in_dim(left, at * rows, rows, 1), right, 0, 0)
                for left, right in zip(lefts, rights)
            )

        if far == 2:
            sent = hop(part(high * far + (1 - low)).astype(BF), 1)
            return (part(me) + sent.astype(F32))[None]
        whole = jnp.concatenate([part(high * far + i) for i in range(far)], axis=0).astype(BF)
        member = [[h * far + i for i in range(far)] for h in range(2)]
        return lax.psum_scatter(
            whole, "head", scatter_dimension=0, axis_index_groups=member, tiled=True
        ).astype(F32)[None]

    grad_down_w = reduced((hidden_here, hidden_far), (scaled_here, scaled_far))
    grad_gate_w = reduced((rows_here, rows_far), (ggp_here, ggp_far))
    grad_up_w = reduced((rows_here, rows_far), (gup_here, gup_far))

    chosen_rows = [jnp.dot(pick, came_back, preferred_element_type=F32) for pick in picks]
    output = mixed + sum(gates[:, k : k + 1] * chosen_rows[k] for k in range(2))
    grad_output = cotangent.astype(F32)
    grad_gates = jnp.stack([jnp.sum(grad_output * rows, axis=1) for rows in chosen_rows], axis=1)
    grad_normed2 = jnp.dot(both, grad_back, preferred_element_type=F32)
    grad_picked = gates * (grad_gates - jnp.sum(gates * grad_gates, axis=1, keepdims=True))
    grad_logits = jnp.sum(chosen * grad_picked[:, :, None], axis=1)
    grad_normed2 = grad_normed2 + contract(grad_logits, w_router.astype(F32), 1, 1, HIGH)
    grad_router = contract(normed2.astype(F32), grad_logits, 0, 0, HIGH)
    grad_mixed, grad_norm2 = norm2_pull(grad_normed2)
    grad_mixed = grad_mixed + grad_output
    grad_branch = grad_mixed.astype(BF)

    grad_wout = contract(attended, grad_branch, 0, 0).astype(BF)
    grad_wout = grad_wout.reshape(replicas, groups, out_rows, width)
    grad_wout = lax.psum_scatter(grad_wout, "dp", scatter_dimension=1, tiled=True)[:, 0]
    if stepwise:
        grad_wout = sum(
            (hop(grad_wout[r], r) if r else grad_wout[r]).astype(F32) for r in range(replicas)
        ).astype(BF)
    else:
        grad_wout = lax.psum_scatter(
            grad_wout.reshape(replicas * out_rows, width), "head", scatter_dimension=0, tiled=True
        )
    grad_out_proj = lax.all_gather(grad_wout, "dp", axis=0, tiled=True).astype(F32)

    grad_heads = contract(grad_branch, w_out_cat, 1, 1).astype(BF)
    sums = jnp.zeros((heads_here, TILE, 2 * length), F32)
    grad_blocks = [grad_heads[:, i * head_cols : (i + 1) * head_cols] for i in range(replicas)]
    grad_total = None
    weight_terms = []
    if stepwise:
        arrived = [hop(grad_blocks[r], r) if r else grad_blocks[0] for r in range(replicas)]
        for r in (0, 2, 3, 1):
            grad_qkv, sums = attend_bwd(order[r].reshape(1), qkv, arrived[r], kept[r], sums, length)
            normed_seq = lax.dynamic_slice_in_dim(normed, order[r] * length, length, 0)
            weight_terms.append(contract(normed_seq, grad_qkv, 0, 0))
            mine = hop(grad_qkv, r) if r else grad_qkv
            weight = lax.dynamic_index_in_dim(w_qkv_all, order[r], 0, keepdims=False)
            term = contract(mine, weight, 1, 1)
            grad_total = term if grad_total is None else grad_total + term
        grad_normed = grad_total
        grad_qkv_w = sum(weight_terms)
    else:
        stacked = jnp.stack(grad_blocks, axis=0)
        stacked = lax.all_to_all(stacked, "head", split_axis=0, concat_axis=0, tiled=True)
        stacked = stacked.reshape(group_rows, head_cols)
        seqs = []
        for s in range(sequences):
            grad_seq = stacked[s * length : (s + 1) * length]
            grad_qkv, sums = attend_bwd(
                jnp.full((1,), s, jnp.int32), qkv, grad_seq, kept[s], sums, length
            )
            seqs.append(grad_qkv)
        grad_qkv = jnp.concatenate(seqs, axis=0)
        grad_qkv_w = contract(normed, grad_qkv, 0, 0)
        grad_qkv = lax.all_to_all(
            grad_qkv.reshape(replicas, own_rows, 3 * head_cols),
            "head",
            split_axis=0,
            concat_axis=0,
            tiled=True,
        )
        grad_normed = sum(contract(grad_qkv[i], w_qkv_all[i], 1, 1) for i in range(replicas))

    _, norm1_pull = jax.vjp(rms_norm, inputs_own, norm1_gain)
    grad_first, grad_norm1 = norm1_pull(grad_normed)
    grad_input = grad_mixed + grad_first
    grad_bias = contract(unskew(sums), line, 1, 1, HIGH)
    grad_qkv_w, grad_bias = lax.psum((grad_qkv_w.astype(BF), grad_bias), "dp")
    grad_qkv_w = grad_qkv_w.astype(F32)
    grad_norm1, grad_norm2, grad_router = lax.psum(
        (grad_norm1, grad_norm2, grad_router), ("dp", "head")
    )
    return (
        output,
        grad_input,
        grad_norm1,
        grad_qkv_w[:, :head_cols],
        grad_qkv_w[:, head_cols : 2 * head_cols],
        grad_qkv_w[:, 2 * head_cols :],
        grad_out_proj,
        jnp.transpose(grad_bias),
        grad_norm2,
        grad_router,
        grad_gate_w,
        grad_up_w,
        grad_down_w,
    )


def body(*args):
    block_input, cotangent, rel_bucket, pos_bias, w_gate, w_router = (
        args[0],
        args[1],
        args[4],
        args[10],
        args[13],
        args[12],
    )
    own_rows = cotangent.shape[0]
    length = (rel_bucket.shape[0] + 1) // 2
    replicas, groups = lax.axis_size("head"), lax.axis_size("dp")
    experts = w_router.shape[1]
    capacity = 5 * 2 * own_rows // (4 * experts)
    stepwise = (
        own_rows == length
        and block_input.shape[0] == replicas * length
        and replicas == 4
        and groups == 8
        and experts == groups
        and capacity % 16 == 0
        and pos_bias.shape[1] in (2, 4, 6)
        and w_gate.shape[2] % 256 == 0
    )
    return body_steps(*args) if stepwise else body_plain(*args)


def body_steps(
    block_input,
    cotangent,
    expert_ids,
    priority,
    rel_bucket,
    norm1_gain,
    w_query,
    w_key,
    w_value,
    w_out,
    pos_bias,
    norm2_gain,
    w_router,
    w_gate,
    w_up,
    w_down,
):
    group_rows, width = block_input.shape
    own_rows = cotangent.shape[0]
    buckets, heads_here = pos_bias.shape
    head_cols = w_query.shape[1]
    length = (rel_bucket.shape[0] + 1) // 2
    experts = w_router.shape[1]
    capacity = 5 * 2 * own_rows // (4 * experts)
    slot_count = experts * capacity
    replicas, groups = lax.axis_size("head"), lax.axis_size("dp")
    me, dp_at = lax.axis_index("head"), lax.axis_index("dp")

    dest = route_slots(expert_ids, priority[0], experts, capacity)
    bits = (dest // capacity) ^ dp_at
    position = sum(p * (bits == offset).astype(jnp.int32) for p, offset in enumerate(OFFSETS))
    mixed_dest = jnp.where(
        dest < slot_count,
        position * capacity + dest % capacity,
        slot_count,
    )
    routing = jnp.concatenate([mixed_dest, expert_ids], axis=1)
    routing_rows = jnp.pad(routing.T, ((0, 4), (0, 0)))
    routing_cols = routing
    router_wide = jnp.pad(w_router, ((0, 0), (0, TILE - experts)))
    line = (rel_bucket[::-1][None, :] == jnp.arange(buckets, dtype=jnp.int32)[:, None]).astype(F32)
    line = jnp.pad(line, ((0, 0), (1, 0)))
    input_weights = (w_query, w_key, w_value)
    (
        attended,
        probs,
        cot_here,
        normed,
        qkv,
        w_cat,
        cot_far,
        routing_far,
        mixed,
        normed2,
    ) = attend_all(
        block_input,
        norm1_gain[None, :],
        input_weights,
        contract(pos_bias, line, 0, 0, HIGH)[:, None, :],
        cotangent,
        routing_rows,
        w_out,
        norm2_gain[None, :],
        groups,
        capacity,
    )

    gate_w, up_w, down_w = w_gate[0], w_up[0], w_down[0]
    tile = 256
    (
        rows_here,
        hidden_here,
        ggp_here,
        gup_here,
        scaled_here,
        back,
        grad_back,
        slot_slope,
        normed2_far,
        cot_far_rest,
    ) = expert_stage(
        normed2,
        routing_rows,
        cot_here,
        router_wide,
        gate_w,
        up_w,
        down_w,
        cotangent,
        groups,
        capacity,
        tile,
    )

    (
        far_rows,
        far_scaled,
        gates,
        grad_mixed,
        grad_router,
        grad_norm2,
        carry,
        part_sum,
        grad_qkv_w,
        grad_wout,
        lines,
    ) = attend_back(
        normed2_far,
        (cot_far, cot_far_rest),
        routing_far,
        router_wide,
        (
            grad_back.reshape(slot_count, width),
            slot_slope.reshape(slot_count, TILE),
            routing_cols,
            mixed,
            normed2,
            cotangent,
            norm2_gain[None, :],
            w_cat,
        ),
        qkv,
        probs,
        normed,
        input_weights,
        attended,
        groups,
        capacity,
        experts,
    )

    (
        wide_kept,
        wide_came,
        tall_kept,
        tall_came,
        grad_qkv_w,
        grad_out_proj,
        summed,
        grad_first,
        expert_sum,
        _,
    ) = last_stage(
        (far_rows.reshape(slot_count, width), far_scaled.reshape(slot_count, width)),
        (rows_here.reshape(slot_count, width), scaled_here.reshape(slot_count, width)),
        (gates, routing_cols, norm1_gain[None, :]),
        (gate_w, up_w, down_w),
        (ggp_here, gup_here),
        hidden_here,
        (
            grad_qkv_w.reshape(groups, width // groups, 3 * head_cols),
            grad_wout.reshape(replicas, groups, head_cols // groups, width),
        ),
        (carry, part_sum, block_input, back),
        (grad_norm2, grad_router, lines),
        tile,
    )
    results = finish(
        (wide_kept, wide_came),
        (tall_kept, tall_came),
        grad_qkv_w,
        grad_out_proj,
        (mixed, expert_sum, grad_mixed, grad_first),
        summed,
        line,
        heads_here,
    )
    output, grad_input, grad_query_w, grad_key_w, grad_value_w, grad_out_proj = results[:6]
    grad_gate_w, grad_up_w, grad_down_w, grad_norm1, grad_norm2, grad_bias, grad_router = results[6:]
    return (
        output,
        grad_input,
        grad_norm1[0],
        grad_query_w,
        grad_key_w,
        grad_value_w,
        grad_out_proj,
        jnp.transpose(grad_bias),
        grad_norm2[0],
        jnp.transpose(grad_router),
        grad_gate_w[None],
        grad_up_w[None],
        grad_down_w[None],
    )


def solution(mesh):
    placed = (
        P("dp", None),
        P(("dp", "head"), None),
        P(("dp", "head"), None),
        P(("dp", "head"), None),
        P(),
        P(),
        P(None, "head"),
        P(None, "head"),
        P(None, "head"),
        P("head", None),
        P(None, "head"),
        P(),
        P(),
        P("dp", None, None),
        P("dp", None, None),
        P("dp", None, None),
    )
    return jax.shard_map(
        body,
        mesh=mesh,
        in_specs=placed,
        out_specs=(
            P(("dp", "head"), None),
            P(("dp", "head"), None),
            P(),
            P(None, "head"),
            P(None, "head"),
            P(None, "head"),
            P("head", None),
            P(None, "head"),
            P(),
            P(),
            P("dp", "head", None),
            P("dp", "head", None),
            P("dp", "head", None),
        ),
        check_vma=False,
    )
```
